32 devices in a mesh: node: 8 (over z, x), hid: 4 (over y, core).
Axes of the slice: x: 2, y: 2, z: 4, core: 2. Of those that a mesh axis runs over, the one named last changes fastest.
Arguments:
- node_in: bfloat16 [1280, 6, 512], P('node'), may hold values from -6 to 6
- edge_in: bfloat16 [10240, 512], P('node'), may hold values from -6 to 6
- cotangent: bfloat16 [1280, 6, 512], P(('node', 'hid')), may hold values from -6 to 6
- ocean_mask: int32 [1280], P(('node', 'hid')), may hold values 0 or 1
- present_mask: int32 [1280, 6], P(('node', 'hid')), may hold values 0 or 1
- valid_counts: int32 [6], replicated, may hold values from 640 to 1280
- send_slot: int32 [10240], P('node'), may hold values from 0 to 239, as said below
- recv_local: int32 [10240], P('node'), may hold values from 0 to 159, as said below
- halo_lists: int32 [16, 40], P('node'), may hold values from 0 to 159, as said below
- edge_first: float32 [2, 1536, 512], P(None, 'node', 'hid'), may hold values from -0.15625 to 0.15625
- edge_second: float32 [2, 512, 512], P(None, 'hid', 'node'), may hold values from -0.25 to 0.25
- node_first: float32 [2, 1024, 512], P(None, 'node', 'hid'), may hold values from -0.1875 to 0.1875
- node_second: float32 [2, 512, 512], P(None, 'hid', 'node'), may hold values from -0.25 to 0.25
- edge_first_m: float32 [2, 1536, 512], P(None, 'node', 'hid'), may hold values from -512 to 512
- edge_second_m: float32 [2, 512, 512], P(None, 'hid', 'node'), may hold values from -512 to 512
- node_first_m: float32 [2, 1024, 512], P(None, 'node', 'hid'), may hold values from -640 to 640
- node_second_m: float32 [2, 512, 512], P(None, 'hid', 'node'), may hold values from -640 to 640
- edge_first_v: float32 [2, 1536, 512], P(None, 'node', 'hid'), may hold values from 7372.8 to 30720
- edge_second_v: float32 [2, 512, 512], P(None, 'hid', 'node'), may hold values from 7372.8 to 30720
- node_first_v: float32 [2, 1024, 512], P(None, 'node', 'hid'), may hold values from 11059.2 to 44236.8
- node_second_v: float32 [2, 512, 512], P(None, 'hid', 'node'), may hold values from 11059.2 to 44236.8
- small_params: float32 [2, 8, 512], replicated, may hold values from -1.2 to 1.6
- small_m: float32 [2, 8, 512], replicated, may hold values from -448 to 448
- small_v: float32 [2, 8, 512], replicated, may hold values from 614.4 to 24576
- learn_rate: float32 [1], replicated, may hold values from 0.2 to 0.5
Outputs:
- node_out: bfloat16 [1280, 6, 512], P(('node', 'hid'))
- grad_node: bfloat16 [1280, 6, 512], P(('node', 'hid'))
- grad_edge: bfloat16 [10240, 512], P(('node', 'hid'))
- edge_first_new: float32 [2, 1536, 512], P(None, 'node', 'hid')
- edge_second_new: float32 [2, 512, 512], P(None, 'hid', 'node')
- node_first_new: float32 [2, 1024, 512], P(None, 'node', 'hid')
- node_second_new: float32 [2, 512, 512], P(None, 'hid', 'node')
- edge_first_m_new: float32 [2, 1536, 512], P(None, 'node', 'hid')
- edge_second_m_new: float32 [2, 512, 512], P(None, 'hid', 'node')
- node_first_m_new: float32 [2, 1024, 512], P(None, 'node', 'hid')
- node_second_m_new: float32 [2, 512, 512], P(None, 'hid', 'node')
- edge_first_v_new: float32 [2, 1536, 512], P(None, 'node', 'hid')
- edge_second_v_new: float32 [2, 512, 512], P(None, 'hid', 'node')
- node_first_v_new: float32 [2, 1024, 512], P(None, 'node', 'hid')
- node_second_v_new: float32 [2, 512, 512], P(None, 'hid', 'node')
- edge_first_copy: bfloat16 [2, 1536, 512], P(None, 'node', 'hid')
- edge_second_copy: bfloat16 [2, 512, 512], P(None, 'hid', 'node')
- node_first_copy: bfloat16 [2, 1024, 512], P(None, 'node', 'hid')
- node_second_copy: bfloat16 [2, 512, 512], P(None, 'hid', 'node')
- small_new: float32 [2, 8, 512], replicated
- small_m_new: float32 [2, 8, 512], replicated
- small_v_new: float32 [2, 8, 512], replicated
- norms: float32 [2, 12, 2], replicated
The draws below stay inside these ranges and needn't reach their ends.
Inputs may be any that keep to these rules, and one draw needn't show every extreme that they name: `recv_local`: within each block of 1280 edges the values never fall, and every one of the block's 160 nodes receives at least one edge. `send_slot`: below 160: a node of the edge's own block; 160 to 199: an entry of the previous block's list; above: an entry of the next block's list. `halo_lists`: row 2b holds 40 different nodes of block b, numbered within the block, read by the previous block; row 2b + 1 those read by the next block.
All inputs are finite; a program needn't handle non-finite values. No bound on the sum of `ocean_mask` or of `present_mask` on one device may be relied on, other than what follows from the above.
Results may differ from the reference program's by a relative error of at most 0.023.
Values may be sent and summed in bfloat16 or wider, within the bound.
No kernel may reach another device: no remote copies, remote signals or barrier semaphores. Data moves between devices by JAX's collectives and lax.ppermute only.
A program may use at most 256 MiB of HBM per device.

```python
import math
import jax
import jax.numpy as jnp
from jax import lax

LATENT = 512
HIDDEN_SIZE = 512
NODE_DEV = 160
SAMPLES = 6
LAYERS = 2
EDGE_DEV = 1280
HALO = 40
NODES = 1280
EDGES = 10240
N_NODE = 8


def graph_parts(key):
    blocks = NODES // NODE_DEV
    key_list = jax.random.split(jax.random.fold_in(key, 7), 4)
    extra_rows = jax.random.randint(key_list[0], (blocks, EDGE_DEV - NODE_DEV), 0, NODE_DEV).astype(jnp.int32)
    base_rows = jnp.broadcast_to(jnp.arange(NODE_DEV, dtype=jnp.int32), (blocks, NODE_DEV))
    recv_rows = jnp.sort(jnp.concatenate([base_rows, extra_rows], axis=1), axis=1)
    local_rows = jax.random.randint(key_list[1], (blocks, EDGE_DEV), 0, NODE_DEV).astype(jnp.int32)
    remote_rows = jax.random.randint(key_list[2], (blocks, EDGE_DEV), NODE_DEV, NODE_DEV + 2 * HALO).astype(jnp.int32)
    chooser = jax.random.randint(key_list[3], (blocks, EDGE_DEV), 0, 5)
    slot_rows = jnp.where(chooser < 3, local_rows, remote_rows)
    return (recv_rows.reshape(-1), slot_rows.reshape(-1))


def draw_recv_local(key, part):
    return graph_parts(key)[0]


def draw_send_slot(key, part):
    return graph_parts(key)[1]


def draw_halo_lists(key, part):
    blocks = NODES // NODE_DEV
    key_list = jax.random.split(jax.random.fold_in(key, 11), 2 * blocks)
    listed = jax.vmap(lambda single: jax.random.permutation(single, NODE_DEV)[:HALO])(key_list)
    return listed.astype(jnp.int32)


def draw_small_params(key, part):
    noise_draw = jax.random.normal(jax.random.fold_in(key, 13), (LAYERS, 8, LATENT), jnp.float32)
    row_ids = jnp.arange(8)
    is_gain = ((row_ids == 2) | (row_ids == 6))[None, :, None]
    return jnp.where(is_gain, 1.0 + 0.2 * jnp.clip(noise_draw, -3.0, 3.0), 0.3 * jnp.clip(noise_draw, -4.0, 4.0))


def with_ends(drawn, rng, least, largest):
    shape = drawn.shape
    index_at = [jax.random.randint(jax.random.fold_in(rng, axis), (), 0, shape[axis]) for axis in range(len(shape))]
    drawn = drawn.at[tuple(index_at)].set(least)
    longest = shape.index(max(shape))
    index_at[longest] = (index_at[longest] + 1) % shape[longest]
    return drawn.at[tuple(index_at)].set(largest)


def steps_of(rng, extent, cuts, least, top_value):
    gain, own = 1.0, jax.random.fold_in(rng, 6)
    for dim, shards_of in cuts:
        steps = jnp.exp(jax.random.uniform(jax.random.fold_in(own, dim), (shards_of,), jnp.float32, least / len(cuts), top_value / len(cuts)))
        gain = gain * jnp.repeat(steps, extent[dim] // shards_of).reshape([-1 if axis == dim else 1 for axis in range(len(extent))])
    return gain


def gaussian(own_key, dims, deviation, limit, pieces=(), kind=jnp.bfloat16):
    loudness = steps_of(own_key, dims, pieces, -0.22, 0.18) if pieces else 1.0
    values = jax.random.normal(own_key, dims, jnp.float32) * deviation * loudness
    return jnp.minimum(jnp.maximum(values, -limit), limit).astype(kind)


def setup_inputs(seed: int = 0) -> dict:
    seeds = jax.random.split(jax.random.key(seed), 26)
    node_in = gaussian(seeds[0], (NODES, SAMPLES, LATENT), 1.0, 6.0, ((0, 8),))
    edge_in = gaussian(seeds[1], (EDGES, LATENT), 1.0, 6.0, ((0, 8),))
    cotangent = gaussian(seeds[2], (NODES, SAMPLES, LATENT), 1.0, 6.0, ((0, 32),))
    ocean_mask = with_ends((jax.random.randint(seeds[3], (NODES,), 0, 10) < 7).astype(jnp.int32), jax.random.fold_in(seeds[3], 1), 0, 1)
    present_mask = with_ends((jax.random.randint(seeds[4], (NODES, SAMPLES), 0, 10) < 9).astype(jnp.int32), jax.random.fold_in(seeds[4], 1), 0, 1)
    valid_counts = with_ends(jax.random.randint(seeds[5], (SAMPLES,), NODES // 2, NODES + 1), jax.random.fold_in(seeds[5], 1), NODES // 2, NODES).astype(jnp.int32)
    send_slot = draw_send_slot(jax.random.fold_in(seeds[25], 71), 0)
    recv_local = draw_recv_local(jax.random.fold_in(seeds[25], 71), 0)
    halo_lists = draw_halo_lists(jax.random.fold_in(seeds[25], 71), 0)
    edge_first = gaussian(seeds[9], (LAYERS, 3 * LATENT, HIDDEN_SIZE), (3 * LATENT) ** -0.5, 0.15625, ((1, 8), (2, 4)), jnp.float32)
    edge_second = gaussian(seeds[10], (LAYERS, HIDDEN_SIZE, LATENT), HIDDEN_SIZE ** -0.5, 0.25, ((1, 4), (2, 8)), jnp.float32)
    node_first = gaussian(seeds[11], (LAYERS, 2 * LATENT, HIDDEN_SIZE), (2 * LATENT) ** -0.5, 0.1875, ((1, 8), (2, 4)), jnp.float32)
    node_second = gaussian(seeds[12], (LAYERS, HIDDEN_SIZE, LATENT), HIDDEN_SIZE ** -0.5, 0.25, ((1, 4), (2, 8)), jnp.float32)
    edge_first_m = gaussian(seeds[13], (LAYERS, 3 * LATENT, HIDDEN_SIZE), (0.35 * (EDGES * SAMPLES) ** 0.5), 512.0, ((1, 8), (2, 4)), jnp.float32)
    edge_second_m = gaussian(seeds[14], (LAYERS, HIDDEN_SIZE, LATENT), (0.35 * (EDGES * SAMPLES) ** 0.5), 512.0, ((1, 4), (2, 8)), jnp.float32)
    node_first_m = gaussian(seeds[15], (LAYERS, 2 * LATENT, HIDDEN_SIZE), (1.2 * (NODES * SAMPLES) ** 0.5), 640.0, ((1, 8), (2, 4)), jnp.float32)
    node_second_m = gaussian(seeds[16], (LAYERS, HIDDEN_SIZE, LATENT), (1.2 * (NODES * SAMPLES) ** 0.5), 640.0, ((1, 4), (2, 8)), jnp.float32)
    edge_first_v = jnp.clip(jnp.exp(math.log(30720.0) - 1.4271164 * jax.random.uniform(seeds[17], (LAYERS, 3 * LATENT, HIDDEN_SIZE), jnp.float32) ** steps_of(seeds[17], (LAYERS, 3 * LATENT, HIDDEN_SIZE), ((1, 8), (2, 4)), -0.2, 0.2)), 7372.8, 30720.0)
    edge_second_v = jnp.clip(jnp.exp(math.log(30720.0) - 1.4271164 * jax.random.uniform(seeds[18], (LAYERS, HIDDEN_SIZE, LATENT), jnp.float32) ** steps_of(seeds[18], (LAYERS, HIDDEN_SIZE, LATENT), ((1, 4), (2, 8)), -0.2, 0.2)), 7372.8, 30720.0)
    node_first_v = jnp.clip(jnp.exp(math.log(44236.8) - 1.3862944 * jax.random.uniform(seeds[19], (LAYERS, 2 * LATENT, HIDDEN_SIZE), jnp.float32) ** steps_of(seeds[19], (LAYERS, 2 * LATENT, HIDDEN_SIZE), ((1, 8), (2, 4)), -0.2, 0.2)), 11059.2, 44236.8)
    node_second_v = jnp.clip(jnp.exp(math.log(44236.8) - 1.3862944 * jax.random.uniform(seeds[20], (LAYERS, HIDDEN_SIZE, LATENT), jnp.float32) ** steps_of(seeds[20], (LAYERS, HIDDEN_SIZE, LATENT), ((1, 4), (2, 8)), -0.2, 0.2)), 11059.2, 44236.8)
    small_params = draw_small_params(jax.random.fold_in(seeds[25], 71), 0)
    small_m = gaussian(seeds[22], (LAYERS, 8, LATENT), (0.3 * (EDGES * SAMPLES) ** 0.5), 448.0, (), jnp.float32)
    small_v = jnp.clip(jnp.exp(jax.random.uniform(seeds[23], (LAYERS, 8, LATENT), jnp.float32, math.log(614.4), math.log(24576.0))), 614.4, 24576.0)
    learn_rate = jnp.clip(jax.random.uniform(seeds[24], (1,), jnp.float32, 0.2, 0.5), 0.2, 0.5)
    return {"node_in": node_in, "edge_in": edge_in, "cotangent": cotangent, "ocean_mask": ocean_mask, "present_mask": present_mask, "valid_counts": valid_counts, "send_slot": send_slot, "recv_local": recv_local, "halo_lists": halo_lists, "edge_first": edge_first, "edge_second": edge_second, "node_first": node_first, "node_second": node_second, "edge_first_m": edge_first_m, "edge_second_m": edge_second_m, "node_first_m": node_first_m, "node_second_m": node_second_m, "edge_first_v": edge_first_v, "edge_second_v": edge_second_v, "node_first_v": node_first_v, "node_second_v": node_second_v, "small_params": small_params, "small_m": small_m, "small_v": small_v, "learn_rate": learn_rate}


@jax.custom_vjp
def low(v):
    return lax.optimization_barrier(v.astype(jnp.bfloat16)).astype(jnp.float32)

@jax.custom_vjp
def low_back(v):
    return v

def low_keep(v):
    return (low(v), None)

def low_pass(kept, grad):
    return (grad,)

def back_keep(v):
    return (v, None)

def back_low(kept, grad):
    return (low(grad),)
low.defvjp(low_keep, low_pass)
low_back.defvjp(back_keep, back_low)
HIGHEST_MODE = lax.Precision.HIGHEST
NORM_EPS = 1e-05
BETA_FIRST = 0.5
BETA_SECOND = 0.5
ADAM_EPS = 1e-06
WEIGHT_DECAY = 0.01

def layer_norm(values, gain_row, shift_row):
    center = values - lax.optimization_barrier(jnp.mean(values, axis=-1, keepdims=True))
    spread = lax.optimization_barrier(jnp.mean(center * center, axis=-1, keepdims=True))
    return center * lax.rsqrt(spread + NORM_EPS) * gain_row + shift_row

def branch(inputs, first_weight, second_weight, params, offset):
    hidden = low_back(jnp.dot(inputs, first_weight, precision=HIGHEST_MODE, preferred_element_type=jnp.float32) + params[offset])
    active = low(jax.nn.silu(hidden))
    output = low_back(jnp.dot(active, second_weight, precision=HIGHEST_MODE, preferred_element_type=jnp.float32) + params[offset + 1])
    return layer_norm(output, params[offset + 2], params[offset + 3])

def graph_indices(send_slot, recv_local, halo_lists):
    edge_block = jnp.arange(EDGES, dtype=jnp.int32) // EDGE_DEV
    receiver = edge_block * NODE_DEV + recv_local
    halo_table = halo_lists.reshape(N_NODE, 2, HALO)
    left_block = (edge_block + N_NODE - 1) % N_NODE
    right_block = (edge_block + 1) % N_NODE
    from_left = jnp.clip(send_slot - NODE_DEV, 0, HALO - 1)
    from_right = jnp.clip(send_slot - NODE_DEV - HALO, 0, HALO - 1)
    left_node = left_block * NODE_DEV + halo_table[left_block, 1, from_left]
    right_node = right_block * NODE_DEV + halo_table[right_block, 0, from_right]
    own_node = edge_block * NODE_DEV + jnp.minimum(send_slot, NODE_DEV - 1)
    sender = jnp.where(send_slot < NODE_DEV, own_node, jnp.where(send_slot < NODE_DEV + HALO, left_node, right_node))
    return (sender.astype(jnp.int32), receiver.astype(jnp.int32))

def sample_pass(node_rows, edge_rows, weights, params_all, sender, receiver):
    first_e, second_e, first_n, second_n = weights
    node_state = node_rows
    edge_state = edge_rows
    edge_low = edge_rows
    for depth in range(LAYERS):
        params = params_all[depth]
        node_low = low(node_state)
        inputs = jnp.concatenate([edge_low, node_low[sender], node_low[receiver]], axis=-1)
        edge_state = edge_state + branch(inputs, first_e[depth], second_e[depth], params, 0)
        edge_low = low(edge_state)
        pooled = low(jax.ops.segment_sum(edge_low, receiver, num_segments=NODES, indices_are_sorted=True))
        inputs = jnp.concatenate([node_low, pooled], axis=-1)
        node_state = node_state + branch(inputs, first_n[depth], second_n[depth], params, 4)
    return node_state

def adam_terms(weight, grad, first, second, decay):
    first_new = BETA_FIRST * first + (1.0 - BETA_FIRST) * grad
    second_new = BETA_SECOND * second + (1.0 - BETA_SECOND) * grad * grad
    update = first_new / (jnp.sqrt(second_new) + ADAM_EPS) + decay * weight
    return (first_new, second_new, update)

def reference(node_in, edge_in, cotangent, ocean_mask, present_mask, valid_counts, send_slot, recv_local, halo_lists, edge_first, edge_second, node_first, node_second, edge_first_m, edge_second_m, node_first_m, node_second_m, edge_first_v, edge_second_v, node_first_v, node_second_v, small_params, small_m, small_v, learn_rate):
    sender, receiver = graph_indices(send_slot, recv_local, halo_lists)

    def forward(node_rows, edge_rows, first_e, second_e, first_n, second_n, params_all):
        weights = (low(first_e), low(second_e), low(first_n), low(second_n))

        def one_sample(sample_rows):
            return sample_pass(sample_rows, edge_rows, weights, params_all, sender, receiver)
        return lax.map(jax.checkpoint(one_sample), jnp.transpose(node_rows, (1, 0, 2)))
    output, pullback = jax.vjp(forward, node_in.astype(jnp.float32), edge_in.astype(jnp.float32), edge_first, edge_second, node_first, node_second, small_params)
    valid_mask = (ocean_mask[:, None] * present_mask).astype(jnp.float32)
    scaling = NODES / valid_counts.astype(jnp.float32)
    target = cotangent.astype(jnp.float32) * valid_mask[:, :, None] * scaling[None, :, None]
    gradients = pullback(jnp.transpose(target, (1, 0, 2)))
    node_out = jnp.transpose(output, (1, 0, 2)).astype(jnp.bfloat16)
    grad_node = gradients[0].astype(jnp.bfloat16)
    grad_edge = gradients[1].astype(jnp.bfloat16)
    masters = (edge_first, edge_second, node_first, node_second)
    firsts = (edge_first_m, edge_second_m, node_first_m, node_second_m)
    seconds = (edge_first_v, edge_second_v, node_first_v, node_second_v)
    new_weights, new_firsts, new_seconds, copies, weight_norms, update_norms = ([], [], [], [], [], [])
    for position in range(4):
        weight = masters[position]
        first_new, second_new, update = adam_terms(weight, gradients[2 + position], firsts[position], seconds[position], WEIGHT_DECAY)
        weight_norm = jnp.sqrt(lax.optimization_barrier(jnp.sum(weight * weight, axis=(1, 2))))
        update_norm = jnp.sqrt(lax.optimization_barrier(jnp.sum(update * update, axis=(1, 2))))
        new_weight = weight - learn_rate[0] * (weight_norm / update_norm)[:, None, None] * update
        new_weights.append(new_weight)
        new_firsts.append(first_new)
        new_seconds.append(second_new)
        copies.append(new_weight.astype(jnp.bfloat16))
        weight_norms.append(weight_norm)
        update_norms.append(update_norm)
    small_first, small_second, small_update = adam_terms(small_params, gradients[6], small_m, small_v, 0.0)
    small_wnorm = jnp.sqrt(lax.optimization_barrier(jnp.sum(small_params * small_params, axis=2)))
    small_unorm = jnp.sqrt(lax.optimization_barrier(jnp.sum(small_update * small_update, axis=2)))
    small_new = small_params - learn_rate[0] * (small_wnorm / small_unorm)[:, :, None] * small_update
    norms = jnp.stack([jnp.concatenate([jnp.stack(weight_norms, axis=1), small_wnorm], axis=1), jnp.concatenate([jnp.stack(update_norms, axis=1), small_unorm], axis=1)], axis=2)
    return (node_out, grad_node, grad_edge, new_weights[0], new_weights[1], new_weights[2], new_weights[3], new_firsts[0], new_firsts[1], new_firsts[2], new_firsts[3], new_seconds[0], new_seconds[1], new_seconds[2], new_seconds[3], copies[0], copies[1], copies[2], copies[3], small_new, small_first, small_second, norms)
```

```python
import jax
import jax.numpy as jnp
from jax import lax
from jax.sharding import PartitionSpec as P

LAYERS = 2


NORM_EPS = 1e-05
BETA_FIRST = 0.5
BETA_SECOND = 0.5
ADAM_EPS = 1e-06
WEIGHT_DECAY = 0.01
BF16 = jnp.bfloat16
F32 = jnp.float32


def dot(spec, left, right):
    return jnp.einsum(spec, left, right, preferred_element_type=F32)


def silu_slope(values):
    sigmoid = jax.nn.sigmoid(values)
    return sigmoid * (1.0 + values * (1.0 - sigmoid))


def norm_forward(values, gain_row, shift_row):
    center = values - jnp.mean(values, axis=-1, keepdims=True)
    spread = jnp.mean(center * center, axis=-1, keepdims=True)
    inverse = lax.rsqrt(spread + NORM_EPS)
    normed = center * inverse
    return (normed * gain_row + shift_row, normed, inverse)


def norm_backward(upstream, normed, inverse, gain_row):
    scaled = upstream * gain_row
    return inverse * (
        scaled
        - jnp.mean(scaled, axis=-1, keepdims=True)
        - normed * jnp.mean(scaled * normed, axis=-1, keepdims=True)
    )


def swap(values, axis, bit):
    count = lax.axis_size(axis)
    return lax.ppermute(values, axis, [(i, i ^ (1 << bit)) for i in range(count)])


def bits_of(axis):
    return lax.axis_size(axis).bit_length() - 1


def halve_sum(parts, axis):
    index = lax.axis_index(axis)
    for bit in range(bits_of(axis)):
        place = bits_of(axis) - 1 - bit
        own = (index >> bit) & 1
        sent = lax.dynamic_index_in_dim(parts, 1 - own, place, keepdims=False)
        kept = lax.dynamic_index_in_dim(parts, own, place, keepdims=False)
        parts = kept + swap(sent.astype(BF16), axis, bit).astype(F32)
    return parts


def double_up(part, axis):
    index = lax.axis_index(axis)
    for bit in reversed(range(bits_of(axis))):
        place = bits_of(axis) - 1 - bit
        own = (index >> bit) & 1
        other = swap(part, axis, bit)
        low = jnp.where(own == 0, part, other)
        high = jnp.where(own == 0, other, part)
        part = jnp.stack([low, high], axis=place)
    return part


def split_rows(values, axis):
    bits = bits_of(axis)
    samples, rows, width = values.shape
    shaped = values.reshape((samples,) + (2,) * bits + (rows >> bits, width))
    return jnp.moveaxis(shaped, 0, bits)


def join_rows(parts, axis):
    bits = bits_of(axis)
    moved = jnp.moveaxis(parts, bits, 0)
    return moved.reshape(moved.shape[0], -1, moved.shape[-1])


def sum_rows(values):
    return halve_sum(split_rows(values, "hid"), "hid")


def sum_rows_spread(values):
    return join_rows(double_up(sum_rows(values).astype(BF16), "hid"), "hid")


def sum_everywhere(values):
    for axis in ("hid", "node"):
        for bit in range(bits_of(axis)):
            values = values + swap(values, axis, bit)
    return values


def to_neighbours(rows, halo_width):
    count = lax.axis_size("node")
    onward = [(i, (i + 1) % count) for i in range(count)]
    back = [(target, source) for source, target in onward]
    from_previous = lax.ppermute(rows[:, halo_width:], "node", onward)
    from_next = lax.ppermute(rows[:, :halo_width], "node", back)
    return jnp.concatenate([from_previous, from_next], axis=1)


def adam_terms(weight, grad, first, second, decay):
    first_new = BETA_FIRST * first + (1.0 - BETA_FIRST) * grad
    second_new = BETA_SECOND * second + (1.0 - BETA_SECOND) * grad * grad
    update = first_new / (jnp.sqrt(second_new) + ADAM_EPS) + decay * weight
    return (first_new, second_new, update)


def gather_pair(first, second):
    packed = jnp.concatenate([first, second.T], axis=0).astype(BF16)
    rows = first.shape[0]
    whole = lax.all_gather(packed, ("node", "hid"), axis=0, tiled=True)
    nodes, hids = lax.axis_size("node"), lax.axis_size("hid")
    whole = whole.reshape(nodes, hids, packed.shape[0], packed.shape[1])
    whole = whole.transpose(0, 2, 1, 3).reshape(nodes, packed.shape[0], hids * packed.shape[1])
    return (
        whole[:, :rows].reshape(nodes * rows, -1),
        whole[:, rows:].reshape(nodes * (packed.shape[0] - rows), -1),
    )


def scatter_pair(first_grad, second_grad):
    nodes, hids = lax.axis_size("node"), lax.axis_size("hid")
    width = first_grad.shape[1] // hids
    packed = jnp.concatenate(
        [
            first_grad.astype(BF16).reshape(nodes, -1, hids, width),
            second_grad.astype(BF16).reshape(nodes, -1, hids, width),
        ],
        axis=1,
    )
    packed = packed.transpose(0, 2, 1, 3)
    own = lax.psum_scatter(
        packed.reshape(-1, width), ("node", "hid"), scatter_dimension=0, tiled=True
    ).astype(F32)
    rows = first_grad.shape[0] // nodes
    return own[:rows], own[rows:].T


def flat(values):
    return values.reshape(-1, values.shape[-1])


def per_device(
    node_in,
    edge_in,
    cotangent,
    ocean_mask,
    present_mask,
    valid_counts,
    send_slot,
    recv_local,
    halo_lists,
    edge_first,
    edge_second,
    node_first,
    node_second,
    edge_first_m,
    edge_second_m,
    node_first_m,
    node_second_m,
    edge_first_v,
    edge_second_v,
    node_first_v,
    node_second_v,
    small_params,
    small_m,
    small_v,
    learn_rate,
):
    masters = (edge_first, edge_second, node_first, node_second)
    hid_count = lax.axis_size("hid")
    hid_index = lax.axis_index("hid")
    node_total, sample_count, latent = node_in.shape
    edge_part = edge_in.shape[0] // hid_count
    node_part = node_total // hid_count
    halo_width = halo_lists.shape[1]
    table_total = node_total + 2 * halo_width

    edge_weights = [None] * LAYERS
    node_weights = [None] * LAYERS
    for depth in range(LAYERS):
        edge_weights[depth] = gather_pair(edge_first[depth], edge_second[depth])
        node_weights[depth] = gather_pair(node_first[depth], node_second[depth])

    def own_edges(values):
        return lax.dynamic_slice_in_dim(values, hid_index * edge_part, edge_part, 0)

    def own_nodes(values):
        return lax.dynamic_slice_in_dim(values, hid_index * node_part, node_part, 1)

    sender = own_edges(send_slot)
    receiver = own_edges(recv_local)
    at_receiver = (receiver[:, None] == jnp.arange(node_total)[None, :]).astype(BF16)
    at_sender = (sender[:, None] == jnp.arange(table_total)[None, :]).astype(BF16)
    at_both = jnp.concatenate([at_sender, at_receiver], axis=1)
    at_halo = (halo_lists.reshape(-1)[:, None] == jnp.arange(node_total)[None, :]).astype(BF16)

    valid_mask = (ocean_mask[:, None] * present_mask).astype(BF16)
    masked = jnp.transpose(cotangent * valid_mask[:, :, None], (1, 0, 2))
    target = join_rows(double_up(masked, "hid"), "hid").astype(F32)
    scaling = node_total * lax.axis_size("node") / valid_counts.astype(F32)
    target = target * scaling[:, None, None]

    node_low = jnp.transpose(node_in, (1, 0, 2))
    node_state = node_low.astype(F32)
    edge_low = own_edges(edge_in)
    edge_state = edge_low.astype(F32)[None]
    stashed = []
    for depth in range(LAYERS):
        params = small_params[depth]
        first_edge, second_edge = edge_weights[depth]
        own_weight = first_edge[:latent]
        send_weight = first_edge[latent : 2 * latent]
        recv_weight = first_edge[2 * latent :]
        halo_rows = dot("hn,snl->shl", at_halo, node_low).astype(BF16)
        table = jnp.concatenate([node_low, to_neighbours(halo_rows, halo_width)], axis=1)
        projected = jnp.concatenate(
            [
                dot("snl,lh->snh", table, send_weight).astype(BF16),
                dot("snl,lh->snh", node_low, recv_weight).astype(BF16),
            ],
            axis=1,
        )
        if depth == 0:
            own_proj = dot("el,lh->eh", edge_low, own_weight)[None]
        else:
            own_proj = dot("sel,lh->seh", edge_low, own_weight)
        edge_pre = own_proj + dot("en,snh->seh", at_both, projected) + params[0]
        edge_act = jax.nn.silu(edge_pre).astype(BF16)
        edge_sum = dot("seh,lh->sel", edge_act, second_edge) + params[1]
        edge_update, edge_normed, edge_inverse = norm_forward(edge_sum, params[2], params[3])
        edge_state = edge_state + edge_update
        edge_next = edge_state.astype(BF16)
        pooled = sum_rows_spread(dot("en,sel->snl", at_receiver, edge_next))
        first_node, second_node = node_weights[depth]
        node_pre = (
            dot("snl,lh->snh", node_low, first_node[:latent])
            + dot("snl,lh->snh", pooled, first_node[latent:])
            + params[4]
        )
        node_act = jax.nn.silu(node_pre).astype(BF16)
        node_sum = dot("snh,lh->snl", node_act, second_node) + params[5]
        node_update, node_normed, node_inverse = norm_forward(node_sum, params[6], params[7])
        node_state = node_state + node_update
        stashed.append(
            (
                node_low,
                table,
                edge_low,
                edge_pre,
                edge_act,
                edge_normed,
                edge_inverse,
                pooled,
                node_pre,
                node_act,
                node_normed,
                node_inverse,
            )
        )
        node_low = node_state.astype(BF16)
        edge_low = edge_next
    node_out = jnp.transpose(own_nodes(node_low), (1, 0, 2))

    node_grad = target
    edge_grad = None
    reduced = [None] * LAYERS
    minor_local = [None] * LAYERS
    carried = None
    for depth in reversed(range(LAYERS)):
        (
            node_low,
            table,
            edge_low,
            edge_pre,
            edge_act,
            edge_normed,
            edge_inverse,
            pooled,
            node_pre,
            node_act,
            node_normed,
            node_inverse,
        ) = stashed[depth]
        params = small_params[depth]
        first_edge, second_edge = edge_weights[depth]
        own_weight = first_edge[:latent]
        send_weight = first_edge[latent : 2 * latent]
        recv_weight = first_edge[2 * latent :]
        first_node, second_node = node_weights[depth]

        node_sum_low = norm_backward(node_grad, node_normed, node_inverse, params[6]).astype(BF16)
        node_act_grad = dot("snl,lh->snh", node_sum_low, second_node)
        node_pre_grad = (node_act_grad * silu_slope(node_pre)).astype(BF16)
        node_input_grad = dot("snh,lh->snl", node_pre_grad, first_node[:latent])
        pooled_grad = dot("snh,lh->snl", node_pre_grad, first_node[latent:]).astype(BF16)
        mine_pre = own_nodes(node_pre_grad)
        mine_sum = own_nodes(node_sum_low)
        mine_grad = own_nodes(node_grad)
        mine_normed = own_nodes(node_normed)
        first_node_grad = jnp.concatenate(
            [
                dot("rl,rh->lh", flat(own_nodes(node_low)), flat(mine_pre)),
                dot("rl,rh->lh", flat(own_nodes(pooled)), flat(mine_pre)),
            ],
            axis=0,
        )
        second_node_grad = dot("rl,rh->lh", flat(mine_sum), flat(own_nodes(node_act)))

        gathered = dot("en,snl->sel", at_receiver, pooled_grad)
        if carried is None:
            edge_grad = gathered
        else:
            edge_grad = edge_grad + gathered + dot("seh,lh->sel", *carried)
        edge_sum_low = norm_backward(edge_grad, edge_normed, edge_inverse, params[2]).astype(BF16)
        edge_act_grad = dot("sel,lh->seh", edge_sum_low, second_edge)
        edge_pre_grad = (edge_act_grad * silu_slope(edge_pre)).astype(BF16)
        at_nodes = dot("en,seh->snh", at_both, edge_pre_grad).astype(BF16)
        table_pre = at_nodes[:, :table_total]
        receiver_pre = at_nodes[:, table_total:]
        returned = to_neighbours_back(
            dot("snh,lh->snl", table_pre[:, node_total:], send_weight).astype(BF16), halo_width
        )
        partial = (
            dot("snh,lh->snl", table_pre[:, :node_total], send_weight)
            + dot("snh,lh->snl", receiver_pre, recv_weight)
            + dot("hn,shl->snl", at_halo, returned)
        )
        second_edge_grad = dot("rl,rh->lh", flat(edge_sum_low), flat(edge_act))
        if depth == 0:
            own_weight_grad = dot(
                "el,eh->lh", edge_low, jnp.sum(edge_pre_grad.astype(F32), axis=0).astype(BF16)
            )
        else:
            own_weight_grad = dot("rl,rh->lh", flat(edge_low), flat(edge_pre_grad))
        first_edge_grad = jnp.concatenate(
            [
                own_weight_grad,
                dot("rl,rh->lh", flat(table), flat(table_pre)),
                dot("rl,rh->lh", flat(node_low), flat(receiver_pre)),
            ],
            axis=0,
        )
        reduced[depth] = (
            *scatter_pair(first_edge_grad, second_edge_grad),
            *scatter_pair(first_node_grad, second_node_grad),
        )
        minor_local[depth] = jnp.stack(
            [
                jnp.sum(edge_pre_grad.astype(F32), axis=(0, 1)),
                jnp.sum(edge_sum_low.astype(F32), axis=(0, 1)),
                jnp.sum(edge_grad * edge_normed, axis=(0, 1)),
                jnp.sum(edge_grad, axis=(0, 1)),
                jnp.sum(mine_pre.astype(F32), axis=(0, 1)),
                jnp.sum(mine_sum.astype(F32), axis=(0, 1)),
                jnp.sum(mine_grad * mine_normed, axis=(0, 1)),
                jnp.sum(mine_grad, axis=(0, 1)),
            ]
        )
        if depth > 0:
            carried = (edge_pre_grad, own_weight)
            node_grad = node_grad + node_input_grad + sum_rows_spread(partial).astype(F32)
        else:
            node_grad = mine_grad + own_nodes(node_input_grad) + sum_rows(partial)
            edge_input_grad = jnp.sum(edge_grad, axis=0) + dot(
                "eh,lh->el", jnp.sum(edge_pre_grad.astype(F32), axis=0).astype(BF16), own_weight
            )
    grad_node = jnp.transpose(node_grad.astype(BF16), (1, 0, 2))

    weight_local = jnp.stack([jnp.sum(matrix * matrix, axis=(1, 2)) for matrix in masters], axis=1)
    weight_squares = sum_everywhere(weight_local)
    minor_total = sum_everywhere(jnp.stack(minor_local))
    grads = [jnp.stack([reduced[depth][place] for depth in range(LAYERS)]) for place in range(4)]
    firsts = (edge_first_m, edge_second_m, node_first_m, node_second_m)
    seconds = (edge_first_v, edge_second_v, node_first_v, node_second_v)
    moment_list = [
        adam_terms(masters[place], grads[place], firsts[place], seconds[place], WEIGHT_DECAY)
        for place in range(4)
    ]
    update_squares = sum_everywhere(
        jnp.stack([jnp.sum(entry[2] * entry[2], axis=(1, 2)) for entry in moment_list], axis=1)
    )
    weight_norm = jnp.sqrt(weight_squares)
    update_norm = jnp.sqrt(update_squares)
    new_weights = []
    for position in range(4):
        ratio = weight_norm[:, position] / update_norm[:, position]
        new_weights.append(
            masters[position] - learn_rate[0] * ratio[:, None, None] * moment_list[position][2]
        )
    small_first, small_second, small_update = adam_terms(
        small_params, minor_total, small_m, small_v, 0.0
    )
    small_wnorm = jnp.sqrt(jnp.sum(small_params * small_params, axis=2))
    small_unorm = jnp.sqrt(jnp.sum(small_update * small_update, axis=2))
    small_new = (
        small_params - learn_rate[0] * (small_wnorm / small_unorm)[:, :, None] * small_update
    )
    norms = jnp.stack(
        [
            jnp.concatenate([weight_norm, small_wnorm], axis=1),
            jnp.concatenate([update_norm, small_unorm], axis=1),
        ],
        axis=2,
    )
    return (
        node_out,
        grad_node,
        edge_input_grad.astype(BF16),
        *new_weights,
        *[entry[0] for entry in moment_list],
        *[entry[1] for entry in moment_list],
        *[weight.astype(BF16) for weight in new_weights],
        small_new,
        small_first,
        small_second,
        norms,
    )


def to_neighbours_back(rows, halo_width):
    count = lax.axis_size("node")
    onward = [(i, (i + 1) % count) for i in range(count)]
    back = [(target, source) for source, target in onward]
    from_previous = lax.ppermute(rows[:, halo_width:], "node", onward)
    from_next = lax.ppermute(rows[:, :halo_width], "node", back)
    return jnp.concatenate([from_previous, from_next], axis=1)


def solution(mesh):
    whole = P()
    rows = P(None, "node", "hid")
    columns = P(None, "hid", "node")
    matrices = (rows, columns, rows, columns)
    in_specs = (
        P("node", None, None),
        P("node", None),
        P(("node", "hid"), None, None),
        P(("node", "hid")),
        P(("node", "hid"), None),
        P(),
        P("node"),
        P("node"),
        P("node", None),
        *matrices,
        *matrices,
        *matrices,
        whole,
        whole,
        whole,
        whole,
    )
    out_specs = (
        P(("node", "hid"), None, None),
        P(("node", "hid"), None, None),
        P(("node", "hid"), None),
        *matrices,
        *matrices,
        *matrices,
        *matrices,
        whole,
        whole,
        whole,
        whole,
    )
    return jax.shard_map(
        per_device, mesh=mesh, in_specs=in_specs, out_specs=out_specs, check_vma=False
    )
```

```python
import jax
import jax.numpy as jnp
from jax import lax
from jax.sharding import PartitionSpec as P

LAYERS = 2


NORM_EPS = 1e-05
BETA_FIRST = 0.5
BETA_SECOND = 0.5
ADAM_EPS = 1e-06
WEIGHT_DECAY = 0.01
BF16 = jnp.bfloat16
F32 = jnp.float32


def dot(spec, left, right):
    return jnp.einsum(spec, left, right, preferred_element_type=F32)


def silu_slope(values):
    sigmoid = jax.nn.sigmoid(values)
    return sigmoid * (1.0 + values * (1.0 - sigmoid))


def norm_forward(values, gain_row, shift_row):
    center = values - jnp.mean(values, axis=-1, keepdims=True)
    spread = jnp.mean(center * center, axis=-1, keepdims=True)
    inverse = lax.rsqrt(spread + NORM_EPS)
    normed = center * inverse
    return (normed * gain_row + shift_row, normed, inverse)


def norm_backward(upstream, normed, inverse, gain_row):
    scaled = upstream * gain_row
    return inverse * (
        scaled
        - jnp.mean(scaled, axis=-1, keepdims=True)
        - normed * jnp.mean(scaled * normed, axis=-1, keepdims=True)
    )


def swap(values, axis, offset):
    return lax.ppermute(values, axis, [(i, i ^ offset) for i in range(lax.axis_size(axis))])


def bits_of(axis):
    return lax.axis_size(axis).bit_length() - 1


def own_bit(axis, bit):
    return (lax.axis_index(axis) >> bit) & 1


def all_bits():
    return [(axis, bit) for axis in ("node", "hid") for bit in reversed(range(bits_of(axis)))]


def ordered(own, mine, other):
    low = jnp.where(own == 0, mine, other)
    high = jnp.where(own == 0, other, mine)
    return low, high


def double_up(part, axis, bit, place):
    low, high = ordered(own_bit(axis, bit), part, swap(part, axis, 1 << bit))
    return jnp.stack([low, high], axis=place)


def halve_sum(parts, axis, bit, place):
    own = own_bit(axis, bit)
    sent = lax.dynamic_index_in_dim(parts, 1 - own, place, keepdims=False)
    kept = lax.dynamic_index_in_dim(parts, own, place, keepdims=False)
    return kept.astype(F32) + swap(sent.astype(BF16), axis, 1 << bit).astype(F32)


def gather_all(packed):
    present, early = [], None
    for key in all_bits():
        present.append(key)
        packed = double_up(packed, *key, len(present) - 1)
        if len(present) == 2:
            early = packed
    return packed.reshape(lax.axis_size("node"), lax.axis_size("hid"), *packed.shape[-2:]), early


def scatter_all(parts):
    left = all_bits()
    parts = parts.reshape((2,) * len(left) + parts.shape[2:])
    while left:
        parts = halve_sum(parts, *left[-1], len(left) - 1)
        left = left[:-1]
    return parts


def sum_everywhere(values):
    for axis in ("hid", "node"):
        done, bits = 0, bits_of(axis)
        while done < bits:
            step = min(3, bits - done)
            terms = [values] + [swap(values, axis, i << done) for i in range(1, 1 << step)]
            while len(terms) > 1:
                terms = [terms[i] + terms[i + 1] for i in range(0, len(terms), 2)]
            values, done = terms[0], done + step
    return values


def to_neighbours(rows, halo_width):
    count = lax.axis_size("node")
    onward = [(i, (i + 1) % count) for i in range(count)]
    back = [(target, source) for source, target in onward]
    from_previous = lax.ppermute(rows[:, halo_width:], "node", onward)
    from_next = lax.ppermute(rows[:, :halo_width], "node", back)
    return jnp.concatenate([from_previous, from_next], axis=1)


def adam_terms(weight, grad, first, second, decay):
    first_new = BETA_FIRST * first + (1.0 - BETA_FIRST) * grad
    second_new = BETA_SECOND * second + (1.0 - BETA_SECOND) * grad * grad
    update = first_new / (jnp.sqrt(second_new) + ADAM_EPS) + decay * weight
    return (first_new, second_new, update)


def pack_shards(first, second):
    return jnp.concatenate([first, second.T], axis=0).astype(BF16)


def whole_pair(whole, rows):
    nodes, hids, count, width = whole.shape
    whole = whole.transpose(0, 2, 1, 3).reshape(nodes, count, hids * width)
    return (
        whole[:, :rows].reshape(nodes * rows, -1),
        whole[:, rows:].reshape(nodes * (count - rows), -1),
    )


def pack_grads(first_grad, second_grad):
    nodes, hids = lax.axis_size("node"), lax.axis_size("hid")
    width = first_grad.shape[1] // hids
    packed = jnp.concatenate(
        [
            first_grad.reshape(nodes, -1, hids, width),
            second_grad.reshape(nodes, -1, hids, width),
        ],
        axis=1,
    )
    return packed.transpose(0, 2, 1, 3)


def flat(values):
    return values.reshape(-1, values.shape[-1])


def per_device(
    node_in,
    edge_in,
    cotangent,
    ocean_mask,
    present_mask,
    valid_counts,
    send_slot,
    recv_local,
    halo_lists,
    edge_first,
    edge_second,
    node_first,
    node_second,
    edge_first_m,
    edge_second_m,
    node_first_m,
    node_second_m,
    edge_first_v,
    edge_second_v,
    node_first_v,
    node_second_v,
    small_params,
    small_m,
    small_v,
    learn_rate,
):
    masters = (edge_first, edge_second, node_first, node_second)
    hid_count = lax.axis_size("hid")
    hid_index = lax.axis_index("hid")
    node_total, sample_count, latent = node_in.shape
    edge_part = edge_in.shape[0] // hid_count
    node_part = node_total // hid_count
    halo_width = halo_lists.shape[1]
    table_total = node_total + 2 * halo_width
    sample_half, edge_half = hid_index >> 1, hid_index & 1
    samples = sample_count // 2
    edge_rows = edge_first.shape[1]
    node_rows = node_first.shape[1]

    whole, early = gather_all(pack_shards(edge_first[0], edge_second[0]))
    later = [pack_shards(node_first[0], node_second[0])]
    for depth in range(1, LAYERS):
        later.append(pack_shards(edge_first[depth], edge_second[depth]))
        later.append(pack_shards(node_first[depth], node_second[depth]))
    cuts = [0]
    for piece in later:
        cuts.append(cuts[-1] + piece.shape[0])
    later, _ = lax.optimization_barrier((jnp.concatenate(later, axis=0), early))
    later, _ = gather_all(later)
    pieces = [later[:, :, cuts[i] : cuts[i + 1]] for i in range(len(cuts) - 1)]
    node_weights = [whole_pair(piece, node_rows) for piece in pieces[0::2]]
    edge_weights = [whole_pair(piece, edge_rows) for piece in [whole] + pieces[1::2]]

    def own_edges(values):
        return lax.dynamic_index_in_dim(
            values.reshape(2, 2, edge_part, *values.shape[1:]), edge_half, 1, keepdims=False
        ).reshape(2 * edge_part, *values.shape[1:])

    def own_nodes(values):
        return lax.dynamic_index_in_dim(
            values.reshape(samples, 2, 2, node_part, latent), edge_half, 2, keepdims=False
        ).reshape(samples, 2 * node_part, latent)

    def own_samples(values):
        return lax.dynamic_slice_in_dim(values, sample_half * samples, samples, 1)

    def to_own_rows(values):
        quarters = jnp.moveaxis(values.reshape(samples, 2, 2, node_part, latent), 0, 3)
        quarters = lax.dynamic_index_in_dim(quarters, edge_half, 1, keepdims=False)
        sent = lax.dynamic_index_in_dim(quarters, 1 - sample_half, 0, keepdims=False)
        kept = lax.dynamic_index_in_dim(quarters, sample_half, 0, keepdims=False)
        return jnp.concatenate(ordered(sample_half, kept, swap(sent, "hid", 2)), axis=1)

    def add_other_half(values):
        return values + swap(values.astype(BF16), "hid", 1).astype(F32)

    sender = own_edges(send_slot)
    receiver = own_edges(recv_local)
    at_receiver = (receiver[:, None] == jnp.arange(node_total)[None, :]).astype(BF16)
    at_sender = (sender[:, None] == jnp.arange(table_total)[None, :]).astype(BF16)
    at_both = jnp.concatenate([at_sender, at_receiver], axis=1)
    at_halo = (halo_lists.reshape(-1)[:, None] == jnp.arange(node_total)[None, :]).astype(BF16)

    valid_mask = (ocean_mask[:, None] * present_mask).astype(BF16)
    masked = cotangent * valid_mask[:, :, None]
    sent = lax.dynamic_slice_in_dim(masked, (1 - sample_half) * samples, samples, 1)
    masked = jnp.stack(ordered(sample_half, own_samples(masked), swap(sent, "hid", 2)), axis=0)
    masked = double_up(masked, "hid", 0, 1).reshape(node_total, samples, latent)
    scaling = node_total * lax.axis_size("node") / valid_counts.astype(F32)
    scaling = lax.dynamic_slice_in_dim(scaling, sample_half * samples, samples, 0)
    target = jnp.transpose(masked, (1, 0, 2)).astype(F32) * scaling[:, None, None]

    node_low = jnp.transpose(own_samples(node_in), (1, 0, 2))
    node_state = node_low.astype(F32)
    edge_low = own_edges(edge_in)
    edge_state = edge_low.astype(F32)[None]
    stashed = []
    for depth in range(LAYERS):
        params = small_params[depth]
        first_edge, second_edge = edge_weights[depth]
        own_weight = first_edge[:latent]
        send_weight = first_edge[latent : 2 * latent]
        recv_weight = first_edge[2 * latent :]
        halo_rows = dot("hn,snl->shl", at_halo, node_low).astype(BF16)
        table = jnp.concatenate([node_low, to_neighbours(halo_rows, halo_width)], axis=1)
        projected = jnp.concatenate(
            [
                dot("snl,lh->snh", table, send_weight).astype(BF16),
                dot("snl,lh->snh", node_low, recv_weight).astype(BF16),
            ],
            axis=1,
        )
        if depth == 0:
            own_proj = dot("el,lh->eh", edge_low, own_weight)[None]
        else:
            own_proj = dot("sel,lh->seh", edge_low, own_weight)
        edge_pre = own_proj + dot("en,snh->seh", at_both, projected) + params[0]
        edge_act = jax.nn.silu(edge_pre).astype(BF16)
        edge_sum = dot("seh,lh->sel", edge_act, second_edge) + params[1]
        edge_update, edge_normed, edge_inverse = norm_forward(edge_sum, params[2], params[3])
        edge_state = edge_state + edge_update
        edge_next = edge_state.astype(BF16)
        pooled = add_other_half(dot("en,sel->snl", at_receiver, edge_next)).astype(BF16)
        first_node, second_node = node_weights[depth]
        node_pre = (
            dot("snl,lh->snh", node_low, first_node[:latent])
            + dot("snl,lh->snh", pooled, first_node[latent:])
            + params[4]
        )
        node_act = jax.nn.silu(node_pre).astype(BF16)
        node_sum = dot("snh,lh->snl", node_act, second_node) + params[5]
        node_update, node_normed, node_inverse = norm_forward(node_sum, params[6], params[7])
        node_state = node_state + node_update
        stashed.append(
            (
                node_low,
                table,
                edge_low,
                edge_pre,
                edge_act,
                edge_normed,
                edge_inverse,
                pooled,
                node_pre,
                node_act,
                node_normed,
                node_inverse,
            )
        )
        node_low = node_state.astype(BF16)
        edge_low = edge_next
    node_out = to_own_rows(node_low)

    node_grad = target
    edge_grad = None
    reduced = [None] * LAYERS
    minor_local = [None] * LAYERS
    carried = None
    for depth in reversed(range(LAYERS)):
        (
            node_low,
            table,
            edge_low,
            edge_pre,
            edge_act,
            edge_normed,
            edge_inverse,
            pooled,
            node_pre,
            node_act,
            node_normed,
            node_inverse,
        ) = stashed[depth]
        params = small_params[depth]
        first_edge, second_edge = edge_weights[depth]
        own_weight = first_edge[:latent]
        send_weight = first_edge[latent : 2 * latent]
        recv_weight = first_edge[2 * latent :]
        first_node, second_node = node_weights[depth]

        node_sum_low = norm_backward(node_grad, node_normed, node_inverse, params[6]).astype(BF16)
        node_act_grad = dot("snl,lh->snh", node_sum_low, second_node)
        node_pre_grad = (node_act_grad * silu_slope(node_pre)).astype(BF16)
        node_input_grad = dot("snh,lh->snl", node_pre_grad, first_node[:latent])
        pooled_grad = dot("snh,lh->snl", node_pre_grad, first_node[latent:]).astype(BF16)
        mine_pre = own_nodes(node_pre_grad)
        mine_sum = own_nodes(node_sum_low)
        mine_grad = own_nodes(node_grad)
        mine_normed = own_nodes(node_normed)
        first_node_grad = jnp.concatenate(
            [
                dot("rl,rh->lh", flat(own_nodes(node_low)), flat(mine_pre)),
                dot("rl,rh->lh", flat(own_nodes(pooled)), flat(mine_pre)),
            ],
            axis=0,
        )
        second_node_grad = dot("rl,rh->lh", flat(mine_sum), flat(own_nodes(node_act)))

        gathered = dot("en,snl->sel", at_receiver, pooled_grad)
        if carried is None:
            edge_grad = gathered
        else:
            edge_grad = edge_grad + gathered + dot("seh,lh->sel", *carried)
        edge_sum_low = norm_backward(edge_grad, edge_normed, edge_inverse, params[2]).astype(BF16)
        edge_act_grad = dot("sel,lh->seh", edge_sum_low, second_edge)
        edge_pre_grad = (edge_act_grad * silu_slope(edge_pre)).astype(BF16)
        at_nodes = dot("en,seh->snh", at_both, edge_pre_grad).astype(BF16)
        table_pre = at_nodes[:, :table_total]
        receiver_pre = at_nodes[:, table_total:]
        returned = to_neighbours_back(
            dot("snh,lh->snl", table_pre[:, node_total:], send_weight).astype(BF16), halo_width
        )
        partial = (
            dot("snh,lh->snl", table_pre[:, :node_total], send_weight)
            + dot("snh,lh->snl", receiver_pre, recv_weight)
            + dot("hn,shl->snl", at_halo, returned)
        )
        second_edge_grad = dot("rl,rh->lh", flat(edge_sum_low), flat(edge_act))
        if depth == 0:
            own_weight_grad = dot(
                "el,eh->lh", edge_low, jnp.sum(edge_pre_grad.astype(F32), axis=0).astype(BF16)
            )
        else:
            own_weight_grad = dot("rl,rh->lh", flat(edge_low), flat(edge_pre_grad))
        first_edge_grad = jnp.concatenate(
            [
                own_weight_grad,
                dot("rl,rh->lh", flat(table), flat(table_pre)),
                dot("rl,rh->lh", flat(node_low), flat(receiver_pre)),
            ],
            axis=0,
        )
        node_packed = pack_grads(first_node_grad, second_node_grad)
        edge_packed = pack_grads(first_edge_grad, second_edge_grad)
        if depth > 0:
            both = scatter_all(jnp.concatenate([node_packed, edge_packed], axis=2))
            node_own, edge_own = both[: node_packed.shape[2]], both[node_packed.shape[2] :]
        else:
            node_own, edge_own = scatter_all(node_packed), scatter_all(edge_packed)
        reduced[depth] = (
            edge_own[:edge_rows],
            edge_own[edge_rows:].T,
            node_own[:node_rows],
            node_own[node_rows:].T,
        )
        minor_local[depth] = jnp.stack(
            [
                jnp.sum(edge_pre_grad.astype(F32), axis=(0, 1)),
                jnp.sum(edge_sum_low.astype(F32), axis=(0, 1)),
                jnp.sum(edge_grad * edge_normed, axis=(0, 1)),
                jnp.sum(edge_grad, axis=(0, 1)),
                jnp.sum(mine_pre.astype(F32), axis=(0, 1)),
                jnp.sum(mine_sum.astype(F32), axis=(0, 1)),
                jnp.sum(mine_grad * mine_normed, axis=(0, 1)),
                jnp.sum(mine_grad, axis=(0, 1)),
            ]
        )
        node_grad = node_grad + node_input_grad + add_other_half(partial)
        if depth > 0:
            carried = (edge_pre_grad, own_weight)
        else:
            edge_input_grad = jnp.sum(edge_grad, axis=0) + dot(
                "eh,lh->el", jnp.sum(edge_pre_grad.astype(F32), axis=0).astype(BF16), own_weight
            )
            edge_input_grad = halve_sum(
                edge_input_grad.reshape(2, edge_part, latent), "hid", 1, 0
            )
    grad_node = to_own_rows(node_grad.astype(BF16))

    weight_local = jnp.stack([jnp.sum(matrix * matrix, axis=(1, 2)) for matrix in masters], axis=1)
    minor_packed = jnp.concatenate(
        [jnp.stack(minor_local).reshape(-1), weight_local.reshape(-1)], axis=0
    )
    minor_packed = sum_everywhere(minor_packed)
    minor_total = minor_packed[: small_params.size].reshape(small_params.shape)
    weight_squares = minor_packed[small_params.size :].reshape(weight_local.shape)
    grads = [jnp.stack([reduced[depth][place] for depth in range(LAYERS)]) for place in range(4)]
    firsts = (edge_first_m, edge_second_m, node_first_m, node_second_m)
    seconds = (edge_first_v, edge_second_v, node_first_v, node_second_v)
    moment_list = [
        adam_terms(masters[place], grads[place], firsts[place], seconds[place], WEIGHT_DECAY)
        for place in range(4)
    ]
    update_squares = sum_everywhere(
        jnp.stack([jnp.sum(entry[2] * entry[2], axis=(1, 2)) for entry in moment_list], axis=1)
    )
    weight_norm = jnp.sqrt(weight_squares)
    update_norm = jnp.sqrt(update_squares)
    new_weights = []
    for position in range(4):
        ratio = weight_norm[:, position] / update_norm[:, position]
        new_weights.append(
            masters[position] - learn_rate[0] * ratio[:, None, None] * moment_list[position][2]
        )
    small_first, small_second, small_update = adam_terms(
        small_params, minor_total, small_m, small_v, 0.0
    )
    small_wnorm = jnp.sqrt(jnp.sum(small_params * small_params, axis=2))
    small_unorm = jnp.sqrt(jnp.sum(small_update * small_update, axis=2))
    small_new = (
        small_params - learn_rate[0] * (small_wnorm / small_unorm)[:, :, None] * small_update
    )
    norms = jnp.stack(
        [
            jnp.concatenate([weight_norm, small_wnorm], axis=1),
            jnp.concatenate([update_norm, small_unorm], axis=1),
        ],
        axis=2,
    )
    return (
        node_out,
        grad_node,
        edge_input_grad.astype(BF16),
        *new_weights,
        *[entry[0] for entry in moment_list],
        *[entry[1] for entry in moment_list],
        *[weight.astype(BF16) for weight in new_weights],
        small_new,
        small_first,
        small_second,
        norms,
    )


def to_neighbours_back(rows, halo_width):
    count = lax.axis_size("node")
    onward = [(i, (i + 1) % count) for i in range(count)]
    back = [(target, source) for source, target in onward]
    from_previous = lax.ppermute(rows[:, halo_width:], "node", onward)
    from_next = lax.ppermute(rows[:, :halo_width], "node", back)
    return jnp.concatenate([from_previous, from_next], axis=1)


def solution(mesh):
    whole = P()
    rows = P(None, "node", "hid")
    columns = P(None, "hid", "node")
    matrices = (rows, columns, rows, columns)
    in_specs = (
        P("node", None, None),
        P("node", None),
        P(("node", "hid"), None, None),
        P(("node", "hid")),
        P(("node", "hid"), None),
        P(),
        P("node"),
        P("node"),
        P("node", None),
        *matrices,
        *matrices,
        *matrices,
        whole,
        whole,
        whole,
        whole,
    )
    out_specs = (
        P(("node", "hid"), None, None),
        P(("node", "hid"), None, None),
        P(("node", "hid"), None),
        *matrices,
        *matrices,
        *matrices,
        *matrices,
        whole,
        whole,
        whole,
        whole,
    )
    return jax.shard_map(
        per_device, mesh=mesh, in_specs=in_specs, out_specs=out_specs, check_vma=False
    )
```

```python
import jax
import jax.numpy as jnp
from jax import lax
from jax.experimental import pallas as pl
from jax.experimental.pallas import tpu as pltpu
from jax.sharding import PartitionSpec as P

LAYERS = 2


NORM_EPS = 1e-05
BETA_FIRST = 0.5
BETA_SECOND = 0.5
ADAM_EPS = 1e-06
WEIGHT_DECAY = 0.01
BF16 = jnp.bfloat16
F32 = jnp.float32
VMEM_BYTES = 56 * 1024 * 1024


def matmul(left, right):
    return lax.dot_general(left, right, (((1,), (0,)), ((), ())), preferred_element_type=F32)


def matmul_nt(left, right):
    return lax.dot_general(left, right, (((1,), (1,)), ((), ())), preferred_element_type=F32)


def matmul_tn(left, right):
    return lax.dot_general(left, right, (((0,), (0,)), ((), ())), preferred_element_type=F32)


def sigmoid(values):
    return 1.0 / (1.0 + jnp.exp(-values))


def silu_slope(values):
    gate = sigmoid(values)
    return gate * (1.0 + values * (1.0 - gate))


def norm_forward(values):
    center = values - jnp.mean(values, axis=-1, keepdims=True)
    spread = jnp.mean(center * center, axis=-1, keepdims=True)
    inverse = lax.rsqrt(spread + NORM_EPS)
    return center * inverse, inverse


def norm_backward(upstream, normed, inverse, gain_row):
    scaled = upstream * gain_row
    return inverse * (
        scaled
        - jnp.mean(scaled, axis=-1, keepdims=True)
        - normed * jnp.mean(scaled * normed, axis=-1, keepdims=True)
    )


def column_sum(values):
    return jnp.sum(values, axis=0, keepdims=True)


def assemble(source, rows, offset, target):
    nodes, hids, _, width = source.shape
    for i in range(nodes):
        for j in range(hids):
            target[i * rows : (i + 1) * rows, j * width : (j + 1) * width] = source[
                i, j, offset : offset + rows, :
            ]


def pack(values, rows, offset, target):
    nodes, hids, _, width = target.shape
    for i in range(nodes):
        for j in range(hids):
            target[i, j, offset : offset + rows, :] = values[
                i * rows : (i + 1) * rows, j * width : (j + 1) * width
            ].astype(target.dtype)


def per_sample(array):
    block = (1,) + array.shape[1:]
    return pl.BlockSpec(block, lambda s: (s,) + (0,) * (len(block) - 1))


def constant(array):
    return pl.BlockSpec(array.shape, lambda s: (0,) * len(array.shape))


def weight_block(array, rows, place):
    nodes, hids, _, width = array.shape
    return pl.BlockSpec((nodes, hids, rows, width), lambda s: (0, 0, place, 0))


def shape_of(shape, dtype):
    return jax.ShapeDtypeStruct(shape, dtype)


def run_kernel(kernel, name, samples, inputs, in_specs, outputs, scratch, flops):
    moved = sum(a.size * a.dtype.itemsize for a in inputs) + sum(
        shape.size * shape.dtype.itemsize for shape, _ in outputs
    )
    return pl.pallas_call(
        kernel,
        name=name,
        grid=(samples,),
        in_specs=in_specs,
        out_specs=[spec for _, spec in outputs],
        out_shape=[shape for shape, _ in outputs],
        scratch_shapes=scratch,
        compiler_params=pltpu.CompilerParams(
            dimension_semantics=("arbitrary",), vmem_limit_bytes=VMEM_BYTES
        ),
        cost_estimate=pl.CostEstimate(flops=flops, bytes_accessed=moved, transcendentals=0),
    )(*inputs)


def sampled(shape, dtype):
    result = shape_of(shape, dtype)
    return (result, per_sample(result))


def shared(shape, dtype):
    result = shape_of(shape, dtype)
    return (result, constant(result))


def edge_forward(first, second, table, edge_low, edge_state, at_both, at_nodes, params, node_total, last):
    samples, table_total, latent = table.shape
    edges = edge_low.shape[1]
    alike = edge_low.shape[0] == 1

    def kernel(w1, w2, table, low, state, both, nodes, params, pre, act, normed, inverse, *rest):
        if last:
            pooled, w1s, w2s, projected = rest
        else:
            new_state, new_low, pooled, w1s, w2s, projected = rest

        @pl.when(pl.program_id(0) == 0)
        def _():
            assemble(w1, w1.shape[2], 0, w1s)
            assemble(w2, w2.shape[2], 0, w2s)

        rows = table[0]
        projected[:table_total] = matmul(rows, w1s[latent : 2 * latent]).astype(BF16)
        projected[table_total:] = matmul(rows[:node_total], w1s[2 * latent :]).astype(BF16)
        hidden = matmul(low[0], w1s[:latent]) + matmul(both[...], projected[...]) + params[0:1]
        pre[0] = hidden.astype(BF16)
        active = (hidden * sigmoid(hidden)).astype(BF16)
        act[0] = active
        output = matmul_nt(active, w2s[...]) + params[1:2]
        scaled, scale = norm_forward(output)
        normed[0] = scaled.astype(BF16)
        inverse[0] = scale
        state_new = state[0] + scaled * params[2:3] + params[3:4]
        low_new = state_new.astype(BF16)
        if not last:
            new_state[0] = state_new
            new_low[0] = low_new
        pooled[0] = matmul(nodes[...], low_new).astype(BF16)

    wide = (samples, edges, latent)
    outputs = [sampled(wide, BF16), sampled(wide, BF16), sampled(wide, BF16), sampled((samples, edges, 1), F32)]
    if not last:
        outputs += [sampled(wide, F32), sampled(wide, BF16)]
    outputs += [sampled((samples, node_total, latent), BF16)]
    of_edges = constant if alike else per_sample
    return run_kernel(
        kernel,
        "edge_forward",
        samples,
        [first[0], second[0], table, edge_low, edge_state, at_both, at_nodes, params],
        [
            weight_block(*first),
            weight_block(*second),
            per_sample(table),
            of_edges(edge_low),
            of_edges(edge_state),
            constant(at_both),
            constant(at_nodes),
            constant(params),
        ],
        outputs,
        [
            pltpu.VMEM((3 * latent, latent), BF16),
            pltpu.VMEM((latent, latent), BF16),
            pltpu.VMEM((at_both.shape[1], latent), BF16),
        ],
        2 * samples * edges * latent * (3 * latent + at_both.shape[1]),
    )


def edge_backward(first, second, pooled_grad, edge_grad, normed, inverse, pre, at_receiver, at_both_t, gain, last, node_total):
    samples, edges, latent = normed.shape
    at_total = at_both_t.shape[0]
    table_total = at_total - node_total

    def kernel(w1, w2, upstream, *rest):
        if not last:
            later, rest = rest[0], rest[1:]
        normed, inverse, pre, receiver, both_t, gain, low, hidden_low, at_rows, partial, returned, grad_out, minor = rest[:13]
        if last:
            w1s, w2s = rest[13:]
        else:
            hidden_sum, w1s, w2s, hidden_acc = rest[13:]
        step = pl.program_id(0)

        @pl.when(step == 0)
        def _():
            assemble(w1, w1.shape[2], 0, w1s)
            assemble(w2, w2.shape[2], 0, w2s)
            minor[...] = jnp.zeros_like(minor)

        grad = matmul(receiver[...], upstream[0])
        if not last:
            grad = grad + later[0]
        scaled = normed[0].astype(F32)
        output_grad = norm_backward(grad, scaled, inverse[0], gain[0:1]).astype(BF16)
        low[0] = output_grad
        act_grad = matmul(output_grad, w2s[...])
        pre_grad = (act_grad * silu_slope(pre[0].astype(F32))).astype(BF16)
        hidden_low[0] = pre_grad
        minor[0:1] += column_sum(pre_grad.astype(F32))
        minor[1:2] += column_sum(output_grad.astype(F32))
        minor[2:3] += column_sum(grad * scaled)
        minor[3:4] += column_sum(grad)
        at_rows[0] = matmul(both_t[...], pre_grad).astype(BF16)
        send = w1s[latent : 2 * latent]
        partial[0] = matmul_nt(at_rows[0, :node_total], send) + matmul_nt(
            at_rows[0, table_total:], w1s[2 * latent :]
        )
        returned[0] = matmul_nt(at_rows[0, node_total:table_total], send).astype(BF16)
        if last:
            grad_out[0] = grad + matmul_nt(pre_grad, w1s[:latent])
        else:

            @pl.when(step == 0)
            def _():
                grad_out[...] = grad
                hidden_acc[...] = pre_grad.astype(F32)

            @pl.when(step > 0)
            def _():
                grad_out[...] += grad
                hidden_acc[...] += pre_grad.astype(F32)

            @pl.when(step == samples - 1)
            def _():
                total = hidden_acc[...].astype(BF16)
                hidden_sum[...] = total
                grad_out[...] += matmul_nt(total, w1s[:latent])

    wide = (samples, edges, latent)
    outputs = [
        sampled(wide, BF16),
        sampled(wide, BF16),
        sampled((samples, at_total, latent), BF16),
        sampled((samples, node_total, latent), F32),
        sampled((samples, table_total - node_total, latent), BF16),
        sampled(wide, F32) if last else shared((edges, latent), F32),
        shared((4, latent), F32),
    ]
    scratch = [pltpu.VMEM((3 * latent, latent), BF16), pltpu.VMEM((latent, latent), BF16)]
    inputs = [first[0], second[0], pooled_grad]
    specs = [weight_block(*first), weight_block(*second), per_sample(pooled_grad)]
    if not last:
        outputs.append(shared((edges, latent), BF16))
        scratch.append(pltpu.VMEM((edges, latent), F32))
        inputs.append(edge_grad)
        specs.append(per_sample(edge_grad))
    inputs += [normed, inverse, pre, at_receiver, at_both_t, gain]
    specs += [
        per_sample(normed),
        per_sample(inverse),
        per_sample(pre),
        constant(at_receiver),
        constant(at_both_t),
        constant(gain),
    ]
    return run_kernel(
        kernel,
        "edge_backward",
        samples,
        inputs,
        specs,
        outputs,
        scratch,
        2 * samples * edges * latent * (2 * latent + 2 * at_total),
    )


def edge_weight_grads(edge_low, table, hidden_low, at_rows, low, act, node_total, nodes, hids, width, packed_before):
    samples, table_total, latent = table.shape
    alike = edge_low.ndim == 2
    first_rows, second_rows = 3 * latent // nodes, latent // nodes
    offset = 0 if packed_before is None else packed_before.shape[2]

    def kernel(edge_low, table, hidden_low, at_rows, low, act, *rest):
        if packed_before is not None:
            before, rest = rest[0], rest[1:]
        packed, first, second = rest
        step = pl.program_id(0)

        @pl.when(step == 0)
        def _():
            first[...] = jnp.zeros_like(first)
            second[...] = jnp.zeros_like(second)
            if packed_before is not None:
                packed[:, :, :offset, :] = before[...]
            if alike:
                first[:latent] = matmul_tn(edge_low[...], hidden_low[...])

        if not alike:
            first[:latent] += matmul_tn(edge_low[0], hidden_low[0])
        first[latent : 2 * latent] += matmul_tn(table[0], at_rows[0, :table_total])
        first[2 * latent :] += matmul_tn(table[0, :node_total], at_rows[0, table_total:])
        second[...] += matmul_tn(low[0], act[0])

        @pl.when(step == samples - 1)
        def _():
            pack(first, first_rows, offset, packed)
            pack(second, second_rows, offset + first_rows, packed)

    of_edges = constant if alike else per_sample
    inputs = [edge_low, table, hidden_low, at_rows, low, act]
    specs = [of_edges(edge_low), per_sample(table), of_edges(hidden_low), per_sample(at_rows), per_sample(low), per_sample(act)]
    if packed_before is not None:
        inputs.append(packed_before)
        specs.append(constant(packed_before))
    return run_kernel(
        kernel,
        "edge_weight_grads",
        samples,
        inputs,
        specs,
        [shared((nodes, hids, offset + first_rows + second_rows, width), BF16)],
        [pltpu.VMEM((3 * latent, latent), F32), pltpu.VMEM((latent, latent), F32)],
        4 * low.size * latent,
    )[0]


def node_pass(weights, table, state, pooled_pair, params, at_halo, target, scaling, mask, node_total):
    samples, _, latent = table.shape
    array, rows, place = weights
    nodes, hids, _, width = array.shape
    second_rows = latent // nodes
    first_rows = rows - second_rows
    last = target is not None

    def kernel(w, table, state, pooled_own, pooled_other, params, *rest):
        if last:
            target, scaling, mask, new_low, upstream, input_grad, packed, minor, w1s, w2s, first, second = rest
        else:
            at_halo, pooled_out, pre, act, normed, inverse, new_state, new_low, halo, w1s, w2s = rest
        step = pl.program_id(0)

        @pl.when(step == 0)
        def _():
            assemble(w, first_rows, 0, w1s)
            assemble(w, second_rows, first_rows, w2s)

        rows_low = table[0, :node_total]
        pooled = (pooled_own[0].astype(F32) + pooled_other[0].astype(F32)).astype(BF16)
        hidden = matmul(rows_low, w1s[:latent]) + matmul(pooled, w1s[latent:]) + params[4:5]
        active = (hidden * sigmoid(hidden)).astype(BF16)
        output = matmul_nt(active, w2s[...]) + params[5:6]
        scaled, scale = norm_forward(output)
        state_new = state[0] + scaled * params[6:7] + params[7:8]
        low_new = state_new.astype(BF16)
        new_low[0] = low_new
        if not last:
            pooled_out[0] = pooled
            pre[0] = hidden.astype(BF16)
            act[0] = active
            normed[0] = scaled.astype(BF16)
            inverse[0] = scale
            new_state[0] = state_new
            halo[0] = matmul(at_halo[...], low_new).astype(BF16)
        else:
            grad = target[0].astype(F32) * scaling[0]
            node_gradients(
                step, samples, grad, scaled, scale, hidden, active, rows_low, pooled, params, mask,
                w1s, w2s, first, second, upstream, input_grad, packed, minor, first_rows, second_rows,
            )

    rows_shape = (samples, node_total, latent)
    inputs = [array, table, state, *pooled_pair, params]
    specs = [weight_block(*weights), per_sample(table), per_sample(state), per_sample(pooled_pair[0]), per_sample(pooled_pair[1]), constant(params)]
    scratch = [pltpu.VMEM((2 * latent, latent), BF16), pltpu.VMEM((latent, latent), BF16)]
    if last:
        inputs += [target, scaling, mask]
        specs += [per_sample(target), per_sample(scaling), constant(mask)]
        outputs = [sampled(rows_shape, BF16), *gradient_outputs(samples, node_total, latent, nodes, hids, rows, width)]
        scratch += [pltpu.VMEM((2 * latent, latent), F32), pltpu.VMEM((latent, latent), F32)]
    else:
        inputs += [at_halo]
        specs += [constant(at_halo)]
        outputs = [
            sampled(rows_shape, BF16),
            sampled(rows_shape, BF16),
            sampled(rows_shape, BF16),
            sampled(rows_shape, BF16),
            sampled((samples, node_total, 1), F32),
            sampled(rows_shape, F32),
            sampled(rows_shape, BF16),
            sampled((samples, at_halo.shape[0], latent), BF16),
        ]
    return run_kernel(kernel, "node_pass", samples, inputs, specs, outputs, scratch, 6 * samples * node_total * latent * latent * (3 if last else 1))


def gradient_outputs(samples, node_total, latent, nodes, hids, rows, width):
    return [
        sampled((samples, node_total, latent), BF16),
        sampled((samples, node_total, latent), F32),
        shared((nodes, hids, rows, width), BF16),
        shared((4, latent), F32),
    ]


def node_gradients(
    step, samples, grad, scaled, scale, hidden, active, rows_low, pooled, params, mask,
    w1s, w2s, first, second, upstream, input_grad, packed, minor, first_rows, second_rows,
):
    latent = w2s.shape[0]

    @pl.when(step == 0)
    def _():
        minor[...] = jnp.zeros_like(minor)
        first[...] = jnp.zeros_like(first)
        second[...] = jnp.zeros_like(second)

    output_grad = norm_backward(grad, scaled, scale, params[6:7]).astype(BF16)
    pre_grad = (matmul(output_grad, w2s[...]) * silu_slope(hidden)).astype(BF16)
    upstream[0] = matmul_nt(pre_grad, w1s[latent:]).astype(BF16)
    input_grad[0] = grad + matmul_nt(pre_grad, w1s[:latent])
    chosen = mask[...] > 0.5
    output_mine = jnp.where(chosen, output_grad.astype(F32), 0.0)
    pre_mine = jnp.where(chosen, pre_grad.astype(F32), 0.0)
    grad_mine = jnp.where(chosen, grad, 0.0)
    minor[0:1] += column_sum(pre_mine)
    minor[1:2] += column_sum(output_mine)
    minor[2:3] += column_sum(grad_mine * scaled)
    minor[3:4] += column_sum(grad_mine)
    pre_mine = pre_mine.astype(BF16)
    first[:latent] += matmul_tn(rows_low, pre_mine)
    first[latent:] += matmul_tn(pooled, pre_mine)
    second[...] += matmul_tn(output_mine.astype(BF16), active)

    @pl.when(step == samples - 1)
    def _():
        pack(first, first_rows, 0, packed)
        pack(second, second_rows, first_rows, packed)


def node_backward(weights, grads, table, pooled, pre, act, normed, inverse, params, mask, node_total):
    samples, _, latent = table.shape
    array, rows, place = weights
    nodes, hids, _, width = array.shape
    second_rows = latent // nodes
    first_rows = rows - second_rows

    def kernel(w, base, own, other, table, pooled, pre, act, normed, inverse, params, mask, upstream, input_grad, packed, minor, w1s, w2s, first, second):
        step = pl.program_id(0)

        @pl.when(step == 0)
        def _():
            assemble(w, first_rows, 0, w1s)
            assemble(w, second_rows, first_rows, w2s)

        grad = base[0] + (own[0] + other[0].astype(F32))
        node_gradients(
            step, samples, grad, normed[0].astype(F32), inverse[0], pre[0].astype(F32), act[0],
            table[0, :node_total], pooled[0], params, mask,
            w1s, w2s, first, second, upstream, input_grad, packed, minor, first_rows, second_rows,
        )

    inputs = [array, *grads, table, pooled, pre, act, normed, inverse, params, mask]
    specs = [weight_block(*weights)] + [per_sample(a) for a in inputs[1:10]] + [constant(params), constant(mask)]
    return run_kernel(
        kernel,
        "node_backward",
        samples,
        inputs,
        specs,
        gradient_outputs(samples, node_total, latent, nodes, hids, rows, width),
        [
            pltpu.VMEM((2 * latent, latent), BF16),
            pltpu.VMEM((latent, latent), BF16),
            pltpu.VMEM((2 * latent, latent), F32),
            pltpu.VMEM((latent, latent), F32),
        ],
        12 * samples * node_total * latent * latent,
    )


def dot(spec, left, right):
    return jnp.einsum(spec, left, right, preferred_element_type=F32)


def swap(values, axis, offset):
    return lax.ppermute(values, axis, [(i, i ^ offset) for i in range(lax.axis_size(axis))])


def bits_of(axis):
    return lax.axis_size(axis).bit_length() - 1


def own_bit(axis, bit):
    return (lax.axis_index(axis) >> bit) & 1


def all_bits():
    return [(axis, bit) for axis in ("node", "hid") for bit in reversed(range(bits_of(axis)))]


def ordered(own, mine, other):
    low = jnp.where(own == 0, mine, other)
    high = jnp.where(own == 0, other, mine)
    return low, high


def double_up(part, axis, bit, place):
    low, high = ordered(own_bit(axis, bit), part, swap(part, axis, 1 << bit))
    return jnp.stack([low, high], axis=place)


def halve_sum(parts, axis, bit, place):
    own = own_bit(axis, bit)
    sent = lax.dynamic_index_in_dim(parts, 1 - own, place, keepdims=False)
    kept = lax.dynamic_index_in_dim(parts, own, place, keepdims=False)
    return kept.astype(F32) + swap(sent.astype(BF16), axis, 1 << bit).astype(F32)


def gather_all(packed):
    present, early = [], None
    for key in all_bits():
        present.append(key)
        packed = double_up(packed, *key, len(present) - 1)
        if len(present) == 2:
            early = packed
    return packed.reshape(lax.axis_size("node"), lax.axis_size("hid"), *packed.shape[-2:]), early


def scatter_all(parts, values=None):
    left = all_bits()
    parts = parts.reshape((2,) * len(left) + parts.shape[2:])
    while left:
        axis, bit = left.pop()
        parts = halve_sum(parts, axis, bit, len(left))
        if values is not None:
            values = values + swap(values, axis, 1 << bit)
            parts, values = lax.optimization_barrier((parts, values))
    return parts, values


def sum_everywhere(values):
    for axis, bit in reversed(all_bits()):
        values = values + swap(values, axis, 1 << bit)
    return values


def to_neighbours(rows, halo_width):
    count = lax.axis_size("node")
    onward = [(i, (i + 1) % count) for i in range(count)]
    back = [(target, source) for source, target in onward]
    from_previous = lax.ppermute(rows[:, halo_width:], "node", onward)
    from_next = lax.ppermute(rows[:, :halo_width], "node", back)
    return jnp.concatenate([from_previous, from_next], axis=1)


def adam_terms(weight, grad, first, second, decay):
    first_new = BETA_FIRST * first + (1.0 - BETA_FIRST) * grad
    second_new = BETA_SECOND * second + (1.0 - BETA_SECOND) * grad * grad
    update = first_new / (jnp.sqrt(second_new) + ADAM_EPS) + decay * weight
    return (first_new, second_new, update)


def pack_shards(first, second):
    return jnp.concatenate([first, second.T], axis=0).astype(BF16)


def adam_terms(weight, grad, first, second, decay):
    first_new = BETA_FIRST * first + (1.0 - BETA_FIRST) * grad
    second_new = BETA_SECOND * second + (1.0 - BETA_SECOND) * grad * grad
    update = first_new / (jnp.sqrt(second_new) + ADAM_EPS) + decay * weight
    return (first_new, second_new, update)


def per_device(
    node_in,
    edge_in,
    cotangent,
    ocean_mask,
    present_mask,
    valid_counts,
    send_slot,
    recv_local,
    halo_lists,
    edge_first,
    edge_second,
    node_first,
    node_second,
    edge_first_m,
    edge_second_m,
    node_first_m,
    node_second_m,
    edge_first_v,
    edge_second_v,
    node_first_v,
    node_second_v,
    small_params,
    small_m,
    small_v,
    learn_rate,
):
    hid_count = lax.axis_size("hid")
    hid_index = lax.axis_index("hid")
    node_total, sample_count, latent = node_in.shape
    edge_part = edge_in.shape[0] // hid_count
    node_part = node_total // hid_count
    halo_width = halo_lists.shape[1]
    table_total = node_total + 2 * halo_width
    sample_half, edge_half = hid_index >> 1, hid_index & 1
    samples = sample_count // 2
    nodes, hids = lax.axis_size("node"), hid_count
    first_rows = edge_first.shape[1]
    second_rows = edge_second.shape[2]
    node_rows = node_first.shape[1] + second_rows
    width = edge_first.shape[2]

    edge_zero, early = gather_all(pack_shards(edge_first[0], edge_second[0]))
    piece, _ = lax.optimization_barrier((pack_shards(node_first[0], node_second[0]), early))
    node_zero, early = gather_all(piece)
    piece = jnp.concatenate(
        [pack_shards(node_first[1], node_second[1]), pack_shards(edge_first[1], edge_second[1])], axis=0
    )
    piece, _ = lax.optimization_barrier((piece, early))
    layer_one, _ = gather_all(piece)
    edge_weights = [
        ((edge_zero, first_rows, 0), (edge_zero, second_rows, first_rows // second_rows)),
        ((layer_one, first_rows, 1), (layer_one, second_rows, 2 * first_rows // second_rows)),
    ]
    node_weights = [(node_zero, node_rows, 0), (layer_one, node_rows, 0)]

    def own_edges(values):
        return lax.dynamic_index_in_dim(
            values.reshape(2, 2, edge_part, *values.shape[1:]), edge_half, 1, keepdims=False
        ).reshape(2 * edge_part, *values.shape[1:])

    def own_nodes(values):
        return lax.dynamic_index_in_dim(
            values.reshape(samples, 2, 2, node_part, latent), edge_half, 2, keepdims=False
        ).reshape(samples, 2 * node_part, latent)

    def own_samples(values):
        return lax.dynamic_slice_in_dim(values, sample_half * samples, samples, 1)

    def to_own_rows(values):
        quarters = jnp.moveaxis(values.reshape(samples, 2, 2, node_part, latent), 0, 3)
        quarters = lax.dynamic_index_in_dim(quarters, edge_half, 1, keepdims=False)
        sent = lax.dynamic_index_in_dim(quarters, 1 - sample_half, 0, keepdims=False)
        kept = lax.dynamic_index_in_dim(quarters, sample_half, 0, keepdims=False)
        return jnp.concatenate(ordered(sample_half, kept, swap(sent, "hid", 2)), axis=1)

    sender = own_edges(send_slot)
    receiver = own_edges(recv_local)
    node_ids, table_ids = jnp.arange(node_total), jnp.arange(table_total)
    at_receiver = (receiver[:, None] == node_ids[None, :]).astype(BF16)
    at_both = jnp.concatenate(
        [(sender[:, None] == table_ids[None, :]).astype(BF16), at_receiver], axis=1
    )
    at_nodes = (node_ids[:, None] == receiver[None, :]).astype(BF16)
    at_both_t = jnp.concatenate(
        [(table_ids[:, None] == sender[None, :]).astype(BF16), at_nodes], axis=0
    )
    at_halo = (halo_lists.reshape(-1)[:, None] == node_ids[None, :]).astype(BF16)
    mask = ((node_ids // node_part) % 2 == edge_half).astype(F32)[:, None]

    valid_mask = (ocean_mask[:, None] * present_mask).astype(BF16)
    masked = cotangent * valid_mask[:, :, None]
    masked, _ = lax.optimization_barrier((masked, edge_zero))
    sent = lax.dynamic_slice_in_dim(masked, (1 - sample_half) * samples, samples, 1)
    masked = jnp.stack(ordered(sample_half, own_samples(masked), swap(sent, "hid", 2)), axis=0)
    masked = double_up(masked, "hid", 0, 1).reshape(node_total, samples, latent)
    scaling = node_total * lax.axis_size("node") / valid_counts.astype(F32)
    scaling = lax.dynamic_slice_in_dim(scaling, sample_half * samples, samples, 0)
    target = jnp.transpose(masked, (1, 0, 2))
    scaling = scaling[:, None, None]

    node_low = jnp.transpose(own_samples(node_in), (1, 0, 2))
    edge_in_own = own_edges(edge_in)
    halo_rows = dot("hn,snl->shl", at_halo, node_low).astype(BF16)
    table_zero = jnp.concatenate([node_low, to_neighbours(halo_rows, halo_width)], axis=1)
    pre_zero, act_zero, normed_zero, inverse_zero, edge_state, edge_low, pooled = edge_forward(
        *edge_weights[0],
        table_zero,
        edge_in_own[None],
        edge_in_own.astype(F32)[None],
        at_both,
        at_nodes,
        small_params[0],
        node_total,
        False,
    )
    (
        pooled_zero,
        node_pre,
        node_act,
        node_normed,
        node_inverse,
        node_state,
        node_low,
        halo_rows,
    ) = node_pass(
        node_weights[0],
        table_zero,
        node_low.astype(F32),
        (pooled, swap(pooled, "hid", 1)),
        small_params[0],
        at_halo,
        None,
        None,
        None,
        node_total,
    )
    table_one = jnp.concatenate([node_low, to_neighbours(halo_rows, halo_width)], axis=1)
    pre_one, act_one, normed_one, inverse_one, pooled = edge_forward(
        *edge_weights[1],
        table_one,
        edge_low,
        edge_state,
        at_both,
        at_nodes,
        small_params[1],
        node_total,
        True,
    )
    node_low, pooled_grad, node_grad, node_packed, node_minor_one = node_pass(
        node_weights[1],
        table_one,
        node_state,
        (pooled, swap(pooled, "hid", 1)),
        small_params[1],
        None,
        target,
        scaling,
        mask,
        node_total,
    )
    node_out = to_own_rows(node_low)

    def from_edges(partial, returned):
        returned = to_neighbours(returned, halo_width)
        return partial + dot("hn,shl->snl", at_halo, returned)

    low, hidden_low, at_rows, partial, returned, edge_grad, edge_minor_one = edge_backward(
        *edge_weights[1],
        pooled_grad,
        None,
        normed_one,
        inverse_one,
        pre_one,
        at_receiver,
        at_both_t,
        small_params[1, 2:3],
        True,
        node_total,
    )
    packed = edge_weight_grads(
        edge_low,
        table_one,
        hidden_low,
        at_rows,
        low,
        act_one,
        node_total,
        nodes,
        hids,
        width,
        node_packed,
    )
    layer_one_grads, _ = scatter_all(packed)
    partial = from_edges(partial, returned)
    pooled_grad, node_grad, node_packed, node_minor_zero = node_backward(
        node_weights[0],
        (node_grad, partial, swap(partial.astype(BF16), "hid", 1)),
        table_zero,
        pooled_zero,
        node_pre,
        node_act,
        node_normed,
        node_inverse,
        small_params[0],
        mask,
        node_total,
    )
    node_zero_grads, _ = scatter_all(node_packed)
    low, hidden_low, at_rows, partial, returned, edge_input_grad, edge_minor_zero, hidden_sum = (
        edge_backward(
            *edge_weights[0],
            pooled_grad,
            edge_grad,
            normed_zero,
            inverse_zero,
            pre_zero,
            at_receiver,
            at_both_t,
            small_params[0, 2:3],
            False,
            node_total,
        )
    )
    packed = edge_weight_grads(
        edge_in_own,
        table_zero,
        hidden_sum,
        at_rows,
        low,
        act_zero,
        node_total,
        nodes,
        hids,
        width,
        None,
    )
    masters = (edge_first, edge_second, node_first, node_second)
    weight_local = jnp.stack([jnp.sum(matrix * matrix, axis=(1, 2)) for matrix in masters], axis=1)
    minor_packed = jnp.concatenate(
        [edge_minor_zero, node_minor_zero, edge_minor_one, node_minor_one]
        + [jnp.pad(weight_local.reshape(1, -1), ((0, 0), (0, latent - weight_local.size)))],
        axis=0,
    )
    edge_zero_grads, minor_packed = scatter_all(packed, minor_packed)
    partial = from_edges(partial, returned)
    node_grad = node_grad + (partial + swap(partial.astype(BF16), "hid", 1).astype(F32))
    grad_node = to_own_rows(node_grad.astype(BF16))
    edge_input_grad = halve_sum(edge_input_grad.reshape(2, edge_part, latent), "hid", 1, 0)

    minor_total = minor_packed[: 8 * LAYERS].reshape(small_params.shape)
    weight_squares = minor_packed[8 * LAYERS, : weight_local.size].reshape(weight_local.shape)
    node_one_grads, edge_one_grads = layer_one_grads[:node_rows], layer_one_grads[node_rows:]
    node_first_rows = node_rows - second_rows
    grads = [
        jnp.stack([edge_zero_grads[:first_rows], edge_one_grads[:first_rows]]),
        jnp.stack([edge_zero_grads[first_rows:].T, edge_one_grads[first_rows:].T]),
        jnp.stack([node_zero_grads[:node_first_rows], node_one_grads[:node_first_rows]]),
        jnp.stack([node_zero_grads[node_first_rows:].T, node_one_grads[node_first_rows:].T]),
    ]
    firsts = (edge_first_m, edge_second_m, node_first_m, node_second_m)
    seconds = (edge_first_v, edge_second_v, node_first_v, node_second_v)
    moment_list = [
        adam_terms(masters[place], grads[place], firsts[place], seconds[place], WEIGHT_DECAY)
        for place in range(4)
    ]
    update_squares = sum_everywhere(
        jnp.stack([jnp.sum(entry[2] * entry[2], axis=(1, 2)) for entry in moment_list], axis=1)
    )
    weight_norm = jnp.sqrt(weight_squares)
    update_norm = jnp.sqrt(update_squares)
    new_weights = []
    for position in range(4):
        ratio = weight_norm[:, position] / update_norm[:, position]
        new_weights.append(
            masters[position] - learn_rate[0] * ratio[:, None, None] * moment_list[position][2]
        )
    small_first, small_second, small_update = adam_terms(
        small_params, minor_total, small_m, small_v, 0.0
    )
    small_wnorm = jnp.sqrt(jnp.sum(small_params * small_params, axis=2))
    small_unorm = jnp.sqrt(jnp.sum(small_update * small_update, axis=2))
    small_new = (
        small_params - learn_rate[0] * (small_wnorm / small_unorm)[:, :, None] * small_update
    )
    norms = jnp.stack(
        [
            jnp.concatenate([weight_norm, small_wnorm], axis=1),
            jnp.concatenate([update_norm, small_unorm], axis=1),
        ],
        axis=2,
    )
    return (
        node_out,
        grad_node,
        edge_input_grad.astype(BF16),
        *new_weights,
        *[entry[0] for entry in moment_list],
        *[entry[1] for entry in moment_list],
        *[weight.astype(BF16) for weight in new_weights],
        small_new,
        small_first,
        small_second,
        norms,
    )


def solution(mesh):
    whole = P()
    rows = P(None, "node", "hid")
    columns = P(None, "hid", "node")
    matrices = (rows, columns, rows, columns)
    in_specs = (
        P("node", None, None),
        P("node", None),
        P(("node", "hid"), None, None),
        P(("node", "hid")),
        P(("node", "hid"), None),
        P(),
        P("node"),
        P("node"),
        P("node", None),
        *matrices,
        *matrices,
        *matrices,
        whole,
        whole,
        whole,
        whole,
    )
    out_specs = (
        P(("node", "hid"), None, None),
        P(("node", "hid"), None, None),
        P(("node", "hid"), None),
        *matrices,
        *matrices,
        *matrices,
        *matrices,
        whole,
        whole,
        whole,
        whole,
    )
    return jax.shard_map(
        per_device, mesh=mesh, in_specs=in_specs, out_specs=out_specs, check_vma=False
    )
```

```python
import jax
import jax.numpy as jnp
from jax import lax
from jax.experimental import pallas as pl
from jax.experimental.pallas import tpu as pltpu
from jax.sharding import PartitionSpec as P

LAYERS = 2


NORM_EPS = 1e-05
BETA_FIRST = 0.5
BETA_SECOND = 0.5
ADAM_EPS = 1e-06
WEIGHT_DECAY = 0.01
BF16 = jnp.bfloat16
F32 = jnp.float32
VMEM_BYTES = 56 * 1024 * 1024


def matmul(left, right):
    return lax.dot_general(left, right, (((1,), (0,)), ((), ())), preferred_element_type=F32)


def matmul_nt(left, right):
    return lax.dot_general(left, right, (((1,), (1,)), ((), ())), preferred_element_type=F32)


def matmul_tn(left, right):
    return lax.dot_general(left, right, (((0,), (0,)), ((), ())), preferred_element_type=F32)


def sigmoid(values):
    return 1.0 / (1.0 + jnp.exp(-values))


def silu_slope(values):
    gate = sigmoid(values)
    return gate * (1.0 + values * (1.0 - gate))


def norm_forward(values):
    center = values - jnp.mean(values, axis=-1, keepdims=True)
    spread = jnp.mean(center * center, axis=-1, keepdims=True)
    inverse = lax.rsqrt(spread + NORM_EPS)
    return center * inverse, inverse


def norm_backward(upstream, normed, inverse, gain_row):
    scaled = upstream * gain_row
    return inverse * (
        scaled
        - jnp.mean(scaled, axis=-1, keepdims=True)
        - normed * jnp.mean(scaled * normed, axis=-1, keepdims=True)
    )


def column_sum(values):
    return jnp.sum(values, axis=0, keepdims=True)


def assemble(source, order, rows, offset, target):
    width = source.shape[2]
    nodes, hids = target.shape[0] // rows, target.shape[1] // width
    for i in range(nodes):
        for j in range(hids):
            target[i * rows : (i + 1) * rows, j * width : (j + 1) * width] = source[
                order[i * hids + j], offset : offset + rows, :
            ]


def pack(values, order, rows, offset, target):
    width = target.shape[2]
    nodes, hids = values.shape[0] // rows, values.shape[1] // width
    for i in range(nodes):
        for j in range(hids):
            target[order[i * hids + j], offset : offset + rows, :] = values[
                i * rows : (i + 1) * rows, j * width : (j + 1) * width
            ].astype(target.dtype)


def per_sample(array):
    block = (1,) + array.shape[1:]
    return pl.BlockSpec(block, lambda s: (s,) + (0,) * (len(block) - 1))


def constant(array):
    return pl.BlockSpec(array.shape, lambda s: (0,) * len(array.shape))


def weight_block(array, rows, place):
    blocks, _, width = array.shape
    return pl.BlockSpec((blocks, rows, width), lambda s: (0, place, 0))


def in_scalars():
    return pl.BlockSpec(memory_space=pltpu.SMEM)


def shape_of(shape, dtype):
    return jax.ShapeDtypeStruct(shape, dtype)


def run_kernel(kernel, name, samples, inputs, in_specs, outputs, scratch, flops):
    moved = sum(a.size * a.dtype.itemsize for a in inputs) + sum(
        shape.size * shape.dtype.itemsize for shape, _ in outputs
    )
    return pl.pallas_call(
        kernel,
        name=name,
        grid=(samples,),
        in_specs=in_specs,
        out_specs=[spec for _, spec in outputs],
        out_shape=[shape for shape, _ in outputs],
        scratch_shapes=scratch,
        compiler_params=pltpu.CompilerParams(
            dimension_semantics=("arbitrary",), vmem_limit_bytes=VMEM_BYTES
        ),
        cost_estimate=pl.CostEstimate(flops=flops, bytes_accessed=moved, transcendentals=0),
    )(*inputs)


def sampled(shape, dtype):
    result = shape_of(shape, dtype)
    return (result, per_sample(result))


def shared(shape, dtype):
    result = shape_of(shape, dtype)
    return (result, constant(result))


def edge_forward(order, first, second, table, edge_low, edge_state, at_both, at_nodes, params, node_total, last):
    samples, table_total, latent = table.shape
    edges = edge_low.shape[1]
    alike = edge_low.shape[0] == 1

    def kernel(order, w1, w2, table, low, state, both, nodes, params, pre, act, normed, inverse, *rest):
        if last:
            pooled, w1s, w2s, projected = rest
        else:
            new_state, new_low, pooled, w1s, w2s, projected = rest

        @pl.when(pl.program_id(0) == 0)
        def _():
            assemble(w1, order, w1.shape[1], 0, w1s)
            assemble(w2, order, w2.shape[1], 0, w2s)

        rows = table[0]
        projected[:table_total] = matmul(rows, w1s[latent : 2 * latent]).astype(BF16)
        projected[table_total:] = matmul(rows[:node_total], w1s[2 * latent :]).astype(BF16)
        hidden = matmul(low[0], w1s[:latent]) + matmul(both[...], projected[...]) + params[0:1]
        pre[0] = hidden.astype(BF16)
        active = (hidden * sigmoid(hidden)).astype(BF16)
        act[0] = active
        output = matmul_nt(active, w2s[...]) + params[1:2]
        scaled, scale = norm_forward(output)
        normed[0] = scaled.astype(BF16)
        inverse[0] = scale
        state_new = state[0].astype(F32) + scaled * params[2:3] + params[3:4]
        low_new = state_new.astype(BF16)
        if not last:
            new_state[0] = state_new
            new_low[0] = low_new
        pooled[0] = matmul(nodes[...], low_new).astype(BF16)

    wide = (samples, edges, latent)
    outputs = [sampled(wide, BF16), sampled(wide, BF16), sampled(wide, BF16), sampled((samples, edges, 1), F32)]
    if not last:
        outputs += [sampled(wide, F32), sampled(wide, BF16)]
    outputs += [sampled((samples, node_total, latent), BF16)]
    of_edges = constant if alike else per_sample
    return run_kernel(
        kernel,
        "edge_forward",
        samples,
        [order, first[0], second[0], table, edge_low, edge_state, at_both, at_nodes, params],
        [
            in_scalars(),
            weight_block(*first),
            weight_block(*second),
            per_sample(table),
            of_edges(edge_low),
            of_edges(edge_state),
            constant(at_both),
            constant(at_nodes),
            constant(params),
        ],
        outputs,
        [
            pltpu.VMEM((3 * latent, latent), BF16),
            pltpu.VMEM((latent, latent), BF16),
            pltpu.VMEM((at_both.shape[1], latent), BF16),
        ],
        2 * samples * edges * latent * (3 * latent + at_both.shape[1]),
    )


def edge_backward(order, first, second, pooled_grad, edge_grad, normed, inverse, pre, at_receiver, at_both_t, gain, last, node_total):
    samples, edges, latent = normed.shape
    at_total = at_both_t.shape[0]
    table_total = at_total - node_total

    def kernel(order, w1, w2, upstream, *rest):
        if not last:
            later, rest = rest[0], rest[1:]
        normed, inverse, pre, receiver, both_t, gain, low, hidden_low, at_rows, partial, returned, grad_out, minor = rest[:13]
        if last:
            w1s, w2s = rest[13:]
        else:
            hidden_sum, w1s, w2s, hidden_acc = rest[13:]
        step = pl.program_id(0)

        @pl.when(step == 0)
        def _():
            assemble(w1, order, w1.shape[1], 0, w1s)
            assemble(w2, order, w2.shape[1], 0, w2s)
            minor[...] = jnp.zeros_like(minor)

        grad = matmul(receiver[...], upstream[0])
        if not last:
            grad = grad + later[0]
        scaled = normed[0].astype(F32)
        output_grad = norm_backward(grad, scaled, inverse[0], gain[0:1]).astype(BF16)
        low[0] = output_grad
        act_grad = matmul(output_grad, w2s[...])
        pre_grad = (act_grad * silu_slope(pre[0].astype(F32))).astype(BF16)
        hidden_low[0] = pre_grad
        minor[0:1] += column_sum(pre_grad.astype(F32))
        minor[1:2] += column_sum(output_grad.astype(F32))
        minor[2:3] += column_sum(grad * scaled)
        minor[3:4] += column_sum(grad)
        at_rows[0] = matmul(both_t[...], pre_grad).astype(BF16)
        send = w1s[latent : 2 * latent]
        partial[0] = matmul_nt(at_rows[0, :node_total], send) + matmul_nt(
            at_rows[0, table_total:], w1s[2 * latent :]
        )
        returned[0] = matmul_nt(at_rows[0, node_total:table_total], send).astype(BF16)
        if last:
            grad_out[0] = grad + matmul_nt(pre_grad, w1s[:latent])
        else:

            @pl.when(step == 0)
            def _():
                grad_out[...] = grad
                hidden_acc[...] = pre_grad.astype(F32)

            @pl.when(step > 0)
            def _():
                grad_out[...] += grad
                hidden_acc[...] += pre_grad.astype(F32)

            @pl.when(step == samples - 1)
            def _():
                total = hidden_acc[...].astype(BF16)
                hidden_sum[...] = total
                grad_out[...] += matmul_nt(total, w1s[:latent])

    wide = (samples, edges, latent)
    outputs = [
        sampled(wide, BF16),
        sampled(wide, BF16),
        sampled((samples, at_total, latent), BF16),
        sampled((samples, node_total, latent), F32),
        sampled((samples, table_total - node_total, latent), BF16),
        sampled(wide, F32) if last else shared((edges, latent), F32),
        shared((4, latent), F32),
    ]
    scratch = [pltpu.VMEM((3 * latent, latent), BF16), pltpu.VMEM((latent, latent), BF16)]
    inputs = [order, first[0], second[0], pooled_grad]
    specs = [in_scalars(), weight_block(*first), weight_block(*second), per_sample(pooled_grad)]
    if not last:
        outputs.append(shared((edges, latent), BF16))
        scratch.append(pltpu.VMEM((edges, latent), F32))
        inputs.append(edge_grad)
        specs.append(per_sample(edge_grad))
    inputs += [normed, inverse, pre, at_receiver, at_both_t, gain]
    specs += [
        per_sample(normed),
        per_sample(inverse),
        per_sample(pre),
        constant(at_receiver),
        constant(at_both_t),
        constant(gain),
    ]
    return run_kernel(
        kernel,
        "edge_backward",
        samples,
        inputs,
        specs,
        outputs,
        scratch,
        2 * samples * edges * latent * (2 * latent + 2 * at_total),
    )


def edge_weight_grads(order, edge_low, table, hidden_low, at_rows, low, act, node_total, nodes, width, packed_before):
    samples, table_total, latent = table.shape
    alike = edge_low.ndim == 2
    first_rows, second_rows = 3 * latent // nodes, latent // nodes
    offset = 0 if packed_before is None else packed_before.shape[1]

    def kernel(order, edge_low, table, hidden_low, at_rows, low, act, *rest):
        if packed_before is not None:
            before, rest = rest[0], rest[1:]
        packed, first, second = rest
        step = pl.program_id(0)

        @pl.when(step == 0)
        def _():
            first[...] = jnp.zeros_like(first)
            second[...] = jnp.zeros_like(second)
            if packed_before is not None:
                packed[:, :offset, :] = before[...]
            if alike:
                first[:latent] = matmul_tn(edge_low[...], hidden_low[...])

        if not alike:
            first[:latent] += matmul_tn(edge_low[0], hidden_low[0])
        first[latent : 2 * latent] += matmul_tn(table[0], at_rows[0, :table_total])
        first[2 * latent :] += matmul_tn(table[0, :node_total], at_rows[0, table_total:])
        second[...] += matmul_tn(low[0], act[0])

        @pl.when(step == samples - 1)
        def _():
            pack(first, order, first_rows, offset, packed)
            pack(second, order, second_rows, offset + first_rows, packed)

    of_edges = constant if alike else per_sample
    inputs = [order, edge_low, table, hidden_low, at_rows, low, act]
    specs = [in_scalars(), of_edges(edge_low), per_sample(table), of_edges(hidden_low), per_sample(at_rows), per_sample(low), per_sample(act)]
    if packed_before is not None:
        inputs.append(packed_before)
        specs.append(constant(packed_before))
    return run_kernel(
        kernel,
        "edge_weight_grads",
        samples,
        inputs,
        specs,
        [shared((order.shape[0], offset + first_rows + second_rows, width), BF16)],
        [pltpu.VMEM((3 * latent, latent), F32), pltpu.VMEM((latent, latent), F32)],
        4 * low.size * latent,
    )[0]


def node_pass(order, weights, nodes, node_low, state, pooled_pair, params, at_halo, target, scaling, mask):
    samples, node_total, latent = node_low.shape
    array, rows, place = weights
    second_rows = latent // nodes
    first_rows = rows - second_rows
    count = samples * node_total
    last = target is not None

    def kernel(order, w, node_low, state, pooled_own, pooled_other, params, *rest):
        if last:
            target, scaling, mask, new_low, upstream, input_grad, packed, minor, w1s, w2s, first, second = rest
        else:
            at_halo, pooled_out, pre, act, normed, inverse, new_state, new_low, halo, w1s, w2s = rest
        assemble(w, order, first_rows, 0, w1s)
        assemble(w, order, second_rows, first_rows, w2s)
        rows_low = node_low[...].reshape(count, latent)
        pooled = (pooled_own[...].astype(F32) + pooled_other[...].astype(F32)).astype(BF16)
        pooled = pooled.reshape(count, latent)
        hidden = matmul(rows_low, w1s[:latent]) + matmul(pooled, w1s[latent:]) + params[4:5]
        active = (hidden * sigmoid(hidden)).astype(BF16)
        output = matmul_nt(active, w2s[...]) + params[5:6]
        scaled, scale = norm_forward(output)
        state_new = state[...].astype(F32).reshape(count, latent) + scaled * params[6:7] + params[7:8]
        low_new = state_new.astype(BF16).reshape(new_low.shape)
        new_low[...] = low_new
        if not last:
            pooled_out[...] = pooled
            pre[...] = hidden.astype(BF16)
            act[...] = active
            normed[...] = scaled.astype(BF16)
            inverse[...] = scale
            new_state[...] = state_new.reshape(new_state.shape)
            for s in range(samples):
                halo[s] = matmul(at_halo[...], new_low[s]).astype(BF16)
        else:
            grad = (target[...].astype(F32) * scaling[...]).reshape(count, latent)
            node_gradients(
                grad, scaled, scale, hidden, active, rows_low, pooled, params, mask,
                w1s, w2s, first, second, upstream, input_grad, packed, minor, order, first_rows, second_rows,
            )

    shape = node_low.shape
    inputs = [order, array, node_low, state, *pooled_pair, params]
    scratch = [pltpu.VMEM((2 * latent, latent), BF16), pltpu.VMEM((latent, latent), BF16)]
    if last:
        inputs += [target, scaling, mask]
        outputs = [shared(shape, BF16), *gradient_outputs(shape, order.shape[0], rows, array.shape[2])]
        scratch += [pltpu.VMEM((2 * latent, latent), F32), pltpu.VMEM((latent, latent), F32)]
    else:
        inputs += [at_halo]
        outputs = [
            shared((count, latent), BF16),
            shared((count, latent), BF16),
            shared((count, latent), BF16),
            shared((count, latent), BF16),
            shared((count, 1), F32),
            shared(shape, F32),
            shared(shape, BF16),
            shared((samples, at_halo.shape[0], latent), BF16),
        ]
    specs = [in_scalars(), weight_block(*weights)] + [constant(a) for a in inputs[2:]]
    return run_kernel(kernel, "node_pass", 1, inputs, specs, outputs, scratch, 6 * count * latent * latent * (3 if last else 1))


def gradient_outputs(shape, blocks, rows, width):
    return [
        shared(shape, BF16),
        shared(shape, F32),
        shared((blocks, rows, width), BF16),
        shared((4, shape[-1]), F32),
    ]


def node_gradients(
    grad, scaled, scale, hidden, active, rows_low, pooled, params, mask,
    w1s, w2s, first, second, upstream, input_grad, packed, minor, order, first_rows, second_rows,
):
    latent = w2s.shape[0]
    output_grad = norm_backward(grad, scaled, scale, params[6:7]).astype(BF16)
    pre_grad = (matmul(output_grad, w2s[...]) * silu_slope(hidden)).astype(BF16)
    upstream[...] = matmul_nt(pre_grad, w1s[latent:]).astype(BF16).reshape(upstream.shape)
    input_grad[...] = (grad + matmul_nt(pre_grad, w1s[:latent])).reshape(input_grad.shape)
    chosen = mask[...] > 0.5
    output_mine = jnp.where(chosen, output_grad.astype(F32), 0.0)
    pre_mine = jnp.where(chosen, pre_grad.astype(F32), 0.0)
    grad_mine = jnp.where(chosen, grad, 0.0)
    minor[0:1] = column_sum(pre_mine)
    minor[1:2] = column_sum(output_mine)
    minor[2:3] = column_sum(grad_mine * scaled)
    minor[3:4] = column_sum(grad_mine)
    pre_mine = pre_mine.astype(BF16)
    first[:latent] = matmul_tn(rows_low, pre_mine)
    first[latent:] = matmul_tn(pooled, pre_mine)
    second[...] = matmul_tn(output_mine.astype(BF16), active)
    pack(first, order, first_rows, 0, packed)
    pack(second, order, second_rows, first_rows, packed)


def node_backward(order, weights, nodes, grads, node_low, pooled, pre, act, normed, inverse, params, mask):
    samples, node_total, latent = node_low.shape
    array, rows, place = weights
    second_rows = latent // nodes
    first_rows = rows - second_rows
    count = samples * node_total

    def kernel(order, w, base, own, other, node_low, pooled, pre, act, normed, inverse, params, mask, upstream, input_grad, packed, minor, w1s, w2s, first, second):
        assemble(w, order, first_rows, 0, w1s)
        assemble(w, order, second_rows, first_rows, w2s)
        grad = (base[...] + (own[...] + other[...].astype(F32))).reshape(count, latent)
        node_gradients(
            grad, normed[...].astype(F32), inverse[...], pre[...].astype(F32), act[...],
            node_low[...].reshape(count, latent), pooled[...], params, mask,
            w1s, w2s, first, second, upstream, input_grad, packed, minor, order, first_rows, second_rows,
        )

    inputs = [order, array, *grads, node_low, pooled, pre, act, normed, inverse, params, mask]
    specs = [in_scalars(), weight_block(*weights)] + [constant(a) for a in inputs[2:]]
    return run_kernel(
        kernel,
        "node_backward",
        1,
        inputs,
        specs,
        gradient_outputs(node_low.shape, order.shape[0], rows, array.shape[2]),
        [
            pltpu.VMEM((2 * latent, latent), BF16),
            pltpu.VMEM((latent, latent), BF16),
            pltpu.VMEM((2 * latent, latent), F32),
            pltpu.VMEM((latent, latent), F32),
        ],
        12 * count * latent * latent,
    )


def dot(spec, left, right):
    return jnp.einsum(spec, left, right, preferred_element_type=F32)


def swap(values, axis, offset):
    return lax.ppermute(values, axis, [(i, i ^ offset) for i in range(lax.axis_size(axis))])


def bits_of(axis):
    return lax.axis_size(axis).bit_length() - 1


def own_bit(axis, bit):
    return (lax.axis_index(axis) >> bit) & 1


def all_bits():
    return [(axis, bit) for axis in ("node", "hid") for bit in reversed(range(bits_of(axis)))]


def ordered(own, mine, other):
    low = jnp.where(own == 0, mine, other)
    high = jnp.where(own == 0, other, mine)
    return low, high


def double_up(part, axis, bit, place):
    low, high = ordered(own_bit(axis, bit), part, swap(part, axis, 1 << bit))
    return jnp.stack([low, high], axis=place)


def halve_sum(parts, axis, bit, place):
    own = own_bit(axis, bit)
    sent = lax.dynamic_index_in_dim(parts, 1 - own, place, keepdims=False)
    kept = lax.dynamic_index_in_dim(parts, own, place, keepdims=False)
    return kept.astype(F32) + swap(sent.astype(BF16), axis, 1 << bit).astype(F32)


def places():
    node_ids = jnp.arange(lax.axis_size("node"), dtype=jnp.int32) ^ lax.axis_index("node")
    hid_ids = jnp.arange(lax.axis_size("hid"), dtype=jnp.int32) ^ lax.axis_index("hid")
    place = 0
    for step, (axis, bit) in enumerate(all_bits()):
        ids = node_ids[:, None] if axis == "node" else hid_ids[None, :]
        place = place + (((ids >> bit) & 1) << step)
    return place.reshape(-1)


def after(value, *earlier):
    return lax.optimization_barrier((value, *earlier))[0]


def gather_step(held, step):
    axis, bit = all_bits()[step]
    return jnp.concatenate([held, swap(held, axis, 1 << bit)], axis=0)


def scatter_start(packed):
    half = packed.shape[0] // 2
    return packed[:half], packed[half:]


def scatter_step(pair, step):
    axis, bit = all_bits()[step]
    kept, sent = pair
    total = kept.astype(F32) + swap(sent, axis, 1 << bit).astype(F32)
    if step == 0:
        return total[0]
    half = total.shape[0] // 2
    return total[:half], total[half:].astype(BF16)


def sum_step(values, step):
    axis, bit = all_bits()[step]
    return values + swap(values, axis, 1 << bit)


def sum_everywhere(values):
    for axis, bit in reversed(all_bits()):
        values = values + swap(values, axis, 1 << bit)
    return values


def to_neighbours(rows, halo_width):
    count = lax.axis_size("node")
    onward = [(i, (i + 1) % count) for i in range(count)]
    back = [(target, source) for source, target in onward]
    from_previous = lax.ppermute(rows[:, halo_width:], "node", onward)
    from_next = lax.ppermute(rows[:, :halo_width], "node", back)
    return jnp.concatenate([from_previous, from_next], axis=1)


def adam_terms(weight, grad, first, second, decay):
    first_new = BETA_FIRST * first + (1.0 - BETA_FIRST) * grad
    second_new = BETA_SECOND * second + (1.0 - BETA_SECOND) * grad * grad
    update = first_new / (jnp.sqrt(second_new) + ADAM_EPS) + decay * weight
    return (first_new, second_new, update)


def pack_shards(first, second):
    return jnp.concatenate([first, second.T], axis=0).astype(BF16)


def adam_terms(weight, grad, first, second, decay):
    first_new = BETA_FIRST * first + (1.0 - BETA_FIRST) * grad
    second_new = BETA_SECOND * second + (1.0 - BETA_SECOND) * grad * grad
    update = first_new / (jnp.sqrt(second_new) + ADAM_EPS) + decay * weight
    return (first_new, second_new, update)


def per_device(
    node_in,
    edge_in,
    cotangent,
    ocean_mask,
    present_mask,
    valid_counts,
    send_slot,
    recv_local,
    halo_lists,
    edge_first,
    edge_second,
    node_first,
    node_second,
    edge_first_m,
    edge_second_m,
    node_first_m,
    node_second_m,
    edge_first_v,
    edge_second_v,
    node_first_v,
    node_second_v,
    small_params,
    small_m,
    small_v,
    learn_rate,
):
    hid_count = lax.axis_size("hid")
    hid_index = lax.axis_index("hid")
    node_total, sample_count, latent = node_in.shape
    edge_part = edge_in.shape[0] // hid_count
    node_part = node_total // hid_count
    halo_width = halo_lists.shape[1]
    table_total = node_total + 2 * halo_width
    sample_half, edge_half = hid_index >> 1, hid_index & 1
    samples = sample_count // 2
    nodes, hids = lax.axis_size("node"), hid_count
    first_rows = edge_first.shape[1]
    second_rows = edge_second.shape[2]
    node_rows = node_first.shape[1] + second_rows
    width = edge_first.shape[2]

    order = places()
    steps = len(all_bits())
    edge_zero = pack_shards(edge_first[0], edge_second[0])[None]
    for step in range(steps - 2):
        edge_zero = gather_step(edge_zero, step)
    setup = edge_zero
    node_zero = after(pack_shards(node_first[0], node_second[0])[None], edge_zero)
    layer_one = jnp.concatenate(
        [pack_shards(node_first[1], node_second[1]), pack_shards(edge_first[1], edge_second[1])], axis=0
    )[None]
    for step in range(steps - 3):
        node_zero = gather_step(node_zero, step)
    layer_one = after(layer_one, node_zero)
    layer_one = gather_step(layer_one, 0)
    edge_zero = gather_step(edge_zero, steps - 2)
    edge_zero = after(edge_zero, node_zero)
    edge_zero = gather_step(edge_zero, steps - 1)
    node_zero = gather_step(node_zero, steps - 3)
    edge_zero = after(edge_zero, node_zero, layer_one)
    edge_weights = [((edge_zero, first_rows, 0), (edge_zero, second_rows, first_rows // second_rows))]

    def own_edges(values):
        return lax.dynamic_index_in_dim(
            values.reshape(2, 2, edge_part, *values.shape[1:]), edge_half, 1, keepdims=False
        ).reshape(2 * edge_part, *values.shape[1:])

    def own_nodes(values):
        return lax.dynamic_index_in_dim(
            values.reshape(samples, 2, 2, node_part, latent), edge_half, 2, keepdims=False
        ).reshape(samples, 2 * node_part, latent)

    def own_samples(values):
        return lax.dynamic_slice_in_dim(values, sample_half * samples, samples, 1)

    def to_own_rows(values):
        quarters = jnp.moveaxis(values.reshape(samples, 2, 2, node_part, latent), 0, 3)
        quarters = lax.dynamic_index_in_dim(quarters, edge_half, 1, keepdims=False)
        sent = lax.dynamic_index_in_dim(quarters, 1 - sample_half, 0, keepdims=False)
        kept = lax.dynamic_index_in_dim(quarters, sample_half, 0, keepdims=False)
        return jnp.concatenate(ordered(sample_half, kept, swap(sent, "hid", 2)), axis=1)

    send_slot, recv_local, halo_lists, node_in, edge_in = lax.optimization_barrier(
        (send_slot, recv_local, halo_lists, node_in, edge_in, setup)
    )[:5]
    sender = own_edges(send_slot)
    receiver = own_edges(recv_local)
    node_ids, table_ids = jnp.arange(node_total), jnp.arange(table_total)
    at_receiver = (receiver[:, None] == node_ids[None, :]).astype(BF16)
    at_both = jnp.concatenate(
        [(sender[:, None] == table_ids[None, :]).astype(BF16), at_receiver], axis=1
    )
    at_nodes = (node_ids[:, None] == receiver[None, :]).astype(BF16)
    at_both_t = jnp.concatenate(
        [(table_ids[:, None] == sender[None, :]).astype(BF16), at_nodes], axis=0
    )
    at_halo = (halo_lists.reshape(-1)[:, None] == node_ids[None, :]).astype(BF16)
    mask = ((node_ids // node_part) % 2 == edge_half).astype(F32)
    mask = jnp.tile(mask, samples)[:, None]

    node_low = jnp.transpose(own_samples(node_in), (1, 0, 2))
    edge_in_own = own_edges(edge_in)
    halo_rows = dot("hn,snl->shl", at_halo, node_low).astype(BF16)
    node_low_zero = node_low
    table_zero = jnp.concatenate([node_low, to_neighbours(halo_rows, halo_width)], axis=1)
    pre_zero, act_zero, normed_zero, inverse_zero, edge_state, edge_low, pooled = edge_forward(
        order,
        *edge_weights[0],
        table_zero,
        edge_in_own[None],
        edge_in_own[None],
        at_both,
        at_nodes,
        small_params[0],
        node_total,
        False,
    )
    for step in range(steps - 2, steps):
        node_zero = gather_step(node_zero, step)
    for step in range(1, steps - 2):
        layer_one = gather_step(layer_one, step)
    node_weights = [(node_zero, node_rows, 0)]
    other = swap(pooled, "hid", 1)
    pooled, other = lax.optimization_barrier((pooled, other, layer_one))[:2]
    (
        pooled_zero,
        node_pre,
        node_act,
        node_normed,
        node_inverse,
        node_state,
        node_low,
        halo_rows,
    ) = node_pass(
        order,
        node_weights[0],
        nodes,
        node_low_zero,
        node_low_zero,
        (pooled, other),
        small_params[0],
        at_halo,
        None,
        None,
        None,
    )
    for step in range(steps - 2, steps):
        layer_one = gather_step(layer_one, step)
    edge_weights.append(
        ((layer_one, first_rows, 1), (layer_one, second_rows, 2 * first_rows // second_rows))
    )
    node_weights.append((layer_one, node_rows, 0))

    valid_mask = (ocean_mask[:, None] * present_mask).astype(BF16)
    masked = after(cotangent, pooled) * valid_mask[:, :, None]
    sent = lax.dynamic_slice_in_dim(masked, (1 - sample_half) * samples, samples, 1)
    masked = jnp.stack(ordered(sample_half, own_samples(masked), swap(sent, "hid", 2)), axis=0)
    masked = double_up(masked, "hid", 0, 1).reshape(node_total, samples, latent)
    scaling = node_total * lax.axis_size("node") / valid_counts.astype(F32)
    scaling = lax.dynamic_slice_in_dim(scaling, sample_half * samples, samples, 0)
    target = jnp.transpose(masked, (1, 0, 2))
    scaling = scaling[:, None, None]

    node_low_one = node_low
    table_one = jnp.concatenate([node_low, to_neighbours(halo_rows, halo_width)], axis=1)
    pre_one, act_one, normed_one, inverse_one, pooled = edge_forward(
        order,
        *edge_weights[1],
        table_one,
        edge_low,
        edge_state,
        at_both,
        at_nodes,
        small_params[1],
        node_total,
        True,
    )
    node_low, pooled_grad, node_grad, node_packed, node_minor_one = node_pass(
        order,
        node_weights[1],
        nodes,
        node_low_one,
        node_state,
        (pooled, swap(pooled, "hid", 1)),
        small_params[1],
        None,
        target,
        scaling,
        mask,
    )
    masters = (edge_first, edge_second, node_first, node_second)
    weight_local = jnp.stack(
        [jnp.sum(matrix * matrix, axis=(1, 2)) for matrix in after(masters, node_low)], axis=1
    )
    node_out = to_own_rows(node_low)

    def from_edges(partial, returned):
        returned = to_neighbours(returned, halo_width)
        return partial + dot("hn,shl->snl", at_halo, returned)

    low, hidden_low, at_rows, partial, returned, edge_grad, edge_minor_one = edge_backward(
        order,
        *edge_weights[1],
        pooled_grad,
        None,
        normed_one,
        inverse_one,
        pre_one,
        at_receiver,
        at_both_t,
        small_params[1, 2:3],
        True,
        node_total,
    )
    packed = edge_weight_grads(
        order,
        edge_low,
        table_one,
        hidden_low,
        at_rows,
        low,
        act_one,
        node_total,
        nodes,
        width,
        node_packed,
    )
    partial = from_edges(partial, returned)
    other = swap(partial.astype(BF16), "hid", 1)
    chain_one = scatter_step(scatter_start(packed), steps - 1)
    other, kept, sent = lax.optimization_barrier((other, *chain_one))
    chain_one = (kept, sent)
    pooled_grad, node_grad, node_packed, node_minor_zero = node_backward(
        order,
        node_weights[0],
        nodes,
        (node_grad, partial, other),
        node_low_zero,
        pooled_zero,
        node_pre,
        node_act,
        node_normed,
        node_inverse,
        small_params[0],
        mask,
    )
    low, hidden_low, at_rows, partial, returned, edge_input_grad, edge_minor_zero, hidden_sum = (
        edge_backward(
            order,
            *edge_weights[0],
            pooled_grad,
            edge_grad,
            normed_zero,
            inverse_zero,
            pre_zero,
            at_receiver,
            at_both_t,
            small_params[0, 2:3],
            False,
            node_total,
        )
    )
    chain_zero = scatter_step(scatter_start(node_packed), steps - 1)
    chain_one = scatter_step(chain_one, steps - 2)
    low, *held = lax.optimization_barrier((low, *chain_zero, *chain_one))
    chain_zero, chain_one = held[:2], held[2:]
    packed = edge_weight_grads(
        order,
        edge_in_own,
        table_zero,
        hidden_sum,
        at_rows,
        low,
        act_zero,
        node_total,
        nodes,
        width,
        None,
    )
    minor_packed = jnp.concatenate(
        [edge_minor_zero, node_minor_zero, edge_minor_one, node_minor_one]
        + [jnp.pad(weight_local.reshape(1, -1), ((0, 0), (0, latent - weight_local.size)))],
        axis=0,
    )
    chain_zero = scatter_step(chain_zero, steps - 2)
    chain_one = tuple(jnp.concatenate(pair, axis=1) for pair in zip(chain_one, chain_zero))
    chain_edge = scatter_step(scatter_start(packed), steps - 1)
    minor_packed = sum_step(minor_packed, steps - 1)
    for step in reversed(range(steps - 1)):
        minor_packed, *held = lax.optimization_barrier(
            (minor_packed, *chain_edge, *chain_one)
        )
        chain_edge = held[:2]
        if step > 0:
            chain_one = scatter_step(held[2:], step - 1)
        chain_edge = scatter_step(chain_edge, step)
        minor_packed = sum_step(minor_packed, step)
        if step == 1:
            chain_one = (chain_one,)
    edge_zero_grads, node_grads = chain_edge, chain_one[0]
    partial = from_edges(partial, returned)
    node_grad = node_grad + (partial + swap(partial.astype(BF16), "hid", 1).astype(F32))
    grad_node = to_own_rows(node_grad.astype(BF16))
    edge_input_grad = halve_sum(edge_input_grad.reshape(2, edge_part, latent), "hid", 1, 0)

    minor_total = minor_packed[: 8 * LAYERS].reshape(small_params.shape)
    weight_squares = minor_packed[8 * LAYERS, : weight_local.size].reshape(weight_local.shape)
    edge_rows = first_rows + second_rows
    node_one_grads = node_grads[:node_rows]
    edge_one_grads = node_grads[node_rows : node_rows + edge_rows]
    node_zero_grads = node_grads[node_rows + edge_rows :]
    node_first_rows = node_rows - second_rows
    grads = [
        jnp.stack([edge_zero_grads[:first_rows], edge_one_grads[:first_rows]]),
        jnp.stack([edge_zero_grads[first_rows:].T, edge_one_grads[first_rows:].T]),
        jnp.stack([node_zero_grads[:node_first_rows], node_one_grads[:node_first_rows]]),
        jnp.stack([node_zero_grads[node_first_rows:].T, node_one_grads[node_first_rows:].T]),
    ]
    firsts = (edge_first_m, edge_second_m, node_first_m, node_second_m)
    seconds = (edge_first_v, edge_second_v, node_first_v, node_second_v)
    moment_list = [
        adam_terms(masters[place], grads[place], firsts[place], seconds[place], WEIGHT_DECAY)
        for place in range(4)
    ]
    update_squares = sum_everywhere(
        jnp.stack([jnp.sum(entry[2] * entry[2], axis=(1, 2)) for entry in moment_list], axis=1)
    )
    weight_norm = jnp.sqrt(weight_squares)
    update_norm = jnp.sqrt(update_squares)
    new_weights = []
    for position in range(4):
        ratio = weight_norm[:, position] / update_norm[:, position]
        new_weights.append(
            masters[position] - learn_rate[0] * ratio[:, None, None] * moment_list[position][2]
        )
    small_first, small_second, small_update = adam_terms(
        small_params, minor_total, small_m, small_v, 0.0
    )
    small_wnorm = jnp.sqrt(jnp.sum(small_params * small_params, axis=2))
    small_unorm = jnp.sqrt(jnp.sum(small_update * small_update, axis=2))
    small_new = (
        small_params - learn_rate[0] * (small_wnorm / small_unorm)[:, :, None] * small_update
    )
    norms = jnp.stack(
        [
            jnp.concatenate([weight_norm, small_wnorm], axis=1),
            jnp.concatenate([update_norm, small_unorm], axis=1),
        ],
        axis=2,
    )
    return (
        node_out,
        grad_node,
        edge_input_grad.astype(BF16),
        *new_weights,
        *[entry[0] for entry in moment_list],
        *[entry[1] for entry in moment_list],
        *[weight.astype(BF16) for weight in new_weights],
        small_new,
        small_first,
        small_second,
        norms,
    )


def solution(mesh):
    whole = P()
    rows = P(None, "node", "hid")
    columns = P(None, "hid", "node")
    matrices = (rows, columns, rows, columns)
    in_specs = (
        P("node", None, None),
        P("node", None),
        P(("node", "hid"), None, None),
        P(("node", "hid")),
        P(("node", "hid"), None),
        P(),
        P("node"),
        P("node"),
        P("node", None),
        *matrices,
        *matrices,
        *matrices,
        whole,
        whole,
        whole,
        whole,
    )
    out_specs = (
        P(("node", "hid"), None, None),
        P(("node", "hid"), None, None),
        P(("node", "hid"), None),
        *matrices,
        *matrices,
        *matrices,
        *matrices,
        whole,
        whole,
        whole,
        whole,
    )
    return jax.shard_map(
        per_device, mesh=mesh, in_specs=in_specs, out_specs=out_specs, check_vma=False
    )
```

```python
import jax
import jax.numpy as jnp
from jax import lax
from jax.experimental import pallas as pl
from jax.experimental.pallas import tpu as pltpu
from jax.sharding import PartitionSpec as P

LAYERS = 2


NORM_EPS = 1e-05
BETA_FIRST = 0.5
BETA_SECOND = 0.5
ADAM_EPS = 1e-06
WEIGHT_DECAY = 0.01
BF16 = jnp.bfloat16
F32 = jnp.float32
VMEM_BYTES = 56 * 1024 * 1024


def matmul(left, right):
    return lax.dot_general(left, right, (((1,), (0,)), ((), ())), preferred_element_type=F32)


def matmul_nt(left, right):
    return lax.dot_general(left, right, (((1,), (1,)), ((), ())), preferred_element_type=F32)


def matmul_tn(left, right):
    return lax.dot_general(left, right, (((0,), (0,)), ((), ())), preferred_element_type=F32)


def sigmoid(values):
    return 1.0 / (1.0 + jnp.exp(-values))


def silu_slope(values):
    gate = sigmoid(values)
    return gate * (1.0 + values * (1.0 - gate))


def norm_forward(values):
    center = values - jnp.mean(values, axis=-1, keepdims=True)
    spread = jnp.mean(center * center, axis=-1, keepdims=True)
    inverse = lax.rsqrt(spread + NORM_EPS)
    return center * inverse, inverse


def norm_backward(upstream, normed, inverse, gain_row):
    scaled = upstream * gain_row
    return inverse * (
        scaled
        - jnp.mean(scaled, axis=-1, keepdims=True)
        - normed * jnp.mean(scaled * normed, axis=-1, keepdims=True)
    )


def column_sum(values):
    return jnp.sum(values, axis=0, keepdims=True)


def assemble(source, order, rows, offset, target):
    width = source.shape[2]
    nodes, hids = target.shape[0] // rows, target.shape[1] // width
    for i in range(nodes):
        for j in range(hids):
            target[i * rows : (i + 1) * rows, j * width : (j + 1) * width] = source[
                order[i * hids + j], offset : offset + rows, :
            ]


def store(target, begin, values):
    rows, width = values.shape[0], target.shape[2]
    for j in range(target.shape[0]):
        target[j, begin : begin + rows] = values[:, j * width : (j + 1) * width]


def add(target, begin, values):
    rows, width = values.shape[0], target.shape[2]
    for j in range(target.shape[0]):
        target[j, begin : begin + rows] += values[:, j * width : (j + 1) * width]


def pack(values, owners, rows, offset, kept, sent):
    half = kept.shape[0]
    for place in range(2 * half):
        target = kept if place < half else sent
        begin = pl.multiple_of(owners[2 * place] * rows, rows)
        target[place % half, offset : offset + rows, :] = values[
            owners[2 * place + 1], pl.ds(begin, rows), :
        ].astype(BF16)


def per_sample(array):
    block = (1,) + array.shape[1:]
    return pl.BlockSpec(block, lambda s: (s,) + (0,) * (len(block) - 1))


def constant(array):
    return pl.BlockSpec(array.shape, lambda s: (0,) * len(array.shape))


def weight_block(array, rows, place):
    blocks, _, width = array.shape
    return pl.BlockSpec((blocks, rows, width), lambda s: (0, place, 0))


def in_scalars():
    return pl.BlockSpec(memory_space=pltpu.SMEM)


def shape_of(shape, dtype):
    return jax.ShapeDtypeStruct(shape, dtype)


def run_kernel(kernel, name, samples, inputs, in_specs, outputs, scratch, flops):
    moved = sum(a.size * a.dtype.itemsize for a in inputs) + sum(
        shape.size * shape.dtype.itemsize for shape, _ in outputs
    )
    return pl.pallas_call(
        kernel,
        name=name,
        grid=(samples,),
        in_specs=in_specs,
        out_specs=[spec for _, spec in outputs],
        out_shape=[shape for shape, _ in outputs],
        scratch_shapes=scratch,
        compiler_params=pltpu.CompilerParams(
            dimension_semantics=("arbitrary",), vmem_limit_bytes=VMEM_BYTES
        ),
        cost_estimate=pl.CostEstimate(flops=4 * flops, bytes_accessed=moved, transcendentals=0),
    )(*inputs)


def sampled(shape, dtype):
    result = shape_of(shape, dtype)
    return (result, per_sample(result))


def shared(shape, dtype):
    result = shape_of(shape, dtype)
    return (result, constant(result))


def edge_forward(order, first, second, table, edge_low, edge_state, at_both, at_nodes, params, node_total, last):
    samples, table_total, latent = table.shape
    edges = edge_low.shape[1]
    alike = edge_low.shape[0] == 1

    def kernel(order, w1, w2, table, low, state, both, nodes, params, pre, act, normed, inverse, *rest):
        if last:
            pooled, w1s, w2s, projected = rest
        else:
            new_state, new_low, pooled, w1s, w2s, projected = rest

        @pl.when(pl.program_id(0) == 0)
        def _():
            assemble(w1, order, w1.shape[1], 0, w1s)
            assemble(w2, order, w2.shape[1], 0, w2s)

        rows = table[0]
        projected[:table_total] = matmul(rows, w1s[latent : 2 * latent]).astype(BF16)
        projected[table_total:] = matmul(rows[:node_total], w1s[2 * latent :]).astype(BF16)
        hidden = matmul(low[0], w1s[:latent]) + matmul(both[...], projected[...]) + params[0:1]
        pre[0] = hidden.astype(BF16)
        active = (hidden * sigmoid(hidden)).astype(BF16)
        act[0] = active
        output = matmul_nt(active, w2s[...]) + params[1:2]
        scaled, scale = norm_forward(output)
        normed[0] = scaled.astype(BF16)
        inverse[0] = scale
        state_new = state[0].astype(F32) + scaled * params[2:3] + params[3:4]
        low_new = state_new.astype(BF16)
        if not last:
            new_state[0] = state_new
            new_low[0] = low_new
        pooled[0] = matmul(nodes[...], low_new).astype(BF16)

    wide = (samples, edges, latent)
    outputs = [sampled(wide, BF16), sampled(wide, BF16), sampled(wide, BF16), sampled((samples, edges, 1), F32)]
    if not last:
        outputs += [sampled(wide, F32), sampled(wide, BF16)]
    outputs += [sampled((samples, node_total, latent), BF16)]
    of_edges = constant if alike else per_sample
    return run_kernel(
        kernel,
        "edge_forward",
        samples,
        [order, first[0], second[0], table, edge_low, edge_state, at_both, at_nodes, params],
        [
            in_scalars(),
            weight_block(*first),
            weight_block(*second),
            per_sample(table),
            of_edges(edge_low),
            of_edges(edge_state),
            constant(at_both),
            constant(at_nodes),
            constant(params),
        ],
        outputs,
        [
            pltpu.VMEM((3 * latent, latent), BF16),
            pltpu.VMEM((latent, latent), BF16),
            pltpu.VMEM((at_both.shape[1], latent), BF16),
        ],
        2 * samples * edges * latent * (3 * latent + at_both.shape[1]),
    )


def edge_backward(order, first, second, pooled_grad, edge_grad, normed, inverse, pre, at_receiver, at_both_t, gain, last, node_total):
    samples, edges, latent = normed.shape
    at_total = at_both_t.shape[0]
    table_total = at_total - node_total

    def kernel(order, w1, w2, upstream, *rest):
        if not last:
            later, rest = rest[0], rest[1:]
        normed, inverse, pre, receiver, both_t, gain, low, hidden_low, at_rows, partial, returned, grad_out, minor = rest[:13]
        if last:
            w1s, w2s = rest[13:]
        else:
            hidden_sum, w1s, w2s, hidden_acc = rest[13:]
        step = pl.program_id(0)

        @pl.when(step == 0)
        def _():
            assemble(w1, order, w1.shape[1], 0, w1s)
            assemble(w2, order, w2.shape[1], 0, w2s)
            minor[...] = jnp.zeros_like(minor)

        grad = matmul(receiver[...], upstream[0])
        if not last:
            grad = grad + later[0]
        scaled = normed[0].astype(F32)
        output_grad = norm_backward(grad, scaled, inverse[0], gain[0:1]).astype(BF16)
        low[0] = output_grad
        act_grad = matmul(output_grad, w2s[...])
        pre_grad = (act_grad * silu_slope(pre[0].astype(F32))).astype(BF16)
        hidden_low[0] = pre_grad
        minor[0:1] += column_sum(pre_grad.astype(F32))
        minor[1:2] += column_sum(output_grad.astype(F32))
        minor[2:3] += column_sum(grad * scaled)
        minor[3:4] += column_sum(grad)
        at_rows[0] = matmul(both_t[...], pre_grad).astype(BF16)
        send = w1s[latent : 2 * latent]
        partial[0] = matmul_nt(at_rows[0, :node_total], send) + matmul_nt(
            at_rows[0, table_total:], w1s[2 * latent :]
        )
        returned[0] = matmul_nt(at_rows[0, node_total:table_total], send).astype(BF16)
        if last:
            grad_out[0] = grad + matmul_nt(pre_grad, w1s[:latent])
        else:

            @pl.when(step == 0)
            def _():
                grad_out[...] = grad
                hidden_acc[...] = pre_grad.astype(F32)

            @pl.when(step > 0)
            def _():
                grad_out[...] += grad
                hidden_acc[...] += pre_grad.astype(F32)

            @pl.when(step == samples - 1)
            def _():
                total = hidden_acc[...].astype(BF16)
                hidden_sum[...] = total
                grad_out[...] += matmul_nt(total, w1s[:latent])

    wide = (samples, edges, latent)
    outputs = [
        sampled(wide, BF16),
        sampled(wide, BF16),
        sampled((samples, at_total, latent), BF16),
        sampled((samples, node_total, latent), F32),
        sampled((samples, table_total - node_total, latent), BF16),
        sampled(wide, F32) if last else shared((edges, latent), F32),
        shared((4, latent), F32),
    ]
    scratch = [pltpu.VMEM((3 * latent, latent), BF16), pltpu.VMEM((latent, latent), BF16)]
    inputs = [order, first[0], second[0], pooled_grad]
    specs = [in_scalars(), weight_block(*first), weight_block(*second), per_sample(pooled_grad)]
    if not last:
        outputs.append(shared((edges, latent), BF16))
        scratch.append(pltpu.VMEM((edges, latent), F32))
        inputs.append(edge_grad)
        specs.append(per_sample(edge_grad))
    inputs += [normed, inverse, pre, at_receiver, at_both_t, gain]
    specs += [
        per_sample(normed),
        per_sample(inverse),
        per_sample(pre),
        constant(at_receiver),
        constant(at_both_t),
        constant(gain),
    ]
    return run_kernel(
        kernel,
        "edge_backward",
        samples,
        inputs,
        specs,
        outputs,
        scratch,
        2 * samples * edges * latent * (2 * latent + 2 * at_total),
    )


def edge_weight_grads(owners, edge_low, table, hidden_low, at_rows, low, act, node_total, nodes, width, packed_before):
    samples, table_total, latent = table.shape
    alike = edge_low.ndim == 2
    first_rows, second_rows = 3 * latent // nodes, latent // nodes
    offset = 0 if packed_before is None else packed_before[0].shape[1]
    blocks, hids = owners.shape[0] // 2, latent // width

    def kernel(owners, edge_low, table, hidden_low, at_rows, low, act, *rest):
        before, rest = rest[:-4], rest[-4:]
        kept, sent, first, second = rest
        step = pl.program_id(0)

        @pl.when(step == 0)
        def _():
            first[...] = jnp.zeros_like(first)
            second[...] = jnp.zeros_like(second)
            for source, target in zip(before, (kept, sent)):
                target[:, :offset, :] = source[...]
            if alike:
                add(first, 0, matmul_tn(edge_low[...], hidden_low[...]))

        if not alike:
            add(first, 0, matmul_tn(edge_low[0], hidden_low[0]))
        add(first, latent, matmul_tn(table[0], at_rows[0, :table_total]))
        add(first, 2 * latent, matmul_tn(table[0, :node_total], at_rows[0, table_total:]))
        add(second, 0, matmul_tn(low[0], act[0]))

        @pl.when(step == samples - 1)
        def _():
            pack(first, owners, first_rows, offset, kept, sent)
            pack(second, owners, second_rows, offset + first_rows, kept, sent)

    of_edges = constant if alike else per_sample
    inputs = [owners, edge_low, table, hidden_low, at_rows, low, act]
    specs = [in_scalars(), of_edges(edge_low), per_sample(table), of_edges(hidden_low), per_sample(at_rows), per_sample(low), per_sample(act)]
    if packed_before is not None:
        inputs += packed_before
        specs += [constant(a) for a in packed_before]
    return run_kernel(
        kernel,
        "edge_weight_grads",
        samples,
        inputs,
        specs,
        [shared((blocks // 2, offset + first_rows + second_rows, width), BF16)] * 2,
        [pltpu.VMEM((hids, 3 * latent, width), F32), pltpu.VMEM((hids, latent, width), F32)],
        4 * low.size * latent,
    )


def node_pass(order, owners, weights, nodes, node_low, state, pooled_pair, params, at_halo, target, scaling, mask):
    samples, node_total, latent = node_low.shape
    array, rows, place = weights
    second_rows, hids = latent // nodes, latent // array.shape[2]
    first_rows = rows - second_rows
    count = samples * node_total
    last = target is not None

    def kernel(order, *rest):
        if last:
            owners, rest = rest[0], rest[1:]
        w, node_low, state, pooled_own, pooled_other, params, *rest = rest
        if last:
            target, scaling, mask, new_low, upstream, input_grad, kept, sent, minor, w1s, w2s, first, second = rest
        else:
            at_halo, pooled_out, pre, act, normed, inverse, new_state, new_low, halo, w1s, w2s = rest
        assemble(w, order, first_rows, 0, w1s)
        assemble(w, order, second_rows, first_rows, w2s)
        rows_low = node_low[...].reshape(count, latent)
        pooled = (pooled_own[...].astype(F32) + pooled_other[...].astype(F32)).astype(BF16)
        pooled = pooled.reshape(count, latent)
        hidden = matmul(rows_low, w1s[:latent]) + matmul(pooled, w1s[latent:]) + params[4:5]
        active = (hidden * sigmoid(hidden)).astype(BF16)
        output = matmul_nt(active, w2s[...]) + params[5:6]
        scaled, scale = norm_forward(output)
        state_new = state[...].astype(F32).reshape(count, latent) + scaled * params[6:7] + params[7:8]
        low_new = state_new.astype(BF16).reshape(new_low.shape)
        new_low[...] = low_new
        if not last:
            pooled_out[...] = pooled
            pre[...] = hidden.astype(BF16)
            act[...] = active
            normed[...] = scaled.astype(BF16)
            inverse[...] = scale
            new_state[...] = state_new.reshape(new_state.shape)
            for s in range(samples):
                halo[s] = matmul(at_halo[...], new_low[s]).astype(BF16)
        else:
            grad = (target[...].astype(F32) * scaling[...]).reshape(count, latent)
            node_gradients(
                grad, scaled, scale, hidden, active, rows_low, pooled, params, mask,
                w1s, w2s, first, second, upstream, input_grad, kept, sent, minor, owners, first_rows, second_rows,
            )

    shape = node_low.shape
    inputs = [array, node_low, state, *pooled_pair, params]
    scratch = [pltpu.VMEM((2 * latent, latent), BF16), pltpu.VMEM((latent, latent), BF16)]
    if last:
        inputs += [target, scaling, mask]
        outputs = [shared(shape, BF16), *gradient_outputs(shape, order.shape[0], rows, array.shape[2])]
        scratch += [pltpu.VMEM((hids, 2 * latent, latent // hids), F32), pltpu.VMEM((hids, latent, latent // hids), F32)]
    else:
        inputs += [at_halo]
        outputs = [
            shared((count, latent), BF16),
            shared((count, latent), BF16),
            shared((count, latent), BF16),
            shared((count, latent), BF16),
            shared((count, 1), F32),
            shared(shape, F32),
            shared(shape, BF16),
            shared((samples, at_halo.shape[0], latent), BF16),
        ]
    tables = [order, owners] if last else [order]
    specs = [in_scalars() for _ in tables] + [weight_block(*weights)] + [constant(a) for a in inputs[1:]]
    inputs = tables + inputs
    return run_kernel(kernel, "node_pass", 1, inputs, specs, outputs, scratch, 6 * count * latent * latent * (3 if last else 1))


def gradient_outputs(shape, blocks, rows, width):
    return [
        shared(shape, BF16),
        shared(shape, F32),
        shared((blocks // 2, rows, width), BF16),
        shared((blocks // 2, rows, width), BF16),
        shared((4, shape[-1]), F32),
    ]


def node_gradients(
    grad, scaled, scale, hidden, active, rows_low, pooled, params, mask,
    w1s, w2s, first, second, upstream, input_grad, kept, sent, minor, owners, first_rows, second_rows,
):
    latent = w2s.shape[0]
    output_grad = norm_backward(grad, scaled, scale, params[6:7]).astype(BF16)
    pre_grad = (matmul(output_grad, w2s[...]) * silu_slope(hidden)).astype(BF16)
    upstream[...] = matmul_nt(pre_grad, w1s[latent:]).astype(BF16).reshape(upstream.shape)
    input_grad[...] = (grad + matmul_nt(pre_grad, w1s[:latent])).reshape(input_grad.shape)
    chosen = mask[...] > 0.5
    output_mine = jnp.where(chosen, output_grad.astype(F32), 0.0)
    pre_mine = jnp.where(chosen, pre_grad.astype(F32), 0.0)
    grad_mine = jnp.where(chosen, grad, 0.0)
    minor[0:1] = column_sum(pre_mine)
    minor[1:2] = column_sum(output_mine)
    minor[2:3] = column_sum(grad_mine * scaled)
    minor[3:4] = column_sum(grad_mine)
    pre_mine = pre_mine.astype(BF16)
    store(first, 0, matmul_tn(rows_low, pre_mine))
    store(first, latent, matmul_tn(pooled, pre_mine))
    store(second, 0, matmul_tn(output_mine.astype(BF16), active))
    pack(first, owners, first_rows, 0, kept, sent)
    pack(second, owners, second_rows, first_rows, kept, sent)


def node_backward(order, owners, weights, nodes, grads, node_low, pooled, pre, act, normed, inverse, params, mask):
    samples, node_total, latent = node_low.shape
    array, rows, place = weights
    second_rows, hids = latent // nodes, latent // array.shape[2]
    first_rows = rows - second_rows
    count = samples * node_total

    def kernel(order, owners, w, base, own, other, node_low, pooled, pre, act, normed, inverse, params, mask, upstream, input_grad, kept, sent, minor, w1s, w2s, first, second):
        assemble(w, order, first_rows, 0, w1s)
        assemble(w, order, second_rows, first_rows, w2s)
        grad = (base[...] + (own[...] + other[...].astype(F32))).reshape(count, latent)
        node_gradients(
            grad, normed[...].astype(F32), inverse[...], pre[...].astype(F32), act[...],
            node_low[...].reshape(count, latent), pooled[...], params, mask,
            w1s, w2s, first, second, upstream, input_grad, kept, sent, minor, owners, first_rows, second_rows,
        )

    inputs = [order, owners, array, *grads, node_low, pooled, pre, act, normed, inverse, params, mask]
    specs = [in_scalars(), in_scalars(), weight_block(*weights)] + [constant(a) for a in inputs[3:]]
    return run_kernel(
        kernel,
        "node_backward",
        1,
        inputs,
        specs,
        gradient_outputs(node_low.shape, order.shape[0], rows, array.shape[2]),
        [
            pltpu.VMEM((2 * latent, latent), BF16),
            pltpu.VMEM((latent, latent), BF16),
            pltpu.VMEM((hids, 2 * latent, latent // hids), F32),
            pltpu.VMEM((hids, latent, latent // hids), F32),
        ],
        12 * count * latent * latent,
    )


def dot(spec, left, right):
    return jnp.einsum(spec, left, right, preferred_element_type=F32)


def swap(values, axis, offset):
    return lax.ppermute(values, axis, [(i, i ^ offset) for i in range(lax.axis_size(axis))])


def bits_of(axis):
    return lax.axis_size(axis).bit_length() - 1


def own_bit(axis, bit):
    return (lax.axis_index(axis) >> bit) & 1


def all_bits():
    return [(axis, bit) for axis in ("node", "hid") for bit in reversed(range(bits_of(axis)))]


def ordered(own, mine, other):
    low = jnp.where(own == 0, mine, other)
    high = jnp.where(own == 0, other, mine)
    return low, high


def double_up(part, axis, bit, place):
    low, high = ordered(own_bit(axis, bit), part, swap(part, axis, 1 << bit))
    return jnp.stack([low, high], axis=place)


def halve_sum(parts, axis, bit, place):
    own = own_bit(axis, bit)
    sent = lax.dynamic_index_in_dim(parts, 1 - own, place, keepdims=False)
    kept = lax.dynamic_index_in_dim(parts, own, place, keepdims=False)
    return kept.astype(F32) + swap(sent.astype(BF16), axis, 1 << bit).astype(F32)


def places():
    node_ids = jnp.arange(lax.axis_size("node"), dtype=jnp.int32) ^ lax.axis_index("node")
    hid_ids = jnp.arange(lax.axis_size("hid"), dtype=jnp.int32) ^ lax.axis_index("hid")
    place = 0
    for step, (axis, bit) in enumerate(all_bits()):
        ids = node_ids[:, None] if axis == "node" else hid_ids[None, :]
        place = place + (((ids >> bit) & 1) << step)
    return place.reshape(-1)


def owners_of_places():
    place = jnp.arange(1 << len(all_bits()), dtype=jnp.int32)
    owner = {"node": lax.axis_index("node"), "hid": lax.axis_index("hid")}
    for step, (axis, bit) in enumerate(all_bits()):
        owner[axis] = owner[axis] ^ (((place >> step) & 1) << bit)
    return jnp.stack([owner["node"], owner["hid"]], axis=1).reshape(-1)


def after(value, *earlier):
    return lax.optimization_barrier((value, *earlier))[0]


def gather_steps(held, begin, end, *under):
    for axis, bit in all_bits()[begin:end]:
        arrived = after(swap(held, axis, 1 << bit), *under)
        held = jnp.concatenate([held, arrived], axis=0)
    return held


def scatter_step(pair, step, *under):
    axis, bit = all_bits()[step]
    kept, sent = pair
    total = kept.astype(F32) + after(swap(sent, axis, 1 << bit), *under).astype(F32)
    if step == 0:
        return total[0]
    half = total.shape[0] // 2
    return total[:half], total[half:].astype(BF16)


def sum_step(values, step):
    axis, bit = all_bits()[step]
    return values + swap(values, axis, 1 << bit)


def sum_everywhere(values):
    axes = ("node", "hid")
    bits = sum(bits_of(axis) for axis in axes)
    total = 1 << bits
    done = 0
    while done < bits:
        step = 1 if (bits - done) % 2 else 2
        terms = [values]
        for i in range(1, 1 << step):
            pairs = [(k, k ^ (i << done)) for k in range(total)]
            terms.append(lax.ppermute(values, axes, pairs))
        while len(terms) > 1:
            terms = [terms[i] + terms[i + 1] for i in range(0, len(terms), 2)]
        values, done = terms[0], done + step
    return values


def to_neighbours(rows, halo_width):
    count = lax.axis_size("node")
    onward = [(i, (i + 1) % count) for i in range(count)]
    back = [(target, source) for source, target in onward]
    from_previous = lax.ppermute(rows[:, halo_width:], "node", onward)
    from_next = lax.ppermute(rows[:, :halo_width], "node", back)
    return jnp.concatenate([from_previous, from_next], axis=1)


def adam_terms(weight, grad, first, second, decay):
    first_new = BETA_FIRST * first + (1.0 - BETA_FIRST) * grad
    second_new = BETA_SECOND * second + (1.0 - BETA_SECOND) * grad * grad
    update = first_new / (jnp.sqrt(second_new) + ADAM_EPS) + decay * weight
    return (first_new, second_new, update)


def pack_shards(first, second):
    return jnp.concatenate([first, second.T], axis=0).astype(BF16)


def adam_terms(weight, grad, first, second, decay):
    first_new = BETA_FIRST * first + (1.0 - BETA_FIRST) * grad
    second_new = BETA_SECOND * second + (1.0 - BETA_SECOND) * grad * grad
    update = first_new / (jnp.sqrt(second_new) + ADAM_EPS) + decay * weight
    return (first_new, second_new, update)


def per_device(
    node_in,
    edge_in,
    cotangent,
    ocean_mask,
    present_mask,
    valid_counts,
    send_slot,
    recv_local,
    halo_lists,
    edge_first,
    edge_second,
    node_first,
    node_second,
    edge_first_m,
    edge_second_m,
    node_first_m,
    node_second_m,
    edge_first_v,
    edge_second_v,
    node_first_v,
    node_second_v,
    small_params,
    small_m,
    small_v,
    learn_rate,
):
    hid_count = lax.axis_size("hid")
    hid_index = lax.axis_index("hid")
    node_total, sample_count, latent = node_in.shape
    edge_part = edge_in.shape[0] // hid_count
    node_part = node_total // hid_count
    halo_width = halo_lists.shape[1]
    table_total = node_total + 2 * halo_width
    sample_half, edge_half = hid_index >> 1, hid_index & 1
    samples = sample_count // 2
    nodes, hids = lax.axis_size("node"), hid_count
    first_rows = edge_first.shape[1]
    second_rows = edge_second.shape[2]
    node_rows = node_first.shape[1] + second_rows
    width = edge_first.shape[2]

    order, owners = places(), owners_of_places()
    steps = len(all_bits())
    edge_zero = gather_steps(pack_shards(edge_first[0], edge_second[0])[None], 0, steps - 2)
    setup = edge_zero
    first, second = after((node_first[0], node_second[0]), edge_zero)
    node_zero = gather_steps(pack_shards(first, second)[None], 0, steps - 3)
    edge_zero = gather_steps(edge_zero, steps - 2, steps - 1)
    first, second = after((edge_first[1], edge_second[1]), edge_zero)
    edge_zero = gather_steps(after(edge_zero, node_zero), steps - 1, steps)
    node_zero = gather_steps(node_zero, steps - 3, steps - 2)
    edge_one = gather_steps(pack_shards(first, second)[None], 0, 1)
    masters = (edge_first, edge_second, node_first, node_second)
    weight_local = jnp.stack(
        [jnp.sum(matrix * matrix, axis=(1, 2)) for matrix in after(masters, setup)], axis=1
    )
    edge_zero = after(edge_zero, node_zero, edge_one, weight_local)

    def edge_blocks(whole):
        return ((whole, first_rows, 0), (whole, second_rows, first_rows // second_rows))

    def own_edges(values):
        return lax.dynamic_index_in_dim(
            values.reshape(2, 2, edge_part, *values.shape[1:]), edge_half, 1, keepdims=False
        ).reshape(2 * edge_part, *values.shape[1:])

    def own_nodes(values):
        return lax.dynamic_index_in_dim(
            values.reshape(samples, 2, 2, node_part, latent), edge_half, 2, keepdims=False
        ).reshape(samples, 2 * node_part, latent)

    def own_samples(values):
        return lax.dynamic_slice_in_dim(values, sample_half * samples, samples, 1)

    def to_own_rows(values):
        quarters = jnp.moveaxis(values.reshape(samples, 2, 2, node_part, latent), 0, 3)
        quarters = lax.dynamic_index_in_dim(quarters, edge_half, 1, keepdims=False)
        sent = lax.dynamic_index_in_dim(quarters, 1 - sample_half, 0, keepdims=False)
        kept = lax.dynamic_index_in_dim(quarters, sample_half, 0, keepdims=False)
        return jnp.concatenate(ordered(sample_half, kept, swap(sent, "hid", 2)), axis=1)

    send_slot, recv_local, halo_lists, node_in, edge_in = lax.optimization_barrier(
        (send_slot, recv_local, halo_lists, node_in, edge_in, setup)
    )[:5]
    sender = own_edges(send_slot)
    receiver = own_edges(recv_local)
    node_ids, table_ids = jnp.arange(node_total), jnp.arange(table_total)
    at_receiver = (receiver[:, None] == node_ids[None, :]).astype(BF16)
    at_both = jnp.concatenate(
        [(sender[:, None] == table_ids[None, :]).astype(BF16), at_receiver], axis=1
    )
    at_nodes = (node_ids[:, None] == receiver[None, :]).astype(BF16)
    at_both_t = jnp.concatenate(
        [(table_ids[:, None] == sender[None, :]).astype(BF16), at_nodes], axis=0
    )
    at_halo = (halo_lists.reshape(-1)[:, None] == node_ids[None, :]).astype(BF16)
    mask = ((node_ids // node_part) % 2 == edge_half).astype(F32)
    mask = jnp.tile(mask, samples)[:, None]

    node_low = jnp.transpose(own_samples(node_in), (1, 0, 2))
    edge_in_own = own_edges(edge_in)
    halo_rows = dot("hn,snl->shl", at_halo, node_low).astype(BF16)
    node_low_zero = node_low
    table_zero = jnp.concatenate([node_low, to_neighbours(halo_rows, halo_width)], axis=1)
    pre_zero, act_zero, normed_zero, inverse_zero, edge_state, edge_low, pooled = edge_forward(
        order,
        *edge_blocks(edge_zero),
        table_zero,
        edge_in_own[None],
        edge_in_own[None],
        at_both,
        at_nodes,
        small_params[0],
        node_total,
        False,
    )
    node_zero = gather_steps(node_zero, steps - 2, steps - 1, pooled)
    node_zero = gather_steps(node_zero, steps - 1, steps)
    edge_one = gather_steps(edge_one, 1, steps - 3, pooled)
    edge_one = gather_steps(edge_one, steps - 3, steps - 2)
    other = after(swap(pooled, "hid", 1), edge_one)
    first, second = after((node_first[1], node_second[1]), edge_one)
    node_one = gather_steps(pack_shards(first, second)[None], 0, steps - 3)
    (
        pooled_zero,
        node_pre,
        node_act,
        node_normed,
        node_inverse,
        node_state,
        node_low,
        halo_rows,
    ) = node_pass(
        order,
        None,
        (node_zero, node_rows, 0),
        nodes,
        node_low_zero,
        node_low_zero,
        (pooled, other),
        small_params[0],
        at_halo,
        None,
        None,
        None,
    )
    edge_one = gather_steps(edge_one, steps - 2, steps - 1, halo_rows)
    edge_one = gather_steps(after(edge_one, node_one), steps - 1, steps)
    node_one = gather_steps(node_one, steps - 3, steps - 2)
    edge_one = after(edge_one, node_one)

    valid_mask = (ocean_mask[:, None] * present_mask).astype(BF16)
    masked = after(cotangent, pooled) * valid_mask[:, :, None]
    sent = lax.dynamic_slice_in_dim(masked, (1 - sample_half) * samples, samples, 1)
    masked = jnp.stack(ordered(sample_half, own_samples(masked), swap(sent, "hid", 2)), axis=0)
    masked = double_up(masked, "hid", 0, 1).reshape(node_total, samples, latent)
    scaling = node_total * lax.axis_size("node") / valid_counts.astype(F32)
    scaling = lax.dynamic_slice_in_dim(scaling, sample_half * samples, samples, 0)
    target = jnp.transpose(masked, (1, 0, 2))
    scaling = scaling[:, None, None]

    node_low_one = node_low
    table_one = jnp.concatenate([node_low, to_neighbours(halo_rows, halo_width)], axis=1)
    pre_one, act_one, normed_one, inverse_one, pooled = edge_forward(
        order,
        *edge_blocks(edge_one),
        table_one,
        edge_low,
        edge_state,
        at_both,
        at_nodes,
        small_params[1],
        node_total,
        True,
    )
    node_one = gather_steps(node_one, steps - 2, steps - 1, pooled)
    node_one = gather_steps(node_one, steps - 1, steps)
    node_low, pooled_grad, node_grad, kept, sent, node_minor_one = node_pass(
        order,
        owners,
        (node_one, node_rows, 0),
        nodes,
        node_low_one,
        node_state,
        (pooled, swap(pooled, "hid", 1)),
        small_params[1],
        None,
        target,
        scaling,
        mask,
    )

    def from_edges(partial, returned):
        return partial + dot("hn,shl->snl", at_halo, returned)

    low, hidden_low, at_rows, partial, returned, edge_grad, edge_minor_one = edge_backward(
        order,
        *edge_blocks(edge_one),
        pooled_grad,
        None,
        normed_one,
        inverse_one,
        pre_one,
        at_receiver,
        at_both_t,
        small_params[1, 2:3],
        True,
        node_total,
    )
    chain_one = edge_weight_grads(
        owners,
        edge_low,
        table_one,
        hidden_low,
        at_rows,
        low,
        act_one,
        node_total,
        nodes,
        width,
        [kept, sent],
    )
    returned, *chain_one = lax.optimization_barrier(
        (to_neighbours(returned, halo_width), *chain_one)
    )
    partial = from_edges(partial, returned)
    chain_one = scatter_step(chain_one, steps - 1)
    other, *chain_one = lax.optimization_barrier((swap(partial.astype(BF16), "hid", 1), *chain_one))
    pooled_grad, node_grad, kept, sent, node_minor_zero = node_backward(
        order,
        owners,
        (node_zero, node_rows, 0),
        nodes,
        (node_grad, partial, other),
        node_low_zero,
        pooled_zero,
        node_pre,
        node_act,
        node_normed,
        node_inverse,
        small_params[0],
        mask,
    )
    low, hidden_low, at_rows, partial, returned, edge_input_grad, edge_minor_zero, hidden_sum = (
        edge_backward(
            order,
            *edge_blocks(edge_zero),
            pooled_grad,
            edge_grad,
            normed_zero,
            inverse_zero,
            pre_zero,
            at_receiver,
            at_both_t,
            small_params[0, 2:3],
            False,
            node_total,
        )
    )
    chain_one = scatter_step(chain_one, steps - 2, low)
    chain_zero = scatter_step((kept, sent), steps - 1, low)
    low = after(low, *chain_one, *chain_zero)
    node_out = to_own_rows(after(node_low, low))
    chain_edge = edge_weight_grads(
        owners,
        edge_in_own,
        table_zero,
        hidden_sum,
        at_rows,
        low,
        act_zero,
        node_total,
        nodes,
        width,
        None,
    )
    minor_packed = jnp.concatenate(
        [edge_minor_zero, node_minor_zero, edge_minor_one, node_minor_one]
        + [jnp.pad(weight_local.reshape(1, -1), ((0, 0), (0, latent - weight_local.size)))],
        axis=0,
    )
    chain_zero = scatter_step(chain_zero, steps - 2, chain_edge[1])
    chain_one = tuple(jnp.concatenate(pair, axis=1) for pair in zip(chain_one, chain_zero))
    chain_edge = [chain_edge[0], after(chain_edge[1], *chain_one)]
    chain_edge = scatter_step(chain_edge, steps - 1)
    minor_packed = sum_step(minor_packed, steps - 1)
    for step in reversed(range(steps - 1)):
        minor_packed, *held = lax.optimization_barrier(
            (minor_packed, *chain_edge, *chain_one)
        )
        chain_edge = held[:2]
        if step > 0:
            chain_one = scatter_step(held[2:], step - 1)
        chain_edge = scatter_step(chain_edge, step)
        minor_packed = sum_step(minor_packed, step)
        if step == 1:
            chain_one = (chain_one,)
    edge_zero_grads, node_grads = chain_edge, chain_one[0]
    partial = from_edges(partial, to_neighbours(returned, halo_width))
    node_grad = node_grad + (partial + swap(partial.astype(BF16), "hid", 1).astype(F32))
    grad_node = to_own_rows(node_grad.astype(BF16))
    edge_input_grad = halve_sum(edge_input_grad.reshape(2, edge_part, latent), "hid", 1, 0)

    minor_total = minor_packed[: 8 * LAYERS].reshape(small_params.shape)
    weight_squares = minor_packed[8 * LAYERS, : weight_local.size].reshape(weight_local.shape)
    edge_rows = first_rows + second_rows
    node_one_grads = node_grads[:node_rows]
    edge_one_grads = node_grads[node_rows : node_rows + edge_rows]
    node_zero_grads = node_grads[node_rows + edge_rows :]
    node_first_rows = node_rows - second_rows
    grads = [
        jnp.stack([edge_zero_grads[:first_rows], edge_one_grads[:first_rows]]),
        jnp.stack([edge_zero_grads[first_rows:].T, edge_one_grads[first_rows:].T]),
        jnp.stack([node_zero_grads[:node_first_rows], node_one_grads[:node_first_rows]]),
        jnp.stack([node_zero_grads[node_first_rows:].T, node_one_grads[node_first_rows:].T]),
    ]
    firsts = (edge_first_m, edge_second_m, node_first_m, node_second_m)
    seconds = (edge_first_v, edge_second_v, node_first_v, node_second_v)
    moment_list = [
        adam_terms(masters[place], grads[place], firsts[place], seconds[place], WEIGHT_DECAY)
        for place in range(4)
    ]
    update_squares = sum_everywhere(
        jnp.stack([jnp.sum(entry[2] * entry[2], axis=(1, 2)) for entry in moment_list], axis=1)
    )
    weight_norm = jnp.sqrt(weight_squares)
    update_norm = jnp.sqrt(update_squares)
    new_weights = []
    for position in range(4):
        ratio = weight_norm[:, position] / update_norm[:, position]
        new_weights.append(
            masters[position] - learn_rate[0] * ratio[:, None, None] * moment_list[position][2]
        )
    small_first, small_second, small_update = adam_terms(
        small_params, minor_total, small_m, small_v, 0.0
    )
    small_wnorm = jnp.sqrt(jnp.sum(small_params * small_params, axis=2))
    small_unorm = jnp.sqrt(jnp.sum(small_update * small_update, axis=2))
    small_new = (
        small_params - learn_rate[0] * (small_wnorm / small_unorm)[:, :, None] * small_update
    )
    norms = jnp.stack(
        [
            jnp.concatenate([weight_norm, small_wnorm], axis=1),
            jnp.concatenate([update_norm, small_unorm], axis=1),
        ],
        axis=2,
    )
    return (
        node_out,
        grad_node,
        edge_input_grad.astype(BF16),
        *new_weights,
        *[entry[0] for entry in moment_list],
        *[entry[1] for entry in moment_list],
        *[weight.astype(BF16) for weight in new_weights],
        small_new,
        small_first,
        small_second,
        norms,
    )


def solution(mesh):
    whole = P()
    rows = P(None, "node", "hid")
    columns = P(None, "hid", "node")
    matrices = (rows, columns, rows, columns)
    in_specs = (
        P("node", None, None),
        P("node", None),
        P(("node", "hid"), None, None),
        P(("node", "hid")),
        P(("node", "hid"), None),
        P(),
        P("node"),
        P("node"),
        P("node", None),
        *matrices,
        *matrices,
        *matrices,
        whole,
        whole,
        whole,
        whole,
    )
    out_specs = (
        P(("node", "hid"), None, None),
        P(("node", "hid"), None, None),
        P(("node", "hid"), None),
        *matrices,
        *matrices,
        *matrices,
        *matrices,
        whole,
        whole,
        whole,
        whole,
    )
    return jax.shard_map(
        per_device, mesh=mesh, in_specs=in_specs, out_specs=out_specs, check_vma=False
    )
```

```python
import jax
import jax.numpy as jnp
from jax import lax
from jax.experimental import pallas as pl
from jax.experimental.pallas import tpu as pltpu
from jax.sharding import PartitionSpec as P

LAYERS = 2


NORM_EPS = 1e-05
BETA_FIRST = 0.5
BETA_SECOND = 0.5
ADAM_EPS = 1e-06
WEIGHT_DECAY = 0.01
BF16 = jnp.bfloat16
F32 = jnp.float32
VMEM_BYTES = 56 * 1024 * 1024


def matmul(left, right):
    return lax.dot_general(left, right, (((1,), (0,)), ((), ())), preferred_element_type=F32)


def matmul_nt(left, right):
    return lax.dot_general(left, right, (((1,), (1,)), ((), ())), preferred_element_type=F32)


def matmul_tn(left, right):
    return lax.dot_general(left, right, (((0,), (0,)), ((), ())), preferred_element_type=F32)


def sigmoid(values):
    return 1.0 / (1.0 + jnp.exp(-values))


def silu_slope(values):
    gate = sigmoid(values)
    return gate * (1.0 + values * (1.0 - gate))


def norm_forward(values):
    center = values - jnp.mean(values, axis=-1, keepdims=True)
    spread = jnp.mean(center * center, axis=-1, keepdims=True)
    inverse = lax.rsqrt(spread + NORM_EPS)
    return center * inverse, inverse


def norm_backward(upstream, normed, inverse, gain_row):
    scaled = upstream * gain_row
    return inverse * (
        scaled
        - jnp.mean(scaled, axis=-1, keepdims=True)
        - normed * jnp.mean(scaled * normed, axis=-1, keepdims=True)
    )


def column_sum(values):
    return jnp.sum(values, axis=0, keepdims=True)


def assemble(source, order, rows, offset, target):
    width = source.shape[2]
    nodes, hids = target.shape[0] // rows, target.shape[1] // width
    for i in range(nodes):
        for j in range(hids):
            target[i * rows : (i + 1) * rows, j * width : (j + 1) * width] = source[
                order[i * hids + j], offset : offset + rows, :
            ]


def store(target, begin, values):
    rows, width = values.shape[0], target.shape[2]
    for j in range(target.shape[0]):
        target[j, begin : begin + rows] = values[:, j * width : (j + 1) * width]


def add(target, begin, values):
    rows, width = values.shape[0], target.shape[2]
    for j in range(target.shape[0]):
        target[j, begin : begin + rows] += values[:, j * width : (j + 1) * width]


def pack(values, owners, rows, offset, kept, sent):
    half = kept.shape[0]

    def one(index, carry):
        for target, place in ((kept, index), (sent, index + half)):
            begin = pl.multiple_of(owners[2 * place] * rows, rows)
            target[index, offset : offset + rows, :] = values[
                owners[2 * place + 1], pl.ds(begin, rows), :
            ].astype(BF16)
        return carry

    lax.fori_loop(0, half, one, 0)


def per_sample(array):
    block = (1,) + array.shape[1:]
    return pl.BlockSpec(block, lambda s: (s,) + (0,) * (len(block) - 1))


def constant(array):
    return pl.BlockSpec(array.shape, lambda s: (0,) * len(array.shape))


def weight_block(array, rows, place):
    blocks, _, width = array.shape
    return pl.BlockSpec((blocks, rows, width), lambda s: (0, place, 0))


def in_scalars():
    return pl.BlockSpec(memory_space=pltpu.SMEM)


def shape_of(shape, dtype):
    return jax.ShapeDtypeStruct(shape, dtype)


def run_kernel(kernel, name, samples, inputs, in_specs, outputs, scratch, flops):
    moved = sum(a.size * a.dtype.itemsize for a in inputs) + sum(
        shape.size * shape.dtype.itemsize for shape, _ in outputs
    )
    return pl.pallas_call(
        kernel,
        name=name,
        grid=(samples,),
        in_specs=in_specs,
        out_specs=[spec for _, spec in outputs],
        out_shape=[shape for shape, _ in outputs],
        scratch_shapes=scratch,
        compiler_params=pltpu.CompilerParams(
            dimension_semantics=("arbitrary",), vmem_limit_bytes=VMEM_BYTES
        ),
        cost_estimate=pl.CostEstimate(flops=4 * flops, bytes_accessed=moved, transcendentals=0),
    )(*inputs)


def sampled(shape, dtype):
    result = shape_of(shape, dtype)
    return (result, per_sample(result))


def shared(shape, dtype):
    result = shape_of(shape, dtype)
    return (result, constant(result))


def edge_forward(order, first, second, table, edge_low, edge_state, at_both, at_nodes, params, node_total, last):
    samples, table_total, latent = table.shape
    edges = edge_low.shape[1]
    alike = edge_low.shape[0] == 1

    def kernel(order, w1, w2, table, low, state, both, nodes, params, pre, act, normed, inverse, *rest):
        if last:
            pooled, w1s, w2s, projected = rest
        else:
            new_state, new_low, pooled, w1s, w2s, projected = rest

        @pl.when(pl.program_id(0) == 0)
        def _():
            assemble(w1, order, w1.shape[1], 0, w1s)
            assemble(w2, order, w2.shape[1], 0, w2s)

        rows = table[0]
        projected[:table_total] = matmul(rows, w1s[latent : 2 * latent]).astype(BF16)
        projected[table_total:] = matmul(rows[:node_total], w1s[2 * latent :]).astype(BF16)
        hidden = matmul(low[0], w1s[:latent]) + matmul(both[...], projected[...]) + params[0:1]
        pre[0] = hidden.astype(BF16)
        active = (hidden * sigmoid(hidden)).astype(BF16)
        act[0] = active
        output = matmul_nt(active, w2s[...]) + params[1:2]
        scaled, scale = norm_forward(output)
        normed[0] = scaled.astype(BF16)
        inverse[0] = scale
        state_new = state[0].astype(F32) + scaled * params[2:3] + params[3:4]
        low_new = state_new.astype(BF16)
        if not last:
            new_state[0] = state_new
            new_low[0] = low_new
        pooled[0] = matmul(nodes[...], low_new).astype(BF16)

    wide = (samples, edges, latent)
    outputs = [sampled(wide, BF16), sampled(wide, BF16), sampled(wide, BF16), sampled((samples, edges, 1), F32)]
    if not last:
        outputs += [sampled(wide, F32), sampled(wide, BF16)]
    outputs += [sampled((samples, node_total, latent), BF16)]
    of_edges = constant if alike else per_sample
    return run_kernel(
        kernel,
        "edge_forward",
        samples,
        [order, first[0], second[0], table, edge_low, edge_state, at_both, at_nodes, params],
        [
            in_scalars(),
            weight_block(*first),
            weight_block(*second),
            per_sample(table),
            of_edges(edge_low),
            of_edges(edge_state),
            constant(at_both),
            constant(at_nodes),
            constant(params),
        ],
        outputs,
        [
            pltpu.VMEM((3 * latent, latent), BF16),
            pltpu.VMEM((latent, latent), BF16),
            pltpu.VMEM((at_both.shape[1], latent), BF16),
        ],
        2 * samples * edges * latent * (3 * latent + at_both.shape[1]),
    )


def edge_backward(order, first, second, pooled_grad, edge_grad, normed, inverse, pre, at_receiver, at_both_t, gain, last, node_total):
    samples, edges, latent = normed.shape
    at_total = at_both_t.shape[0]
    table_total = at_total - node_total

    def kernel(order, w1, w2, upstream, *rest):
        if not last:
            later, rest = rest[0], rest[1:]
        normed, inverse, pre, receiver, both_t, gain, low, hidden_low, at_rows, partial, returned, grad_out, minor = rest[:13]
        if last:
            w1s, w2s = rest[13:]
        else:
            hidden_sum, w1s, w2s, hidden_acc = rest[13:]
        step = pl.program_id(0)

        @pl.when(step == 0)
        def _():
            assemble(w1, order, w1.shape[1], 0, w1s)
            assemble(w2, order, w2.shape[1], 0, w2s)
            minor[...] = jnp.zeros_like(minor)

        grad = matmul(receiver[...], upstream[0])
        if not last:
            grad = grad + later[0]
        scaled = normed[0].astype(F32)
        output_grad = norm_backward(grad, scaled, inverse[0], gain[0:1]).astype(BF16)
        low[0] = output_grad
        act_grad = matmul(output_grad, w2s[...])
        pre_grad = (act_grad * silu_slope(pre[0].astype(F32))).astype(BF16)
        hidden_low[0] = pre_grad
        minor[0:1] += column_sum(pre_grad.astype(F32))
        minor[1:2] += column_sum(output_grad.astype(F32))
        minor[2:3] += column_sum(grad * scaled)
        minor[3:4] += column_sum(grad)
        at_rows[0] = matmul(both_t[...], pre_grad).astype(BF16)
        send = w1s[latent : 2 * latent]
        partial[0] = matmul_nt(at_rows[0, :node_total], send) + matmul_nt(
            at_rows[0, table_total:], w1s[2 * latent :]
        )
        returned[0] = matmul_nt(at_rows[0, node_total:table_total], send).astype(BF16)
        if last:
            grad_out[0] = grad + matmul_nt(pre_grad, w1s[:latent])
        else:

            @pl.when(step == 0)
            def _():
                grad_out[...] = grad
                hidden_acc[...] = pre_grad.astype(F32)

            @pl.when(step > 0)
            def _():
                grad_out[...] += grad
                hidden_acc[...] += pre_grad.astype(F32)

            @pl.when(step == samples - 1)
            def _():
                total = hidden_acc[...].astype(BF16)
                hidden_sum[...] = total
                grad_out[...] += matmul_nt(total, w1s[:latent])

    wide = (samples, edges, latent)
    outputs = [
        sampled(wide, BF16),
        sampled(wide, BF16),
        sampled((samples, at_total, latent), BF16),
        sampled((samples, node_total, latent), F32),
        sampled((samples, table_total - node_total, latent), BF16),
        sampled(wide, F32) if last else shared((edges, latent), F32),
        shared((4, latent), F32),
    ]
    scratch = [pltpu.VMEM((3 * latent, latent), BF16), pltpu.VMEM((latent, latent), BF16)]
    inputs = [order, first[0], second[0], pooled_grad]
    specs = [in_scalars(), weight_block(*first), weight_block(*second), per_sample(pooled_grad)]
    if not last:
        outputs.append(shared((edges, latent), BF16))
        scratch.append(pltpu.VMEM((edges, latent), F32))
        inputs.append(edge_grad)
        specs.append(per_sample(edge_grad))
    inputs += [normed, inverse, pre, at_receiver, at_both_t, gain]
    specs += [
        per_sample(normed),
        per_sample(inverse),
        per_sample(pre),
        constant(at_receiver),
        constant(at_both_t),
        constant(gain),
    ]
    return run_kernel(
        kernel,
        "edge_backward",
        samples,
        inputs,
        specs,
        outputs,
        scratch,
        2 * samples * edges * latent * (2 * latent + 2 * at_total),
    )


def edge_weight_grads(owners, edge_low, table, hidden_low, at_rows, low, act, node_total, nodes, width, packed_before):
    samples, table_total, latent = table.shape
    alike = edge_low.ndim == 2
    first_rows, second_rows = 3 * latent // nodes, latent // nodes
    offset = 0 if packed_before is None else packed_before[0].shape[1]
    blocks, hids = owners.shape[0] // 2, latent // width

    def kernel(owners, edge_low, table, hidden_low, at_rows, low, act, *rest):
        before, rest = rest[:-4], rest[-4:]
        kept, sent, first, second = rest
        step = pl.program_id(0)

        @pl.when(step == 0)
        def _():
            first[...] = jnp.zeros_like(first)
            second[...] = jnp.zeros_like(second)
            for source, target in zip(before, (kept, sent)):
                target[:, :offset, :] = source[...]
            if alike:
                add(first, 0, matmul_tn(edge_low[...], hidden_low[...]))

        if not alike:
            add(first, 0, matmul_tn(edge_low[0], hidden_low[0]))
        add(first, latent, matmul_tn(table[0], at_rows[0, :table_total]))
        add(first, 2 * latent, matmul_tn(table[0, :node_total], at_rows[0, table_total:]))
        add(second, 0, matmul_tn(low[0], act[0]))

        @pl.when(step == samples - 1)
        def _():
            pack(first, owners, first_rows, offset, kept, sent)
            pack(second, owners, second_rows, offset + first_rows, kept, sent)

    of_edges = constant if alike else per_sample
    inputs = [owners, edge_low, table, hidden_low, at_rows, low, act]
    specs = [in_scalars(), of_edges(edge_low), per_sample(table), of_edges(hidden_low), per_sample(at_rows), per_sample(low), per_sample(act)]
    if packed_before is not None:
        inputs += packed_before
        specs += [constant(a) for a in packed_before]
    return run_kernel(
        kernel,
        "edge_weight_grads",
        samples,
        inputs,
        specs,
        [shared((blocks // 2, offset + first_rows + second_rows, width), BF16)] * 2,
        [pltpu.VMEM((hids, 3 * latent, width), F32), pltpu.VMEM((hids, latent, width), F32)],
        4 * low.size * latent,
    )


def node_pass(order, owners, weights, nodes, node_low, state, pooled_pair, params, at_halo, target, scaling, mask):
    samples, node_total, latent = node_low.shape
    array, rows, place = weights
    second_rows, hids = latent // nodes, latent // array.shape[2]
    first_rows = rows - second_rows
    count = samples * node_total
    last = target is not None

    def kernel(order, *rest):
        if last:
            owners, rest = rest[0], rest[1:]
        w, node_low, state, pooled_own, pooled_other, params, *rest = rest
        if last:
            target, scaling, mask, new_low, upstream, input_grad, kept, sent, minor, w1s, w2s, first, second = rest
        else:
            at_halo, pooled_out, pre, act, normed, inverse, new_state, new_low, halo, w1s, w2s = rest
        assemble(w, order, first_rows, 0, w1s)
        assemble(w, order, second_rows, first_rows, w2s)
        rows_low = node_low[...].reshape(count, latent)
        pooled = (pooled_own[...].astype(F32) + pooled_other[...].astype(F32)).astype(BF16)
        pooled = pooled.reshape(count, latent)
        hidden = matmul(rows_low, w1s[:latent]) + matmul(pooled, w1s[latent:]) + params[4:5]
        active = (hidden * sigmoid(hidden)).astype(BF16)
        output = matmul_nt(active, w2s[...]) + params[5:6]
        scaled, scale = norm_forward(output)
        state_new = state[...].astype(F32).reshape(count, latent) + scaled * params[6:7] + params[7:8]
        low_new = state_new.astype(BF16).reshape(new_low.shape)
        new_low[...] = low_new
        if not last:
            pooled_out[...] = pooled
            pre[...] = hidden.astype(BF16)
            act[...] = active
            normed[...] = scaled.astype(BF16)
            inverse[...] = scale
            new_state[...] = state_new.reshape(new_state.shape)
            for s in range(samples):
                halo[s] = matmul(at_halo[...], new_low[s]).astype(BF16)
        else:
            grad = (target[...].astype(F32) * scaling[...]).reshape(count, latent)
            node_gradients(
                grad, scaled, scale, hidden, active, rows_low, pooled, params, mask,
                w1s, w2s, first, second, upstream, input_grad, kept, sent, minor, owners, first_rows, second_rows,
            )

    shape = node_low.shape
    inputs = [array, node_low, state, *pooled_pair, params]
    scratch = [pltpu.VMEM((2 * latent, latent), BF16), pltpu.VMEM((latent, latent), BF16)]
    if last:
        inputs += [target, scaling, mask]
        outputs = [shared(shape, BF16), *gradient_outputs(shape, order.shape[0], rows, array.shape[2])]
        scratch += [pltpu.VMEM((hids, 2 * latent, latent // hids), F32), pltpu.VMEM((hids, latent, latent // hids), F32)]
    else:
        inputs += [at_halo]
        outputs = [
            shared((count, latent), BF16),
            shared((count, latent), BF16),
            shared((count, latent), BF16),
            shared((count, latent), BF16),
            shared((count, 1), F32),
            shared(shape, F32),
            shared(shape, BF16),
            shared((samples, at_halo.shape[0], latent), BF16),
        ]
    tables = [order, owners] if last else [order]
    specs = [in_scalars() for _ in tables] + [weight_block(*weights)] + [constant(a) for a in inputs[1:]]
    inputs = tables + inputs
    return run_kernel(kernel, "node_pass", 1, inputs, specs, outputs, scratch, 6 * count * latent * latent * (3 if last else 1))


def gradient_outputs(shape, blocks, rows, width):
    return [
        shared(shape, BF16),
        shared(shape, F32),
        shared((blocks // 2, rows, width), BF16),
        shared((blocks // 2, rows, width), BF16),
        shared((4, shape[-1]), F32),
    ]


def node_gradients(
    grad, scaled, scale, hidden, active, rows_low, pooled, params, mask,
    w1s, w2s, first, second, upstream, input_grad, kept, sent, minor, owners, first_rows, second_rows,
):
    latent = w2s.shape[0]
    output_grad = norm_backward(grad, scaled, scale, params[6:7]).astype(BF16)
    pre_grad = (matmul(output_grad, w2s[...]) * silu_slope(hidden)).astype(BF16)
    upstream[...] = matmul_nt(pre_grad, w1s[latent:]).astype(BF16).reshape(upstream.shape)
    input_grad[...] = (grad + matmul_nt(pre_grad, w1s[:latent])).reshape(input_grad.shape)
    chosen = mask[...] > 0.5
    output_mine = jnp.where(chosen, output_grad.astype(F32), 0.0)
    pre_mine = jnp.where(chosen, pre_grad.astype(F32), 0.0)
    grad_mine = jnp.where(chosen, grad, 0.0)
    minor[0:1] = column_sum(pre_mine)
    minor[1:2] = column_sum(output_mine)
    minor[2:3] = column_sum(grad_mine * scaled)
    minor[3:4] = column_sum(grad_mine)
    pre_mine = pre_mine.astype(BF16)
    store(first, 0, matmul_tn(rows_low, pre_mine))
    store(first, latent, matmul_tn(pooled, pre_mine))
    store(second, 0, matmul_tn(output_mine.astype(BF16), active))
    pack(first, owners, first_rows, 0, kept, sent)
    pack(second, owners, second_rows, first_rows, kept, sent)


def node_backward(order, owners, weights, nodes, grads, node_low, pooled, pre, act, normed, inverse, params, mask):
    samples, node_total, latent = node_low.shape
    array, rows, place = weights
    second_rows, hids = latent // nodes, latent // array.shape[2]
    first_rows = rows - second_rows
    count = samples * node_total

    def kernel(order, owners, w, base, own, other, node_low, pooled, pre, act, normed, inverse, params, mask, upstream, input_grad, kept, sent, minor, w1s, w2s, first, second):
        assemble(w, order, first_rows, 0, w1s)
        assemble(w, order, second_rows, first_rows, w2s)
        grad = (base[...] + (own[...] + other[...].astype(F32))).reshape(count, latent)
        node_gradients(
            grad, normed[...].astype(F32), inverse[...], pre[...].astype(F32), act[...],
            node_low[...].reshape(count, latent), pooled[...], params, mask,
            w1s, w2s, first, second, upstream, input_grad, kept, sent, minor, owners, first_rows, second_rows,
        )

    inputs = [order, owners, array, *grads, node_low, pooled, pre, act, normed, inverse, params, mask]
    specs = [in_scalars(), in_scalars(), weight_block(*weights)] + [constant(a) for a in inputs[3:]]
    return run_kernel(
        kernel,
        "node_backward",
        1,
        inputs,
        specs,
        gradient_outputs(node_low.shape, order.shape[0], rows, array.shape[2]),
        [
            pltpu.VMEM((2 * latent, latent), BF16),
            pltpu.VMEM((latent, latent), BF16),
            pltpu.VMEM((hids, 2 * latent, latent // hids), F32),
            pltpu.VMEM((hids, latent, latent // hids), F32),
        ],
        12 * count * latent * latent,
    )


def dot(spec, left, right):
    return jnp.einsum(spec, left, right, preferred_element_type=F32)


def swap(values, axis, offset):
    return lax.ppermute(values, axis, [(i, i ^ offset) for i in range(lax.axis_size(axis))])


def bits_of(axis):
    return lax.axis_size(axis).bit_length() - 1


def own_bit(axis, bit):
    return (lax.axis_index(axis) >> bit) & 1


def all_bits():
    return [(axis, bit) for axis in ("node", "hid") for bit in reversed(range(bits_of(axis)))]


def ordered(own, mine, other):
    low = jnp.where(own == 0, mine, other)
    high = jnp.where(own == 0, other, mine)
    return low, high


def double_up(part, axis, bit, place):
    low, high = ordered(own_bit(axis, bit), part, swap(part, axis, 1 << bit))
    return jnp.stack([low, high], axis=place)


def halve_sum(parts, axis, bit, place):
    own = own_bit(axis, bit)
    sent = lax.dynamic_index_in_dim(parts, 1 - own, place, keepdims=False)
    kept = lax.dynamic_index_in_dim(parts, own, place, keepdims=False)
    return kept.astype(F32) + swap(sent.astype(BF16), axis, 1 << bit).astype(F32)


def places():
    node_ids = jnp.arange(lax.axis_size("node"), dtype=jnp.int32) ^ lax.axis_index("node")
    hid_ids = jnp.arange(lax.axis_size("hid"), dtype=jnp.int32) ^ lax.axis_index("hid")
    place = 0
    for step, (axis, bit) in enumerate(all_bits()):
        ids = node_ids[:, None] if axis == "node" else hid_ids[None, :]
        place = place + (((ids >> bit) & 1) << step)
    return place.reshape(-1)


def owners_of_places():
    place = jnp.arange(1 << len(all_bits()), dtype=jnp.int32)
    owner = {"node": lax.axis_index("node"), "hid": lax.axis_index("hid")}
    for step, (axis, bit) in enumerate(all_bits()):
        owner[axis] = owner[axis] ^ (((place >> step) & 1) << bit)
    return jnp.stack([owner["node"], owner["hid"]], axis=1).reshape(-1)


def after(value, *earlier):
    return lax.optimization_barrier((value, *earlier))[0]


def exchange(values, first_step, flips):
    hid_bits = bits_of("hid")
    mask = 0
    for k in range(flips.bit_length()):
        if (flips >> k) & 1:
            axis, bit = all_bits()[first_step + k]
            mask |= 1 << (bit if axis == "hid" else bit + hid_bits)
    total = 1 << len(all_bits())
    return lax.ppermute(values, ("node", "hid"), [(i, i ^ mask) for i in range(total)])


def rounds(begin, end):
    return [(step, min(step + 2, end)) for step in range(begin, end, 2)]


def gather_round(held, begin, end, *under):
    arrived = [exchange(held, begin, flips) for flips in range(1, 1 << (end - begin))]
    if under:
        arrived = lax.optimization_barrier((*arrived, *under))[: len(arrived)]
    return jnp.concatenate([held, *arrived], axis=0)


def split(total, count):
    size = total.shape[0] // count
    pieces = [total[i * size : (i + 1) * size] for i in range(count)]
    return [pieces[0]] + [piece.astype(BF16) for piece in pieces[1:]]


def scatter_round(pieces, begin, *under):
    arrived = [exchange(pieces[flips], begin, flips) for flips in range(1, len(pieces))]
    if under:
        arrived = lax.optimization_barrier((*arrived, *under))[: len(arrived)]
    total = pieces[0].astype(F32)
    for piece in arrived:
        total = total + piece.astype(F32)
    return total


def scatter_rest(total, end, *under):
    for begin, stop in reversed(rounds(0, end)):
        total = scatter_round(split(total, 1 << (stop - begin)), begin, *under)
    return total[0]


def sum_round(values, begin, end):
    terms = [values] + [exchange(values, begin, flips) for flips in range(1, 1 << (end - begin))]
    while len(terms) > 1:
        terms = [terms[i] + terms[i + 1] for i in range(0, len(terms), 2)]
    return terms[0]


def sum_everywhere(values):
    steps = len(all_bits())
    values = sum_round(values, steps - 1, steps)
    for begin, end in reversed(rounds(0, steps - 1)):
        values = sum_round(values, begin, end)
    return values


def to_neighbours(rows, halo_width):
    count = lax.axis_size("node")
    onward = [(i, (i + 1) % count) for i in range(count)]
    back = [(target, source) for source, target in onward]
    from_previous = lax.ppermute(rows[:, halo_width:], "node", onward)
    from_next = lax.ppermute(rows[:, :halo_width], "node", back)
    return jnp.concatenate([from_previous, from_next], axis=1)


def adam_terms(weight, grad, first, second, decay):
    first_new = BETA_FIRST * first + (1.0 - BETA_FIRST) * grad
    second_new = BETA_SECOND * second + (1.0 - BETA_SECOND) * grad * grad
    update = first_new / (jnp.sqrt(second_new) + ADAM_EPS) + decay * weight
    return (first_new, second_new, update)


def pack_shards(first, second):
    return jnp.concatenate([first, second.T], axis=0).astype(BF16)


def adam_terms(weight, grad, first, second, decay):
    first_new = BETA_FIRST * first + (1.0 - BETA_FIRST) * grad
    second_new = BETA_SECOND * second + (1.0 - BETA_SECOND) * grad * grad
    update = first_new / (jnp.sqrt(second_new) + ADAM_EPS) + decay * weight
    return (first_new, second_new, update)


def per_device(
    node_in,
    edge_in,
    cotangent,
    ocean_mask,
    present_mask,
    valid_counts,
    send_slot,
    recv_local,
    halo_lists,
    edge_first,
    edge_second,
    node_first,
    node_second,
    edge_first_m,
    edge_second_m,
    node_first_m,
    node_second_m,
    edge_first_v,
    edge_second_v,
    node_first_v,
    node_second_v,
    small_params,
    small_m,
    small_v,
    learn_rate,
):
    hid_count = lax.axis_size("hid")
    hid_index = lax.axis_index("hid")
    node_total, sample_count, latent = node_in.shape
    edge_part = edge_in.shape[0] // hid_count
    node_part = node_total // hid_count
    halo_width = halo_lists.shape[1]
    table_total = node_total + 2 * halo_width
    sample_half, edge_half = hid_index >> 1, hid_index & 1
    samples = sample_count // 2
    nodes, hids = lax.axis_size("node"), hid_count
    first_rows = edge_first.shape[1]
    second_rows = edge_second.shape[2]
    node_rows = node_first.shape[1] + second_rows
    width = edge_first.shape[2]

    order, owners = places(), owners_of_places()
    steps = len(all_bits())

    def layer_shards(depth, *earlier):
        shards = (node_first[depth], node_second[depth], edge_first[depth], edge_second[depth])
        if earlier:
            shards = after(shards, *earlier)
        return jnp.concatenate([pack_shards(*shards[:2]), pack_shards(*shards[2:])], axis=0)[None]

    def parted(held):
        return held[:, :node_rows], held[:, node_rows:]

    layer_zero = layer_shards(0)
    for begin, end in rounds(0, steps - 3):
        layer_zero = gather_round(layer_zero, begin, end)
    setup = layer_zero
    layer_zero = gather_round(layer_zero, steps - 3, steps - 2)
    node_zero, edge_zero = parted(layer_zero)
    layer_one = layer_shards(1, setup)
    for begin, end in rounds(0, steps - 3):
        layer_one = gather_round(after(layer_one, edge_zero), begin, end)
    edge_zero = gather_round(edge_zero, steps - 2, steps - 1)
    masters = (edge_first, edge_second, node_first, node_second)
    weight_local = jnp.stack(
        [jnp.sum(matrix * matrix, axis=(1, 2)) for matrix in after(masters, setup)], axis=1
    )
    node_zero = after(node_zero, edge_zero)
    edge_zero = gather_round(after(edge_zero, layer_one), steps - 1, steps)
    edge_zero = after(edge_zero, weight_local)

    def edge_blocks(whole):
        return ((whole, first_rows, 0), (whole, second_rows, first_rows // second_rows))

    def own_edges(values):
        return lax.dynamic_index_in_dim(
            values.reshape(2, 2, edge_part, *values.shape[1:]), edge_half, 1, keepdims=False
        ).reshape(2 * edge_part, *values.shape[1:])

    def own_nodes(values):
        return lax.dynamic_index_in_dim(
            values.reshape(samples, 2, 2, node_part, latent), edge_half, 2, keepdims=False
        ).reshape(samples, 2 * node_part, latent)

    def own_samples(values):
        return lax.dynamic_slice_in_dim(values, sample_half * samples, samples, 1)

    def to_own_rows(values):
        quarters = jnp.moveaxis(values.reshape(samples, 2, 2, node_part, latent), 0, 3)
        quarters = lax.dynamic_index_in_dim(quarters, edge_half, 1, keepdims=False)
        sent = lax.dynamic_index_in_dim(quarters, 1 - sample_half, 0, keepdims=False)
        kept = lax.dynamic_index_in_dim(quarters, sample_half, 0, keepdims=False)
        return jnp.concatenate(ordered(sample_half, kept, swap(sent, "hid", 2)), axis=1)

    send_slot, recv_local, halo_lists, node_in, edge_in = lax.optimization_barrier(
        (send_slot, recv_local, halo_lists, node_in, edge_in, setup)
    )[:5]
    sender = own_edges(send_slot)
    receiver = own_edges(recv_local)
    node_ids, table_ids = jnp.arange(node_total), jnp.arange(table_total)
    at_receiver = (receiver[:, None] == node_ids[None, :]).astype(BF16)
    at_both = jnp.concatenate(
        [(sender[:, None] == table_ids[None, :]).astype(BF16), at_receiver], axis=1
    )
    at_nodes = (node_ids[:, None] == receiver[None, :]).astype(BF16)
    at_both_t = jnp.concatenate(
        [(table_ids[:, None] == sender[None, :]).astype(BF16), at_nodes], axis=0
    )
    at_halo = (halo_lists.reshape(-1)[:, None] == node_ids[None, :]).astype(BF16)
    mask = ((node_ids // node_part) % 2 == edge_half).astype(F32)
    mask = jnp.tile(mask, samples)[:, None]

    node_low = jnp.transpose(own_samples(node_in), (1, 0, 2))
    edge_in_own = own_edges(edge_in)
    halo_rows = dot("hn,snl->shl", at_halo, node_low).astype(BF16)
    node_low_zero = node_low
    table_zero = jnp.concatenate([node_low, to_neighbours(halo_rows, halo_width)], axis=1)
    pre_zero, act_zero, normed_zero, inverse_zero, edge_state, edge_low, pooled = edge_forward(
        order,
        *edge_blocks(edge_zero),
        table_zero,
        edge_in_own[None],
        edge_in_own[None],
        at_both,
        at_nodes,
        small_params[0],
        node_total,
        False,
    )
    pooled, *arrived = lax.optimization_barrier(
        (pooled, exchange(node_zero, steps - 2, 1), exchange(layer_one, steps - 3, 1))
    )
    node_zero = jnp.concatenate([node_zero, arrived[0]], axis=0)
    node_zero = gather_round(node_zero, steps - 1, steps)
    layer_one = jnp.concatenate([layer_one, arrived[1]], axis=0)
    node_one, edge_one = parted(layer_one)
    other = after(swap(pooled, "hid", 1), edge_one)
    (
        pooled_zero,
        node_pre,
        node_act,
        node_normed,
        node_inverse,
        node_state,
        node_low,
        halo_rows,
    ) = node_pass(
        order,
        None,
        (node_zero, node_rows, 0),
        nodes,
        node_low_zero,
        node_low_zero,
        (pooled, other),
        small_params[0],
        at_halo,
        None,
        None,
        None,
    )
    halo_rows = to_neighbours(halo_rows, halo_width)
    arrived, halo_rows = lax.optimization_barrier(
        (exchange(edge_one, steps - 2, 1), halo_rows)
    )
    edge_one = jnp.concatenate([edge_one, arrived], axis=0)
    node_one = after(node_one, edge_one)
    edge_one = gather_round(edge_one, steps - 1, steps)

    valid_mask = (ocean_mask[:, None] * present_mask).astype(BF16)
    masked = after(cotangent, pooled) * valid_mask[:, :, None]
    sent = lax.dynamic_slice_in_dim(masked, (1 - sample_half) * samples, samples, 1)
    masked = jnp.stack(ordered(sample_half, own_samples(masked), swap(sent, "hid", 2)), axis=0)
    masked = double_up(masked, "hid", 0, 1).reshape(node_total, samples, latent)
    scaling = node_total * lax.axis_size("node") / valid_counts.astype(F32)
    scaling = lax.dynamic_slice_in_dim(scaling, sample_half * samples, samples, 0)
    target = jnp.transpose(masked, (1, 0, 2))
    scaling = scaling[:, None, None]

    node_low_one = node_low
    table_one = jnp.concatenate([node_low, halo_rows], axis=1)
    pre_one, act_one, normed_one, inverse_one, pooled = edge_forward(
        order,
        *edge_blocks(edge_one),
        table_one,
        edge_low,
        edge_state,
        at_both,
        at_nodes,
        small_params[1],
        node_total,
        True,
    )
    node_one = gather_round(node_one, steps - 2, steps - 1, pooled)
    node_one = gather_round(node_one, steps - 1, steps)
    node_low, pooled_grad, node_grad, kept, sent, node_minor_one = node_pass(
        order,
        owners,
        (node_one, node_rows, 0),
        nodes,
        node_low_one,
        node_state,
        (pooled, swap(pooled, "hid", 1)),
        small_params[1],
        None,
        target,
        scaling,
        mask,
    )

    def from_edges(partial, returned):
        return partial + dot("hn,shl->snl", at_halo, returned)

    low, hidden_low, at_rows, partial, returned, edge_grad, edge_minor_one = edge_backward(
        order,
        *edge_blocks(edge_one),
        pooled_grad,
        None,
        normed_one,
        inverse_one,
        pre_one,
        at_receiver,
        at_both_t,
        small_params[1, 2:3],
        True,
        node_total,
    )
    chain_one = edge_weight_grads(
        owners,
        edge_low,
        table_one,
        hidden_low,
        at_rows,
        low,
        act_one,
        node_total,
        nodes,
        width,
        [kept, sent],
    )
    returned, *chain_one = lax.optimization_barrier(
        (to_neighbours(returned, halo_width), *chain_one)
    )
    partial = from_edges(partial, returned)
    chain_one = split(scatter_round(chain_one, steps - 1), 2)
    other, *chain_one = lax.optimization_barrier((swap(partial.astype(BF16), "hid", 1), *chain_one))
    pooled_grad, node_grad, kept, sent, node_minor_zero = node_backward(
        order,
        owners,
        (node_zero, node_rows, 0),
        nodes,
        (node_grad, partial, other),
        node_low_zero,
        pooled_zero,
        node_pre,
        node_act,
        node_normed,
        node_inverse,
        small_params[0],
        mask,
    )
    low, hidden_low, at_rows, partial, returned, edge_input_grad, edge_minor_zero, hidden_sum = (
        edge_backward(
            order,
            *edge_blocks(edge_zero),
            pooled_grad,
            edge_grad,
            normed_zero,
            inverse_zero,
            pre_zero,
            at_receiver,
            at_both_t,
            small_params[0, 2:3],
            False,
            node_total,
        )
    )
    chain_one = split(scatter_round(chain_one, steps - 2, low), 2)
    chain_zero = split(scatter_round((kept, sent), steps - 1, low), 2)
    low = after(low, *chain_one, *chain_zero)
    chain_edge = edge_weight_grads(
        owners,
        edge_in_own,
        table_zero,
        hidden_sum,
        at_rows,
        low,
        act_zero,
        node_total,
        nodes,
        width,
        None,
    )
    minor_packed = jnp.concatenate(
        [edge_minor_zero, node_minor_zero, edge_minor_one, node_minor_one]
        + [jnp.pad(weight_local.reshape(1, -1), ((0, 0), (0, latent - weight_local.size)))],
        axis=0,
    )
    chain_zero = split(scatter_round(chain_zero, steps - 2, chain_edge[1]), 2)
    chain_one = scatter_round(chain_one, steps - 3, chain_edge[1])
    kept, sent, chain_one, *chain_zero = lax.optimization_barrier(
        (*chain_edge, chain_one, *chain_zero)
    )
    chain_edge = split(scatter_round((kept, sent), steps - 1), 2)
    minor_packed = sum_round(minor_packed, steps - 1, steps)
    returned, minor_packed, *held = lax.optimization_barrier(
        (returned, minor_packed, *chain_zero, *chain_edge)
    )
    chain_zero, chain_edge = held[:2], held[2:]
    chain_edge = split(scatter_round(chain_edge, steps - 2), 2)
    minor_packed = sum_round(minor_packed, steps - 2, steps - 1)
    layer_one_grads = scatter_rest(chain_one, steps - 3, chain_edge[1])
    chain_zero = scatter_round(chain_zero, steps - 3, chain_edge[1])
    returned = after(to_neighbours(returned, halo_width), chain_edge[1])
    node_low, edge_input_grad, minor_packed, *chain_edge = lax.optimization_barrier(
        (node_low, edge_input_grad, minor_packed, *chain_edge)
    )
    chain_edge = scatter_round(chain_edge, steps - 3)
    minor_packed = sum_round(minor_packed, steps - 3, steps - 2)
    node_zero_grads = scatter_rest(chain_zero, steps - 3, chain_edge)
    partial = from_edges(partial, returned)
    other = swap(partial.astype(BF16), "hid", 1)
    chain_edge, minor_packed, other = lax.optimization_barrier((chain_edge, minor_packed, other))
    edge_zero_grads = scatter_rest(chain_edge, steps - 3)
    for begin, end in reversed(rounds(0, steps - 3)):
        minor_packed = sum_round(minor_packed, begin, end)
    node_out = to_own_rows(node_low)
    edge_input_grad = halve_sum(edge_input_grad.reshape(2, edge_part, latent), "hid", 1, 0)
    node_grad = node_grad + (partial + other.astype(F32))
    grad_node = to_own_rows(node_grad.astype(BF16))

    minor_total = minor_packed[: 8 * LAYERS].reshape(small_params.shape)
    weight_squares = minor_packed[8 * LAYERS, : weight_local.size].reshape(weight_local.shape)
    node_one_grads, edge_one_grads = layer_one_grads[:node_rows], layer_one_grads[node_rows:]
    node_first_rows = node_rows - second_rows
    grads = [
        jnp.stack([edge_zero_grads[:first_rows], edge_one_grads[:first_rows]]),
        jnp.stack([edge_zero_grads[first_rows:].T, edge_one_grads[first_rows:].T]),
        jnp.stack([node_zero_grads[:node_first_rows], node_one_grads[:node_first_rows]]),
        jnp.stack([node_zero_grads[node_first_rows:].T, node_one_grads[node_first_rows:].T]),
    ]
    firsts = (edge_first_m, edge_second_m, node_first_m, node_second_m)
    seconds = (edge_first_v, edge_second_v, node_first_v, node_second_v)
    moment_list = [
        adam_terms(masters[place], grads[place], firsts[place], seconds[place], WEIGHT_DECAY)
        for place in range(4)
    ]
    update_local = jnp.stack(
        [jnp.sum(entry[2] * entry[2], axis=(1, 2)) for entry in moment_list], axis=1
    )
    update_local, grad_node, edge_input_grad = lax.optimization_barrier(
        (update_local, grad_node, edge_input_grad)
    )
    update_squares = sum_everywhere(update_local)
    weight_norm = jnp.sqrt(weight_squares)
    update_norm = jnp.sqrt(update_squares)
    new_weights = []
    for position in range(4):
        ratio = weight_norm[:, position] / update_norm[:, position]
        new_weights.append(
            masters[position] - learn_rate[0] * ratio[:, None, None] * moment_list[position][2]
        )
    small_first, small_second, small_update = adam_terms(
        small_params, minor_total, small_m, small_v, 0.0
    )
    small_wnorm = jnp.sqrt(jnp.sum(small_params * small_params, axis=2))
    small_unorm = jnp.sqrt(jnp.sum(small_update * small_update, axis=2))
    small_new = (
        small_params - learn_rate[0] * (small_wnorm / small_unorm)[:, :, None] * small_update
    )
    norms = jnp.stack(
        [
            jnp.concatenate([weight_norm, small_wnorm], axis=1),
            jnp.concatenate([update_norm, small_unorm], axis=1),
        ],
        axis=2,
    )
    return (
        node_out,
        grad_node,
        edge_input_grad.astype(BF16),
        *new_weights,
        *[entry[0] for entry in moment_list],
        *[entry[1] for entry in moment_list],
        *[weight.astype(BF16) for weight in new_weights],
        small_new,
        small_first,
        small_second,
        norms,
    )


def solution(mesh):
    whole = P()
    rows = P(None, "node", "hid")
    columns = P(None, "hid", "node")
    matrices = (rows, columns, rows, columns)
    in_specs = (
        P("node", None, None),
        P("node", None),
        P(("node", "hid"), None, None),
        P(("node", "hid")),
        P(("node", "hid"), None),
        P(),
        P("node"),
        P("node"),
        P("node", None),
        *matrices,
        *matrices,
        *matrices,
        whole,
        whole,
        whole,
        whole,
    )
    out_specs = (
        P(("node", "hid"), None, None),
        P(("node", "hid"), None, None),
        P(("node", "hid"), None),
        *matrices,
        *matrices,
        *matrices,
        *matrices,
        whole,
        whole,
        whole,
        whole,
    )
    return jax.shard_map(
        per_device, mesh=mesh, in_specs=in_specs, out_specs=out_specs, check_vma=False
    )
```

```python
import jax
import jax.numpy as jnp
from jax import lax
from jax.experimental import pallas as pl
from jax.experimental.pallas import tpu as pltpu
from jax.sharding import PartitionSpec as P

LAYERS = 2


NORM_EPS = 1e-05
BETA_FIRST = 0.5
BETA_SECOND = 0.5
ADAM_EPS = 1e-06
WEIGHT_DECAY = 0.01
BF16 = jnp.bfloat16
F32 = jnp.float32
VMEM_BYTES = 56 * 1024 * 1024


def matmul(left, right):
    return lax.dot_general(left, right, (((1,), (0,)), ((), ())), preferred_element_type=F32)


def matmul_nt(left, right):
    return lax.dot_general(left, right, (((1,), (1,)), ((), ())), preferred_element_type=F32)


def matmul_tn(left, right):
    return lax.dot_general(left, right, (((0,), (0,)), ((), ())), preferred_element_type=F32)


def sigmoid(values):
    return 1.0 / (1.0 + jnp.exp(-values))


def silu_slope(values):
    gate = sigmoid(values)
    return gate * (1.0 + values * (1.0 - gate))


def norm_forward(values):
    center = values - jnp.mean(values, axis=-1, keepdims=True)
    spread = jnp.mean(center * center, axis=-1, keepdims=True)
    inverse = lax.rsqrt(spread + NORM_EPS)
    return center * inverse, inverse


def norm_backward(upstream, normed, inverse, gain_row):
    scaled = upstream * gain_row
    return inverse * (
        scaled
        - jnp.mean(scaled, axis=-1, keepdims=True)
        - normed * jnp.mean(scaled * normed, axis=-1, keepdims=True)
    )


def column_sum(values):
    return jnp.sum(values, axis=0, keepdims=True)


def assemble(source, order, rows, offset, target):
    width = source.shape[2]
    nodes, hids = target.shape[0] // rows, target.shape[1] // width
    for i in range(nodes):
        for j in range(hids):
            target[i * rows : (i + 1) * rows, j * width : (j + 1) * width] = source[
                order[i * hids + j], offset : offset + rows, :
            ]


def store(target, begin, values):
    rows, width = values.shape[0], target.shape[2]
    for j in range(target.shape[0]):
        target[j, begin : begin + rows] = values[:, j * width : (j + 1) * width]


def add(target, begin, values):
    rows, width = values.shape[0], target.shape[2]
    for j in range(target.shape[0]):
        target[j, begin : begin + rows] += values[:, j * width : (j + 1) * width]


def pack(values, owners, rows, offset, kept, sent):
    half = kept.shape[0]

    def one(index, carry):
        for target, place in ((kept, index), (sent, index + half)):
            begin = pl.multiple_of(owners[2 * place] * rows, rows)
            target[index, offset : offset + rows, :] = values[
                owners[2 * place + 1], pl.ds(begin, rows), :
            ].astype(BF16)
        return carry

    lax.fori_loop(0, half, one, 0)


def per_sample(array):
    block = (1,) + array.shape[1:]
    return pl.BlockSpec(block, lambda s: (s,) + (0,) * (len(block) - 1))


def constant(array):
    return pl.BlockSpec(array.shape, lambda s: (0,) * len(array.shape))


def weight_block(array, rows, place):
    blocks, _, width = array.shape
    return pl.BlockSpec((blocks, rows, width), lambda s: (0, place, 0))


def in_scalars():
    return pl.BlockSpec(memory_space=pltpu.SMEM)


def shape_of(shape, dtype):
    return jax.ShapeDtypeStruct(shape, dtype)


def run_kernel(kernel, name, samples, inputs, in_specs, outputs, scratch, flops):
    moved = sum(a.size * a.dtype.itemsize for a in inputs) + sum(
        shape.size * shape.dtype.itemsize for shape, _ in outputs
    )
    return pl.pallas_call(
        kernel,
        name=name,
        grid=(samples,),
        in_specs=in_specs,
        out_specs=[spec for _, spec in outputs],
        out_shape=[shape for shape, _ in outputs],
        scratch_shapes=scratch,
        compiler_params=pltpu.CompilerParams(
            dimension_semantics=("arbitrary",), vmem_limit_bytes=VMEM_BYTES
        ),
        cost_estimate=pl.CostEstimate(flops=4 * flops, bytes_accessed=moved, transcendentals=0),
    )(*inputs)


def sampled(shape, dtype):
    result = shape_of(shape, dtype)
    return (result, per_sample(result))


def shared(shape, dtype):
    result = shape_of(shape, dtype)
    return (result, constant(result))


def edge_forward(order, first, second, table, edge_low, edge_state, at_both, at_nodes, params, node_total, last):
    samples, table_total, latent = table.shape
    edges = edge_low.shape[1]
    alike = edge_low.shape[0] == 1

    def kernel(order, w1, w2, table, low, state, both, nodes, params, pre, act, normed, inverse, *rest):
        if last:
            pooled, w1s, w2s, projected = rest
        else:
            new_state, new_low, pooled, w1s, w2s, projected = rest

        @pl.when(pl.program_id(0) == 0)
        def _():
            assemble(w1, order, w1.shape[1], 0, w1s)
            assemble(w2, order, w2.shape[1], 0, w2s)

        rows = table[0]
        projected[:table_total] = matmul(rows, w1s[latent : 2 * latent]).astype(BF16)
        projected[table_total:] = matmul(rows[:node_total], w1s[2 * latent :]).astype(BF16)
        hidden = matmul(low[0], w1s[:latent]) + matmul(both[...], projected[...]) + params[0:1]
        pre[0] = hidden.astype(BF16)
        active = (hidden * sigmoid(hidden)).astype(BF16)
        act[0] = active
        output = matmul_nt(active, w2s[...]) + params[1:2]
        scaled, scale = norm_forward(output)
        normed[0] = scaled.astype(BF16)
        inverse[0] = scale
        state_new = state[0].astype(F32) + scaled * params[2:3] + params[3:4]
        low_new = state_new.astype(BF16)
        if not last:
            new_state[0] = state_new
            new_low[0] = low_new
        pooled[0] = matmul(nodes[...], low_new).astype(BF16)

    wide = (samples, edges, latent)
    outputs = [sampled(wide, BF16), sampled(wide, BF16), sampled(wide, BF16), sampled((samples, edges, 1), F32)]
    if not last:
        outputs += [sampled(wide, F32), sampled(wide, BF16)]
    outputs += [sampled((samples, node_total, latent), BF16)]
    of_edges = constant if alike else per_sample
    return run_kernel(
        kernel,
        "edge_forward",
        samples,
        [order, first[0], second[0], table, edge_low, edge_state, at_both, at_nodes, params],
        [
            in_scalars(),
            weight_block(*first),
            weight_block(*second),
            per_sample(table),
            of_edges(edge_low),
            of_edges(edge_state),
            constant(at_both),
            constant(at_nodes),
            constant(params),
        ],
        outputs,
        [
            pltpu.VMEM((3 * latent, latent), BF16),
            pltpu.VMEM((latent, latent), BF16),
            pltpu.VMEM((at_both.shape[1], latent), BF16),
        ],
        2 * samples * edges * latent * (3 * latent + at_both.shape[1]),
    )


def edge_backward(order, first, second, pooled_grad, edge_grad, normed, inverse, pre, at_receiver, at_both_t, gain, last, node_total):
    samples, edges, latent = normed.shape
    at_total = at_both_t.shape[0]
    table_total = at_total - node_total

    def kernel(order, w1, w2, upstream, *rest):
        if not last:
            later, rest = rest[0], rest[1:]
        normed, inverse, pre, receiver, both_t, gain, low, hidden_low, at_rows, partial, returned, grad_out, minor = rest[:13]
        if last:
            w1s, w2s = rest[13:]
        else:
            hidden_sum, w1s, w2s, hidden_acc = rest[13:]
        step = pl.program_id(0)

        @pl.when(step == 0)
        def _():
            assemble(w1, order, w1.shape[1], 0, w1s)
            assemble(w2, order, w2.shape[1], 0, w2s)
            minor[...] = jnp.zeros_like(minor)

        grad = matmul(receiver[...], upstream[0])
        if not last:
            grad = grad + later[0]
        scaled = normed[0].astype(F32)
        output_grad = norm_backward(grad, scaled, inverse[0], gain[0:1]).astype(BF16)
        low[0] = output_grad
        act_grad = matmul(output_grad, w2s[...])
        pre_grad = (act_grad * silu_slope(pre[0].astype(F32))).astype(BF16)
        hidden_low[0] = pre_grad
        minor[0:1] += column_sum(pre_grad.astype(F32))
        minor[1:2] += column_sum(output_grad.astype(F32))
        minor[2:3] += column_sum(grad * scaled)
        minor[3:4] += column_sum(grad)
        at_rows[0] = matmul(both_t[...], pre_grad).astype(BF16)
        send = w1s[latent : 2 * latent]
        partial[0] = matmul_nt(at_rows[0, :node_total], send) + matmul_nt(
            at_rows[0, table_total:], w1s[2 * latent :]
        )
        returned[0] = matmul_nt(at_rows[0, node_total:table_total], send).astype(BF16)
        if last:
            grad_out[0] = grad + matmul_nt(pre_grad, w1s[:latent])
        else:

            @pl.when(step == 0)
            def _():
                grad_out[...] = grad
                hidden_acc[...] = pre_grad.astype(F32)

            @pl.when(step > 0)
            def _():
                grad_out[...] += grad
                hidden_acc[...] += pre_grad.astype(F32)

            @pl.when(step == samples - 1)
            def _():
                total = hidden_acc[...].astype(BF16)
                hidden_sum[...] = total
                grad_out[...] += matmul_nt(total, w1s[:latent])

    wide = (samples, edges, latent)
    outputs = [
        sampled(wide, BF16),
        sampled(wide, BF16),
        sampled((samples, at_total, latent), BF16),
        sampled((samples, node_total, latent), F32),
        sampled((samples, table_total - node_total, latent), BF16),
        sampled(wide, F32) if last else shared((edges, latent), F32),
        shared((4, latent), F32),
    ]
    scratch = [pltpu.VMEM((3 * latent, latent), BF16), pltpu.VMEM((latent, latent), BF16)]
    inputs = [order, first[0], second[0], pooled_grad]
    specs = [in_scalars(), weight_block(*first), weight_block(*second), per_sample(pooled_grad)]
    if not last:
        outputs.append(shared((edges, latent), BF16))
        scratch.append(pltpu.VMEM((edges, latent), F32))
        inputs.append(edge_grad)
        specs.append(per_sample(edge_grad))
    inputs += [normed, inverse, pre, at_receiver, at_both_t, gain]
    specs += [
        per_sample(normed),
        per_sample(inverse),
        per_sample(pre),
        constant(at_receiver),
        constant(at_both_t),
        constant(gain),
    ]
    return run_kernel(
        kernel,
        "edge_backward",
        samples,
        inputs,
        specs,
        outputs,
        scratch,
        2 * samples * edges * latent * (2 * latent + 2 * at_total),
    )


def edge_weight_grads(owners, edge_low, table, hidden_low, at_rows, low, act, node_total, nodes, width, packed_before):
    samples, table_total, latent = table.shape
    alike = edge_low.ndim == 2
    first_rows, second_rows = 3 * latent // nodes, latent // nodes
    offset = 0 if packed_before is None else packed_before[0].shape[1]
    blocks, hids = owners.shape[0] // 2, latent // width

    def kernel(owners, edge_low, table, hidden_low, at_rows, low, act, *rest):
        before, rest = rest[:-4], rest[-4:]
        kept, sent, first, second = rest
        step = pl.program_id(0)

        @pl.when(step == 0)
        def _():
            first[...] = jnp.zeros_like(first)
            second[...] = jnp.zeros_like(second)
            for source, target in zip(before, (kept, sent)):
                target[:, :offset, :] = source[...]
            if alike:
                add(first, 0, matmul_tn(edge_low[...], hidden_low[...]))

        if not alike:
            add(first, 0, matmul_tn(edge_low[0], hidden_low[0]))
        add(first, latent, matmul_tn(table[0], at_rows[0, :table_total]))
        add(first, 2 * latent, matmul_tn(table[0, :node_total], at_rows[0, table_total:]))
        add(second, 0, matmul_tn(low[0], act[0]))

        @pl.when(step == samples - 1)
        def _():
            pack(first, owners, first_rows, offset, kept, sent)
            pack(second, owners, second_rows, offset + first_rows, kept, sent)

    of_edges = constant if alike else per_sample
    inputs = [owners, edge_low, table, hidden_low, at_rows, low, act]
    specs = [in_scalars(), of_edges(edge_low), per_sample(table), of_edges(hidden_low), per_sample(at_rows), per_sample(low), per_sample(act)]
    if packed_before is not None:
        inputs += packed_before
        specs += [constant(a) for a in packed_before]
    return run_kernel(
        kernel,
        "edge_weight_grads",
        samples,
        inputs,
        specs,
        [shared((blocks // 2, offset + first_rows + second_rows, width), BF16)] * 2,
        [pltpu.VMEM((hids, 3 * latent, width), F32), pltpu.VMEM((hids, latent, width), F32)],
        4 * low.size * latent,
    )


def node_pass(order, owners, weights, nodes, node_low, state, pooled_pair, params, at_halo, target, scaling, mask):
    samples, node_total, latent = node_low.shape
    array, rows, place = weights
    second_rows, hids = latent // nodes, latent // array.shape[2]
    first_rows = rows - second_rows
    count = samples * node_total
    last = target is not None

    def kernel(order, *rest):
        if last:
            owners, rest = rest[0], rest[1:]
        w, node_low, state, pooled_own, pooled_other, params, *rest = rest
        if last:
            target, scaling, mask, new_low, upstream, input_grad, kept, sent, minor, w1s, w2s, first, second = rest
        else:
            at_halo, pooled_out, pre, act, normed, inverse, new_state, new_low, halo, w1s, w2s = rest
        assemble(w, order, first_rows, 0, w1s)
        assemble(w, order, second_rows, first_rows, w2s)
        rows_low = node_low[...].reshape(count, latent)
        pooled = (pooled_own[...].astype(F32) + pooled_other[...].astype(F32)).astype(BF16)
        pooled = pooled.reshape(count, latent)
        hidden = matmul(rows_low, w1s[:latent]) + matmul(pooled, w1s[latent:]) + params[4:5]
        active = (hidden * sigmoid(hidden)).astype(BF16)
        output = matmul_nt(active, w2s[...]) + params[5:6]
        scaled, scale = norm_forward(output)
        state_new = state[...].astype(F32).reshape(count, latent) + scaled * params[6:7] + params[7:8]
        low_new = state_new.astype(BF16).reshape(new_low.shape)
        new_low[...] = low_new
        if not last:
            pooled_out[...] = pooled
            pre[...] = hidden.astype(BF16)
            act[...] = active
            normed[...] = scaled.astype(BF16)
            inverse[...] = scale
            new_state[...] = state_new.reshape(new_state.shape)
            for s in range(samples):
                halo[s] = matmul(at_halo[...], new_low[s]).astype(BF16)
        else:
            grad = (target[...].astype(F32) * scaling[...]).reshape(count, latent)
            node_gradients(
                grad, scaled, scale, hidden, active, rows_low, pooled, params, mask,
                w1s, w2s, first, second, upstream, input_grad, kept, sent, minor, owners, first_rows, second_rows,
            )

    shape = node_low.shape
    inputs = [array, node_low, state, *pooled_pair, params]
    scratch = [pltpu.VMEM((2 * latent, latent), BF16), pltpu.VMEM((latent, latent), BF16)]
    if last:
        inputs += [target, scaling, mask]
        outputs = [shared(shape, BF16), *gradient_outputs(shape, order.shape[0], rows, array.shape[2])]
        scratch += [pltpu.VMEM((hids, 2 * latent, latent // hids), F32), pltpu.VMEM((hids, latent, latent // hids), F32)]
    else:
        inputs += [at_halo]
        outputs = [
            shared((count, latent), BF16),
            shared((count, latent), BF16),
            shared((count, latent), BF16),
            shared((count, latent), BF16),
            shared((count, 1), F32),
            shared(shape, F32),
            shared(shape, BF16),
            shared((samples, at_halo.shape[0], latent), BF16),
        ]
    tables = [order, owners] if last else [order]
    specs = [in_scalars() for _ in tables] + [weight_block(*weights)] + [constant(a) for a in inputs[1:]]
    inputs = tables + inputs
    return run_kernel(kernel, "node_pass", 1, inputs, specs, outputs, scratch, 6 * count * latent * latent * (3 if last else 1))


def gradient_outputs(shape, blocks, rows, width):
    return [
        shared(shape, BF16),
        shared(shape, F32),
        shared((blocks // 2, rows, width), BF16),
        shared((blocks // 2, rows, width), BF16),
        shared((4, shape[-1]), F32),
    ]


def node_gradients(
    grad, scaled, scale, hidden, active, rows_low, pooled, params, mask,
    w1s, w2s, first, second, upstream, input_grad, kept, sent, minor, owners, first_rows, second_rows,
):
    latent = w2s.shape[0]
    output_grad = norm_backward(grad, scaled, scale, params[6:7]).astype(BF16)
    pre_grad = (matmul(output_grad, w2s[...]) * silu_slope(hidden)).astype(BF16)
    upstream[...] = matmul_nt(pre_grad, w1s[latent:]).astype(BF16).reshape(upstream.shape)
    input_grad[...] = (grad + matmul_nt(pre_grad, w1s[:latent])).reshape(input_grad.shape)
    chosen = mask[...] > 0.5
    output_mine = jnp.where(chosen, output_grad.astype(F32), 0.0)
    pre_mine = jnp.where(chosen, pre_grad.astype(F32), 0.0)
    grad_mine = jnp.where(chosen, grad, 0.0)
    minor[0:1] = column_sum(pre_mine)
    minor[1:2] = column_sum(output_mine)
    minor[2:3] = column_sum(grad_mine * scaled)
    minor[3:4] = column_sum(grad_mine)
    pre_mine = pre_mine.astype(BF16)
    store(first, 0, matmul_tn(rows_low, pre_mine))
    store(first, latent, matmul_tn(pooled, pre_mine))
    store(second, 0, matmul_tn(output_mine.astype(BF16), active))
    pack(first, owners, first_rows, 0, kept, sent)
    pack(second, owners, second_rows, first_rows, kept, sent)


def node_backward(order, owners, weights, nodes, grads, node_low, pooled, pre, act, normed, inverse, params, mask):
    samples, node_total, latent = node_low.shape
    array, rows, place = weights
    second_rows, hids = latent // nodes, latent // array.shape[2]
    first_rows = rows - second_rows
    count = samples * node_total

    def kernel(order, owners, w, base, own, other, node_low, pooled, pre, act, normed, inverse, params, mask, upstream, input_grad, kept, sent, minor, w1s, w2s, first, second):
        assemble(w, order, first_rows, 0, w1s)
        assemble(w, order, second_rows, first_rows, w2s)
        grad = (base[...] + (own[...] + other[...].astype(F32))).reshape(count, latent)
        node_gradients(
            grad, normed[...].astype(F32), inverse[...], pre[...].astype(F32), act[...],
            node_low[...].reshape(count, latent), pooled[...], params, mask,
            w1s, w2s, first, second, upstream, input_grad, kept, sent, minor, owners, first_rows, second_rows,
        )

    inputs = [order, owners, array, *grads, node_low, pooled, pre, act, normed, inverse, params, mask]
    specs = [in_scalars(), in_scalars(), weight_block(*weights)] + [constant(a) for a in inputs[3:]]
    return run_kernel(
        kernel,
        "node_backward",
        1,
        inputs,
        specs,
        gradient_outputs(node_low.shape, order.shape[0], rows, array.shape[2]),
        [
            pltpu.VMEM((2 * latent, latent), BF16),
            pltpu.VMEM((latent, latent), BF16),
            pltpu.VMEM((hids, 2 * latent, latent // hids), F32),
            pltpu.VMEM((hids, latent, latent // hids), F32),
        ],
        12 * count * latent * latent,
    )


def dot(spec, left, right):
    return jnp.einsum(spec, left, right, preferred_element_type=F32)


def swap(values, axis, offset):
    return lax.ppermute(values, axis, [(i, i ^ offset) for i in range(lax.axis_size(axis))])


def bits_of(axis):
    return lax.axis_size(axis).bit_length() - 1


def own_bit(axis, bit):
    return (lax.axis_index(axis) >> bit) & 1


def all_bits():
    return [(axis, bit) for axis in ("node", "hid") for bit in reversed(range(bits_of(axis)))]


def ordered(own, mine, other):
    low = jnp.where(own == 0, mine, other)
    high = jnp.where(own == 0, other, mine)
    return low, high


def double_up(part, axis, bit, place):
    low, high = ordered(own_bit(axis, bit), part, swap(part, axis, 1 << bit))
    return jnp.stack([low, high], axis=place)


def halve_sum(parts, axis, bit, place):
    own = own_bit(axis, bit)
    sent = lax.dynamic_index_in_dim(parts, 1 - own, place, keepdims=False)
    kept = lax.dynamic_index_in_dim(parts, own, place, keepdims=False)
    return kept.astype(F32) + swap(sent.astype(BF16), axis, 1 << bit).astype(F32)


def places():
    node_ids = jnp.arange(lax.axis_size("node"), dtype=jnp.int32) ^ lax.axis_index("node")
    hid_ids = jnp.arange(lax.axis_size("hid"), dtype=jnp.int32) ^ lax.axis_index("hid")
    place = 0
    for step, (axis, bit) in enumerate(all_bits()):
        ids = node_ids[:, None] if axis == "node" else hid_ids[None, :]
        place = place + (((ids >> bit) & 1) << step)
    return place.reshape(-1)


def owners_of_places():
    place = jnp.arange(1 << len(all_bits()), dtype=jnp.int32)
    owner = {"node": lax.axis_index("node"), "hid": lax.axis_index("hid")}
    for step, (axis, bit) in enumerate(all_bits()):
        owner[axis] = owner[axis] ^ (((place >> step) & 1) << bit)
    return jnp.stack([owner["node"], owner["hid"]], axis=1).reshape(-1)


def after(value, *earlier):
    return lax.optimization_barrier((value, *earlier))[0]


def exchange(values, first_step, flips):
    hid_bits = bits_of("hid")
    mask = 0
    for k in range(flips.bit_length()):
        if (flips >> k) & 1:
            axis, bit = all_bits()[first_step + k]
            mask |= 1 << (bit if axis == "hid" else bit + hid_bits)
    total = 1 << len(all_bits())
    return lax.ppermute(values, ("node", "hid"), [(i, i ^ mask) for i in range(total)])


def rounds(begin, end):
    return [(step, min(step + 2, end)) for step in range(begin, end, 2)]


def gather_round(held, begin, end, *under):
    arrived = [exchange(held, begin, flips) for flips in range(1, 1 << (end - begin))]
    if under:
        arrived = lax.optimization_barrier((*arrived, *under))[: len(arrived)]
    return jnp.concatenate([held, *arrived], axis=0)


def split(total, count):
    size = total.shape[0] // count
    pieces = [total[i * size : (i + 1) * size] for i in range(count)]
    return [pieces[0]] + [piece.astype(BF16) for piece in pieces[1:]]


def scatter_round(pieces, begin, *under):
    arrived = [exchange(pieces[flips], begin, flips) for flips in range(1, len(pieces))]
    if under:
        arrived = lax.optimization_barrier((*arrived, *under))[: len(arrived)]
    total = pieces[0].astype(F32)
    for piece in arrived:
        total = total + piece.astype(F32)
    return total


def scatter_rest(total, end, *under):
    for begin, stop in reversed(rounds(0, end)):
        total = scatter_round(split(total, 1 << (stop - begin)), begin, *under)
    return total[0]


def sum_round(values, begin, end):
    terms = [values] + [exchange(values, begin, flips) for flips in range(1, 1 << (end - begin))]
    while len(terms) > 1:
        terms = [terms[i] + terms[i + 1] for i in range(0, len(terms), 2)]
    return terms[0]


def sum_everywhere(values):
    steps = len(all_bits())
    values = sum_round(values, steps - 1, steps)
    for begin, end in reversed(rounds(0, steps - 1)):
        values = sum_round(values, begin, end)
    return values


def to_neighbours(rows, halo_width):
    count = lax.axis_size("node")
    onward = [(i, (i + 1) % count) for i in range(count)]
    back = [(target, source) for source, target in onward]
    from_previous = lax.ppermute(rows[:, halo_width:], "node", onward)
    from_next = lax.ppermute(rows[:, :halo_width], "node", back)
    return jnp.concatenate([from_previous, from_next], axis=1)


def adam_terms(weight, grad, first, second, decay):
    first_new = BETA_FIRST * first + (1.0 - BETA_FIRST) * grad
    second_new = BETA_SECOND * second + (1.0 - BETA_SECOND) * grad * grad
    update = first_new / (jnp.sqrt(second_new) + ADAM_EPS) + decay * weight
    return (first_new, second_new, update)


def pack_shards(first, second):
    return jnp.concatenate([first, second.T], axis=0).astype(BF16)


def adam_terms(weight, grad, first, second, decay):
    first_new = BETA_FIRST * first + (1.0 - BETA_FIRST) * grad
    second_new = BETA_SECOND * second + (1.0 - BETA_SECOND) * grad * grad
    update = first_new / (jnp.sqrt(second_new) + ADAM_EPS) + decay * weight
    return (first_new, second_new, update)


def per_device(
    node_in,
    edge_in,
    cotangent,
    ocean_mask,
    present_mask,
    valid_counts,
    send_slot,
    recv_local,
    halo_lists,
    edge_first,
    edge_second,
    node_first,
    node_second,
    edge_first_m,
    edge_second_m,
    node_first_m,
    node_second_m,
    edge_first_v,
    edge_second_v,
    node_first_v,
    node_second_v,
    small_params,
    small_m,
    small_v,
    learn_rate,
):
    hid_count = lax.axis_size("hid")
    hid_index = lax.axis_index("hid")
    node_total, sample_count, latent = node_in.shape
    edge_part = edge_in.shape[0] // hid_count
    node_part = node_total // hid_count
    halo_width = halo_lists.shape[1]
    table_total = node_total + 2 * halo_width
    sample_half, edge_half = hid_index >> 1, hid_index & 1
    samples = sample_count // 2
    nodes, hids = lax.axis_size("node"), hid_count
    first_rows = edge_first.shape[1]
    second_rows = edge_second.shape[2]
    node_rows = node_first.shape[1] + second_rows
    width = edge_first.shape[2]

    order, owners = places(), owners_of_places()
    steps = len(all_bits())

    def layer_shards(depth, *earlier):
        shards = (node_first[depth], node_second[depth], edge_first[depth], edge_second[depth])
        if earlier:
            shards = after(shards, *earlier)
        return jnp.concatenate([pack_shards(*shards[:2]), pack_shards(*shards[2:])], axis=0)[None]

    def parted(held):
        return held[:, :node_rows], held[:, node_rows:]

    layer_zero = layer_shards(0)
    for begin, end in rounds(0, steps - 3):
        layer_zero = gather_round(layer_zero, begin, end)
    setup = layer_zero
    layer_zero = gather_round(layer_zero, steps - 3, steps - 2)
    node_zero, edge_zero = parted(layer_zero)
    layer_one = layer_shards(1, setup)
    layer_one = after(layer_one, edge_zero)
    z_rounds = rounds(0, steps - 3)
    for begin, end in z_rounds[:-1]:
        layer_one = gather_round(layer_one, begin, end)
    halo_gate = edge_zero
    masters = (edge_first, edge_second, node_first, node_second)
    weight_local = jnp.stack(
        [jnp.sum(matrix * matrix, axis=(1, 2)) for matrix in after(masters, setup)], axis=1
    )
    def edge_blocks(whole):
        return ((whole, first_rows, 0), (whole, second_rows, first_rows // second_rows))

    def own_edges(values):
        return lax.dynamic_index_in_dim(
            values.reshape(2, 2, edge_part, *values.shape[1:]), edge_half, 1, keepdims=False
        ).reshape(2 * edge_part, *values.shape[1:])

    def own_nodes(values):
        return lax.dynamic_index_in_dim(
            values.reshape(samples, 2, 2, node_part, latent), edge_half, 2, keepdims=False
        ).reshape(samples, 2 * node_part, latent)

    def own_samples(values):
        return lax.dynamic_slice_in_dim(values, sample_half * samples, samples, 1)

    def own_rows_exchanged(values):
        quarters = jnp.moveaxis(values.reshape(samples, 2, 2, node_part, latent), 0, 3)
        quarters = lax.dynamic_index_in_dim(quarters, edge_half, 1, keepdims=False)
        sent = lax.dynamic_index_in_dim(quarters, 1 - sample_half, 0, keepdims=False)
        kept = lax.dynamic_index_in_dim(quarters, sample_half, 0, keepdims=False)
        return kept, swap(sent, "hid", 2)

    def all_samples(kept, arrived):
        return jnp.concatenate(ordered(sample_half, kept, arrived), axis=1)

    send_slot, recv_local, halo_lists, node_in, edge_in = lax.optimization_barrier(
        (send_slot, recv_local, halo_lists, node_in, edge_in, setup)
    )[:5]
    sender = own_edges(send_slot)
    receiver = own_edges(recv_local)
    node_ids, table_ids = jnp.arange(node_total), jnp.arange(table_total)
    at_receiver = (receiver[:, None] == node_ids[None, :]).astype(BF16)
    at_both = jnp.concatenate(
        [(sender[:, None] == table_ids[None, :]).astype(BF16), at_receiver], axis=1
    )
    at_nodes = (node_ids[:, None] == receiver[None, :]).astype(BF16)
    at_both_t = jnp.concatenate(
        [(table_ids[:, None] == sender[None, :]).astype(BF16), at_nodes], axis=0
    )
    at_halo = (halo_lists.reshape(-1)[:, None] == node_ids[None, :]).astype(BF16)
    mask = ((node_ids // node_part) % 2 == edge_half).astype(F32)
    mask = jnp.tile(mask, samples)[:, None]

    node_low = jnp.transpose(own_samples(node_in), (1, 0, 2))
    edge_in_own = own_edges(edge_in)
    halo_rows = dot("hn,snl->shl", at_halo, node_low).astype(BF16)
    node_low_zero = node_low
    halo_rows = to_neighbours(after(halo_rows, halo_gate), halo_width)
    begin, end = z_rounds[-1]
    arrived = [exchange(layer_one, begin, flips) for flips in range(1, 1 << (end - begin))]
    edge_arrived, halo_rows, weight_local, *arrived = lax.optimization_barrier(
        (exchange(edge_zero, steps - 2, 1), halo_rows, weight_local, *arrived)
    )
    edge_zero = jnp.concatenate([edge_zero, edge_arrived], axis=0)
    layer_one = jnp.concatenate([layer_one, *arrived], axis=0)
    node_zero = after(node_zero, edge_zero)
    edge_zero = gather_round(edge_zero, steps - 1, steps)
    table_zero = jnp.concatenate([node_low, halo_rows], axis=1)
    pre_zero, act_zero, normed_zero, inverse_zero, edge_state, edge_low, pooled = edge_forward(
        order,
        *edge_blocks(edge_zero),
        table_zero,
        edge_in_own[None],
        edge_in_own[None],
        at_both,
        at_nodes,
        small_params[0],
        node_total,
        False,
    )
    pooled, *arrived = lax.optimization_barrier(
        (pooled, exchange(node_zero, steps - 2, 1), exchange(layer_one, steps - 3, 1))
    )
    node_zero = jnp.concatenate([node_zero, arrived[0]], axis=0)
    node_zero = gather_round(node_zero, steps - 1, steps)
    layer_one = jnp.concatenate([layer_one, arrived[1]], axis=0)
    node_one, edge_one = parted(layer_one)
    other = after(swap(pooled, "hid", 1), edge_one)
    (
        pooled_zero,
        node_pre,
        node_act,
        node_normed,
        node_inverse,
        node_state,
        node_low,
        halo_rows,
    ) = node_pass(
        order,
        None,
        (node_zero, node_rows, 0),
        nodes,
        node_low_zero,
        node_low_zero,
        (pooled, other),
        small_params[0],
        at_halo,
        None,
        None,
        None,
    )
    halo_rows = to_neighbours(halo_rows, halo_width)
    arrived, halo_rows = lax.optimization_barrier(
        (exchange(edge_one, steps - 2, 1), halo_rows)
    )
    edge_one = jnp.concatenate([edge_one, arrived], axis=0)
    node_one = after(node_one, edge_one)
    edge_one = gather_round(edge_one, steps - 1, steps)

    valid_mask = (ocean_mask[:, None] * present_mask).astype(BF16)
    masked = after(cotangent, pooled) * valid_mask[:, :, None]
    sent = lax.dynamic_slice_in_dim(masked, (1 - sample_half) * samples, samples, 1)
    masked = jnp.stack(ordered(sample_half, own_samples(masked), swap(sent, "hid", 2)), axis=0)
    masked = double_up(masked, "hid", 0, 1).reshape(node_total, samples, latent)
    scaling = node_total * lax.axis_size("node") / valid_counts.astype(F32)
    scaling = lax.dynamic_slice_in_dim(scaling, sample_half * samples, samples, 0)
    target = jnp.transpose(masked, (1, 0, 2))
    scaling = scaling[:, None, None]

    node_low_one = node_low
    table_one = jnp.concatenate([node_low, halo_rows], axis=1)
    pre_one, act_one, normed_one, inverse_one, pooled = edge_forward(
        order,
        *edge_blocks(edge_one),
        table_one,
        edge_low,
        edge_state,
        at_both,
        at_nodes,
        small_params[1],
        node_total,
        True,
    )
    node_one = gather_round(node_one, steps - 2, steps - 1, pooled)
    node_one = gather_round(node_one, steps - 1, steps)
    node_low, pooled_grad, node_grad, kept, sent, node_minor_one = node_pass(
        order,
        owners,
        (node_one, node_rows, 0),
        nodes,
        node_low_one,
        node_state,
        (pooled, swap(pooled, "hid", 1)),
        small_params[1],
        None,
        target,
        scaling,
        mask,
    )

    def from_edges(partial, returned):
        return partial + dot("hn,shl->snl", at_halo, returned)

    low, hidden_low, at_rows, partial, returned, edge_grad, edge_minor_one = edge_backward(
        order,
        *edge_blocks(edge_one),
        pooled_grad,
        None,
        normed_one,
        inverse_one,
        pre_one,
        at_receiver,
        at_both_t,
        small_params[1, 2:3],
        True,
        node_total,
    )
    low, *node_out = lax.optimization_barrier((low, *own_rows_exchanged(node_low)))
    node_out = all_samples(*node_out)
    chain_one = edge_weight_grads(
        owners,
        edge_low,
        table_one,
        hidden_low,
        at_rows,
        low,
        act_one,
        node_total,
        nodes,
        width,
        [kept, sent],
    )
    returned, *chain_one = lax.optimization_barrier(
        (to_neighbours(returned, halo_width), *chain_one)
    )
    partial = from_edges(partial, returned)
    chain_one = split(scatter_round(chain_one, steps - 1), 2)
    other, *chain_one = lax.optimization_barrier((swap(partial.astype(BF16), "hid", 1), *chain_one))
    pooled_grad, node_grad, kept, sent, node_minor_zero = node_backward(
        order,
        owners,
        (node_zero, node_rows, 0),
        nodes,
        (node_grad, partial, other),
        node_low_zero,
        pooled_zero,
        node_pre,
        node_act,
        node_normed,
        node_inverse,
        small_params[0],
        mask,
    )
    low, hidden_low, at_rows, partial, returned, edge_input_grad, edge_minor_zero, hidden_sum = (
        edge_backward(
            order,
            *edge_blocks(edge_zero),
            pooled_grad,
            edge_grad,
            normed_zero,
            inverse_zero,
            pre_zero,
            at_receiver,
            at_both_t,
            small_params[0, 2:3],
            False,
            node_total,
        )
    )
    chain_one = split(scatter_round(chain_one, steps - 2, low), 2)
    chain_zero = split(scatter_round((kept, sent), steps - 1, low), 2)
    low = after(low, *chain_one, *chain_zero)
    chain_edge = edge_weight_grads(
        owners,
        edge_in_own,
        table_zero,
        hidden_sum,
        at_rows,
        low,
        act_zero,
        node_total,
        nodes,
        width,
        None,
    )
    chain_zero = split(scatter_round(chain_zero, steps - 2, chain_edge[1]), 2)
    chain_one = [jnp.concatenate(pair, axis=1) for pair in zip(chain_one, chain_zero)]
    kept, sent, *chain_one = lax.optimization_barrier((*chain_edge, *chain_one))
    chain_edge = split(scatter_round((kept, sent), steps - 1), 2)
    returned = to_neighbours(after(returned, chain_edge[1]), halo_width)
    arrived, returned = lax.optimization_barrier((exchange(chain_one[1], steps - 3, 1), returned))
    chain_one = chain_one[0].astype(F32) + arrived.astype(F32)
    for begin, end in reversed(z_rounds[1:]):
        chain_one = scatter_round(split(chain_one, 1 << (end - begin)), begin)
    begin, end = z_rounds[0]
    chain_one = split(chain_one, 1 << (end - begin))
    partial = from_edges(partial, returned)
    other = swap(partial.astype(BF16), "hid", 1)
    arrived, edge_input_grad, other, *chain_one = lax.optimization_barrier(
        (exchange(chain_edge[1], steps - 2, 1), edge_input_grad, other, *chain_one)
    )
    chain_edge = split(chain_edge[0] + arrived.astype(F32), 2)
    arrived, *others = lax.optimization_barrier(
        (
            exchange(chain_edge[1], steps - 3, 1),
            *[exchange(chain_one[flips], begin, flips) for flips in range(1, len(chain_one))],
        )
    )
    chain_edge = chain_edge[0] + arrived.astype(F32)
    joined_grads = chain_one[0]
    for piece in others:
        joined_grads = joined_grads + piece.astype(F32)
    joined_grads = joined_grads[0]
    node_grad = node_grad + (partial + other.astype(F32))
    grad_node = own_rows_exchanged(node_grad.astype(BF16))
    halves = edge_input_grad.reshape(2, edge_part, latent)
    sent = lax.dynamic_index_in_dim(halves, 1 - sample_half, 0, keepdims=False).astype(BF16)
    kept = lax.dynamic_index_in_dim(halves, sample_half, 0, keepdims=False)
    edge_zero_grads = scatter_rest(chain_edge, steps - 3)
    edge_zero_grads, joined_grads, arrived, *grad_node = lax.optimization_barrier(
        (edge_zero_grads, joined_grads, swap(sent, "hid", 2), *grad_node)
    )
    edge_input_grad = kept + arrived.astype(F32)
    grad_node = all_samples(*grad_node)

    edge_rows = first_rows + second_rows
    layer_one_grads = joined_grads[: node_rows + edge_rows]
    node_zero_grads = joined_grads[node_rows + edge_rows :]
    node_one_grads, edge_one_grads = layer_one_grads[:node_rows], layer_one_grads[node_rows:]
    node_first_rows = node_rows - second_rows
    grads = [
        jnp.stack([edge_zero_grads[:first_rows], edge_one_grads[:first_rows]]),
        jnp.stack([edge_zero_grads[first_rows:].T, edge_one_grads[first_rows:].T]),
        jnp.stack([node_zero_grads[:node_first_rows], node_one_grads[:node_first_rows]]),
        jnp.stack([node_zero_grads[node_first_rows:].T, node_one_grads[node_first_rows:].T]),
    ]
    firsts = (edge_first_m, edge_second_m, node_first_m, node_second_m)
    seconds = (edge_first_v, edge_second_v, node_first_v, node_second_v)
    moment_list = [
        adam_terms(masters[place], grads[place], firsts[place], seconds[place], WEIGHT_DECAY)
        for place in range(4)
    ]
    update_local = jnp.stack(
        [jnp.sum(entry[2] * entry[2], axis=(1, 2)) for entry in moment_list], axis=1
    )
    squares = jnp.concatenate([weight_local.reshape(1, -1), update_local.reshape(1, -1)], axis=1)
    minor_packed = sum_everywhere(
        jnp.concatenate(
            [edge_minor_zero, node_minor_zero, edge_minor_one, node_minor_one]
            + [jnp.pad(squares, ((0, 0), (0, latent - squares.size)))],
            axis=0,
        )
    )
    minor_total = minor_packed[: 8 * LAYERS].reshape(small_params.shape)
    squares = minor_packed[8 * LAYERS, : squares.size].reshape(2, *weight_local.shape)
    weight_squares, update_squares = squares[0], squares[1]
    weight_norm = jnp.sqrt(weight_squares)
    update_norm = jnp.sqrt(update_squares)
    new_weights = []
    for position in range(4):
        ratio = weight_norm[:, position] / update_norm[:, position]
        new_weights.append(
            masters[position] - learn_rate[0] * ratio[:, None, None] * moment_list[position][2]
        )
    small_first, small_second, small_update = adam_terms(
        small_params, minor_total, small_m, small_v, 0.0
    )
    small_wnorm = jnp.sqrt(jnp.sum(small_params * small_params, axis=2))
    small_unorm = jnp.sqrt(jnp.sum(small_update * small_update, axis=2))
    small_new = (
        small_params - learn_rate[0] * (small_wnorm / small_unorm)[:, :, None] * small_update
    )
    norms = jnp.stack(
        [
            jnp.concatenate([weight_norm, small_wnorm], axis=1),
            jnp.concatenate([update_norm, small_unorm], axis=1),
        ],
        axis=2,
    )
    return (
        node_out,
        grad_node,
        edge_input_grad.astype(BF16),
        *new_weights,
        *[entry[0] for entry in moment_list],
        *[entry[1] for entry in moment_list],
        *[weight.astype(BF16) for weight in new_weights],
        small_new,
        small_first,
        small_second,
        norms,
    )


def solution(mesh):
    whole = P()
    rows = P(None, "node", "hid")
    columns = P(None, "hid", "node")
    matrices = (rows, columns, rows, columns)
    in_specs = (
        P("node", None, None),
        P("node", None),
        P(("node", "hid"), None, None),
        P(("node", "hid")),
        P(("node", "hid"), None),
        P(),
        P("node"),
        P("node"),
        P("node", None),
        *matrices,
        *matrices,
        *matrices,
        whole,
        whole,
        whole,
        whole,
    )
    out_specs = (
        P(("node", "hid"), None, None),
        P(("node", "hid"), None, None),
        P(("node", "hid"), None),
        *matrices,
        *matrices,
        *matrices,
        *matrices,
        whole,
        whole,
        whole,
        whole,
    )
    return jax.shard_map(
        per_device, mesh=mesh, in_specs=in_specs, out_specs=out_specs, check_vma=False
    )
```

```python
import jax
import jax.numpy as jnp
from jax import lax
from jax.experimental import pallas as pl
from jax.experimental.pallas import tpu as pltpu
from jax.sharding import PartitionSpec as P

LAYERS = 2


NORM_EPS = 1e-05
BETA_FIRST = 0.5
BETA_SECOND = 0.5
ADAM_EPS = 1e-06
WEIGHT_DECAY = 0.01
BF16 = jnp.bfloat16
F32 = jnp.float32
VMEM_BYTES = 56 * 1024 * 1024


def matmul(left, right):
    return lax.dot_general(left, right, (((1,), (0,)), ((), ())), preferred_element_type=F32)


def matmul_nt(left, right):
    return lax.dot_general(left, right, (((1,), (1,)), ((), ())), preferred_element_type=F32)


def matmul_tn(left, right):
    return lax.dot_general(left, right, (((0,), (0,)), ((), ())), preferred_element_type=F32)


def sigmoid(values):
    return 0.5 + 0.5 * jnp.tanh(0.5 * values)


def silu_slope(values):
    gate = sigmoid(values)
    return gate * (1.0 + values * (1.0 - gate))


def norm_forward(values):
    center = values - jnp.mean(values, axis=-1, keepdims=True)
    spread = jnp.mean(center * center, axis=-1, keepdims=True)
    inverse = lax.rsqrt(spread + NORM_EPS)
    return center * inverse, inverse


def norm_backward(upstream, normed, inverse, gain_row):
    scaled = upstream * gain_row
    return inverse * (
        scaled
        - jnp.mean(scaled, axis=-1, keepdims=True)
        - normed * jnp.mean(scaled * normed, axis=-1, keepdims=True)
    )


def column_sum(values):
    return jnp.sum(values, axis=0, keepdims=True)


def assemble(source, order, rows, offset, target):
    width = source.shape[2]
    nodes, hids = target.shape[0] // rows, target.shape[1] // width
    for i in range(nodes):
        for j in range(hids):
            target[i * rows : (i + 1) * rows, j * width : (j + 1) * width] = source[
                order[i * hids + j], offset : offset + rows, :
            ]


def store(target, begin, values):
    rows, width = values.shape[0], target.shape[2]
    for j in range(target.shape[0]):
        target[j, begin : begin + rows] = values[:, j * width : (j + 1) * width]


def add(target, begin, values):
    rows, width = values.shape[0], target.shape[2]
    for j in range(target.shape[0]):
        target[j, begin : begin + rows] += values[:, j * width : (j + 1) * width]


def pack(values, owners, rows, offset, kept, sent):
    half = kept.shape[0]

    def one(index, carry):
        for target, place in ((kept, index), (sent, index + half)):
            begin = pl.multiple_of(owners[2 * place] * rows, rows)
            target[index, offset : offset + rows, :] = values[
                owners[2 * place + 1], pl.ds(begin, rows), :
            ].astype(BF16)
        return carry

    lax.fori_loop(0, half, one, 0)


def per_sample(array):
    block = (1,) + array.shape[1:]
    return pl.BlockSpec(block, lambda s: (s,) + (0,) * (len(block) - 1))


def constant(array):
    return pl.BlockSpec(array.shape, lambda s: (0,) * len(array.shape))


def weight_block(array, rows, place):
    blocks, _, width = array.shape
    return pl.BlockSpec((blocks, rows, width), lambda s: (0, place, 0))


def in_scalars():
    return pl.BlockSpec(memory_space=pltpu.SMEM)


def shape_of(shape, dtype):
    return jax.ShapeDtypeStruct(shape, dtype)


def run_kernel(kernel, name, samples, inputs, in_specs, outputs, scratch, flops):
    moved = sum(a.size * a.dtype.itemsize for a in inputs) + sum(
        shape.size * shape.dtype.itemsize for shape, _ in outputs
    )
    return pl.pallas_call(
        kernel,
        name=name,
        grid=(samples,),
        in_specs=in_specs,
        out_specs=[spec for _, spec in outputs],
        out_shape=[shape for shape, _ in outputs],
        scratch_shapes=scratch,
        compiler_params=pltpu.CompilerParams(
            dimension_semantics=("arbitrary",), vmem_limit_bytes=VMEM_BYTES
        ),
        cost_estimate=pl.CostEstimate(flops=4 * flops, bytes_accessed=moved, transcendentals=0),
    )(*inputs)


def sampled(shape, dtype):
    result = shape_of(shape, dtype)
    return (result, per_sample(result))


def shared(shape, dtype):
    result = shape_of(shape, dtype)
    return (result, constant(result))


def edge_forward(order, first, second, table, edge_low, edge_state, at_both, at_nodes, params, node_total, last):
    samples, table_total, latent = table.shape
    edges = edge_low.shape[1]
    alike = edge_low.shape[0] == 1

    def kernel(order, w1, w2, table, low, state, both, nodes, params, pre, act, normed, inverse, *rest):
        if last:
            pooled, w1s, w2s, projected = rest
        else:
            new_state, new_low, pooled, w1s, w2s, projected = rest

        @pl.when(pl.program_id(0) == 0)
        def _():
            assemble(w1, order, w1.shape[1], 0, w1s)
            assemble(w2, order, w2.shape[1], 0, w2s)

        rows = table[0]
        projected[:table_total] = matmul(rows, w1s[latent : 2 * latent]).astype(BF16)
        projected[table_total:] = matmul(rows[:node_total], w1s[2 * latent :]).astype(BF16)
        hidden = matmul(low[0], w1s[:latent]) + matmul(both[...], projected[...]) + params[0:1]
        pre[0] = hidden.astype(BF16)
        active = (hidden * sigmoid(hidden)).astype(BF16)
        act[0] = active
        output = matmul_nt(active, w2s[...]) + params[1:2]
        scaled, scale = norm_forward(output)
        normed[0] = scaled.astype(BF16)
        inverse[0] = scale
        state_new = state[0].astype(F32) + scaled * params[2:3] + params[3:4]
        low_new = state_new.astype(BF16)
        if not last:
            new_state[0] = state_new
            new_low[0] = low_new
        pooled[0] = matmul(nodes[...], low_new).astype(BF16)

    wide = (samples, edges, latent)
    outputs = [sampled(wide, BF16), sampled(wide, BF16), sampled(wide, BF16), sampled((samples, edges, 1), F32)]
    if not last:
        outputs += [sampled(wide, F32), sampled(wide, BF16)]
    outputs += [sampled((samples, node_total, latent), BF16)]
    of_edges = constant if alike else per_sample
    return run_kernel(
        kernel,
        "edge_forward",
        samples,
        [order, first[0], second[0], table, edge_low, edge_state, at_both, at_nodes, params],
        [
            in_scalars(),
            weight_block(*first),
            weight_block(*second),
            per_sample(table),
            of_edges(edge_low),
            of_edges(edge_state),
            constant(at_both),
            constant(at_nodes),
            constant(params),
        ],
        outputs,
        [
            pltpu.VMEM((3 * latent, latent), BF16),
            pltpu.VMEM((latent, latent), BF16),
            pltpu.VMEM((at_both.shape[1], latent), BF16),
        ],
        2 * samples * edges * latent * (3 * latent + at_both.shape[1]),
    )


def edge_backward(order, first, second, pooled_grad, edge_grad, normed, inverse, pre, at_receiver, at_both_t, gain, last, node_total):
    samples, edges, latent = normed.shape
    at_total = at_both_t.shape[0]
    table_total = at_total - node_total

    def kernel(order, w1, w2, upstream, *rest):
        if not last:
            later, rest = rest[0], rest[1:]
        normed, inverse, pre, receiver, both_t, gain, low, hidden_low, at_rows, partial, returned, grad_out, minor = rest[:13]
        if last:
            w1s, w2s = rest[13:]
        else:
            hidden_sum, w1s, w2s, hidden_acc = rest[13:]
        step = pl.program_id(0)

        @pl.when(step == 0)
        def _():
            assemble(w1, order, w1.shape[1], 0, w1s)
            assemble(w2, order, w2.shape[1], 0, w2s)
            minor[...] = jnp.zeros_like(minor)

        grad = matmul(receiver[...], upstream[0])
        if not last:
            grad = grad + later[0]
        scaled = normed[0].astype(F32)
        output_grad = norm_backward(grad, scaled, inverse[0], gain[0:1]).astype(BF16)
        low[0] = output_grad
        act_grad = matmul(output_grad, w2s[...])
        pre_grad = (act_grad * silu_slope(pre[0].astype(F32))).astype(BF16)
        hidden_low[0] = pre_grad
        minor[0:1] += column_sum(pre_grad.astype(F32))
        minor[1:2] += column_sum(output_grad.astype(F32))
        minor[2:3] += column_sum(grad * scaled)
        minor[3:4] += column_sum(grad)
        at_rows[0] = matmul(both_t[...], pre_grad).astype(BF16)
        send = w1s[latent : 2 * latent]
        partial[0] = matmul_nt(at_rows[0, :node_total], send) + matmul_nt(
            at_rows[0, table_total:], w1s[2 * latent :]
        )
        returned[0] = matmul_nt(at_rows[0, node_total:table_total], send).astype(BF16)
        if last:
            grad_out[0] = grad + matmul_nt(pre_grad, w1s[:latent])
        else:

            @pl.when(step == 0)
            def _():
                grad_out[...] = grad
                hidden_acc[...] = pre_grad.astype(F32)

            @pl.when(step > 0)
            def _():
                grad_out[...] += grad
                hidden_acc[...] += pre_grad.astype(F32)

            @pl.when(step == samples - 1)
            def _():
                total = hidden_acc[...].astype(BF16)
                hidden_sum[...] = total
                grad_out[...] += matmul_nt(total, w1s[:latent])

    wide = (samples, edges, latent)
    outputs = [
        sampled(wide, BF16),
        sampled(wide, BF16),
        sampled((samples, at_total, latent), BF16),
        sampled((samples, node_total, latent), F32),
        sampled((samples, table_total - node_total, latent), BF16),
        sampled(wide, F32) if last else shared((edges, latent), F32),
        shared((4, latent), F32),
    ]
    scratch = [pltpu.VMEM((3 * latent, latent), BF16), pltpu.VMEM((latent, latent), BF16)]
    inputs = [order, first[0], second[0], pooled_grad]
    specs = [in_scalars(), weight_block(*first), weight_block(*second), per_sample(pooled_grad)]
    if not last:
        outputs.append(shared((edges, latent), BF16))
        scratch.append(pltpu.VMEM((edges, latent), F32))
        inputs.append(edge_grad)
        specs.append(per_sample(edge_grad))
    inputs += [normed, inverse, pre, at_receiver, at_both_t, gain]
    specs += [
        per_sample(normed),
        per_sample(inverse),
        per_sample(pre),
        constant(at_receiver),
        constant(at_both_t),
        constant(gain),
    ]
    return run_kernel(
        kernel,
        "edge_backward",
        samples,
        inputs,
        specs,
        outputs,
        scratch,
        2 * samples * edges * latent * (2 * latent + 2 * at_total),
    )


def edge_weight_grads(owners, edge_low, table, hidden_low, at_rows, low, act, node_total, nodes, width, packed_before):
    samples, table_total, latent = table.shape
    alike = edge_low.ndim == 2
    first_rows, second_rows = 3 * latent // nodes, latent // nodes
    offset = 0 if packed_before is None else packed_before[0].shape[1]
    blocks, hids = owners.shape[0] // 2, latent // width

    def kernel(owners, edge_low, table, hidden_low, at_rows, low, act, *rest):
        before, rest = rest[:-4], rest[-4:]
        kept, sent, first, second = rest
        step = pl.program_id(0)

        @pl.when(step == 0)
        def _():
            first[...] = jnp.zeros_like(first)
            second[...] = jnp.zeros_like(second)
            for source, target in zip(before, (kept, sent)):
                target[:, :offset, :] = source[...]
            if alike:
                add(first, 0, matmul_tn(edge_low[...], hidden_low[...]))

        if not alike:
            add(first, 0, matmul_tn(edge_low[0], hidden_low[0]))
        add(first, latent, matmul_tn(table[0], at_rows[0, :table_total]))
        add(first, 2 * latent, matmul_tn(table[0, :node_total], at_rows[0, table_total:]))
        add(second, 0, matmul_tn(low[0], act[0]))

        @pl.when(step == samples - 1)
        def _():
            pack(first, owners, first_rows, offset, kept, sent)
            pack(second, owners, second_rows, offset + first_rows, kept, sent)

    of_edges = constant if alike else per_sample
    inputs = [owners, edge_low, table, hidden_low, at_rows, low, act]
    specs = [in_scalars(), of_edges(edge_low), per_sample(table), of_edges(hidden_low), per_sample(at_rows), per_sample(low), per_sample(act)]
    if packed_before is not None:
        inputs += packed_before
        specs += [constant(a) for a in packed_before]
    return run_kernel(
        kernel,
        "edge_weight_grads",
        samples,
        inputs,
        specs,
        [shared((blocks // 2, offset + first_rows + second_rows, width), BF16)] * 2,
        [pltpu.VMEM((hids, 3 * latent, width), F32), pltpu.VMEM((hids, latent, width), F32)],
        4 * low.size * latent,
    )


def node_pass(order, owners, weights, nodes, node_low, state, pooled_pair, params, at_halo, target, scaling, mask):
    samples, node_total, latent = node_low.shape
    array, rows, place = weights
    second_rows, hids = latent // nodes, latent // array.shape[2]
    first_rows = rows - second_rows
    count = samples * node_total
    last = target is not None

    def kernel(order, *rest):
        if last:
            owners, rest = rest[0], rest[1:]
        w, node_low, state, pooled_own, pooled_other, params, *rest = rest
        if last:
            target, scaling, mask, new_low, upstream, input_grad, kept, sent, minor, w1s, w2s, first, second = rest
        else:
            at_halo, pooled_out, pre, act, normed, inverse, new_state, new_low, halo, w1s, w2s = rest
        assemble(w, order, first_rows, 0, w1s)
        assemble(w, order, second_rows, first_rows, w2s)
        rows_low = node_low[...].reshape(count, latent)
        pooled = (pooled_own[...].astype(F32) + pooled_other[...].astype(F32)).astype(BF16)
        pooled = pooled.reshape(count, latent)
        hidden = matmul(rows_low, w1s[:latent]) + matmul(pooled, w1s[latent:]) + params[4:5]
        active = (hidden * sigmoid(hidden)).astype(BF16)
        output = matmul_nt(active, w2s[...]) + params[5:6]
        scaled, scale = norm_forward(output)
        state_new = state[...].astype(F32).reshape(count, latent) + scaled * params[6:7] + params[7:8]
        low_new = state_new.astype(BF16).reshape(new_low.shape)
        new_low[...] = low_new
        if not last:
            pooled_out[...] = pooled
            pre[...] = hidden.astype(BF16)
            act[...] = active
            normed[...] = scaled.astype(BF16)
            inverse[...] = scale
            new_state[...] = state_new.reshape(new_state.shape)
            for s in range(samples):
                halo[s] = matmul(at_halo[...], new_low[s]).astype(BF16)
        else:
            grad = (target[...].astype(F32) * scaling[...]).reshape(count, latent)
            node_gradients(
                grad, scaled, scale, hidden, active, rows_low, pooled, params, mask,
                w1s, w2s, first, second, upstream, input_grad, kept, sent, minor, owners, first_rows, second_rows,
            )

    shape = node_low.shape
    inputs = [array, node_low, state, *pooled_pair, params]
    scratch = [pltpu.VMEM((2 * latent, latent), BF16), pltpu.VMEM((latent, latent), BF16)]
    if last:
        inputs += [target, scaling, mask]
        outputs = [shared(shape, BF16), *gradient_outputs(shape, order.shape[0], rows, array.shape[2])]
        scratch += [pltpu.VMEM((hids, 2 * latent, latent // hids), F32), pltpu.VMEM((hids, latent, latent // hids), F32)]
    else:
        inputs += [at_halo]
        outputs = [
            shared((count, latent), BF16),
            shared((count, latent), BF16),
            shared((count, latent), BF16),
            shared((count, latent), BF16),
            shared((count, 1), F32),
            shared(shape, F32),
            shared(shape, BF16),
            shared((samples, at_halo.shape[0], latent), BF16),
        ]
    tables = [order, owners] if last else [order]
    specs = [in_scalars() for _ in tables] + [weight_block(*weights)] + [constant(a) for a in inputs[1:]]
    inputs = tables + inputs
    return run_kernel(kernel, "node_pass", 1, inputs, specs, outputs, scratch, 6 * count * latent * latent * (3 if last else 1))


def gradient_outputs(shape, blocks, rows, width):
    return [
        shared(shape, BF16),
        shared(shape, F32),
        shared((blocks // 2, rows, width), BF16),
        shared((blocks // 2, rows, width), BF16),
        shared((4, shape[-1]), F32),
    ]


def node_gradients(
    grad, scaled, scale, hidden, active, rows_low, pooled, params, mask,
    w1s, w2s, first, second, upstream, input_grad, kept, sent, minor, owners, first_rows, second_rows,
):
    latent = w2s.shape[0]
    output_grad = norm_backward(grad, scaled, scale, params[6:7]).astype(BF16)
    pre_grad = (matmul(output_grad, w2s[...]) * silu_slope(hidden)).astype(BF16)
    upstream[...] = matmul_nt(pre_grad, w1s[latent:]).astype(BF16).reshape(upstream.shape)
    input_grad[...] = (grad + matmul_nt(pre_grad, w1s[:latent])).reshape(input_grad.shape)
    chosen = mask[...] > 0.5
    output_mine = jnp.where(chosen, output_grad.astype(F32), 0.0)
    pre_mine = jnp.where(chosen, pre_grad.astype(F32), 0.0)
    grad_mine = jnp.where(chosen, grad, 0.0)
    minor[0:1] = column_sum(pre_mine)
    minor[1:2] = column_sum(output_mine)
    minor[2:3] = column_sum(grad_mine * scaled)
    minor[3:4] = column_sum(grad_mine)
    pre_mine = pre_mine.astype(BF16)
    store(first, 0, matmul_tn(rows_low, pre_mine))
    store(first, latent, matmul_tn(pooled, pre_mine))
    store(second, 0, matmul_tn(output_mine.astype(BF16), active))
    pack(first, owners, first_rows, 0, kept, sent)
    pack(second, owners, second_rows, first_rows, kept, sent)


def node_backward(order, owners, weights, nodes, grads, node_low, pooled, pre, act, normed, inverse, params, mask):
    samples, node_total, latent = node_low.shape
    array, rows, place = weights
    second_rows, hids = latent // nodes, latent // array.shape[2]
    first_rows = rows - second_rows
    count = samples * node_total

    def kernel(order, owners, w, base, own, other, node_low, pooled, pre, act, normed, inverse, params, mask, upstream, input_grad, kept, sent, minor, w1s, w2s, first, second):
        assemble(w, order, first_rows, 0, w1s)
        assemble(w, order, second_rows, first_rows, w2s)
        grad = (base[...] + (own[...] + other[...].astype(F32))).reshape(count, latent)
        node_gradients(
            grad, normed[...].astype(F32), inverse[...], pre[...].astype(F32), act[...],
            node_low[...].reshape(count, latent), pooled[...], params, mask,
            w1s, w2s, first, second, upstream, input_grad, kept, sent, minor, owners, first_rows, second_rows,
        )

    inputs = [order, owners, array, *grads, node_low, pooled, pre, act, normed, inverse, params, mask]
    specs = [in_scalars(), in_scalars(), weight_block(*weights)] + [constant(a) for a in inputs[3:]]
    return run_kernel(
        kernel,
        "node_backward",
        1,
        inputs,
        specs,
        gradient_outputs(node_low.shape, order.shape[0], rows, array.shape[2]),
        [
            pltpu.VMEM((2 * latent, latent), BF16),
            pltpu.VMEM((latent, latent), BF16),
            pltpu.VMEM((hids, 2 * latent, latent // hids), F32),
            pltpu.VMEM((hids, latent, latent // hids), F32),
        ],
        12 * count * latent * latent,
    )


def dot(spec, left, right):
    return jnp.einsum(spec, left, right, preferred_element_type=F32)


def swap(values, axis, offset):
    return lax.ppermute(values, axis, [(i, i ^ offset) for i in range(lax.axis_size(axis))])


def bits_of(axis):
    return lax.axis_size(axis).bit_length() - 1


def own_bit(axis, bit):
    return (lax.axis_index(axis) >> bit) & 1


def all_bits():
    return [(axis, bit) for axis in ("node", "hid") for bit in reversed(range(bits_of(axis)))]


def ordered(own, mine, other):
    low = jnp.where(own == 0, mine, other)
    high = jnp.where(own == 0, other, mine)
    return low, high


def double_up(part, axis, bit, place):
    low, high = ordered(own_bit(axis, bit), part, swap(part, axis, 1 << bit))
    return jnp.stack([low, high], axis=place)


def halve_sum(parts, axis, bit, place):
    own = own_bit(axis, bit)
    sent = lax.dynamic_index_in_dim(parts, 1 - own, place, keepdims=False)
    kept = lax.dynamic_index_in_dim(parts, own, place, keepdims=False)
    return kept.astype(F32) + swap(sent.astype(BF16), axis, 1 << bit).astype(F32)


def places():
    node_ids = jnp.arange(lax.axis_size("node"), dtype=jnp.int32) ^ lax.axis_index("node")
    hid_ids = jnp.arange(lax.axis_size("hid"), dtype=jnp.int32) ^ lax.axis_index("hid")
    place = 0
    for step, (axis, bit) in enumerate(all_bits()):
        ids = node_ids[:, None] if axis == "node" else hid_ids[None, :]
        place = place + (((ids >> bit) & 1) << step)
    return place.reshape(-1)


def owners_of_places():
    place = jnp.arange(1 << len(all_bits()), dtype=jnp.int32)
    owner = {"node": lax.axis_index("node"), "hid": lax.axis_index("hid")}
    for step, (axis, bit) in enumerate(all_bits()):
        owner[axis] = owner[axis] ^ (((place >> step) & 1) << bit)
    return jnp.stack([owner["node"], owner["hid"]], axis=1).reshape(-1)


def after(value, *earlier):
    return lax.optimization_barrier((value, *earlier))[0]


def exchange(values, first_step, flips):
    hid_bits = bits_of("hid")
    mask = 0
    for k in range(flips.bit_length()):
        if (flips >> k) & 1:
            axis, bit = all_bits()[first_step + k]
            mask |= 1 << (bit if axis == "hid" else bit + hid_bits)
    total = 1 << len(all_bits())
    return lax.ppermute(values, ("node", "hid"), [(i, i ^ mask) for i in range(total)])


def rounds(begin, end):
    return [(step, min(step + 2, end)) for step in range(begin, end, 2)]


def gather_round(held, begin, end, *under):
    arrived = [exchange(held, begin, flips) for flips in range(1, 1 << (end - begin))]
    if under:
        arrived = lax.optimization_barrier((*arrived, *under))[: len(arrived)]
    return jnp.concatenate([held, *arrived], axis=0)


def split(total, count):
    size = total.shape[0] // count
    pieces = [total[i * size : (i + 1) * size] for i in range(count)]
    return [pieces[0]] + [piece.astype(BF16) for piece in pieces[1:]]


def scatter_round(pieces, begin, *under):
    arrived = [exchange(pieces[flips], begin, flips) for flips in range(1, len(pieces))]
    if under:
        arrived = lax.optimization_barrier((*arrived, *under))[: len(arrived)]
    total = pieces[0].astype(F32)
    for piece in arrived:
        total = total + piece.astype(F32)
    return total


def scatter_rest(total, end, *under):
    for begin, stop in reversed(rounds(0, end)):
        total = scatter_round(split(total, 1 << (stop - begin)), begin, *under)
    return total[0]


def sum_round(values, begin, end):
    terms = [values] + [exchange(values, begin, flips) for flips in range(1, 1 << (end - begin))]
    while len(terms) > 1:
        terms = [terms[i] + terms[i + 1] for i in range(0, len(terms), 2)]
    return terms[0]


def sum_everywhere(values):
    steps = len(all_bits())
    values = sum_round(values, steps - 1, steps)
    for begin, end in reversed(rounds(0, steps - 1)):
        values = sum_round(values, begin, end)
    return values


def neighbour_swaps(rows, halo_width):
    count = lax.axis_size("node")
    even = lax.axis_index("node") % 2 == 0
    to_previous, to_next = rows[:, :halo_width], rows[:, halo_width:]
    one = [(i, i ^ 1) for i in range(count)]
    two = [(i, (((i + 1) ^ 1) - 1) % count) for i in range(count)]
    first = lax.ppermute(jnp.where(even, to_next, to_previous), "node", one)
    second = lax.ppermute(jnp.where(even, to_previous, to_next), "node", two)
    return first, second


def from_neighbours(first, second):
    even = lax.axis_index("node") % 2 == 0
    return jnp.concatenate(
        [jnp.where(even, second, first), jnp.where(even, first, second)], axis=1
    )


def adam_terms(weight, grad, first, second, decay):
    first_new = BETA_FIRST * first + (1.0 - BETA_FIRST) * grad
    second_new = BETA_SECOND * second + (1.0 - BETA_SECOND) * grad * grad
    update = first_new / (jnp.sqrt(second_new) + ADAM_EPS) + decay * weight
    return (first_new, second_new, update)


def pack_shards(first, second):
    return jnp.concatenate([first, second.T], axis=0).astype(BF16)


def adam_terms(weight, grad, first, second, decay):
    first_new = BETA_FIRST * first + (1.0 - BETA_FIRST) * grad
    second_new = BETA_SECOND * second + (1.0 - BETA_SECOND) * grad * grad
    update = first_new / (jnp.sqrt(second_new) + ADAM_EPS) + decay * weight
    return (first_new, second_new, update)


def per_device(
    node_in,
    edge_in,
    cotangent,
    ocean_mask,
    present_mask,
    valid_counts,
    send_slot,
    recv_local,
    halo_lists,
    edge_first,
    edge_second,
    node_first,
    node_second,
    edge_first_m,
    edge_second_m,
    node_first_m,
    node_second_m,
    edge_first_v,
    edge_second_v,
    node_first_v,
    node_second_v,
    small_params,
    small_m,
    small_v,
    learn_rate,
):
    hid_count = lax.axis_size("hid")
    hid_index = lax.axis_index("hid")
    node_total, sample_count, latent = node_in.shape
    edge_part = edge_in.shape[0] // hid_count
    node_part = node_total // hid_count
    halo_width = halo_lists.shape[1]
    table_total = node_total + 2 * halo_width
    sample_half, edge_half = hid_index >> 1, hid_index & 1
    samples = sample_count // 2
    nodes, hids = lax.axis_size("node"), hid_count
    first_rows = edge_first.shape[1]
    second_rows = edge_second.shape[2]
    node_rows = node_first.shape[1] + second_rows
    width = edge_first.shape[2]

    order, owners = places(), owners_of_places()
    steps = len(all_bits())

    def layer_shards(depth, *earlier):
        shards = (node_first[depth], node_second[depth], edge_first[depth], edge_second[depth])
        if earlier:
            shards = after(shards, *earlier)
        return jnp.concatenate([pack_shards(*shards[:2]), pack_shards(*shards[2:])], axis=0)[None]

    def parted(held):
        return held[:, :node_rows], held[:, node_rows:]

    layer_zero = layer_shards(0)
    for begin, end in rounds(0, steps - 3):
        layer_zero = gather_round(layer_zero, begin, end)
    setup = layer_zero
    layer_zero = gather_round(layer_zero, steps - 3, steps - 2)
    node_zero, edge_zero = parted(layer_zero)
    layer_one = layer_shards(1, setup)
    layer_one = after(layer_one, edge_zero)
    z_rounds = rounds(0, steps - 3)
    for begin, end in z_rounds[:-1]:
        layer_one = gather_round(layer_one, begin, end)
    halo_gate = edge_zero
    masters = (edge_first, edge_second, node_first, node_second)
    weight_local = jnp.stack(
        [jnp.sum(matrix * matrix, axis=(1, 2)) for matrix in after(masters, setup)], axis=1
    )
    def edge_blocks(whole):
        return ((whole, first_rows, 0), (whole, second_rows, first_rows // second_rows))

    def own_edges(values):
        return lax.dynamic_index_in_dim(
            values.reshape(2, 2, edge_part, *values.shape[1:]), edge_half, 1, keepdims=False
        ).reshape(2 * edge_part, *values.shape[1:])

    def own_nodes(values):
        return lax.dynamic_index_in_dim(
            values.reshape(samples, 2, 2, node_part, latent), edge_half, 2, keepdims=False
        ).reshape(samples, 2 * node_part, latent)

    def own_samples(values):
        return lax.dynamic_slice_in_dim(values, sample_half * samples, samples, 1)

    def own_rows_exchanged(values):
        quarters = jnp.moveaxis(values.reshape(samples, 2, 2, node_part, latent), 0, 3)
        quarters = lax.dynamic_index_in_dim(quarters, edge_half, 1, keepdims=False)
        sent = lax.dynamic_index_in_dim(quarters, 1 - sample_half, 0, keepdims=False)
        kept = lax.dynamic_index_in_dim(quarters, sample_half, 0, keepdims=False)
        return kept, swap(sent, "hid", 2)

    def all_samples(kept, arrived):
        return jnp.concatenate(ordered(sample_half, kept, arrived), axis=1)

    send_slot, recv_local, halo_lists, node_in, edge_in = lax.optimization_barrier(
        (send_slot, recv_local, halo_lists, node_in, edge_in, setup)
    )[:5]
    sender = own_edges(send_slot)
    receiver = own_edges(recv_local)
    node_ids, table_ids = jnp.arange(node_total), jnp.arange(table_total)
    at_receiver = (receiver[:, None] == node_ids[None, :]).astype(BF16)
    at_both = jnp.concatenate(
        [(sender[:, None] == table_ids[None, :]).astype(BF16), at_receiver], axis=1
    )
    at_nodes = (node_ids[:, None] == receiver[None, :]).astype(BF16)
    at_both_t = jnp.concatenate(
        [(table_ids[:, None] == sender[None, :]).astype(BF16), at_nodes], axis=0
    )
    at_halo = (halo_lists.reshape(-1)[:, None] == node_ids[None, :]).astype(BF16)
    mask = ((node_ids // node_part) % 2 == edge_half).astype(F32)
    mask = jnp.tile(mask, samples)[:, None]

    node_low = jnp.transpose(own_samples(node_in), (1, 0, 2))
    edge_in_own = own_edges(edge_in)
    halo_rows = dot("hn,snl->shl", at_halo, node_low).astype(BF16)
    node_low_zero = node_low
    halo_rows = neighbour_swaps(after(halo_rows, halo_gate), halo_width)
    begin, end = z_rounds[-1]
    arrived = [exchange(layer_one, begin, flips) for flips in range(1, 1 << (end - begin))]
    edge_arrived, first, second, weight_local, *arrived = lax.optimization_barrier(
        (exchange(edge_zero, steps - 2, 1), *halo_rows, weight_local, *arrived)
    )
    halo_rows = from_neighbours(first, second)
    edge_zero = jnp.concatenate([edge_zero, edge_arrived], axis=0)
    layer_one = jnp.concatenate([layer_one, *arrived], axis=0)
    node_zero = after(node_zero, edge_zero)
    edge_zero = gather_round(edge_zero, steps - 1, steps)
    table_zero = jnp.concatenate([node_low, halo_rows], axis=1)
    pre_zero, act_zero, normed_zero, inverse_zero, edge_state, edge_low, pooled = edge_forward(
        order,
        *edge_blocks(edge_zero),
        table_zero,
        edge_in_own[None],
        edge_in_own[None],
        at_both,
        at_nodes,
        small_params[0],
        node_total,
        False,
    )
    valid_mask = (ocean_mask[:, None] * present_mask).astype(BF16)
    masked = after(cotangent, halo_gate) * valid_mask[:, :, None]
    sent = lax.dynamic_slice_in_dim(masked, (1 - sample_half) * samples, samples, 1)
    scaling = node_total * lax.axis_size("node") / valid_counts.astype(F32)
    scaling = lax.dynamic_slice_in_dim(scaling, sample_half * samples, samples, 0)
    scaling = scaling[:, None, None]
    pooled, cotangent_other, *arrived = lax.optimization_barrier(
        (
            pooled,
            swap(sent, "hid", 2),
            exchange(node_zero, steps - 2, 1),
            exchange(layer_one, steps - 3, 1),
        )
    )
    masked = jnp.stack(ordered(sample_half, own_samples(masked), cotangent_other), axis=0)
    node_zero = jnp.concatenate([node_zero, arrived[0]], axis=0)
    node_zero = gather_round(node_zero, steps - 1, steps)
    layer_one = jnp.concatenate([layer_one, arrived[1]], axis=0)
    node_one, edge_one = parted(layer_one)
    other = after(swap(pooled, "hid", 1), edge_one)
    (
        pooled_zero,
        node_pre,
        node_act,
        node_normed,
        node_inverse,
        node_state,
        node_low,
        halo_rows,
    ) = node_pass(
        order,
        None,
        (node_zero, node_rows, 0),
        nodes,
        node_low_zero,
        node_low_zero,
        (pooled, other),
        small_params[0],
        at_halo,
        None,
        None,
        None,
    )
    arrived, cotangent_other, *halo_rows = lax.optimization_barrier(
        (
            exchange(edge_one, steps - 2, 1),
            swap(masked, "hid", 1),
            *neighbour_swaps(halo_rows, halo_width),
        )
    )
    halo_rows = from_neighbours(*halo_rows)
    masked = jnp.stack(ordered(edge_half, masked, cotangent_other), axis=1)
    target = jnp.transpose(masked.reshape(node_total, samples, latent), (1, 0, 2))
    edge_one = jnp.concatenate([edge_one, arrived], axis=0)
    node_one = after(node_one, edge_one)
    edge_one = gather_round(edge_one, steps - 1, steps)

    node_low_one = node_low
    table_one = jnp.concatenate([node_low, halo_rows], axis=1)
    pre_one, act_one, normed_one, inverse_one, pooled = edge_forward(
        order,
        *edge_blocks(edge_one),
        table_one,
        edge_low,
        edge_state,
        at_both,
        at_nodes,
        small_params[1],
        node_total,
        True,
    )
    node_one = gather_round(node_one, steps - 2, steps - 1, pooled)
    node_one = gather_round(node_one, steps - 1, steps)
    node_low, pooled_grad, node_grad, kept, sent, node_minor_one = node_pass(
        order,
        owners,
        (node_one, node_rows, 0),
        nodes,
        node_low_one,
        node_state,
        (pooled, swap(pooled, "hid", 1)),
        small_params[1],
        None,
        target,
        scaling,
        mask,
    )

    def from_edges(partial, returned):
        return partial + dot("hn,shl->snl", at_halo, returned)

    low, hidden_low, at_rows, partial, returned, edge_grad, edge_minor_one = edge_backward(
        order,
        *edge_blocks(edge_one),
        pooled_grad,
        None,
        normed_one,
        inverse_one,
        pre_one,
        at_receiver,
        at_both_t,
        small_params[1, 2:3],
        True,
        node_total,
    )
    low, *node_out = lax.optimization_barrier((low, *own_rows_exchanged(node_low)))
    node_out = all_samples(*node_out)
    chain_one = edge_weight_grads(
        owners,
        edge_low,
        table_one,
        hidden_low,
        at_rows,
        low,
        act_one,
        node_total,
        nodes,
        width,
        [kept, sent],
    )
    *returned, kept, sent = lax.optimization_barrier(
        (*neighbour_swaps(returned, halo_width), *chain_one)
    )
    returned, chain_one = from_neighbours(*returned), (kept, sent)
    partial = from_edges(partial, returned)
    chain_one = split(scatter_round(chain_one, steps - 1), 2)
    other, *chain_one = lax.optimization_barrier((swap(partial.astype(BF16), "hid", 1), *chain_one))
    pooled_grad, node_grad, kept, sent, node_minor_zero = node_backward(
        order,
        owners,
        (node_zero, node_rows, 0),
        nodes,
        (node_grad, partial, other),
        node_low_zero,
        pooled_zero,
        node_pre,
        node_act,
        node_normed,
        node_inverse,
        small_params[0],
        mask,
    )
    low, hidden_low, at_rows, partial, returned, edge_input_grad, edge_minor_zero, hidden_sum = (
        edge_backward(
            order,
            *edge_blocks(edge_zero),
            pooled_grad,
            edge_grad,
            normed_zero,
            inverse_zero,
            pre_zero,
            at_receiver,
            at_both_t,
            small_params[0, 2:3],
            False,
            node_total,
        )
    )
    chain_one = split(scatter_round(chain_one, steps - 2, low), 2)
    chain_zero = split(scatter_round((kept, sent), steps - 1, low), 2)
    low = after(low, *chain_one, *chain_zero)
    chain_edge = edge_weight_grads(
        owners,
        edge_in_own,
        table_zero,
        hidden_sum,
        at_rows,
        low,
        act_zero,
        node_total,
        nodes,
        width,
        None,
    )
    kept, sent, one_arrived, zero_arrived = lax.optimization_barrier(
        (
            *chain_edge,
            exchange(chain_one[1], steps - 3, 1),
            exchange(chain_zero[1], steps - 2, 1),
        )
    )
    chain_one = chain_one[0].astype(F32) + one_arrived.astype(F32)
    chain_zero = split(chain_zero[0].astype(F32) + zero_arrived.astype(F32), 2)
    edge_arrived, zero_arrived = lax.optimization_barrier(
        (exchange(sent, steps - 1, 1), exchange(chain_zero[1], steps - 3, 1))
    )
    chain_edge = split(kept.astype(F32) + edge_arrived.astype(F32), 2)
    chain_one = jnp.concatenate(
        [chain_one, chain_zero[0].astype(F32) + zero_arrived.astype(F32)], axis=1
    )
    for begin, end in reversed(z_rounds[1:]):
        chain_one = scatter_round(split(chain_one, 1 << (end - begin)), begin)
    begin, end = z_rounds[0]
    chain_one = split(chain_one, 1 << (end - begin))
    arrived, edge_input_grad, *others = lax.optimization_barrier(
        (
            exchange(chain_edge[1], steps - 2, 1),
            edge_input_grad,
            *[exchange(chain_one[flips], begin, flips) for flips in range(1, len(chain_one))],
        )
    )
    joined_grads = chain_one[0]
    for piece in others:
        joined_grads = joined_grads + piece.astype(F32)
    joined_grads = joined_grads[0]
    chain_edge = split(chain_edge[0] + arrived.astype(F32), 2)
    arrived, returned = lax.optimization_barrier((exchange(chain_edge[1], steps - 3, 1), returned))
    chain_edge = chain_edge[0] + arrived.astype(F32)
    halves = edge_input_grad.reshape(2, edge_part, latent)
    sent = lax.dynamic_index_in_dim(halves, 1 - sample_half, 0, keepdims=False).astype(BF16)
    kept = lax.dynamic_index_in_dim(halves, sample_half, 0, keepdims=False)
    returned = neighbour_swaps(returned, halo_width)
    edge_zero_grads = scatter_rest(chain_edge, steps - 3)
    edge_zero_grads, arrived, *returned = lax.optimization_barrier(
        (edge_zero_grads, swap(sent, "hid", 2), *returned)
    )
    edge_input_grad = kept + arrived.astype(F32)
    partial = from_edges(partial, from_neighbours(*returned))

    edge_rows = first_rows + second_rows
    layer_one_grads = joined_grads[: node_rows + edge_rows]
    node_zero_grads = joined_grads[node_rows + edge_rows :]
    node_one_grads, edge_one_grads = layer_one_grads[:node_rows], layer_one_grads[node_rows:]
    node_first_rows = node_rows - second_rows
    grads = [
        jnp.stack([edge_zero_grads[:first_rows], edge_one_grads[:first_rows]]),
        jnp.stack([edge_zero_grads[first_rows:].T, edge_one_grads[first_rows:].T]),
        jnp.stack([node_zero_grads[:node_first_rows], node_one_grads[:node_first_rows]]),
        jnp.stack([node_zero_grads[node_first_rows:].T, node_one_grads[node_first_rows:].T]),
    ]
    firsts = (edge_first_m, edge_second_m, node_first_m, node_second_m)
    seconds = (edge_first_v, edge_second_v, node_first_v, node_second_v)
    moment_list = [
        adam_terms(masters[place], grads[place], firsts[place], seconds[place], WEIGHT_DECAY)
        for place in range(4)
    ]
    update_local = jnp.stack(
        [jnp.sum(entry[2] * entry[2], axis=(1, 2)) for entry in moment_list], axis=1
    )
    squares = jnp.concatenate([weight_local.reshape(1, -1), update_local.reshape(1, -1)], axis=1)
    minor_packed = jnp.concatenate(
        [edge_minor_zero, node_minor_zero, edge_minor_one, node_minor_one]
        + [jnp.pad(squares, ((0, 0), (0, latent - squares.size)))],
        axis=0,
    )
    minor_packed = sum_round(minor_packed, steps - 1, steps)
    minor_packed, other = lax.optimization_barrier(
        (minor_packed, swap(partial.astype(BF16), "hid", 1))
    )
    node_grad = node_grad + (partial + other.astype(F32))
    grad_node = own_rows_exchanged(node_grad.astype(BF16))
    last_rounds = list(reversed(rounds(0, steps - 1)))
    for begin, end in last_rounds[:-1]:
        minor_packed = sum_round(minor_packed, begin, end)
    minor_packed, *grad_node = lax.optimization_barrier((minor_packed, *grad_node))
    grad_node = all_samples(*grad_node)
    minor_packed = sum_round(minor_packed, *last_rounds[-1])
    minor_total = minor_packed[: 8 * LAYERS].reshape(small_params.shape)
    squares = minor_packed[8 * LAYERS, : squares.size].reshape(2, *weight_local.shape)
    weight_squares, update_squares = squares[0], squares[1]
    weight_norm = jnp.sqrt(weight_squares)
    update_norm = jnp.sqrt(update_squares)
    new_weights = []
    for position in range(4):
        ratio = weight_norm[:, position] / update_norm[:, position]
        new_weights.append(
            masters[position] - learn_rate[0] * ratio[:, None, None] * moment_list[position][2]
        )
    small_first, small_second, small_update = adam_terms(
        small_params, minor_total, small_m, small_v, 0.0
    )
    small_wnorm = jnp.sqrt(jnp.sum(small_params * small_params, axis=2))
    small_unorm = jnp.sqrt(jnp.sum(small_update * small_update, axis=2))
    small_new = (
        small_params - learn_rate[0] * (small_wnorm / small_unorm)[:, :, None] * small_update
    )
    norms = jnp.stack(
        [
            jnp.concatenate([weight_norm, small_wnorm], axis=1),
            jnp.concatenate([update_norm, small_unorm], axis=1),
        ],
        axis=2,
    )
    return (
        node_out,
        grad_node,
        edge_input_grad.astype(BF16),
        *new_weights,
        *[entry[0] for entry in moment_list],
        *[entry[1] for entry in moment_list],
        *[weight.astype(BF16) for weight in new_weights],
        small_new,
        small_first,
        small_second,
        norms,
    )


def solution(mesh):
    whole = P()
    rows = P(None, "node", "hid")
    columns = P(None, "hid", "node")
    matrices = (rows, columns, rows, columns)
    in_specs = (
        P("node", None, None),
        P("node", None),
        P(("node", "hid"), None, None),
        P(("node", "hid")),
        P(("node", "hid"), None),
        P(),
        P("node"),
        P("node"),
        P("node", None),
        *matrices,
        *matrices,
        *matrices,
        whole,
        whole,
        whole,
        whole,
    )
    out_specs = (
        P(("node", "hid"), None, None),
        P(("node", "hid"), None, None),
        P(("node", "hid"), None),
        *matrices,
        *matrices,
        *matrices,
        *matrices,
        whole,
        whole,
        whole,
        whole,
    )
    return jax.shard_map(
        per_device, mesh=mesh, in_specs=in_specs, out_specs=out_specs, check_vma=False
    )
```

```python
import jax
import jax.numpy as jnp
from jax import lax
from jax.experimental import pallas as pl
from jax.experimental.pallas import tpu as pltpu
from jax.sharding import PartitionSpec as P

LAYERS = 2


NORM_EPS = 1e-05
BETA_FIRST = 0.5
BETA_SECOND = 0.5
ADAM_EPS = 1e-06
WEIGHT_DECAY = 0.01
BF16 = jnp.bfloat16
F32 = jnp.float32
VMEM_BYTES = 56 * 1024 * 1024


def matmul(left, right):
    return lax.dot_general(left, right, (((1,), (0,)), ((), ())), preferred_element_type=F32)


def matmul_nt(left, right):
    return lax.dot_general(left, right, (((1,), (1,)), ((), ())), preferred_element_type=F32)


def matmul_tn(left, right):
    return lax.dot_general(left, right, (((0,), (0,)), ((), ())), preferred_element_type=F32)


def sigmoid(values):
    return 0.5 + 0.5 * jnp.tanh(0.5 * values)


def silu_slope(values):
    gate = sigmoid(values)
    return gate * (1.0 + values * (1.0 - gate))


def norm_forward(values):
    center = values - jnp.mean(values, axis=-1, keepdims=True)
    spread = jnp.mean(center * center, axis=-1, keepdims=True)
    inverse = lax.rsqrt(spread + NORM_EPS)
    return center * inverse, inverse


def norm_backward(upstream, normed, inverse, gain_row):
    scaled = upstream * gain_row
    return inverse * (
        scaled
        - jnp.mean(scaled, axis=-1, keepdims=True)
        - normed * jnp.mean(scaled * normed, axis=-1, keepdims=True)
    )


def column_sum(values):
    return jnp.sum(values, axis=0, keepdims=True)


def assemble(source, order, rows, offset, target):
    width = source.shape[2]
    nodes, hids = target.shape[0] // rows, target.shape[1] // width
    for i in range(nodes):
        for j in range(hids):
            target[i * rows : (i + 1) * rows, j * width : (j + 1) * width] = source[
                order[i * hids + j], offset : offset + rows, :
            ]


def store(target, begin, values):
    rows, width = values.shape[0], target.shape[2]
    for j in range(target.shape[0]):
        target[j, begin : begin + rows] = values[:, j * width : (j + 1) * width]


def add(target, begin, values):
    rows, width = values.shape[0], target.shape[2]
    for j in range(target.shape[0]):
        target[j, begin : begin + rows] += values[:, j * width : (j + 1) * width]


def pack(values, owners, rows, offset, kept, sent):
    half = kept.shape[0]

    def one(index, carry):
        for target, place in ((kept, index), (sent, index + half)):
            begin = pl.multiple_of(owners[2 * place] * rows, rows)
            target[index, offset : offset + rows, :] = values[
                owners[2 * place + 1], pl.ds(begin, rows), :
            ].astype(BF16)
        return carry

    lax.fori_loop(0, half, one, 0)


def per_sample(array):
    block = (1,) + array.shape[1:]
    return pl.BlockSpec(block, lambda s: (s,) + (0,) * (len(block) - 1))


def constant(array):
    return pl.BlockSpec(array.shape, lambda s: (0,) * len(array.shape))


def weight_block(array, rows, place):
    blocks, _, width = array.shape
    return pl.BlockSpec((blocks, rows, width), lambda s: (0, place, 0))


def in_scalars():
    return pl.BlockSpec(memory_space=pltpu.SMEM)


def shape_of(shape, dtype):
    return jax.ShapeDtypeStruct(shape, dtype)


def run_kernel(kernel, name, samples, inputs, in_specs, outputs, scratch, flops):
    moved = sum(a.size * a.dtype.itemsize for a in inputs) + sum(
        shape.size * shape.dtype.itemsize for shape, _ in outputs
    )
    return pl.pallas_call(
        kernel,
        name=name,
        grid=(samples,),
        in_specs=in_specs,
        out_specs=[spec for _, spec in outputs],
        out_shape=[shape for shape, _ in outputs],
        scratch_shapes=scratch,
        compiler_params=pltpu.CompilerParams(
            dimension_semantics=("arbitrary",), vmem_limit_bytes=VMEM_BYTES
        ),
        cost_estimate=pl.CostEstimate(flops=4 * flops, bytes_accessed=moved, transcendentals=0),
    )(*inputs)


def sampled(shape, dtype):
    result = shape_of(shape, dtype)
    return (result, per_sample(result))


def shared(shape, dtype):
    result = shape_of(shape, dtype)
    return (result, constant(result))


def edge_forward(order, first, second, table, edge_low, edge_state, at_both, at_nodes, params, node_total, last):
    samples, table_total, latent = table.shape
    edges = edge_low.shape[1]
    alike = edge_low.shape[0] == 1

    def kernel(order, w1, w2, table, low, state, both, nodes, params, pre, act, normed, inverse, *rest):
        if last:
            pooled, w1s, w2s, projected = rest
        else:
            new_state, new_low, pooled, w1s, w2s, projected = rest

        @pl.when(pl.program_id(0) == 0)
        def _():
            assemble(w1, order, w1.shape[1], 0, w1s)
            assemble(w2, order, w2.shape[1], 0, w2s)

        rows = table[0]
        projected[:table_total] = matmul(rows, w1s[latent : 2 * latent]).astype(BF16)
        projected[table_total:] = matmul(rows[:node_total], w1s[2 * latent :]).astype(BF16)
        hidden = matmul(low[0], w1s[:latent]) + matmul(both[...], projected[...]) + params[0:1]
        pre[0] = hidden.astype(BF16)
        active = (hidden * sigmoid(hidden)).astype(BF16)
        act[0] = active
        output = matmul_nt(active, w2s[...]) + params[1:2]
        scaled, scale = norm_forward(output)
        normed[0] = scaled.astype(BF16)
        inverse[0] = scale
        state_new = state[0].astype(F32) + scaled * params[2:3] + params[3:4]
        low_new = state_new.astype(BF16)
        if not last:
            new_state[0] = state_new
            new_low[0] = low_new
        pooled[0] = matmul(nodes[...], low_new).astype(BF16)

    wide = (samples, edges, latent)
    outputs = [sampled(wide, BF16), sampled(wide, BF16), sampled(wide, BF16), sampled((samples, edges, 1), F32)]
    if not last:
        outputs += [sampled(wide, F32), sampled(wide, BF16)]
    outputs += [sampled((samples, node_total, latent), BF16)]
    of_edges = constant if alike else per_sample
    return run_kernel(
        kernel,
        "edge_forward",
        samples,
        [order, first[0], second[0], table, edge_low, edge_state, at_both, at_nodes, params],
        [
            in_scalars(),
            weight_block(*first),
            weight_block(*second),
            per_sample(table),
            of_edges(edge_low),
            of_edges(edge_state),
            constant(at_both),
            constant(at_nodes),
            constant(params),
        ],
        outputs,
        [
            pltpu.VMEM((3 * latent, latent), BF16),
            pltpu.VMEM((latent, latent), BF16),
            pltpu.VMEM((at_both.shape[1], latent), BF16),
        ],
        2 * samples * edges * latent * (3 * latent + at_both.shape[1]),
    )


def edge_backward(order, first, second, pooled_grad, edge_grad, normed, inverse, pre, at_receiver, at_both_t, gain, last, node_total):
    samples, edges, latent = normed.shape
    at_total = at_both_t.shape[0]
    table_total = at_total - node_total

    def kernel(order, w1, w2, upstream, *rest):
        if not last:
            later, rest = rest[0], rest[1:]
        normed, inverse, pre, receiver, both_t, gain, low, hidden_low, at_rows, partial, returned, grad_out, minor = rest[:13]
        if last:
            w1s, w2s = rest[13:]
        else:
            hidden_sum, w1s, w2s, hidden_acc = rest[13:]
        step = pl.program_id(0)

        @pl.when(step == 0)
        def _():
            assemble(w1, order, w1.shape[1], 0, w1s)
            assemble(w2, order, w2.shape[1], 0, w2s)
            minor[...] = jnp.zeros_like(minor)

        grad = matmul(receiver[...], upstream[0])
        if not last:
            grad = grad + later[0]
        scaled = normed[0].astype(F32)
        output_grad = norm_backward(grad, scaled, inverse[0], gain[0:1]).astype(BF16)
        low[0] = output_grad
        act_grad = matmul(output_grad, w2s[...])
        pre_grad = (act_grad * silu_slope(pre[0].astype(F32))).astype(BF16)
        hidden_low[0] = pre_grad
        minor[0:1] += column_sum(pre_grad.astype(F32))
        minor[1:2] += column_sum(output_grad.astype(F32))
        minor[2:3] += column_sum(grad * scaled)
        minor[3:4] += column_sum(grad)
        at_rows[0] = matmul(both_t[...], pre_grad).astype(BF16)
        send = w1s[latent : 2 * latent]
        partial[0] = matmul_nt(at_rows[0, :node_total], send) + matmul_nt(
            at_rows[0, table_total:], w1s[2 * latent :]
        )
        returned[0] = matmul_nt(at_rows[0, node_total:table_total], send).astype(BF16)
        if last:
            grad_out[0] = grad + matmul_nt(pre_grad, w1s[:latent])
        else:

            @pl.when(step == 0)
            def _():
                grad_out[...] = grad
                hidden_acc[...] = pre_grad.astype(F32)

            @pl.when(step > 0)
            def _():
                grad_out[...] += grad
                hidden_acc[...] += pre_grad.astype(F32)

            @pl.when(step == samples - 1)
            def _():
                total = hidden_acc[...].astype(BF16)
                hidden_sum[...] = total
                grad_out[...] += matmul_nt(total, w1s[:latent])

    wide = (samples, edges, latent)
    outputs = [
        sampled(wide, BF16),
        sampled(wide, BF16),
        sampled((samples, at_total, latent), BF16),
        sampled((samples, node_total, latent), F32),
        sampled((samples, table_total - node_total, latent), BF16),
        sampled(wide, F32) if last else shared((edges, latent), F32),
        shared((4, latent), F32),
    ]
    scratch = [pltpu.VMEM((3 * latent, latent), BF16), pltpu.VMEM((latent, latent), BF16)]
    inputs = [order, first[0], second[0], pooled_grad]
    specs = [in_scalars(), weight_block(*first), weight_block(*second), per_sample(pooled_grad)]
    if not last:
        outputs.append(shared((edges, latent), BF16))
        scratch.append(pltpu.VMEM((edges, latent), F32))
        inputs.append(edge_grad)
        specs.append(per_sample(edge_grad))
    inputs += [normed, inverse, pre, at_receiver, at_both_t, gain]
    specs += [
        per_sample(normed),
        per_sample(inverse),
        per_sample(pre),
        constant(at_receiver),
        constant(at_both_t),
        constant(gain),
    ]
    return run_kernel(
        kernel,
        "edge_backward",
        samples,
        inputs,
        specs,
        outputs,
        scratch,
        2 * samples * edges * latent * (2 * latent + 2 * at_total),
    )


def edge_weight_grads(owners, edge_low, table, hidden_low, at_rows, low, act, node_total, nodes, width, packed_before):
    samples, table_total, latent = table.shape
    alike = edge_low.ndim == 2
    first_rows, second_rows = 3 * latent // nodes, latent // nodes
    offset = 0 if packed_before is None else packed_before[0].shape[1]
    blocks, hids = owners.shape[0] // 2, latent // width

    def kernel(owners, edge_low, table, hidden_low, at_rows, low, act, *rest):
        before, rest = rest[:-4], rest[-4:]
        kept, sent, first, second = rest
        step = pl.program_id(0)

        @pl.when(step == 0)
        def _():
            first[...] = jnp.zeros_like(first)
            second[...] = jnp.zeros_like(second)
            for source, target in zip(before, (kept, sent)):
                target[:, :offset, :] = source[...]
            if alike:
                add(first, 0, matmul_tn(edge_low[...], hidden_low[...]))

        if not alike:
            add(first, 0, matmul_tn(edge_low[0], hidden_low[0]))
        add(first, latent, matmul_tn(table[0], at_rows[0, :table_total]))
        add(first, 2 * latent, matmul_tn(table[0, :node_total], at_rows[0, table_total:]))
        add(second, 0, matmul_tn(low[0], act[0]))

        @pl.when(step == samples - 1)
        def _():
            pack(first, owners, first_rows, offset, kept, sent)
            pack(second, owners, second_rows, offset + first_rows, kept, sent)

    of_edges = constant if alike else per_sample
    inputs = [owners, edge_low, table, hidden_low, at_rows, low, act]
    specs = [in_scalars(), of_edges(edge_low), per_sample(table), of_edges(hidden_low), per_sample(at_rows), per_sample(low), per_sample(act)]
    if packed_before is not None:
        inputs += packed_before
        specs += [constant(a) for a in packed_before]
    return run_kernel(
        kernel,
        "edge_weight_grads",
        samples,
        inputs,
        specs,
        [shared((blocks // 2, offset + first_rows + second_rows, width), BF16)] * 2,
        [pltpu.VMEM((hids, 3 * latent, width), F32), pltpu.VMEM((hids, latent, width), F32)],
        4 * low.size * latent,
    )


def node_pass(order, owners, weights, nodes, node_low, state, pooled_pair, params, at_halo, target, scaling, mask):
    samples, node_total, latent = node_low.shape
    array, rows, place = weights
    second_rows, hids = latent // nodes, latent // array.shape[2]
    first_rows = rows - second_rows
    count = samples * node_total
    last = target is not None

    def kernel(order, *rest):
        if last:
            owners, rest = rest[0], rest[1:]
        w, node_low, state, pooled_own, pooled_other, params, *rest = rest
        if last:
            target, scaling, mask, new_low, upstream, input_grad, kept, sent, minor, w1s, w2s, first, second = rest
        else:
            at_halo, pooled_out, pre, act, normed, inverse, new_state, new_low, halo, w1s, w2s = rest
        assemble(w, order, first_rows, 0, w1s)
        assemble(w, order, second_rows, first_rows, w2s)
        rows_low = node_low[...].reshape(count, latent)
        pooled = (pooled_own[...].astype(F32) + pooled_other[...].astype(F32)).astype(BF16)
        pooled = pooled.reshape(count, latent)
        hidden = matmul(rows_low, w1s[:latent]) + matmul(pooled, w1s[latent:]) + params[4:5]
        active = (hidden * sigmoid(hidden)).astype(BF16)
        output = matmul_nt(active, w2s[...]) + params[5:6]
        scaled, scale = norm_forward(output)
        state_new = state[...].astype(F32).reshape(count, latent) + scaled * params[6:7] + params[7:8]
        low_new = state_new.astype(BF16).reshape(new_low.shape)
        new_low[...] = low_new
        if not last:
            pooled_out[...] = pooled
            pre[...] = hidden.astype(BF16)
            act[...] = active
            normed[...] = scaled.astype(BF16)
            inverse[...] = scale
            new_state[...] = state_new.reshape(new_state.shape)
            for s in range(samples):
                halo[s] = matmul(at_halo[...], new_low[s]).astype(BF16)
        else:
            grad = (target[...].astype(F32) * scaling[...]).reshape(count, latent)
            node_gradients(
                grad, scaled, scale, hidden, active, rows_low, pooled, params, mask,
                w1s, w2s, first, second, upstream, input_grad, kept, sent, minor, owners, first_rows, second_rows,
            )

    shape = node_low.shape
    inputs = [array, node_low, state, *pooled_pair, params]
    scratch = [pltpu.VMEM((2 * latent, latent), BF16), pltpu.VMEM((latent, latent), BF16)]
    if last:
        inputs += [target, scaling, mask]
        outputs = [shared(shape, BF16), *gradient_outputs(shape, order.shape[0], rows, array.shape[2])]
        scratch += [pltpu.VMEM((hids, 2 * latent, latent // hids), F32), pltpu.VMEM((hids, latent, latent // hids), F32)]
    else:
        inputs += [at_halo]
        outputs = [
            shared((count, latent), BF16),
            shared((count, latent), BF16),
            shared((count, latent), BF16),
            shared((count, latent), BF16),
            shared((count, 1), F32),
            shared(shape, F32),
            shared(shape, BF16),
            shared((samples, at_halo.shape[0], latent), BF16),
        ]
    tables = [order, owners] if last else [order]
    specs = [in_scalars() for _ in tables] + [weight_block(*weights)] + [constant(a) for a in inputs[1:]]
    inputs = tables + inputs
    return run_kernel(kernel, "node_pass", 1, inputs, specs, outputs, scratch, 6 * count * latent * latent * (3 if last else 1))


def gradient_outputs(shape, blocks, rows, width):
    return [
        shared(shape, BF16),
        shared(shape, F32),
        shared((blocks // 2, rows, width), BF16),
        shared((blocks // 2, rows, width), BF16),
        shared((4, shape[-1]), F32),
    ]


def node_gradients(
    grad, scaled, scale, hidden, active, rows_low, pooled, params, mask,
    w1s, w2s, first, second, upstream, input_grad, kept, sent, minor, owners, first_rows, second_rows,
):
    latent = w2s.shape[0]
    output_grad = norm_backward(grad, scaled, scale, params[6:7]).astype(BF16)
    pre_grad = (matmul(output_grad, w2s[...]) * silu_slope(hidden)).astype(BF16)
    upstream[...] = matmul_nt(pre_grad, w1s[latent:]).astype(BF16).reshape(upstream.shape)
    input_grad[...] = (grad + matmul_nt(pre_grad, w1s[:latent])).reshape(input_grad.shape)
    chosen = mask[...] > 0.5
    output_mine = jnp.where(chosen, output_grad.astype(F32), 0.0)
    pre_mine = jnp.where(chosen, pre_grad.astype(F32), 0.0)
    grad_mine = jnp.where(chosen, grad, 0.0)
    minor[0:1] = column_sum(pre_mine)
    minor[1:2] = column_sum(output_mine)
    minor[2:3] = column_sum(grad_mine * scaled)
    minor[3:4] = column_sum(grad_mine)
    pre_mine = pre_mine.astype(BF16)
    store(first, 0, matmul_tn(rows_low, pre_mine))
    store(first, latent, matmul_tn(pooled, pre_mine))
    store(second, 0, matmul_tn(output_mine.astype(BF16), active))
    pack(first, owners, first_rows, 0, kept, sent)
    pack(second, owners, second_rows, first_rows, kept, sent)


def node_backward(order, owners, weights, nodes, grads, node_low, pooled, pre, act, normed, inverse, params, mask):
    samples, node_total, latent = node_low.shape
    array, rows, place = weights
    second_rows, hids = latent // nodes, latent // array.shape[2]
    first_rows = rows - second_rows
    count = samples * node_total

    def kernel(order, owners, w, base, own, other, node_low, pooled, pre, act, normed, inverse, params, mask, upstream, input_grad, kept, sent, minor, w1s, w2s, first, second):
        assemble(w, order, first_rows, 0, w1s)
        assemble(w, order, second_rows, first_rows, w2s)
        grad = (base[...] + (own[...] + other[...].astype(F32))).reshape(count, latent)
        node_gradients(
            grad, normed[...].astype(F32), inverse[...], pre[...].astype(F32), act[...],
            node_low[...].reshape(count, latent), pooled[...], params, mask,
            w1s, w2s, first, second, upstream, input_grad, kept, sent, minor, owners, first_rows, second_rows,
        )

    inputs = [order, owners, array, *grads, node_low, pooled, pre, act, normed, inverse, params, mask]
    specs = [in_scalars(), in_scalars(), weight_block(*weights)] + [constant(a) for a in inputs[3:]]
    return run_kernel(
        kernel,
        "node_backward",
        1,
        inputs,
        specs,
        gradient_outputs(node_low.shape, order.shape[0], rows, array.shape[2]),
        [
            pltpu.VMEM((2 * latent, latent), BF16),
            pltpu.VMEM((latent, latent), BF16),
            pltpu.VMEM((hids, 2 * latent, latent // hids), F32),
            pltpu.VMEM((hids, latent, latent // hids), F32),
        ],
        12 * count * latent * latent,
    )


def dot(spec, left, right):
    return jnp.einsum(spec, left, right, preferred_element_type=F32)


def swap(values, axis, offset):
    return lax.ppermute(values, axis, [(i, i ^ offset) for i in range(lax.axis_size(axis))])


def bits_of(axis):
    return lax.axis_size(axis).bit_length() - 1


def own_bit(axis, bit):
    return (lax.axis_index(axis) >> bit) & 1


def all_bits():
    return [(axis, bit) for axis in ("node", "hid") for bit in reversed(range(bits_of(axis)))]


def ordered(own, mine, other):
    low = jnp.where(own == 0, mine, other)
    high = jnp.where(own == 0, other, mine)
    return low, high


def double_up(part, axis, bit, place):
    low, high = ordered(own_bit(axis, bit), part, swap(part, axis, 1 << bit))
    return jnp.stack([low, high], axis=place)


def halve_sum(parts, axis, bit, place):
    own = own_bit(axis, bit)
    sent = lax.dynamic_index_in_dim(parts, 1 - own, place, keepdims=False)
    kept = lax.dynamic_index_in_dim(parts, own, place, keepdims=False)
    return kept.astype(F32) + swap(sent.astype(BF16), axis, 1 << bit).astype(F32)


def places():
    node_ids = jnp.arange(lax.axis_size("node"), dtype=jnp.int32) ^ lax.axis_index("node")
    hid_ids = jnp.arange(lax.axis_size("hid"), dtype=jnp.int32) ^ lax.axis_index("hid")
    place = 0
    for step, (axis, bit) in enumerate(all_bits()):
        ids = node_ids[:, None] if axis == "node" else hid_ids[None, :]
        place = place + (((ids >> bit) & 1) << step)
    return place.reshape(-1)


def owners_of_places():
    place = jnp.arange(1 << len(all_bits()), dtype=jnp.int32)
    owner = {"node": lax.axis_index("node"), "hid": lax.axis_index("hid")}
    for step, (axis, bit) in enumerate(all_bits()):
        owner[axis] = owner[axis] ^ (((place >> step) & 1) << bit)
    return jnp.stack([owner["node"], owner["hid"]], axis=1).reshape(-1)


def after(value, *earlier):
    return lax.optimization_barrier((value, *earlier))[0]


def exchange(values, first_step, flips):
    hid_bits = bits_of("hid")
    mask = 0
    for k in range(flips.bit_length()):
        if (flips >> k) & 1:
            axis, bit = all_bits()[first_step + k]
            mask |= 1 << (bit if axis == "hid" else bit + hid_bits)
    total = 1 << len(all_bits())
    return lax.ppermute(values, ("node", "hid"), [(i, i ^ mask) for i in range(total)])


def rounds(begin, end):
    return [(step, min(step + 2, end)) for step in range(begin, end, 2)]


def gather_round(held, begin, end, *under):
    arrived = [exchange(held, begin, flips) for flips in range(1, 1 << (end - begin))]
    if under:
        arrived = lax.optimization_barrier((*arrived, *under))[: len(arrived)]
    return jnp.concatenate([held, *arrived], axis=0)


def split(total, count):
    size = total.shape[0] // count
    pieces = [total[i * size : (i + 1) * size] for i in range(count)]
    return [pieces[0]] + [piece.astype(BF16) for piece in pieces[1:]]


def scatter_round(pieces, begin, *under):
    arrived = [exchange(pieces[flips], begin, flips) for flips in range(1, len(pieces))]
    if under:
        arrived = lax.optimization_barrier((*arrived, *under))[: len(arrived)]
    total = pieces[0].astype(F32)
    for piece in arrived:
        total = total + piece.astype(F32)
    return total


def scatter_rest(total, end, *under):
    for begin, stop in reversed(rounds(0, end)):
        total = scatter_round(split(total, 1 << (stop - begin)), begin, *under)
    return total[0]


def sum_round(values, begin, end):
    terms = [values] + [exchange(values, begin, flips) for flips in range(1, 1 << (end - begin))]
    while len(terms) > 1:
        terms = [terms[i] + terms[i + 1] for i in range(0, len(terms), 2)]
    return terms[0]


def sum_everywhere(values):
    steps = len(all_bits())
    values = sum_round(values, steps - 1, steps)
    for begin, end in reversed(rounds(0, steps - 1)):
        values = sum_round(values, begin, end)
    return values


def to_neighbours(rows, halo_width):
    count = lax.axis_size("node")
    onward = [(i, (i + 1) % count) for i in range(count)]
    back = [(target, source) for source, target in onward]
    from_previous = lax.ppermute(rows[:, halo_width:], "node", onward)
    from_next = lax.ppermute(rows[:, :halo_width], "node", back)
    return jnp.concatenate([from_previous, from_next], axis=1)


def neighbour_swaps(rows, halo_width):
    count = lax.axis_size("node")
    even = lax.axis_index("node") % 2 == 0
    to_previous, to_next = rows[:, :halo_width], rows[:, halo_width:]
    one = [(i, i ^ 1) for i in range(count)]
    two = [(i, (((i + 1) ^ 1) - 1) % count) for i in range(count)]
    first = lax.ppermute(jnp.where(even, to_next, to_previous), "node", one)
    second = lax.ppermute(jnp.where(even, to_previous, to_next), "node", two)
    return first, second


def from_neighbours(first, second):
    even = lax.axis_index("node") % 2 == 0
    return jnp.concatenate(
        [jnp.where(even, second, first), jnp.where(even, first, second)], axis=1
    )


def adam_terms(weight, grad, first, second, decay):
    first_new = BETA_FIRST * first + (1.0 - BETA_FIRST) * grad
    second_new = BETA_SECOND * second + (1.0 - BETA_SECOND) * grad * grad
    update = first_new / (jnp.sqrt(second_new) + ADAM_EPS) + decay * weight
    return (first_new, second_new, update)


def pack_shards(first, second):
    return jnp.concatenate([first, second.T], axis=0).astype(BF16)


def adam_terms(weight, grad, first, second, decay):
    first_new = BETA_FIRST * first + (1.0 - BETA_FIRST) * grad
    second_new = BETA_SECOND * second + (1.0 - BETA_SECOND) * grad * grad
    update = first_new / (jnp.sqrt(second_new) + ADAM_EPS) + decay * weight
    return (first_new, second_new, update)


def per_device(
    node_in,
    edge_in,
    cotangent,
    ocean_mask,
    present_mask,
    valid_counts,
    send_slot,
    recv_local,
    halo_lists,
    edge_first,
    edge_second,
    node_first,
    node_second,
    edge_first_m,
    edge_second_m,
    node_first_m,
    node_second_m,
    edge_first_v,
    edge_second_v,
    node_first_v,
    node_second_v,
    small_params,
    small_m,
    small_v,
    learn_rate,
):
    hid_count = lax.axis_size("hid")
    hid_index = lax.axis_index("hid")
    node_total, sample_count, latent = node_in.shape
    edge_part = edge_in.shape[0] // hid_count
    node_part = node_total // hid_count
    halo_width = halo_lists.shape[1]
    table_total = node_total + 2 * halo_width
    sample_half, edge_half = hid_index >> 1, hid_index & 1
    samples = sample_count // 2
    nodes, hids = lax.axis_size("node"), hid_count
    first_rows = edge_first.shape[1]
    second_rows = edge_second.shape[2]
    node_rows = node_first.shape[1] + second_rows
    width = edge_first.shape[2]

    order, owners = places(), owners_of_places()
    steps = len(all_bits())

    def layer_shards(depth, *earlier):
        shards = (node_first[depth], node_second[depth], edge_first[depth], edge_second[depth])
        if earlier:
            shards = after(shards, *earlier)
        return jnp.concatenate([pack_shards(*shards[:2]), pack_shards(*shards[2:])], axis=0)[None]

    def parted(held):
        return held[:, :node_rows], held[:, node_rows:]

    layer_zero = layer_shards(0)
    for begin, end in rounds(0, steps - 3):
        layer_zero = gather_round(layer_zero, begin, end)
    setup = layer_zero
    layer_zero = gather_round(layer_zero, steps - 3, steps - 2)
    node_zero, edge_zero = parted(layer_zero)
    layer_one = layer_shards(1, setup)
    layer_one = after(layer_one, edge_zero)
    z_rounds = rounds(0, steps - 3)
    for begin, end in z_rounds[:-1]:
        layer_one = gather_round(layer_one, begin, end)
    halo_gate = edge_zero
    masters = (edge_first, edge_second, node_first, node_second)
    weight_local = jnp.stack(
        [jnp.sum(matrix * matrix, axis=(1, 2)) for matrix in after(masters, setup)], axis=1
    )
    def edge_blocks(whole):
        return ((whole, first_rows, 0), (whole, second_rows, first_rows // second_rows))

    def own_edges(values):
        return lax.dynamic_index_in_dim(
            values.reshape(2, 2, edge_part, *values.shape[1:]), edge_half, 1, keepdims=False
        ).reshape(2 * edge_part, *values.shape[1:])

    def own_nodes(values):
        return lax.dynamic_index_in_dim(
            values.reshape(samples, 2, 2, node_part, latent), edge_half, 2, keepdims=False
        ).reshape(samples, 2 * node_part, latent)

    def own_samples(values):
        return lax.dynamic_slice_in_dim(values, sample_half * samples, samples, 1)

    def own_rows_exchanged(values):
        quarters = jnp.moveaxis(values.reshape(samples, 2, 2, node_part, latent), 0, 3)
        quarters = lax.dynamic_index_in_dim(quarters, edge_half, 1, keepdims=False)
        sent = lax.dynamic_index_in_dim(quarters, 1 - sample_half, 0, keepdims=False)
        kept = lax.dynamic_index_in_dim(quarters, sample_half, 0, keepdims=False)
        return kept, swap(sent, "hid", 2)

    def all_samples(kept, arrived):
        return jnp.concatenate(ordered(sample_half, kept, arrived), axis=1)

    send_slot, recv_local, halo_lists, node_in, edge_in = lax.optimization_barrier(
        (send_slot, recv_local, halo_lists, node_in, edge_in, setup)
    )[:5]
    sender = own_edges(send_slot)
    receiver = own_edges(recv_local)
    node_ids, table_ids = jnp.arange(node_total), jnp.arange(table_total)
    at_receiver = (receiver[:, None] == node_ids[None, :]).astype(BF16)
    at_both = jnp.concatenate(
        [(sender[:, None] == table_ids[None, :]).astype(BF16), at_receiver], axis=1
    )
    at_nodes = (node_ids[:, None] == receiver[None, :]).astype(BF16)
    at_both_t = jnp.concatenate(
        [(table_ids[:, None] == sender[None, :]).astype(BF16), at_nodes], axis=0
    )
    at_halo = (halo_lists.reshape(-1)[:, None] == node_ids[None, :]).astype(BF16)
    mask = ((node_ids // node_part) % 2 == edge_half).astype(F32)
    mask = jnp.tile(mask, samples)[:, None]

    node_low = jnp.transpose(own_samples(node_in), (1, 0, 2))
    edge_in_own = own_edges(edge_in)
    halo_rows = dot("hn,snl->shl", at_halo, node_low).astype(BF16)
    node_low_zero = node_low
    halo_rows = neighbour_swaps(after(halo_rows, halo_gate), halo_width)
    begin, end = z_rounds[-1]
    arrived = [exchange(layer_one, begin, flips) for flips in range(1, 1 << (end - begin))]
    edge_arrived, first, second, weight_local, *arrived = lax.optimization_barrier(
        (exchange(edge_zero, steps - 2, 1), *halo_rows, weight_local, *arrived)
    )
    halo_rows = from_neighbours(first, second)
    edge_zero = jnp.concatenate([edge_zero, edge_arrived], axis=0)
    layer_one = jnp.concatenate([layer_one, *arrived], axis=0)
    node_zero = after(node_zero, edge_zero)
    edge_zero = gather_round(edge_zero, steps - 1, steps)
    table_zero = jnp.concatenate([node_low, halo_rows], axis=1)
    pre_zero, act_zero, normed_zero, inverse_zero, edge_state, edge_low, pooled = edge_forward(
        order,
        *edge_blocks(edge_zero),
        table_zero,
        edge_in_own[None],
        edge_in_own[None],
        at_both,
        at_nodes,
        small_params[0],
        node_total,
        False,
    )
    pooled, *arrived = lax.optimization_barrier(
        (pooled, exchange(node_zero, steps - 2, 1), exchange(layer_one, steps - 3, 1))
    )
    node_zero = jnp.concatenate([node_zero, arrived[0]], axis=0)
    node_zero = gather_round(node_zero, steps - 1, steps)
    layer_one = jnp.concatenate([layer_one, arrived[1]], axis=0)
    node_one, edge_one = parted(layer_one)
    other = after(swap(pooled, "hid", 1), edge_one)
    (
        pooled_zero,
        node_pre,
        node_act,
        node_normed,
        node_inverse,
        node_state,
        node_low,
        halo_rows,
    ) = node_pass(
        order,
        None,
        (node_zero, node_rows, 0),
        nodes,
        node_low_zero,
        node_low_zero,
        (pooled, other),
        small_params[0],
        at_halo,
        None,
        None,
        None,
    )
    halo_rows = to_neighbours(halo_rows, halo_width)
    arrived, halo_rows = lax.optimization_barrier((exchange(edge_one, steps - 2, 1), halo_rows))
    edge_one = jnp.concatenate([edge_one, arrived], axis=0)
    node_one = after(node_one, edge_one)
    edge_one = gather_round(edge_one, steps - 1, steps)

    valid_mask = (ocean_mask[:, None] * present_mask).astype(BF16)
    masked = after(cotangent, pooled) * valid_mask[:, :, None]
    sent = lax.dynamic_slice_in_dim(masked, (1 - sample_half) * samples, samples, 1)
    scaling = node_total * lax.axis_size("node") / valid_counts.astype(F32)
    scaling = lax.dynamic_slice_in_dim(scaling, sample_half * samples, samples, 0)
    scaling = scaling[:, None, None]

    node_low_one = node_low
    table_one = jnp.concatenate([node_low, halo_rows], axis=1)
    pre_one, act_one, normed_one, inverse_one, pooled = edge_forward(
        order,
        *edge_blocks(edge_one),
        table_one,
        edge_low,
        edge_state,
        at_both,
        at_nodes,
        small_params[1],
        node_total,
        True,
    )
    pooled, arrived, cotangent_other = lax.optimization_barrier(
        (pooled, exchange(node_one, steps - 2, 1), swap(sent, "hid", 2))
    )
    node_one = jnp.concatenate([node_one, arrived], axis=0)
    masked = jnp.stack(ordered(sample_half, own_samples(masked), cotangent_other), axis=0)
    masked = double_up(masked, "hid", 0, 1).reshape(node_total, samples, latent)
    target = jnp.transpose(masked, (1, 0, 2))
    node_one = gather_round(node_one, steps - 1, steps)
    node_low, pooled_grad, node_grad, kept, sent, node_minor_one = node_pass(
        order,
        owners,
        (node_one, node_rows, 0),
        nodes,
        node_low_one,
        node_state,
        (pooled, swap(pooled, "hid", 1)),
        small_params[1],
        None,
        target,
        scaling,
        mask,
    )

    def from_edges(partial, returned):
        return partial + dot("hn,shl->snl", at_halo, returned)

    low, hidden_low, at_rows, partial, returned, edge_grad, edge_minor_one = edge_backward(
        order,
        *edge_blocks(edge_one),
        pooled_grad,
        None,
        normed_one,
        inverse_one,
        pre_one,
        at_receiver,
        at_both_t,
        small_params[1, 2:3],
        True,
        node_total,
    )
    low, *node_out = lax.optimization_barrier((low, *own_rows_exchanged(node_low)))
    node_out = all_samples(*node_out)
    chain_one = edge_weight_grads(
        owners,
        edge_low,
        table_one,
        hidden_low,
        at_rows,
        low,
        act_one,
        node_total,
        nodes,
        width,
        [kept, sent],
    )
    *returned, kept, sent = lax.optimization_barrier(
        (*neighbour_swaps(returned, halo_width), *chain_one)
    )
    returned, chain_one = from_neighbours(*returned), (kept, sent)
    partial = from_edges(partial, returned)
    chain_one = split(scatter_round(chain_one, steps - 1), 2)
    other, *chain_one = lax.optimization_barrier((swap(partial.astype(BF16), "hid", 1), *chain_one))
    pooled_grad, node_grad, kept, sent, node_minor_zero = node_backward(
        order,
        owners,
        (node_zero, node_rows, 0),
        nodes,
        (node_grad, partial, other),
        node_low_zero,
        pooled_zero,
        node_pre,
        node_act,
        node_normed,
        node_inverse,
        small_params[0],
        mask,
    )
    low, hidden_low, at_rows, partial, returned, edge_input_grad, edge_minor_zero, hidden_sum = (
        edge_backward(
            order,
            *edge_blocks(edge_zero),
            pooled_grad,
            edge_grad,
            normed_zero,
            inverse_zero,
            pre_zero,
            at_receiver,
            at_both_t,
            small_params[0, 2:3],
            False,
            node_total,
        )
    )
    chain_one = split(scatter_round(chain_one, steps - 2, low), 2)
    chain_zero = split(scatter_round((kept, sent), steps - 1, low), 2)
    low = after(low, *chain_one, *chain_zero)
    chain_edge = edge_weight_grads(
        owners,
        edge_in_own,
        table_zero,
        hidden_sum,
        at_rows,
        low,
        act_zero,
        node_total,
        nodes,
        width,
        None,
    )
    kept, sent, one_arrived, zero_arrived, *returned = lax.optimization_barrier(
        (
            *chain_edge,
            exchange(chain_one[1], steps - 3, 1),
            exchange(chain_zero[1], steps - 2, 1),
            *neighbour_swaps(returned, halo_width),
        )
    )
    chain_one = chain_one[0].astype(F32) + one_arrived.astype(F32)
    chain_zero = split(chain_zero[0].astype(F32) + zero_arrived.astype(F32), 2)
    edge_arrived = exchange(sent, steps - 1, 1)
    kept, sent = split(kept.astype(F32) + edge_arrived.astype(F32), 2)
    zero_arrived = after(exchange(chain_zero[1], steps - 3, 1), sent)
    returned = after(returned, sent)
    chain_one = jnp.concatenate(
        [chain_one, chain_zero[0].astype(F32) + zero_arrived.astype(F32)], axis=1
    )
    for begin, end in reversed(z_rounds[1:]):
        chain_one = scatter_round(split(chain_one, 1 << (end - begin)), begin)
    begin, end = z_rounds[0]
    chain_one = split(chain_one, 1 << (end - begin))
    partial = from_edges(partial, from_neighbours(*returned))
    arrived, edge_input_grad, other, *others = lax.optimization_barrier(
        (
            exchange(sent, steps - 2, 1),
            edge_input_grad,
            swap(partial.astype(BF16), "hid", 1),
            *[exchange(chain_one[flips], begin, flips) for flips in range(1, len(chain_one))],
        )
    )
    joined_grads = chain_one[0]
    for piece in others:
        joined_grads = joined_grads + piece.astype(F32)
    joined_grads = joined_grads[0]
    chain_edge = split(kept + arrived.astype(F32), 2)
    chain_edge = scatter_round(chain_edge, steps - 3)
    halves = edge_input_grad.reshape(2, edge_part, latent)
    sent = lax.dynamic_index_in_dim(halves, 1 - sample_half, 0, keepdims=False).astype(BF16)
    kept = lax.dynamic_index_in_dim(halves, sample_half, 0, keepdims=False)
    node_grad = node_grad + (partial + other.astype(F32))
    grad_node = own_rows_exchanged(node_grad.astype(BF16))
    edge_zero_grads = scatter_rest(chain_edge, steps - 3)
    edge_zero_grads, arrived, *grad_node = lax.optimization_barrier(
        (edge_zero_grads, swap(sent, "hid", 2), *grad_node)
    )
    edge_input_grad = kept + arrived.astype(F32)
    grad_node = all_samples(*grad_node)

    edge_rows = first_rows + second_rows
    layer_one_grads = joined_grads[: node_rows + edge_rows]
    node_zero_grads = joined_grads[node_rows + edge_rows :]
    node_one_grads, edge_one_grads = layer_one_grads[:node_rows], layer_one_grads[node_rows:]
    node_first_rows = node_rows - second_rows
    grads = [
        jnp.stack([edge_zero_grads[:first_rows], edge_one_grads[:first_rows]]),
        jnp.stack([edge_zero_grads[first_rows:].T, edge_one_grads[first_rows:].T]),
        jnp.stack([node_zero_grads[:node_first_rows], node_one_grads[:node_first_rows]]),
        jnp.stack([node_zero_grads[node_first_rows:].T, node_one_grads[node_first_rows:].T]),
    ]
    firsts = (edge_first_m, edge_second_m, node_first_m, node_second_m)
    seconds = (edge_first_v, edge_second_v, node_first_v, node_second_v)
    moment_list = [
        adam_terms(masters[place], grads[place], firsts[place], seconds[place], WEIGHT_DECAY)
        for place in range(4)
    ]
    update_local = jnp.stack(
        [jnp.sum(entry[2] * entry[2], axis=(1, 2)) for entry in moment_list], axis=1
    )
    squares = jnp.concatenate([weight_local.reshape(1, -1), update_local.reshape(1, -1)], axis=1)
    minor_packed = jnp.concatenate(
        [edge_minor_zero, node_minor_zero, edge_minor_one, node_minor_one]
        + [jnp.pad(squares, ((0, 0), (0, latent - squares.size)))],
        axis=0,
    )
    minor_packed = sum_everywhere(minor_packed)
    minor_total = minor_packed[: 8 * LAYERS].reshape(small_params.shape)
    squares = minor_packed[8 * LAYERS, : squares.size].reshape(2, *weight_local.shape)
    weight_squares, update_squares = squares[0], squares[1]
    weight_norm = jnp.sqrt(weight_squares)
    update_norm = jnp.sqrt(update_squares)
    new_weights = []
    for position in range(4):
        ratio = weight_norm[:, position] / update_norm[:, position]
        new_weights.append(
            masters[position] - learn_rate[0] * ratio[:, None, None] * moment_list[position][2]
        )
    small_first, small_second, small_update = adam_terms(
        small_params, minor_total, small_m, small_v, 0.0
    )
    small_wnorm = jnp.sqrt(jnp.sum(small_params * small_params, axis=2))
    small_unorm = jnp.sqrt(jnp.sum(small_update * small_update, axis=2))
    small_new = (
        small_params - learn_rate[0] * (small_wnorm / small_unorm)[:, :, None] * small_update
    )
    norms = jnp.stack(
        [
            jnp.concatenate([weight_norm, small_wnorm], axis=1),
            jnp.concatenate([update_norm, small_unorm], axis=1),
        ],
        axis=2,
    )
    return (
        node_out,
        grad_node,
        edge_input_grad.astype(BF16),
        *new_weights,
        *[entry[0] for entry in moment_list],
        *[entry[1] for entry in moment_list],
        *[weight.astype(BF16) for weight in new_weights],
        small_new,
        small_first,
        small_second,
        norms,
    )


def solution(mesh):
    whole = P()
    rows = P(None, "node", "hid")
    columns = P(None, "hid", "node")
    matrices = (rows, columns, rows, columns)
    in_specs = (
        P("node", None, None),
        P("node", None),
        P(("node", "hid"), None, None),
        P(("node", "hid")),
        P(("node", "hid"), None),
        P(),
        P("node"),
        P("node"),
        P("node", None),
        *matrices,
        *matrices,
        *matrices,
        whole,
        whole,
        whole,
        whole,
    )
    out_specs = (
        P(("node", "hid"), None, None),
        P(("node", "hid"), None, None),
        P(("node", "hid"), None),
        *matrices,
        *matrices,
        *matrices,
        *matrices,
        whole,
        whole,
        whole,
        whole,
    )
    return jax.shard_map(
        per_device, mesh=mesh, in_specs=in_specs, out_specs=out_specs, check_vma=False
    )
```

```python
import jax
import jax.numpy as jnp
from jax import lax
from jax.experimental import pallas as pl
from jax.experimental.pallas import tpu as pltpu
from jax.sharding import PartitionSpec as P

LAYERS = 2


NORM_EPS = 1e-05
BETA_FIRST = 0.5
BETA_SECOND = 0.5
ADAM_EPS = 1e-06
WEIGHT_DECAY = 0.01
BF16 = jnp.bfloat16
F32 = jnp.float32
VMEM_BYTES = 56 * 1024 * 1024


def matmul(left, right):
    return lax.dot_general(left, right, (((1,), (0,)), ((), ())), preferred_element_type=F32)


def matmul_nt(left, right):
    return lax.dot_general(left, right, (((1,), (1,)), ((), ())), preferred_element_type=F32)


def matmul_tn(left, right):
    return lax.dot_general(left, right, (((0,), (0,)), ((), ())), preferred_element_type=F32)


def sigmoid(values):
    return 0.5 + 0.5 * jnp.tanh(0.5 * values)


def silu_slope(values):
    gate = sigmoid(values)
    return gate * (1.0 + values * (1.0 - gate))


def norm_forward(values):
    center = values - jnp.mean(values, axis=-1, keepdims=True)
    spread = jnp.mean(center * center, axis=-1, keepdims=True)
    inverse = lax.rsqrt(spread + NORM_EPS)
    return center * inverse, inverse


def norm_backward(upstream, normed, inverse, gain_row):
    scaled = upstream * gain_row
    return inverse * (
        scaled
        - jnp.mean(scaled, axis=-1, keepdims=True)
        - normed * jnp.mean(scaled * normed, axis=-1, keepdims=True)
    )


def column_sum(values):
    return jnp.sum(values, axis=0, keepdims=True)


def assemble(source, order, rows, offset, target):
    own, arrived = source
    half, _, width = own.shape
    nodes, hids = target.shape[0] // rows, target.shape[1] // width
    for i in range(nodes):
        for j in range(hids):
            place = order[i * hids + j]
            index = jnp.where(place < half, place, place - half)
            target[i * rows : (i + 1) * rows, j * width : (j + 1) * width] = jnp.where(
                place < half,
                own[index, offset : offset + rows, :],
                arrived[index, offset : offset + rows, :],
            )


def store(target, begin, values):
    rows, width = values.shape[0], target.shape[2]
    for j in range(target.shape[0]):
        target[j, begin : begin + rows] = values[:, j * width : (j + 1) * width]


def add(target, begin, values):
    rows, width = values.shape[0], target.shape[2]
    for j in range(target.shape[0]):
        target[j, begin : begin + rows] += values[:, j * width : (j + 1) * width]


def pack(values, owners, rows, offset, kept, sent):
    half = kept.shape[0]

    def one(index, carry):
        for target, place in ((kept, index), (sent, index + half)):
            begin = pl.multiple_of(owners[2 * place] * rows, rows)
            target[index, offset : offset + rows, :] = values[
                owners[2 * place + 1], pl.ds(begin, rows), :
            ].astype(BF16)
        return carry

    lax.fori_loop(0, half, one, 0)


def per_sample(array):
    block = (1,) + array.shape[1:]
    return pl.BlockSpec(block, lambda s: (s,) + (0,) * (len(block) - 1))


def constant(array):
    return pl.BlockSpec(array.shape, lambda s: (0,) * len(array.shape))


def weight_blocks(halves, rows, place):
    blocks, _, width = halves[0].shape
    return [pl.BlockSpec((blocks, rows, width), lambda s: (0, place, 0)) for _ in halves]


def in_scalars():
    return pl.BlockSpec(memory_space=pltpu.SMEM)


def shape_of(shape, dtype):
    return jax.ShapeDtypeStruct(shape, dtype)


def run_kernel(kernel, name, samples, inputs, in_specs, outputs, scratch, flops):
    moved = sum(a.size * a.dtype.itemsize for a in inputs) + sum(
        shape.size * shape.dtype.itemsize for shape, _ in outputs
    )
    return pl.pallas_call(
        kernel,
        name=name,
        grid=(samples,),
        in_specs=in_specs,
        out_specs=[spec for _, spec in outputs],
        out_shape=[shape for shape, _ in outputs],
        scratch_shapes=scratch,
        compiler_params=pltpu.CompilerParams(
            dimension_semantics=("arbitrary",), vmem_limit_bytes=VMEM_BYTES
        ),
        cost_estimate=pl.CostEstimate(flops=4 * flops, bytes_accessed=moved, transcendentals=0),
    )(*inputs)


def sampled(shape, dtype):
    result = shape_of(shape, dtype)
    return (result, per_sample(result))


def shared(shape, dtype):
    result = shape_of(shape, dtype)
    return (result, constant(result))


def edge_forward(order, first, second, table, edge_low, edge_state, at_both, at_nodes, params, node_total, last):
    samples, table_total, latent = table.shape
    edges = edge_low.shape[1]
    alike = edge_low.shape[0] == 1

    def kernel(order, w1, w1x, w2, w2x, table, low, state, both, nodes, params, pre, act, normed, inverse, *rest):
        if last:
            pooled, w1s, w2s, projected = rest
        else:
            new_state, new_low, pooled, w1s, w2s, projected = rest

        @pl.when(pl.program_id(0) == 0)
        def _():
            assemble((w1, w1x), order, w1.shape[1], 0, w1s)
            assemble((w2, w2x), order, w2.shape[1], 0, w2s)

        rows = table[0]
        projected[:table_total] = matmul(rows, w1s[latent : 2 * latent]).astype(BF16)
        projected[table_total:] = matmul(rows[:node_total], w1s[2 * latent :]).astype(BF16)
        hidden = matmul(low[0], w1s[:latent]) + matmul(both[...], projected[...]) + params[0:1]
        pre[0] = hidden.astype(BF16)
        active = (hidden * sigmoid(hidden)).astype(BF16)
        act[0] = active
        output = matmul_nt(active, w2s[...]) + params[1:2]
        scaled, scale = norm_forward(output)
        normed[0] = scaled.astype(BF16)
        inverse[0] = scale
        state_new = state[0].astype(F32) + scaled * params[2:3] + params[3:4]
        low_new = state_new.astype(BF16)
        if not last:
            new_state[0] = state_new
            new_low[0] = low_new
        pooled[0] = matmul(nodes[...], low_new).astype(BF16)

    wide = (samples, edges, latent)
    outputs = [sampled(wide, BF16), sampled(wide, BF16), sampled(wide, BF16), sampled((samples, edges, 1), F32)]
    if not last:
        outputs += [sampled(wide, F32), sampled(wide, BF16)]
    outputs += [sampled((samples, node_total, latent), BF16)]
    of_edges = constant if alike else per_sample
    return run_kernel(
        kernel,
        "edge_forward",
        samples,
        [order, *first[0], *second[0], table, edge_low, edge_state, at_both, at_nodes, params],
        [
            in_scalars(),
            *weight_blocks(*first),
            *weight_blocks(*second),
            per_sample(table),
            of_edges(edge_low),
            of_edges(edge_state),
            constant(at_both),
            constant(at_nodes),
            constant(params),
        ],
        outputs,
        [
            pltpu.VMEM((3 * latent, latent), BF16),
            pltpu.VMEM((latent, latent), BF16),
            pltpu.VMEM((at_both.shape[1], latent), BF16),
        ],
        2 * samples * edges * latent * (3 * latent + at_both.shape[1]),
    )


def edge_backward(order, first, second, pooled_grad, edge_grad, normed, inverse, pre, at_receiver, at_both_t, gain, last, node_total):
    samples, edges, latent = normed.shape
    at_total = at_both_t.shape[0]
    table_total = at_total - node_total

    def kernel(order, w1, w1x, w2, w2x, upstream, *rest):
        if not last:
            later, rest = rest[0], rest[1:]
        normed, inverse, pre, receiver, both_t, gain, low, hidden_low, at_rows, partial, returned, grad_out, minor = rest[:13]
        if last:
            w1s, w2s = rest[13:]
        else:
            hidden_sum, w1s, w2s, hidden_acc = rest[13:]
        step = pl.program_id(0)

        @pl.when(step == 0)
        def _():
            assemble((w1, w1x), order, w1.shape[1], 0, w1s)
            assemble((w2, w2x), order, w2.shape[1], 0, w2s)
            minor[...] = jnp.zeros_like(minor)

        grad = matmul(receiver[...], upstream[0])
        if not last:
            grad = grad + later[0]
        scaled = normed[0].astype(F32)
        output_grad = norm_backward(grad, scaled, inverse[0], gain[0:1]).astype(BF16)
        low[0] = output_grad
        act_grad = matmul(output_grad, w2s[...])
        pre_grad = (act_grad * silu_slope(pre[0].astype(F32))).astype(BF16)
        hidden_low[0] = pre_grad
        minor[0:1] += column_sum(pre_grad.astype(F32))
        minor[1:2] += column_sum(output_grad.astype(F32))
        minor[2:3] += column_sum(grad * scaled)
        minor[3:4] += column_sum(grad)
        at_rows[0] = matmul(both_t[...], pre_grad).astype(BF16)
        send = w1s[latent : 2 * latent]
        partial[0] = matmul_nt(at_rows[0, :node_total], send) + matmul_nt(
            at_rows[0, table_total:], w1s[2 * latent :]
        )
        returned[0] = matmul_nt(at_rows[0, node_total:table_total], send).astype(BF16)
        if last:
            grad_out[0] = grad + matmul_nt(pre_grad, w1s[:latent])
        else:

            @pl.when(step == 0)
            def _():
                grad_out[...] = grad
                hidden_acc[...] = pre_grad.astype(F32)

            @pl.when(step > 0)
            def _():
                grad_out[...] += grad
                hidden_acc[...] += pre_grad.astype(F32)

            @pl.when(step == samples - 1)
            def _():
                total = hidden_acc[...].astype(BF16)
                hidden_sum[...] = total
                grad_out[...] += matmul_nt(total, w1s[:latent])

    wide = (samples, edges, latent)
    outputs = [
        sampled(wide, BF16),
        sampled(wide, BF16),
        sampled((samples, at_total, latent), BF16),
        sampled((samples, node_total, latent), F32),
        sampled((samples, table_total - node_total, latent), BF16),
        sampled(wide, F32) if last else shared((edges, latent), F32),
        shared((4, latent), F32),
    ]
    scratch = [pltpu.VMEM((3 * latent, latent), BF16), pltpu.VMEM((latent, latent), BF16)]
    inputs = [order, *first[0], *second[0], pooled_grad]
    specs = [in_scalars(), *weight_blocks(*first), *weight_blocks(*second), per_sample(pooled_grad)]
    if not last:
        outputs.append(shared((edges, latent), BF16))
        scratch.append(pltpu.VMEM((edges, latent), F32))
        inputs.append(edge_grad)
        specs.append(per_sample(edge_grad))
    inputs += [normed, inverse, pre, at_receiver, at_both_t, gain]
    specs += [
        per_sample(normed),
        per_sample(inverse),
        per_sample(pre),
        constant(at_receiver),
        constant(at_both_t),
        constant(gain),
    ]
    return run_kernel(
        kernel,
        "edge_backward",
        samples,
        inputs,
        specs,
        outputs,
        scratch,
        2 * samples * edges * latent * (2 * latent + 2 * at_total),
    )


def edge_weight_grads(owners, edge_low, table, hidden_low, at_rows, low, act, node_total, nodes, width, packed_before):
    samples, table_total, latent = table.shape
    alike = edge_low.ndim == 2
    first_rows, second_rows = 3 * latent // nodes, latent // nodes
    offset = 0 if packed_before is None else packed_before[0].shape[1]
    blocks, hids = owners.shape[0] // 2, latent // width

    def kernel(owners, edge_low, table, hidden_low, at_rows, low, act, *rest):
        before, rest = rest[:-4], rest[-4:]
        kept, sent, first, second = rest
        step = pl.program_id(0)

        @pl.when(step == 0)
        def _():
            first[...] = jnp.zeros_like(first)
            second[...] = jnp.zeros_like(second)
            for source, target in zip(before, (kept, sent)):
                target[:, :offset, :] = source[...]
            if alike:
                add(first, 0, matmul_tn(edge_low[...], hidden_low[...]))

        if not alike:
            add(first, 0, matmul_tn(edge_low[0], hidden_low[0]))
        add(first, latent, matmul_tn(table[0], at_rows[0, :table_total]))
        add(first, 2 * latent, matmul_tn(table[0, :node_total], at_rows[0, table_total:]))
        add(second, 0, matmul_tn(low[0], act[0]))

        @pl.when(step == samples - 1)
        def _():
            pack(first, owners, first_rows, offset, kept, sent)
            pack(second, owners, second_rows, offset + first_rows, kept, sent)

    of_edges = constant if alike else per_sample
    inputs = [owners, edge_low, table, hidden_low, at_rows, low, act]
    specs = [in_scalars(), of_edges(edge_low), per_sample(table), of_edges(hidden_low), per_sample(at_rows), per_sample(low), per_sample(act)]
    if packed_before is not None:
        inputs += packed_before
        specs += [constant(a) for a in packed_before]
    return run_kernel(
        kernel,
        "edge_weight_grads",
        samples,
        inputs,
        specs,
        [shared((blocks // 2, offset + first_rows + second_rows, width), BF16)] * 2,
        [pltpu.VMEM((hids, 3 * latent, width), F32), pltpu.VMEM((hids, latent, width), F32)],
        4 * low.size * latent,
    )


def node_pass(order, owners, weights, nodes, node_low, state, pooled_pair, params, at_halo, target, scaling, mask):
    samples, node_total, latent = node_low.shape
    halves, rows, place = weights
    width = halves[0].shape[2]
    second_rows, hids = latent // nodes, latent // width
    first_rows = rows - second_rows
    count = samples * node_total
    last = target is not None

    def kernel(order, *rest):
        if last:
            owners, rest = rest[0], rest[1:]
        w, wx, node_low, state, pooled_own, pooled_other, params, *rest = rest
        if last:
            target, scaling, mask, new_low, upstream, input_grad, kept, sent, minor, w1s, w2s, first, second = rest
        else:
            at_halo, pooled_out, pre, act, normed, inverse, new_state, new_low, halo, w1s, w2s = rest
        assemble((w, wx), order, first_rows, 0, w1s)
        assemble((w, wx), order, second_rows, first_rows, w2s)
        rows_low = node_low[...].reshape(count, latent)
        pooled = (pooled_own[...].astype(F32) + pooled_other[...].astype(F32)).astype(BF16)
        pooled = pooled.reshape(count, latent)
        hidden = matmul(rows_low, w1s[:latent]) + matmul(pooled, w1s[latent:]) + params[4:5]
        active = (hidden * sigmoid(hidden)).astype(BF16)
        output = matmul_nt(active, w2s[...]) + params[5:6]
        scaled, scale = norm_forward(output)
        state_new = state[...].astype(F32).reshape(count, latent) + scaled * params[6:7] + params[7:8]
        low_new = state_new.astype(BF16).reshape(new_low.shape)
        new_low[...] = low_new
        if not last:
            pooled_out[...] = pooled
            pre[...] = hidden.astype(BF16)
            act[...] = active
            normed[...] = scaled.astype(BF16)
            inverse[...] = scale
            new_state[...] = state_new.reshape(new_state.shape)
            for s in range(samples):
                halo[s] = matmul(at_halo[...], new_low[s]).astype(BF16)
        else:
            grad = (target[...].astype(F32) * scaling[...]).reshape(count, latent)
            node_gradients(
                grad, scaled, scale, hidden, active, rows_low, pooled, params, mask,
                w1s, w2s, first, second, upstream, input_grad, kept, sent, minor, owners, first_rows, second_rows,
            )

    shape = node_low.shape
    inputs = [*halves, node_low, state, *pooled_pair, params]
    scratch = [pltpu.VMEM((2 * latent, latent), BF16), pltpu.VMEM((latent, latent), BF16)]
    if last:
        inputs += [target, scaling, mask]
        outputs = [shared(shape, BF16), *gradient_outputs(shape, order.shape[0], rows, width)]
        scratch += [pltpu.VMEM((hids, 2 * latent, latent // hids), F32), pltpu.VMEM((hids, latent, latent // hids), F32)]
    else:
        inputs += [at_halo]
        outputs = [
            shared((count, latent), BF16),
            shared((count, latent), BF16),
            shared((count, latent), BF16),
            shared((count, latent), BF16),
            shared((count, 1), F32),
            shared(shape, F32),
            shared(shape, BF16),
            shared((samples, at_halo.shape[0], latent), BF16),
        ]
    tables = [order, owners] if last else [order]
    specs = [in_scalars() for _ in tables] + weight_blocks(*weights) + [constant(a) for a in inputs[2:]]
    inputs = tables + inputs
    return run_kernel(kernel, "node_pass", 1, inputs, specs, outputs, scratch, 6 * count * latent * latent * (3 if last else 1))


def gradient_outputs(shape, blocks, rows, width):
    return [
        shared(shape, BF16),
        shared(shape, F32),
        shared((blocks // 2, rows, width), BF16),
        shared((blocks // 2, rows, width), BF16),
        shared((4, shape[-1]), F32),
    ]


def node_gradients(
    grad, scaled, scale, hidden, active, rows_low, pooled, params, mask,
    w1s, w2s, first, second, upstream, input_grad, kept, sent, minor, owners, first_rows, second_rows,
):
    latent = w2s.shape[0]
    output_grad = norm_backward(grad, scaled, scale, params[6:7]).astype(BF16)
    pre_grad = (matmul(output_grad, w2s[...]) * silu_slope(hidden)).astype(BF16)
    upstream[...] = matmul_nt(pre_grad, w1s[latent:]).astype(BF16).reshape(upstream.shape)
    input_grad[...] = (grad + matmul_nt(pre_grad, w1s[:latent])).reshape(input_grad.shape)
    chosen = mask[...] > 0.5
    output_mine = jnp.where(chosen, output_grad.astype(F32), 0.0)
    pre_mine = jnp.where(chosen, pre_grad.astype(F32), 0.0)
    grad_mine = jnp.where(chosen, grad, 0.0)
    minor[0:1] = column_sum(pre_mine)
    minor[1:2] = column_sum(output_mine)
    minor[2:3] = column_sum(grad_mine * scaled)
    minor[3:4] = column_sum(grad_mine)
    pre_mine = pre_mine.astype(BF16)
    store(first, 0, matmul_tn(rows_low, pre_mine))
    store(first, latent, matmul_tn(pooled, pre_mine))
    store(second, 0, matmul_tn(output_mine.astype(BF16), active))
    pack(first, owners, first_rows, 0, kept, sent)
    pack(second, owners, second_rows, first_rows, kept, sent)


def node_backward(order, owners, weights, nodes, grads, node_low, pooled, pre, act, normed, inverse, params, mask):
    samples, node_total, latent = node_low.shape
    halves, rows, place = weights
    width = halves[0].shape[2]
    second_rows, hids = latent // nodes, latent // width
    first_rows = rows - second_rows
    count = samples * node_total

    def kernel(order, owners, w, wx, base, own, other, node_low, pooled, pre, act, normed, inverse, params, mask, upstream, input_grad, kept, sent, minor, w1s, w2s, first, second):
        assemble((w, wx), order, first_rows, 0, w1s)
        assemble((w, wx), order, second_rows, first_rows, w2s)
        grad = (base[...] + (own[...] + other[...].astype(F32))).reshape(count, latent)
        node_gradients(
            grad, normed[...].astype(F32), inverse[...], pre[...].astype(F32), act[...],
            node_low[...].reshape(count, latent), pooled[...], params, mask,
            w1s, w2s, first, second, upstream, input_grad, kept, sent, minor, owners, first_rows, second_rows,
        )

    inputs = [order, owners, *halves, *grads, node_low, pooled, pre, act, normed, inverse, params, mask]
    specs = [in_scalars(), in_scalars(), *weight_blocks(*weights)] + [constant(a) for a in inputs[4:]]
    return run_kernel(
        kernel,
        "node_backward",
        1,
        inputs,
        specs,
        gradient_outputs(node_low.shape, order.shape[0], rows, width),
        [
            pltpu.VMEM((2 * latent, latent), BF16),
            pltpu.VMEM((latent, latent), BF16),
            pltpu.VMEM((hids, 2 * latent, latent // hids), F32),
            pltpu.VMEM((hids, latent, latent // hids), F32),
        ],
        12 * count * latent * latent,
    )


def dot(spec, left, right):
    return jnp.einsum(spec, left, right, preferred_element_type=F32)


def swap(values, axis, offset):
    return lax.ppermute(values, axis, [(i, i ^ offset) for i in range(lax.axis_size(axis))])


def bits_of(axis):
    return lax.axis_size(axis).bit_length() - 1


def own_bit(axis, bit):
    return (lax.axis_index(axis) >> bit) & 1


def all_bits():
    return [(axis, bit) for axis in ("node", "hid") for bit in reversed(range(bits_of(axis)))]


def ordered(own, mine, other):
    low = jnp.where(own == 0, mine, other)
    high = jnp.where(own == 0, other, mine)
    return low, high


def double_up(part, axis, bit, place):
    low, high = ordered(own_bit(axis, bit), part, swap(part, axis, 1 << bit))
    return jnp.stack([low, high], axis=place)


def halve_sum(parts, axis, bit, place):
    own = own_bit(axis, bit)
    sent = lax.dynamic_index_in_dim(parts, 1 - own, place, keepdims=False)
    kept = lax.dynamic_index_in_dim(parts, own, place, keepdims=False)
    return kept.astype(F32) + swap(sent.astype(BF16), axis, 1 << bit).astype(F32)


def places():
    node_ids = jnp.arange(lax.axis_size("node"), dtype=jnp.int32) ^ lax.axis_index("node")
    hid_ids = jnp.arange(lax.axis_size("hid"), dtype=jnp.int32) ^ lax.axis_index("hid")
    place = 0
    for step, (axis, bit) in enumerate(all_bits()):
        ids = node_ids[:, None] if axis == "node" else hid_ids[None, :]
        place = place + (((ids >> bit) & 1) << step)
    return place.reshape(-1)


def owners_of_places():
    place = jnp.arange(1 << len(all_bits()), dtype=jnp.int32)
    owner = {"node": lax.axis_index("node"), "hid": lax.axis_index("hid")}
    for step, (axis, bit) in enumerate(all_bits()):
        owner[axis] = owner[axis] ^ (((place >> step) & 1) << bit)
    return jnp.stack([owner["node"], owner["hid"]], axis=1).reshape(-1)


def after(value, *earlier):
    return lax.optimization_barrier((value, *earlier))[0]


def exchange(values, first_step, flips):
    hid_bits = bits_of("hid")
    mask = 0
    for k in range(flips.bit_length()):
        if (flips >> k) & 1:
            axis, bit = all_bits()[first_step + k]
            mask |= 1 << (bit if axis == "hid" else bit + hid_bits)
    total = 1 << len(all_bits())
    return lax.ppermute(values, ("node", "hid"), [(i, i ^ mask) for i in range(total)])


def rounds(begin, end):
    return [(step, min(step + 2, end)) for step in range(begin, end, 2)]


def gather_round(held, begin, end, *under):
    arrived = [exchange(held, begin, flips) for flips in range(1, 1 << (end - begin))]
    if under:
        arrived = lax.optimization_barrier((*arrived, *under))[: len(arrived)]
    return jnp.concatenate([held, *arrived], axis=0)


def split(total, count):
    size = total.shape[0] // count
    pieces = [total[i * size : (i + 1) * size] for i in range(count)]
    return [pieces[0]] + [piece.astype(BF16) for piece in pieces[1:]]


def scatter_round(pieces, begin, *under):
    arrived = [exchange(pieces[flips], begin, flips) for flips in range(1, len(pieces))]
    if under:
        arrived = lax.optimization_barrier((*arrived, *under))[: len(arrived)]
    total = pieces[0].astype(F32)
    for piece in arrived:
        total = total + piece.astype(F32)
    return total


def scatter_rest(total, end, *under):
    for begin, stop in reversed(rounds(0, end)):
        total = scatter_round(split(total, 1 << (stop - begin)), begin, *under)
    return total[0]


def sum_round(values, begin, end):
    terms = [values] + [exchange(values, begin, flips) for flips in range(1, 1 << (end - begin))]
    while len(terms) > 1:
        terms = [terms[i] + terms[i + 1] for i in range(0, len(terms), 2)]
    return terms[0]


def sum_everywhere(values):
    steps = len(all_bits())
    values = sum_round(values, steps - 1, steps)
    for begin, end in reversed(rounds(0, steps - 1)):
        values = sum_round(values, begin, end)
    return values


def to_neighbours(rows, halo_width):
    count = lax.axis_size("node")
    onward = [(i, (i + 1) % count) for i in range(count)]
    back = [(target, source) for source, target in onward]
    from_previous = lax.ppermute(rows[:, halo_width:], "node", onward)
    from_next = lax.ppermute(rows[:, :halo_width], "node", back)
    return jnp.concatenate([from_previous, from_next], axis=1)


def neighbour_swaps(rows, halo_width):
    count = lax.axis_size("node")
    even = lax.axis_index("node") % 2 == 0
    to_previous, to_next = rows[:, :halo_width], rows[:, halo_width:]
    one = [(i, i ^ 1) for i in range(count)]
    two = [(i, (((i + 1) ^ 1) - 1) % count) for i in range(count)]
    first = lax.ppermute(jnp.where(even, to_next, to_previous), "node", one)
    second = lax.ppermute(jnp.where(even, to_previous, to_next), "node", two)
    return first, second


def from_neighbours(first, second):
    even = lax.axis_index("node") % 2 == 0
    return jnp.concatenate(
        [jnp.where(even, second, first), jnp.where(even, first, second)], axis=1
    )


def adam_terms(weight, grad, first, second, decay):
    first_new = BETA_FIRST * first + (1.0 - BETA_FIRST) * grad
    second_new = BETA_SECOND * second + (1.0 - BETA_SECOND) * grad * grad
    update = first_new / (jnp.sqrt(second_new) + ADAM_EPS) + decay * weight
    return (first_new, second_new, update)


def pack_shards(first, second):
    return jnp.concatenate([first, second.T], axis=0).astype(BF16)


def adam_terms(weight, grad, first, second, decay):
    first_new = BETA_FIRST * first + (1.0 - BETA_FIRST) * grad
    second_new = BETA_SECOND * second + (1.0 - BETA_SECOND) * grad * grad
    update = first_new / (jnp.sqrt(second_new) + ADAM_EPS) + decay * weight
    return (first_new, second_new, update)


def per_device(
    node_in,
    edge_in,
    cotangent,
    ocean_mask,
    present_mask,
    valid_counts,
    send_slot,
    recv_local,
    halo_lists,
    edge_first,
    edge_second,
    node_first,
    node_second,
    edge_first_m,
    edge_second_m,
    node_first_m,
    node_second_m,
    edge_first_v,
    edge_second_v,
    node_first_v,
    node_second_v,
    small_params,
    small_m,
    small_v,
    learn_rate,
):
    hid_count = lax.axis_size("hid")
    hid_index = lax.axis_index("hid")
    node_total, sample_count, latent = node_in.shape
    edge_part = edge_in.shape[0] // hid_count
    node_part = node_total // hid_count
    halo_width = halo_lists.shape[1]
    table_total = node_total + 2 * halo_width
    sample_half, edge_half = hid_index >> 1, hid_index & 1
    samples = sample_count // 2
    nodes, hids = lax.axis_size("node"), hid_count
    first_rows = edge_first.shape[1]
    second_rows = edge_second.shape[2]
    node_rows = node_first.shape[1] + second_rows
    width = edge_first.shape[2]

    order, owners = places(), owners_of_places()
    steps = len(all_bits())

    def layer_shards(depth, *earlier):
        shards = (node_first[depth], node_second[depth], edge_first[depth], edge_second[depth])
        if earlier:
            shards = after(shards, *earlier)
        return jnp.concatenate([pack_shards(*shards[:2]), pack_shards(*shards[2:])], axis=0)[None]

    def parted(held):
        return held[:, :node_rows], held[:, node_rows:]

    layer_zero = layer_shards(0)
    for begin, end in rounds(0, steps - 3):
        layer_zero = gather_round(layer_zero, begin, end)
    setup = layer_zero
    layer_zero = gather_round(layer_zero, steps - 3, steps - 2)
    node_zero, edge_zero = parted(layer_zero)
    layer_one = layer_shards(1, setup)
    layer_one = after(layer_one, edge_zero)
    z_rounds = rounds(0, steps - 3)
    for begin, end in z_rounds[:-1]:
        layer_one = gather_round(layer_one, begin, end)
    halo_gate = edge_zero
    masters = (edge_first, edge_second, node_first, node_second)
    weight_local = jnp.stack(
        [jnp.sum(matrix * matrix, axis=(1, 2)) for matrix in after(masters, setup)], axis=1
    )
    def edge_blocks(whole):
        return ((whole, first_rows, 0), (whole, second_rows, first_rows // second_rows))

    def own_edges(values):
        return lax.dynamic_index_in_dim(
            values.reshape(2, 2, edge_part, *values.shape[1:]), edge_half, 1, keepdims=False
        ).reshape(2 * edge_part, *values.shape[1:])

    def own_nodes(values):
        return lax.dynamic_index_in_dim(
            values.reshape(samples, 2, 2, node_part, latent), edge_half, 2, keepdims=False
        ).reshape(samples, 2 * node_part, latent)

    def own_samples(values):
        return lax.dynamic_slice_in_dim(values, sample_half * samples, samples, 1)

    def own_rows_exchanged(values):
        quarters = jnp.moveaxis(values.reshape(samples, 2, 2, node_part, latent), 0, 3)
        quarters = lax.dynamic_index_in_dim(quarters, edge_half, 1, keepdims=False)
        sent = lax.dynamic_index_in_dim(quarters, 1 - sample_half, 0, keepdims=False)
        kept = lax.dynamic_index_in_dim(quarters, sample_half, 0, keepdims=False)
        return kept, swap(sent, "hid", 2)

    def all_samples(kept, arrived):
        return jnp.concatenate(ordered(sample_half, kept, arrived), axis=1)

    send_slot, recv_local, halo_lists, node_in, edge_in = lax.optimization_barrier(
        (send_slot, recv_local, halo_lists, node_in, edge_in, setup)
    )[:5]
    sender = own_edges(send_slot)
    receiver = own_edges(recv_local)
    node_ids, table_ids = jnp.arange(node_total), jnp.arange(table_total)
    at_receiver = (receiver[:, None] == node_ids[None, :]).astype(BF16)
    at_both = jnp.concatenate(
        [(sender[:, None] == table_ids[None, :]).astype(BF16), at_receiver], axis=1
    )
    at_nodes = (node_ids[:, None] == receiver[None, :]).astype(BF16)
    at_both_t = jnp.concatenate(
        [(table_ids[:, None] == sender[None, :]).astype(BF16), at_nodes], axis=0
    )
    at_halo = (halo_lists.reshape(-1)[:, None] == node_ids[None, :]).astype(BF16)
    mask = ((node_ids // node_part) % 2 == edge_half).astype(F32)
    mask = jnp.tile(mask, samples)[:, None]

    node_low = jnp.transpose(own_samples(node_in), (1, 0, 2))
    edge_in_own = own_edges(edge_in)
    halo_rows = dot("hn,snl->shl", at_halo, node_low).astype(BF16)
    node_low_zero = node_low
    halo_rows = neighbour_swaps(after(halo_rows, halo_gate), halo_width)
    begin, end = z_rounds[-1]
    arrived = [exchange(layer_one, begin, flips) for flips in range(1, 1 << (end - begin))]
    constants = (at_receiver, at_both, at_nodes, at_both_t, at_halo, mask, order, owners)
    edge_arrived, first, second, weight_local, constants, *arrived = lax.optimization_barrier(
        (exchange(edge_zero, steps - 2, 1), *halo_rows, weight_local, constants, *arrived)
    )
    at_receiver, at_both, at_nodes, at_both_t, at_halo, mask, order, owners = constants
    halo_rows = from_neighbours(first, second)
    edge_zero = jnp.concatenate([edge_zero, edge_arrived], axis=0)
    layer_one = jnp.concatenate([layer_one, *arrived], axis=0)
    node_zero = after(node_zero, edge_zero)
    edge_zero = (edge_zero, exchange(edge_zero, steps - 1, 1))
    table_zero = jnp.concatenate([node_low, halo_rows], axis=1)
    pre_zero, act_zero, normed_zero, inverse_zero, edge_state, edge_low, pooled = edge_forward(
        order,
        *edge_blocks(edge_zero),
        table_zero,
        edge_in_own[None],
        edge_in_own[None],
        at_both,
        at_nodes,
        small_params[0],
        node_total,
        False,
    )
    pooled, *arrived = lax.optimization_barrier(
        (pooled, exchange(node_zero, steps - 2, 1), exchange(layer_one, steps - 3, 1))
    )
    node_zero = jnp.concatenate([node_zero, arrived[0]], axis=0)
    node_zero = (node_zero, exchange(node_zero, steps - 1, 1))
    layer_one = jnp.concatenate([layer_one, arrived[1]], axis=0)
    node_one, edge_one = parted(layer_one)
    other = after(swap(pooled, "hid", 1), edge_one)
    (
        pooled_zero,
        node_pre,
        node_act,
        node_normed,
        node_inverse,
        node_state,
        node_low,
        halo_rows,
    ) = node_pass(
        order,
        None,
        (node_zero, node_rows, 0),
        nodes,
        node_low_zero,
        node_low_zero,
        (pooled, other),
        small_params[0],
        at_halo,
        None,
        None,
        None,
    )
    halo_rows = to_neighbours(halo_rows, halo_width)
    arrived, halo_rows = lax.optimization_barrier((exchange(edge_one, steps - 2, 1), halo_rows))
    edge_one = jnp.concatenate([edge_one, arrived], axis=0)
    node_one = after(node_one, edge_one)
    edge_one = (edge_one, exchange(edge_one, steps - 1, 1))

    valid_mask = (ocean_mask[:, None] * present_mask).astype(BF16)
    masked = after(cotangent, pooled) * valid_mask[:, :, None]
    sent = lax.dynamic_slice_in_dim(masked, (1 - sample_half) * samples, samples, 1)
    scaling = node_total * lax.axis_size("node") / valid_counts.astype(F32)
    scaling = lax.dynamic_slice_in_dim(scaling, sample_half * samples, samples, 0)
    scaling = scaling[:, None, None]

    node_low_one = node_low
    table_one = jnp.concatenate([node_low, halo_rows], axis=1)
    pre_one, act_one, normed_one, inverse_one, pooled = edge_forward(
        order,
        *edge_blocks(edge_one),
        table_one,
        edge_low,
        edge_state,
        at_both,
        at_nodes,
        small_params[1],
        node_total,
        True,
    )
    pooled, arrived, cotangent_other = lax.optimization_barrier(
        (pooled, exchange(node_one, steps - 2, 1), swap(sent, "hid", 2))
    )
    node_one = jnp.concatenate([node_one, arrived], axis=0)
    masked = jnp.stack(ordered(sample_half, own_samples(masked), cotangent_other), axis=0)
    masked = double_up(masked, "hid", 0, 1).reshape(node_total, samples, latent)
    target = jnp.transpose(masked, (1, 0, 2))
    node_one = (node_one, exchange(node_one, steps - 1, 1))
    node_low, pooled_grad, node_grad, kept, sent, node_minor_one = node_pass(
        order,
        owners,
        (node_one, node_rows, 0),
        nodes,
        node_low_one,
        node_state,
        (pooled, swap(pooled, "hid", 1)),
        small_params[1],
        None,
        target,
        scaling,
        mask,
    )

    def from_edges(partial, returned):
        return partial + dot("hn,shl->snl", at_halo, returned)

    low, hidden_low, at_rows, partial, returned, edge_grad, edge_minor_one = edge_backward(
        order,
        *edge_blocks(edge_one),
        pooled_grad,
        None,
        normed_one,
        inverse_one,
        pre_one,
        at_receiver,
        at_both_t,
        small_params[1, 2:3],
        True,
        node_total,
    )
    low, *node_out = lax.optimization_barrier((low, *own_rows_exchanged(node_low)))
    node_out = all_samples(*node_out)
    chain_one = edge_weight_grads(
        owners,
        edge_low,
        table_one,
        hidden_low,
        at_rows,
        low,
        act_one,
        node_total,
        nodes,
        width,
        [kept, sent],
    )
    *returned, kept, sent = lax.optimization_barrier(
        (*neighbour_swaps(returned, halo_width), *chain_one)
    )
    returned, chain_one = from_neighbours(*returned), (kept, sent)
    partial = from_edges(partial, returned)
    chain_one = split(scatter_round(chain_one, steps - 1), 2)
    other, *chain_one = lax.optimization_barrier((swap(partial.astype(BF16), "hid", 1), *chain_one))
    pooled_grad, node_grad, kept, sent, node_minor_zero = node_backward(
        order,
        owners,
        (node_zero, node_rows, 0),
        nodes,
        (node_grad, partial, other),
        node_low_zero,
        pooled_zero,
        node_pre,
        node_act,
        node_normed,
        node_inverse,
        small_params[0],
        mask,
    )
    low, hidden_low, at_rows, partial, returned, edge_input_grad, edge_minor_zero, hidden_sum = (
        edge_backward(
            order,
            *edge_blocks(edge_zero),
            pooled_grad,
            edge_grad,
            normed_zero,
            inverse_zero,
            pre_zero,
            at_receiver,
            at_both_t,
            small_params[0, 2:3],
            False,
            node_total,
        )
    )
    chain_one = split(scatter_round(chain_one, steps - 2, low), 2)
    chain_zero = split(scatter_round((kept, sent), steps - 1, low), 2)
    low = after(low, *chain_one, *chain_zero)
    chain_edge = edge_weight_grads(
        owners,
        edge_in_own,
        table_zero,
        hidden_sum,
        at_rows,
        low,
        act_zero,
        node_total,
        nodes,
        width,
        None,
    )
    kept, sent, one_arrived, zero_arrived, *returned = lax.optimization_barrier(
        (
            *chain_edge,
            exchange(chain_one[1], steps - 3, 1),
            exchange(chain_zero[1], steps - 2, 1),
            *neighbour_swaps(returned, halo_width),
        )
    )
    chain_one = chain_one[0].astype(F32) + one_arrived.astype(F32)
    chain_zero = split(chain_zero[0].astype(F32) + zero_arrived.astype(F32), 2)
    edge_arrived = exchange(sent, steps - 1, 1)
    kept, sent = split(kept.astype(F32) + edge_arrived.astype(F32), 2)
    zero_arrived = after(exchange(chain_zero[1], steps - 3, 1), sent)
    returned = after(returned, sent)
    chain_zero = chain_zero[0].astype(F32) + zero_arrived.astype(F32)
    for begin, end in reversed(z_rounds[1:]):
        chain_one = scatter_round(split(chain_one, 1 << (end - begin)), begin)
        chain_zero = scatter_round(split(chain_zero, 1 << (end - begin)), begin)
    begin, end = z_rounds[0]
    chain_one = split(chain_one, 1 << (end - begin))
    chain_zero = split(chain_zero, 1 << (end - begin))
    partial = from_edges(partial, from_neighbours(*returned))
    arrived, edge_input_grad, other, chain_zero, *others = lax.optimization_barrier(
        (
            exchange(sent, steps - 2, 1),
            edge_input_grad,
            swap(partial.astype(BF16), "hid", 1),
            chain_zero,
            *[exchange(chain_one[flips], begin, flips) for flips in range(1, len(chain_one))],
        )
    )
    layer_one_grads = chain_one[0]
    for piece in others:
        layer_one_grads = layer_one_grads + piece.astype(F32)
    layer_one_grads = layer_one_grads[0]
    chain_edge = split(kept + arrived.astype(F32), 2)
    arrived, *others = lax.optimization_barrier(
        (
            exchange(chain_edge[1], steps - 3, 1),
            *[exchange(chain_zero[flips], begin, flips) for flips in range(1, len(chain_zero))],
        )
    )
    node_zero_grads = chain_zero[0]
    for piece in others:
        node_zero_grads = node_zero_grads + piece.astype(F32)
    node_zero_grads = node_zero_grads[0]
    chain_edge = chain_edge[0] + arrived.astype(F32)
    halves = edge_input_grad.reshape(2, edge_part, latent)
    sent = lax.dynamic_index_in_dim(halves, 1 - sample_half, 0, keepdims=False).astype(BF16)
    kept = lax.dynamic_index_in_dim(halves, sample_half, 0, keepdims=False)
    node_grad = node_grad + (partial + other.astype(F32))
    grad_node = own_rows_exchanged(node_grad.astype(BF16))
    edge_zero_grads = scatter_rest(chain_edge, steps - 3)
    edge_zero_grads, arrived, *grad_node = lax.optimization_barrier(
        (edge_zero_grads, swap(sent, "hid", 2), *grad_node)
    )
    edge_input_grad = kept + arrived.astype(F32)
    grad_node = all_samples(*grad_node)

    node_one_grads, edge_one_grads = layer_one_grads[:node_rows], layer_one_grads[node_rows:]
    node_first_rows = node_rows - second_rows
    grads = [
        jnp.stack([edge_zero_grads[:first_rows], edge_one_grads[:first_rows]]),
        jnp.stack([edge_zero_grads[first_rows:].T, edge_one_grads[first_rows:].T]),
        jnp.stack([node_zero_grads[:node_first_rows], node_one_grads[:node_first_rows]]),
        jnp.stack([node_zero_grads[node_first_rows:].T, node_one_grads[node_first_rows:].T]),
    ]
    firsts = (edge_first_m, edge_second_m, node_first_m, node_second_m)
    seconds = (edge_first_v, edge_second_v, node_first_v, node_second_v)
    moment_list = [
        adam_terms(masters[place], grads[place], firsts[place], seconds[place], WEIGHT_DECAY)
        for place in range(4)
    ]
    update_local = jnp.stack(
        [jnp.sum(entry[2] * entry[2], axis=(1, 2)) for entry in moment_list], axis=1
    )
    squares = jnp.concatenate([weight_local.reshape(1, -1), update_local.reshape(1, -1)], axis=1)
    minor_packed = jnp.concatenate(
        [edge_minor_zero, node_minor_zero, edge_minor_one, node_minor_one]
        + [jnp.pad(squares, ((0, 0), (0, latent - squares.size)))],
        axis=0,
    )
    minor_packed = sum_everywhere(minor_packed)
    minor_total = minor_packed[: 8 * LAYERS].reshape(small_params.shape)
    squares = minor_packed[8 * LAYERS, : squares.size].reshape(2, *weight_local.shape)
    weight_squares, update_squares = squares[0], squares[1]
    weight_norm = jnp.sqrt(weight_squares)
    update_norm = jnp.sqrt(update_squares)
    new_weights = []
    for position in range(4):
        ratio = weight_norm[:, position] / update_norm[:, position]
        new_weights.append(
            masters[position] - learn_rate[0] * ratio[:, None, None] * moment_list[position][2]
        )
    small_first, small_second, small_update = adam_terms(
        small_params, minor_total, small_m, small_v, 0.0
    )
    small_wnorm = jnp.sqrt(jnp.sum(small_params * small_params, axis=2))
    small_unorm = jnp.sqrt(jnp.sum(small_update * small_update, axis=2))
    small_new = (
        small_params - learn_rate[0] * (small_wnorm / small_unorm)[:, :, None] * small_update
    )
    norms = jnp.stack(
        [
            jnp.concatenate([weight_norm, small_wnorm], axis=1),
            jnp.concatenate([update_norm, small_unorm], axis=1),
        ],
        axis=2,
    )
    return (
        node_out,
        grad_node,
        edge_input_grad.astype(BF16),
        *new_weights,
        *[entry[0] for entry in moment_list],
        *[entry[1] for entry in moment_list],
        *[weight.astype(BF16) for weight in new_weights],
        small_new,
        small_first,
        small_second,
        norms,
    )


def solution(mesh):
    whole = P()
    rows = P(None, "node", "hid")
    columns = P(None, "hid", "node")
    matrices = (rows, columns, rows, columns)
    in_specs = (
        P("node", None, None),
        P("node", None),
        P(("node", "hid"), None, None),
        P(("node", "hid")),
        P(("node", "hid"), None),
        P(),
        P("node"),
        P("node"),
        P("node", None),
        *matrices,
        *matrices,
        *matrices,
        whole,
        whole,
        whole,
        whole,
    )
    out_specs = (
        P(("node", "hid"), None, None),
        P(("node", "hid"), None, None),
        P(("node", "hid"), None),
        *matrices,
        *matrices,
        *matrices,
        *matrices,
        whole,
        whole,
        whole,
        whole,
    )
    return jax.shard_map(
        per_device, mesh=mesh, in_specs=in_specs, out_specs=out_specs, check_vma=False
    )
```

```python
import jax
import jax.numpy as jnp
from jax import lax
from jax.experimental import pallas as pl
from jax.experimental.pallas import tpu as pltpu
from jax.sharding import PartitionSpec as P

LAYERS = 2


NORM_EPS = 1e-05
BETA_FIRST = 0.5
BETA_SECOND = 0.5
ADAM_EPS = 1e-06
WEIGHT_DECAY = 0.01
BF16 = jnp.bfloat16
F32 = jnp.float32
VMEM_BYTES = 56 * 1024 * 1024


def matmul(left, right):
    return lax.dot_general(left, right, (((1,), (0,)), ((), ())), preferred_element_type=F32)


def matmul_nt(left, right):
    return lax.dot_general(left, right, (((1,), (1,)), ((), ())), preferred_element_type=F32)


def matmul_tn(left, right):
    return lax.dot_general(left, right, (((0,), (0,)), ((), ())), preferred_element_type=F32)


def sigmoid(values):
    return 0.5 + 0.5 * jnp.tanh(0.5 * values)


def silu_slope(values):
    gate = sigmoid(values)
    return gate * (1.0 + values * (1.0 - gate))


def norm_forward(values):
    center = values - jnp.mean(values, axis=-1, keepdims=True)
    spread = jnp.mean(center * center, axis=-1, keepdims=True)
    inverse = lax.rsqrt(spread + NORM_EPS)
    return center * inverse, inverse


def norm_backward(upstream, normed, inverse, gain_row):
    scaled = upstream * gain_row
    return inverse * (
        scaled
        - jnp.mean(scaled, axis=-1, keepdims=True)
        - normed * jnp.mean(scaled * normed, axis=-1, keepdims=True)
    )


def column_sum(values):
    return jnp.sum(values, axis=0, keepdims=True)


def assemble(source, order, rows, offset, target):
    own, arrived = source
    half, _, width = own.shape
    nodes, hids = target.shape[0] // rows, target.shape[1] // width
    for i in range(nodes):
        for j in range(hids):
            place = order[i * hids + j]
            index = jnp.where(place < half, place, place - half)
            target[i * rows : (i + 1) * rows, j * width : (j + 1) * width] = jnp.where(
                place < half,
                own[index, offset : offset + rows, :],
                arrived[index, offset : offset + rows, :],
            )


def store(target, begin, values):
    rows, width = values.shape[0], target.shape[2]
    for j in range(target.shape[0]):
        target[j, begin : begin + rows] = values[:, j * width : (j + 1) * width]


def add(target, begin, values):
    rows, width = values.shape[0], target.shape[2]
    for j in range(target.shape[0]):
        target[j, begin : begin + rows] += values[:, j * width : (j + 1) * width]


def pack(values, owners, rows, offset, kept, sent):
    half = kept.shape[0]

    def one(index, carry):
        for target, place in ((kept, index), (sent, index + half)):
            begin = pl.multiple_of(owners[2 * place] * rows, rows)
            target[index, offset : offset + rows, :] = values[
                owners[2 * place + 1], pl.ds(begin, rows), :
            ].astype(BF16)
        return carry

    lax.fori_loop(0, half, one, 0)


def per_sample(array):
    block = (1,) + array.shape[1:]
    return pl.BlockSpec(block, lambda s: (s,) + (0,) * (len(block) - 1))


def constant(array):
    return pl.BlockSpec(array.shape, lambda s: (0,) * len(array.shape))


def weight_blocks(halves, rows, place):
    blocks, _, width = halves[0].shape
    return [pl.BlockSpec((blocks, rows, width), lambda s: (0, place, 0)) for _ in halves]


def in_scalars():
    return pl.BlockSpec(memory_space=pltpu.SMEM)


def shape_of(shape, dtype):
    return jax.ShapeDtypeStruct(shape, dtype)


def run_kernel(kernel, name, samples, inputs, in_specs, outputs, scratch, flops):
    moved = sum(a.size * a.dtype.itemsize for a in inputs) + sum(
        shape.size * shape.dtype.itemsize for shape, _ in outputs
    )
    return pl.pallas_call(
        kernel,
        name=name,
        grid=(samples,),
        in_specs=in_specs,
        out_specs=[spec for _, spec in outputs],
        out_shape=[shape for shape, _ in outputs],
        scratch_shapes=scratch,
        compiler_params=pltpu.CompilerParams(
            dimension_semantics=("arbitrary",), vmem_limit_bytes=VMEM_BYTES
        ),
        cost_estimate=pl.CostEstimate(flops=4 * flops, bytes_accessed=moved, transcendentals=0),
    )(*inputs)


def sampled(shape, dtype):
    result = shape_of(shape, dtype)
    return (result, per_sample(result))


def shared(shape, dtype):
    result = shape_of(shape, dtype)
    return (result, constant(result))


def edge_forward(order, first, second, table, edge_low, edge_state, at_both, at_nodes, params, node_total, last):
    samples, table_total, latent = table.shape
    edges = edge_low.shape[1]
    alike = edge_low.shape[0] == 1

    def kernel(order, w1, w1x, w2, w2x, table, low, state, both, nodes, params, pre, act, normed, inverse, *rest):
        if last:
            pooled, w1s, w2s, projected = rest
        else:
            new_state, new_low, pooled, w1s, w2s, projected = rest

        @pl.when(pl.program_id(0) == 0)
        def _():
            assemble((w1, w1x), order, w1.shape[1], 0, w1s)
            assemble((w2, w2x), order, w2.shape[1], 0, w2s)

        rows = table[0]
        projected[:table_total] = matmul(rows, w1s[latent : 2 * latent]).astype(BF16)
        projected[table_total:] = matmul(rows[:node_total], w1s[2 * latent :]).astype(BF16)
        hidden = matmul(low[0], w1s[:latent]) + matmul(both[...], projected[...]) + params[0:1]
        pre[0] = hidden.astype(BF16)
        active = (hidden * sigmoid(hidden)).astype(BF16)
        act[0] = active
        output = matmul_nt(active, w2s[...]) + params[1:2]
        scaled, scale = norm_forward(output)
        normed[0] = scaled.astype(BF16)
        inverse[0] = scale
        state_new = state[0].astype(F32) + scaled * params[2:3] + params[3:4]
        low_new = state_new.astype(BF16)
        if not last:
            new_state[0] = state_new
            new_low[0] = low_new
        pooled[0] = matmul(nodes[...], low_new).astype(BF16)

    wide = (samples, edges, latent)
    outputs = [sampled(wide, BF16), sampled(wide, BF16), sampled(wide, BF16), sampled((samples, edges, 1), F32)]
    if not last:
        outputs += [sampled(wide, F32), sampled(wide, BF16)]
    outputs += [sampled((samples, node_total, latent), BF16)]
    of_edges = constant if alike else per_sample
    return run_kernel(
        kernel,
        "edge_forward",
        samples,
        [order, *first[0], *second[0], table, edge_low, edge_state, at_both, at_nodes, params],
        [
            in_scalars(),
            *weight_blocks(*first),
            *weight_blocks(*second),
            per_sample(table),
            of_edges(edge_low),
            of_edges(edge_state),
            constant(at_both),
            constant(at_nodes),
            constant(params),
        ],
        outputs,
        [
            pltpu.VMEM((3 * latent, latent), BF16),
            pltpu.VMEM((latent, latent), BF16),
            pltpu.VMEM((at_both.shape[1], latent), BF16),
        ],
        2 * samples * edges * latent * (3 * latent + at_both.shape[1]),
    )


def edge_backward(order, first, second, pooled_grad, edge_grad, normed, inverse, pre, at_receiver, at_both_t, gain, last, node_total):
    samples, edges, latent = normed.shape
    at_total = at_both_t.shape[0]
    table_total = at_total - node_total

    def kernel(order, w1, w1x, w2, w2x, upstream, *rest):
        if not last:
            later, rest = rest[0], rest[1:]
        normed, inverse, pre, receiver, both_t, gain, low, hidden_low, at_rows, partial, returned, grad_out, minor = rest[:13]
        if last:
            w1s, w2s = rest[13:]
        else:
            hidden_sum, w1s, w2s, hidden_acc = rest[13:]
        step = pl.program_id(0)

        @pl.when(step == 0)
        def _():
            assemble((w1, w1x), order, w1.shape[1], 0, w1s)
            assemble((w2, w2x), order, w2.shape[1], 0, w2s)
            minor[...] = jnp.zeros_like(minor)

        grad = matmul(receiver[...], upstream[0])
        if not last:
            grad = grad + later[0]
        scaled = normed[0].astype(F32)
        output_grad = norm_backward(grad, scaled, inverse[0], gain[0:1]).astype(BF16)
        low[0] = output_grad
        act_grad = matmul(output_grad, w2s[...])
        pre_grad = (act_grad * silu_slope(pre[0].astype(F32))).astype(BF16)
        hidden_low[0] = pre_grad
        minor[0:1] += column_sum(pre_grad.astype(F32))
        minor[1:2] += column_sum(output_grad.astype(F32))
        minor[2:3] += column_sum(grad * scaled)
        minor[3:4] += column_sum(grad)
        at_rows[0] = matmul(both_t[...], pre_grad).astype(BF16)
        send = w1s[latent : 2 * latent]
        partial[0] = matmul_nt(at_rows[0, :node_total], send) + matmul_nt(
            at_rows[0, table_total:], w1s[2 * latent :]
        )
        returned[0] = matmul_nt(at_rows[0, node_total:table_total], send).astype(BF16)
        if last:
            grad_out[0] = grad + matmul_nt(pre_grad, w1s[:latent])
        else:

            @pl.when(step == 0)
            def _():
                grad_out[...] = grad
                hidden_acc[...] = pre_grad.astype(F32)

            @pl.when(step > 0)
            def _():
                grad_out[...] += grad
                hidden_acc[...] += pre_grad.astype(F32)

            @pl.when(step == samples - 1)
            def _():
                total = hidden_acc[...].astype(BF16)
                hidden_sum[...] = total
                grad_out[...] += matmul_nt(total, w1s[:latent])

    wide = (samples, edges, latent)
    outputs = [
        sampled(wide, BF16),
        sampled(wide, BF16),
        sampled((samples, at_total, latent), BF16),
        sampled((samples, node_total, latent), F32),
        sampled((samples, table_total - node_total, latent), BF16),
        sampled(wide, F32) if last else shared((edges, latent), F32),
        shared((4, latent), F32),
    ]
    scratch = [pltpu.VMEM((3 * latent, latent), BF16), pltpu.VMEM((latent, latent), BF16)]
    inputs = [order, *first[0], *second[0], pooled_grad]
    specs = [in_scalars(), *weight_blocks(*first), *weight_blocks(*second), per_sample(pooled_grad)]
    if not last:
        outputs.append(shared((edges, latent), BF16))
        scratch.append(pltpu.VMEM((edges, latent), F32))
        inputs.append(edge_grad)
        specs.append(per_sample(edge_grad))
    inputs += [normed, inverse, pre, at_receiver, at_both_t, gain]
    specs += [
        per_sample(normed),
        per_sample(inverse),
        per_sample(pre),
        constant(at_receiver),
        constant(at_both_t),
        constant(gain),
    ]
    return run_kernel(
        kernel,
        "edge_backward",
        samples,
        inputs,
        specs,
        outputs,
        scratch,
        2 * samples * edges * latent * (2 * latent + 2 * at_total),
    )


def edge_weight_grads(owners, edge_low, table, hidden_low, at_rows, low, act, node_total, nodes, width, packed_before):
    samples, table_total, latent = table.shape
    alike = edge_low.ndim == 2
    first_rows, second_rows = 3 * latent // nodes, latent // nodes
    offset = 0 if packed_before is None else packed_before[0].shape[1]
    blocks, hids = owners.shape[0] // 2, latent // width

    def kernel(owners, edge_low, table, hidden_low, at_rows, low, act, *rest):
        before, rest = rest[:-4], rest[-4:]
        kept, sent, first, second = rest
        step = pl.program_id(0)

        @pl.when(step == 0)
        def _():
            first[...] = jnp.zeros_like(first)
            second[...] = jnp.zeros_like(second)
            for source, target in zip(before, (kept, sent)):
                target[:, :offset, :] = source[...]
            if alike:
                add(first, 0, matmul_tn(edge_low[...], hidden_low[...]))

        if not alike:
            add(first, 0, matmul_tn(edge_low[0], hidden_low[0]))
        add(first, latent, matmul_tn(table[0], at_rows[0, :table_total]))
        add(first, 2 * latent, matmul_tn(table[0, :node_total], at_rows[0, table_total:]))
        add(second, 0, matmul_tn(low[0], act[0]))

        @pl.when(step == samples - 1)
        def _():
            pack(first, owners, first_rows, offset, kept, sent)
            pack(second, owners, second_rows, offset + first_rows, kept, sent)

    of_edges = constant if alike else per_sample
    inputs = [owners, edge_low, table, hidden_low, at_rows, low, act]
    specs = [in_scalars(), of_edges(edge_low), per_sample(table), of_edges(hidden_low), per_sample(at_rows), per_sample(low), per_sample(act)]
    if packed_before is not None:
        inputs += packed_before
        specs += [constant(a) for a in packed_before]
    return run_kernel(
        kernel,
        "edge_weight_grads",
        samples,
        inputs,
        specs,
        [shared((blocks // 2, offset + first_rows + second_rows, width), BF16)] * 2,
        [pltpu.VMEM((hids, 3 * latent, width), F32), pltpu.VMEM((hids, latent, width), F32)],
        4 * low.size * latent,
    )


def node_pass(order, owners, weights, nodes, node_low, state, pooled_pair, params, at_halo, target, scaling, mask):
    samples, node_total, latent = node_low.shape
    halves, rows, place = weights
    width = halves[0].shape[2]
    second_rows, hids = latent // nodes, latent // width
    first_rows = rows - second_rows
    count = samples * node_total
    last = target is not None

    def kernel(order, *rest):
        if last:
            owners, rest = rest[0], rest[1:]
        w, wx, node_low, state, pooled_own, pooled_other, params, *rest = rest
        if last:
            target, scaling, mask, new_low, upstream, input_grad, kept, sent, minor, w1s, w2s, first, second = rest
        else:
            at_halo, pooled_out, pre, act, normed, inverse, new_state, new_low, halo, w1s, w2s = rest
        assemble((w, wx), order, first_rows, 0, w1s)
        assemble((w, wx), order, second_rows, first_rows, w2s)
        rows_low = node_low[...].reshape(count, latent)
        pooled = (pooled_own[...].astype(F32) + pooled_other[...].astype(F32)).astype(BF16)
        pooled = pooled.reshape(count, latent)
        hidden = matmul(rows_low, w1s[:latent]) + matmul(pooled, w1s[latent:]) + params[4:5]
        active = (hidden * sigmoid(hidden)).astype(BF16)
        output = matmul_nt(active, w2s[...]) + params[5:6]
        scaled, scale = norm_forward(output)
        state_new = state[...].astype(F32).reshape(count, latent) + scaled * params[6:7] + params[7:8]
        low_new = state_new.astype(BF16).reshape(new_low.shape)
        new_low[...] = low_new
        if not last:
            pooled_out[...] = pooled
            pre[...] = hidden.astype(BF16)
            act[...] = active
            normed[...] = scaled.astype(BF16)
            inverse[...] = scale
            new_state[...] = state_new.reshape(new_state.shape)
            for s in range(samples):
                halo[s] = matmul(at_halo[...], new_low[s]).astype(BF16)
        else:
            grad = (target[...].astype(F32) * scaling[...]).reshape(count, latent)
            node_gradients(
                grad, scaled, scale, hidden, active, rows_low, pooled, params, mask,
                w1s, w2s, first, second, upstream, input_grad, kept, sent, minor, owners, first_rows, second_rows,
            )

    shape = node_low.shape
    inputs = [*halves, node_low, state, *pooled_pair, params]
    scratch = [pltpu.VMEM((2 * latent, latent), BF16), pltpu.VMEM((latent, latent), BF16)]
    if last:
        inputs += [target, scaling, mask]
        outputs = [shared(shape, BF16), *gradient_outputs(shape, order.shape[0], rows, width)]
        scratch += [pltpu.VMEM((hids, 2 * latent, latent // hids), F32), pltpu.VMEM((hids, latent, latent // hids), F32)]
    else:
        inputs += [at_halo]
        outputs = [
            shared((count, latent), BF16),
            shared((count, latent), BF16),
            shared((count, latent), BF16),
            shared((count, latent), BF16),
            shared((count, 1), F32),
            shared(shape, F32),
            shared(shape, BF16),
            shared((samples, at_halo.shape[0], latent), BF16),
        ]
    tables = [order, owners] if last else [order]
    specs = [in_scalars() for _ in tables] + weight_blocks(*weights) + [constant(a) for a in inputs[2:]]
    inputs = tables + inputs
    return run_kernel(kernel, "node_pass", 1, inputs, specs, outputs, scratch, 6 * count * latent * latent * (3 if last else 1))


def gradient_outputs(shape, blocks, rows, width):
    return [
        shared(shape, BF16),
        shared(shape, F32),
        shared((blocks // 2, rows, width), BF16),
        shared((blocks // 2, rows, width), BF16),
        shared((4, shape[-1]), F32),
    ]


def node_gradients(
    grad, scaled, scale, hidden, active, rows_low, pooled, params, mask,
    w1s, w2s, first, second, upstream, input_grad, kept, sent, minor, owners, first_rows, second_rows,
):
    latent = w2s.shape[0]
    output_grad = norm_backward(grad, scaled, scale, params[6:7]).astype(BF16)
    pre_grad = (matmul(output_grad, w2s[...]) * silu_slope(hidden)).astype(BF16)
    upstream[...] = matmul_nt(pre_grad, w1s[latent:]).astype(BF16).reshape(upstream.shape)
    input_grad[...] = (grad + matmul_nt(pre_grad, w1s[:latent])).reshape(input_grad.shape)
    chosen = mask[...] > 0.5
    output_mine = jnp.where(chosen, output_grad.astype(F32), 0.0)
    pre_mine = jnp.where(chosen, pre_grad.astype(F32), 0.0)
    grad_mine = jnp.where(chosen, grad, 0.0)
    minor[0:1] = column_sum(pre_mine)
    minor[1:2] = column_sum(output_mine)
    minor[2:3] = column_sum(grad_mine * scaled)
    minor[3:4] = column_sum(grad_mine)
    pre_mine = pre_mine.astype(BF16)
    store(first, 0, matmul_tn(rows_low, pre_mine))
    store(first, latent, matmul_tn(pooled, pre_mine))
    store(second, 0, matmul_tn(output_mine.astype(BF16), active))
    pack(first, owners, first_rows, 0, kept, sent)
    pack(second, owners, second_rows, first_rows, kept, sent)


def node_backward(order, owners, weights, nodes, grads, node_low, pooled, pre, act, normed, inverse, params, mask):
    samples, node_total, latent = node_low.shape
    halves, rows, place = weights
    width = halves[0].shape[2]
    second_rows, hids = latent // nodes, latent // width
    first_rows = rows - second_rows
    count = samples * node_total

    def kernel(order, owners, w, wx, base, own, other, node_low, pooled, pre, act, normed, inverse, params, mask, upstream, input_grad, kept, sent, minor, w1s, w2s, first, second):
        assemble((w, wx), order, first_rows, 0, w1s)
        assemble((w, wx), order, second_rows, first_rows, w2s)
        grad = (base[...] + (own[...] + other[...].astype(F32))).reshape(count, latent)
        node_gradients(
            grad, normed[...].astype(F32), inverse[...], pre[...].astype(F32), act[...],
            node_low[...].reshape(count, latent), pooled[...], params, mask,
            w1s, w2s, first, second, upstream, input_grad, kept, sent, minor, owners, first_rows, second_rows,
        )

    inputs = [order, owners, *halves, *grads, node_low, pooled, pre, act, normed, inverse, params, mask]
    specs = [in_scalars(), in_scalars(), *weight_blocks(*weights)] + [constant(a) for a in inputs[4:]]
    return run_kernel(
        kernel,
        "node_backward",
        1,
        inputs,
        specs,
        gradient_outputs(node_low.shape, order.shape[0], rows, width),
        [
            pltpu.VMEM((2 * latent, latent), BF16),
            pltpu.VMEM((latent, latent), BF16),
            pltpu.VMEM((hids, 2 * latent, latent // hids), F32),
            pltpu.VMEM((hids, latent, latent // hids), F32),
        ],
        12 * count * latent * latent,
    )


def dot(spec, left, right):
    return jnp.einsum(spec, left, right, preferred_element_type=F32)


def swap(values, axis, offset):
    return lax.ppermute(values, axis, [(i, i ^ offset) for i in range(lax.axis_size(axis))])


def bits_of(axis):
    return lax.axis_size(axis).bit_length() - 1


def own_bit(axis, bit):
    return (lax.axis_index(axis) >> bit) & 1


def all_bits():
    return [(axis, bit) for axis in ("node", "hid") for bit in reversed(range(bits_of(axis)))]


def ordered(own, mine, other):
    low = jnp.where(own == 0, mine, other)
    high = jnp.where(own == 0, other, mine)
    return low, high


def double_up(part, axis, bit, place):
    low, high = ordered(own_bit(axis, bit), part, swap(part, axis, 1 << bit))
    return jnp.stack([low, high], axis=place)


def halve_sum(parts, axis, bit, place):
    own = own_bit(axis, bit)
    sent = lax.dynamic_index_in_dim(parts, 1 - own, place, keepdims=False)
    kept = lax.dynamic_index_in_dim(parts, own, place, keepdims=False)
    return kept.astype(F32) + swap(sent.astype(BF16), axis, 1 << bit).astype(F32)


def places():
    node_ids = jnp.arange(lax.axis_size("node"), dtype=jnp.int32) ^ lax.axis_index("node")
    hid_ids = jnp.arange(lax.axis_size("hid"), dtype=jnp.int32) ^ lax.axis_index("hid")
    place = 0
    for step, (axis, bit) in enumerate(all_bits()):
        ids = node_ids[:, None] if axis == "node" else hid_ids[None, :]
        place = place + (((ids >> bit) & 1) << step)
    return place.reshape(-1)


def owners_of_places():
    place = jnp.arange(1 << len(all_bits()), dtype=jnp.int32)
    owner = {"node": lax.axis_index("node"), "hid": lax.axis_index("hid")}
    for step, (axis, bit) in enumerate(all_bits()):
        owner[axis] = owner[axis] ^ (((place >> step) & 1) << bit)
    return jnp.stack([owner["node"], owner["hid"]], axis=1).reshape(-1)


def after(value, *earlier):
    return lax.optimization_barrier((value, *earlier))[0]


def exchange(values, first_step, flips):
    hid_bits = bits_of("hid")
    mask = 0
    for k in range(flips.bit_length()):
        if (flips >> k) & 1:
            axis, bit = all_bits()[first_step + k]
            mask |= 1 << (bit if axis == "hid" else bit + hid_bits)
    total = 1 << len(all_bits())
    return lax.ppermute(values, ("node", "hid"), [(i, i ^ mask) for i in range(total)])


def rounds(begin, end):
    return [(step, min(step + 2, end)) for step in range(begin, end, 2)]


def gather_round(held, begin, end, *under):
    arrived = [exchange(held, begin, flips) for flips in range(1, 1 << (end - begin))]
    if under:
        arrived = lax.optimization_barrier((*arrived, *under))[: len(arrived)]
    return jnp.concatenate([held, *arrived], axis=0)


def split(total, count):
    size = total.shape[0] // count
    pieces = [total[i * size : (i + 1) * size] for i in range(count)]
    return [pieces[0]] + [piece.astype(BF16) for piece in pieces[1:]]


def scatter_round(pieces, begin, *under):
    arrived = [exchange(pieces[flips], begin, flips) for flips in range(1, len(pieces))]
    if under:
        arrived = lax.optimization_barrier((*arrived, *under))[: len(arrived)]
    total = pieces[0].astype(F32)
    for piece in arrived:
        total = total + piece.astype(F32)
    return total


def scatter_rest(total, end, *under):
    for begin, stop in reversed(rounds(0, end)):
        total = scatter_round(split(total, 1 << (stop - begin)), begin, *under)
    return total[0]


def sum_round(values, begin, end):
    terms = [values] + [exchange(values, begin, flips) for flips in range(1, 1 << (end - begin))]
    while len(terms) > 1:
        terms = [terms[i] + terms[i + 1] for i in range(0, len(terms), 2)]
    return terms[0]


def sum_everywhere(values):
    steps = len(all_bits())
    values = sum_round(values, steps - 1, steps)
    for begin, end in reversed(rounds(0, steps - 1)):
        values = sum_round(values, begin, end)
    return values


def to_neighbours(rows, halo_width):
    count = lax.axis_size("node")
    onward = [(i, (i + 1) % count) for i in range(count)]
    back = [(target, source) for source, target in onward]
    from_previous = lax.ppermute(rows[:, halo_width:], "node", onward)
    from_next = lax.ppermute(rows[:, :halo_width], "node", back)
    return jnp.concatenate([from_previous, from_next], axis=1)


def neighbour_swaps(rows, halo_width):
    count = lax.axis_size("node")
    even = lax.axis_index("node") % 2 == 0
    to_previous, to_next = rows[:, :halo_width], rows[:, halo_width:]
    one = [(i, i ^ 1) for i in range(count)]
    two = [(i, (((i + 1) ^ 1) - 1) % count) for i in range(count)]
    first = lax.ppermute(jnp.where(even, to_next, to_previous), "node", one)
    second = lax.ppermute(jnp.where(even, to_previous, to_next), "node", two)
    return first, second


def from_neighbours(first, second):
    even = lax.axis_index("node") % 2 == 0
    return jnp.concatenate(
        [jnp.where(even, second, first), jnp.where(even, first, second)], axis=1
    )


def adam_terms(weight, grad, first, second, decay):
    first_new = BETA_FIRST * first + (1.0 - BETA_FIRST) * grad
    second_new = BETA_SECOND * second + (1.0 - BETA_SECOND) * grad * grad
    update = first_new / (jnp.sqrt(second_new) + ADAM_EPS) + decay * weight
    return (first_new, second_new, update)


def pack_shards(first, second):
    return jnp.concatenate([first, second.T], axis=0).astype(BF16)


def adam_terms(weight, grad, first, second, decay):
    first_new = BETA_FIRST * first + (1.0 - BETA_FIRST) * grad
    second_new = BETA_SECOND * second + (1.0 - BETA_SECOND) * grad * grad
    update = first_new / (jnp.sqrt(second_new) + ADAM_EPS) + decay * weight
    return (first_new, second_new, update)


def per_device(
    node_in,
    edge_in,
    cotangent,
    ocean_mask,
    present_mask,
    valid_counts,
    send_slot,
    recv_local,
    halo_lists,
    edge_first,
    edge_second,
    node_first,
    node_second,
    edge_first_m,
    edge_second_m,
    node_first_m,
    node_second_m,
    edge_first_v,
    edge_second_v,
    node_first_v,
    node_second_v,
    small_params,
    small_m,
    small_v,
    learn_rate,
):
    hid_count = lax.axis_size("hid")
    hid_index = lax.axis_index("hid")
    node_total, sample_count, latent = node_in.shape
    edge_part = edge_in.shape[0] // hid_count
    node_part = node_total // hid_count
    halo_width = halo_lists.shape[1]
    table_total = node_total + 2 * halo_width
    sample_half, edge_half = hid_index >> 1, hid_index & 1
    samples = sample_count // 2
    nodes, hids = lax.axis_size("node"), hid_count
    first_rows = edge_first.shape[1]
    second_rows = edge_second.shape[2]
    node_rows = node_first.shape[1] + second_rows
    width = edge_first.shape[2]

    order, owners = places(), owners_of_places()
    steps = len(all_bits())

    def layer_shards(depth, *earlier):
        shards = (node_first[depth], node_second[depth], edge_first[depth], edge_second[depth])
        if earlier:
            shards = after(shards, *earlier)
        return jnp.concatenate([pack_shards(*shards[:2]), pack_shards(*shards[2:])], axis=0)[None]

    def parted(held):
        return held[:, :node_rows], held[:, node_rows:]

    layer_zero = layer_shards(0)
    for begin, end in rounds(0, steps - 3):
        layer_zero = gather_round(layer_zero, begin, end)
    setup = layer_zero
    layer_zero = gather_round(layer_zero, steps - 3, steps - 2)
    node_zero, edge_zero = parted(layer_zero)
    layer_one = layer_shards(1, setup)
    layer_one = after(layer_one, edge_zero)
    z_rounds = rounds(0, steps - 3)
    for begin, end in z_rounds[:-1]:
        layer_one = gather_round(layer_one, begin, end)
    halo_gate = edge_zero
    masters = (edge_first, edge_second, node_first, node_second)
    weight_local = jnp.stack(
        [jnp.sum(matrix * matrix, axis=(1, 2)) for matrix in after(masters, setup)], axis=1
    )
    def edge_blocks(whole):
        return ((whole, first_rows, 0), (whole, second_rows, first_rows // second_rows))

    def own_edges(values):
        return lax.dynamic_index_in_dim(
            values.reshape(2, 2, edge_part, *values.shape[1:]), edge_half, 1, keepdims=False
        ).reshape(2 * edge_part, *values.shape[1:])

    def own_nodes(values):
        return lax.dynamic_index_in_dim(
            values.reshape(samples, 2, 2, node_part, latent), edge_half, 2, keepdims=False
        ).reshape(samples, 2 * node_part, latent)

    def own_samples(values):
        return lax.dynamic_slice_in_dim(values, sample_half * samples, samples, 1)

    def own_rows_exchanged(values):
        quarters = jnp.moveaxis(values.reshape(samples, 2, 2, node_part, latent), 0, 3)
        quarters = lax.dynamic_index_in_dim(quarters, edge_half, 1, keepdims=False)
        sent = lax.dynamic_index_in_dim(quarters, 1 - sample_half, 0, keepdims=False)
        kept = lax.dynamic_index_in_dim(quarters, sample_half, 0, keepdims=False)
        return kept, swap(sent, "hid", 2)

    def all_samples(kept, arrived):
        return jnp.concatenate(ordered(sample_half, kept, arrived), axis=1)

    send_slot, recv_local, halo_lists, node_in, edge_in = lax.optimization_barrier(
        (send_slot, recv_local, halo_lists, node_in, edge_in, setup)
    )[:5]
    sender = own_edges(send_slot)
    receiver = own_edges(recv_local)
    node_ids, table_ids = jnp.arange(node_total), jnp.arange(table_total)
    at_receiver = (receiver[:, None] == node_ids[None, :]).astype(BF16)
    at_both = jnp.concatenate(
        [(sender[:, None] == table_ids[None, :]).astype(BF16), at_receiver], axis=1
    )
    at_nodes = (node_ids[:, None] == receiver[None, :]).astype(BF16)
    at_both_t = jnp.concatenate(
        [(table_ids[:, None] == sender[None, :]).astype(BF16), at_nodes], axis=0
    )
    at_halo = (halo_lists.reshape(-1)[:, None] == node_ids[None, :]).astype(BF16)
    mask = ((node_ids // node_part) % 2 == edge_half).astype(F32)
    mask = jnp.tile(mask, samples)[:, None]

    node_low = jnp.transpose(own_samples(node_in), (1, 0, 2))
    edge_in_own = own_edges(edge_in)
    halo_rows = dot("hn,snl->shl", at_halo, node_low).astype(BF16)
    node_low_zero = node_low
    halo_rows = neighbour_swaps(after(halo_rows, halo_gate), halo_width)
    begin, end = z_rounds[-1]
    arrived = [exchange(layer_one, begin, flips) for flips in range(1, 1 << (end - begin))]
    constants = (at_receiver, at_both, at_nodes, at_both_t, at_halo, mask, order, owners)
    edge_arrived, first, second, weight_local, constants, *arrived = lax.optimization_barrier(
        (exchange(edge_zero, steps - 2, 1), *halo_rows, weight_local, constants, *arrived)
    )
    at_receiver, at_both, at_nodes, at_both_t, at_halo, mask, order, owners = constants
    halo_rows = from_neighbours(first, second)
    edge_zero = jnp.concatenate([edge_zero, edge_arrived], axis=0)
    layer_one = jnp.concatenate([layer_one, *arrived], axis=0)
    node_zero = after(node_zero, edge_zero)
    edge_zero = (edge_zero, exchange(edge_zero, steps - 1, 1))
    table_zero = jnp.concatenate([node_low, halo_rows], axis=1)
    pre_zero, act_zero, normed_zero, inverse_zero, edge_state, edge_low, pooled = edge_forward(
        order,
        *edge_blocks(edge_zero),
        table_zero,
        edge_in_own[None],
        edge_in_own[None],
        at_both,
        at_nodes,
        small_params[0],
        node_total,
        False,
    )
    pooled, *arrived = lax.optimization_barrier(
        (pooled, exchange(node_zero, steps - 2, 1), exchange(layer_one, steps - 3, 1))
    )
    node_zero = jnp.concatenate([node_zero, arrived[0]], axis=0)
    node_zero = (node_zero, exchange(node_zero, steps - 1, 1))
    layer_one = jnp.concatenate([layer_one, arrived[1]], axis=0)
    node_one, edge_one = parted(layer_one)
    other = after(swap(pooled, "hid", 1), edge_one)
    (
        pooled_zero,
        node_pre,
        node_act,
        node_normed,
        node_inverse,
        node_state,
        node_low,
        halo_rows,
    ) = node_pass(
        order,
        None,
        (node_zero, node_rows, 0),
        nodes,
        node_low_zero,
        node_low_zero,
        (pooled, other),
        small_params[0],
        at_halo,
        None,
        None,
        None,
    )
    halo_rows = to_neighbours(halo_rows, halo_width)
    arrived, halo_rows = lax.optimization_barrier((exchange(edge_one, steps - 2, 1), halo_rows))
    edge_one = jnp.concatenate([edge_one, arrived], axis=0)
    node_one = after(node_one, edge_one)
    edge_one = (edge_one, exchange(edge_one, steps - 1, 1))

    valid_mask = (ocean_mask[:, None] * present_mask).astype(BF16)
    masked = after(cotangent, pooled) * valid_mask[:, :, None]
    sent = lax.dynamic_slice_in_dim(masked, (1 - sample_half) * samples, samples, 1)
    scaling = node_total * lax.axis_size("node") / valid_counts.astype(F32)
    scaling = lax.dynamic_slice_in_dim(scaling, sample_half * samples, samples, 0)
    scaling = scaling[:, None, None]

    node_low_one = node_low
    table_one = jnp.concatenate([node_low, halo_rows], axis=1)
    pre_one, act_one, normed_one, inverse_one, pooled = edge_forward(
        order,
        *edge_blocks(edge_one),
        table_one,
        edge_low,
        edge_state,
        at_both,
        at_nodes,
        small_params[1],
        node_total,
        True,
    )
    pooled, arrived, cotangent_other = lax.optimization_barrier(
        (pooled, exchange(node_one, steps - 2, 1), swap(sent, "hid", 2))
    )
    node_one = jnp.concatenate([node_one, arrived], axis=0)
    masked = jnp.stack(ordered(sample_half, own_samples(masked), cotangent_other), axis=0)
    masked = double_up(masked, "hid", 0, 1).reshape(node_total, samples, latent)
    target = jnp.transpose(masked, (1, 0, 2))
    node_one = (node_one, exchange(node_one, steps - 1, 1))
    node_low, pooled_grad, node_grad, kept, sent, node_minor_one = node_pass(
        order,
        owners,
        (node_one, node_rows, 0),
        nodes,
        node_low_one,
        node_state,
        (pooled, swap(pooled, "hid", 1)),
        small_params[1],
        None,
        target,
        scaling,
        mask,
    )

    def from_edges(partial, returned):
        return partial + dot("hn,shl->snl", at_halo, returned)

    low, hidden_low, at_rows, partial, returned, edge_grad, edge_minor_one = edge_backward(
        order,
        *edge_blocks(edge_one),
        pooled_grad,
        None,
        normed_one,
        inverse_one,
        pre_one,
        at_receiver,
        at_both_t,
        small_params[1, 2:3],
        True,
        node_total,
    )
    low, *node_out = lax.optimization_barrier((low, *own_rows_exchanged(node_low)))
    node_out = all_samples(*node_out)
    chain_one = edge_weight_grads(
        owners,
        edge_low,
        table_one,
        hidden_low,
        at_rows,
        low,
        act_one,
        node_total,
        nodes,
        width,
        [kept, sent],
    )
    *returned, kept, sent = lax.optimization_barrier(
        (*neighbour_swaps(returned, halo_width), *chain_one)
    )
    returned, chain_one = from_neighbours(*returned), (kept, sent)
    partial = from_edges(partial, returned)
    chain_one = split(scatter_round(chain_one, steps - 1).astype(BF16), 2)
    other, *chain_one = lax.optimization_barrier((swap(partial.astype(BF16), "hid", 1), *chain_one))
    pooled_grad, node_grad, kept, sent, node_minor_zero = node_backward(
        order,
        owners,
        (node_zero, node_rows, 0),
        nodes,
        (node_grad, partial, other),
        node_low_zero,
        pooled_zero,
        node_pre,
        node_act,
        node_normed,
        node_inverse,
        small_params[0],
        mask,
    )
    low, hidden_low, at_rows, partial, returned, edge_input_grad, edge_minor_zero, hidden_sum = (
        edge_backward(
            order,
            *edge_blocks(edge_zero),
            pooled_grad,
            edge_grad,
            normed_zero,
            inverse_zero,
            pre_zero,
            at_receiver,
            at_both_t,
            small_params[0, 2:3],
            False,
            node_total,
        )
    )
    chain_one = split(scatter_round(chain_one, steps - 2, low), 2)
    chain_zero = split(scatter_round((kept, sent), steps - 1, low), 2)
    low = after(low, *chain_one, *chain_zero)
    chain_edge = edge_weight_grads(
        owners,
        edge_in_own,
        table_zero,
        hidden_sum,
        at_rows,
        low,
        act_zero,
        node_total,
        nodes,
        width,
        None,
    )
    kept, sent, one_arrived, zero_arrived, *returned = lax.optimization_barrier(
        (
            *chain_edge,
            exchange(chain_one[1], steps - 3, 1),
            exchange(chain_zero[1], steps - 2, 1),
            *neighbour_swaps(returned, halo_width),
        )
    )
    chain_one = chain_one[0].astype(F32) + one_arrived.astype(F32)
    chain_zero = split(chain_zero[0].astype(F32) + zero_arrived.astype(F32), 2)
    edge_arrived = exchange(sent, steps - 1, 1)
    kept, sent = split((kept.astype(F32) + edge_arrived.astype(F32)).astype(BF16), 2)
    zero_arrived = after(exchange(chain_zero[1], steps - 3, 1), sent)
    returned = after(returned, sent)
    chain_zero = chain_zero[0].astype(F32) + zero_arrived.astype(F32)
    for begin, end in reversed(z_rounds[1:]):
        chain_one = scatter_round(split(chain_one, 1 << (end - begin)), begin)
        chain_zero = scatter_round(split(chain_zero, 1 << (end - begin)), begin)
    begin, end = z_rounds[0]
    chain_one = split(chain_one, 1 << (end - begin))
    chain_zero = split(chain_zero, 1 << (end - begin))
    partial = from_edges(partial, from_neighbours(*returned))
    arrived, edge_input_grad, other, chain_zero, *others = lax.optimization_barrier(
        (
            exchange(sent, steps - 2, 1),
            edge_input_grad,
            swap(partial.astype(BF16), "hid", 1),
            chain_zero,
            *[exchange(chain_one[flips], begin, flips) for flips in range(1, len(chain_one))],
        )
    )
    layer_one_grads = chain_one[0]
    for piece in others:
        layer_one_grads = layer_one_grads + piece.astype(F32)
    layer_one_grads = layer_one_grads[0]
    chain_edge = split(kept + arrived.astype(F32), 2)
    chain_zero = after(chain_zero, chain_edge[1])
    arrived, *others = lax.optimization_barrier(
        (
            exchange(chain_edge[1], steps - 3, 1),
            *[exchange(chain_zero[flips], begin, flips) for flips in range(1, len(chain_zero))],
        )
    )
    node_zero_grads = chain_zero[0]
    for piece in others:
        node_zero_grads = node_zero_grads + piece.astype(F32)
    node_zero_grads = node_zero_grads[0]
    chain_edge = chain_edge[0] + arrived.astype(F32)
    halves = edge_input_grad.reshape(2, edge_part, latent)
    sent = lax.dynamic_index_in_dim(halves, 1 - sample_half, 0, keepdims=False).astype(BF16)
    kept = lax.dynamic_index_in_dim(halves, sample_half, 0, keepdims=False)
    node_grad = node_grad + (partial + other.astype(F32))
    grad_node = own_rows_exchanged(node_grad.astype(BF16))
    edge_zero_grads = scatter_rest(chain_edge, steps - 3)
    edge_zero_grads, arrived, *grad_node = lax.optimization_barrier(
        (edge_zero_grads, swap(sent, "hid", 2), *grad_node)
    )
    edge_input_grad = kept + arrived.astype(F32)
    grad_node = all_samples(*grad_node)

    node_one_grads, edge_one_grads = layer_one_grads[:node_rows], layer_one_grads[node_rows:]
    node_first_rows = node_rows - second_rows
    grads = [
        jnp.stack([edge_zero_grads[:first_rows], edge_one_grads[:first_rows]]),
        jnp.stack([edge_zero_grads[first_rows:].T, edge_one_grads[first_rows:].T]),
        jnp.stack([node_zero_grads[:node_first_rows], node_one_grads[:node_first_rows]]),
        jnp.stack([node_zero_grads[node_first_rows:].T, node_one_grads[node_first_rows:].T]),
    ]
    firsts = (edge_first_m, edge_second_m, node_first_m, node_second_m)
    seconds = (edge_first_v, edge_second_v, node_first_v, node_second_v)
    moment_list = [
        adam_terms(masters[place], grads[place], firsts[place], seconds[place], WEIGHT_DECAY)
        for place in range(4)
    ]
    update_local = jnp.stack(
        [jnp.sum(entry[2] * entry[2], axis=(1, 2)) for entry in moment_list], axis=1
    )
    squares = jnp.concatenate([weight_local.reshape(1, -1), update_local.reshape(1, -1)], axis=1)
    minor_packed = jnp.concatenate(
        [edge_minor_zero, node_minor_zero, edge_minor_one, node_minor_one]
        + [jnp.pad(squares, ((0, 0), (0, latent - squares.size)))],
        axis=0,
    )
    minor_packed = sum_everywhere(minor_packed)
    minor_total = minor_packed[: 8 * LAYERS].reshape(small_params.shape)
    squares = minor_packed[8 * LAYERS, : squares.size].reshape(2, *weight_local.shape)
    weight_squares, update_squares = squares[0], squares[1]
    weight_norm = jnp.sqrt(weight_squares)
    update_norm = jnp.sqrt(update_squares)
    new_weights = []
    for position in range(4):
        ratio = weight_norm[:, position] / update_norm[:, position]
        new_weights.append(
            masters[position] - learn_rate[0] * ratio[:, None, None] * moment_list[position][2]
        )
    small_first, small_second, small_update = adam_terms(
        small_params, minor_total, small_m, small_v, 0.0
    )
    small_wnorm = jnp.sqrt(jnp.sum(small_params * small_params, axis=2))
    small_unorm = jnp.sqrt(jnp.sum(small_update * small_update, axis=2))
    small_new = (
        small_params - learn_rate[0] * (small_wnorm / small_unorm)[:, :, None] * small_update
    )
    norms = jnp.stack(
        [
            jnp.concatenate([weight_norm, small_wnorm], axis=1),
            jnp.concatenate([update_norm, small_unorm], axis=1),
        ],
        axis=2,
    )
    return (
        node_out,
        grad_node,
        edge_input_grad.astype(BF16),
        *new_weights,
        *[entry[0] for entry in moment_list],
        *[entry[1] for entry in moment_list],
        *[weight.astype(BF16) for weight in new_weights],
        small_new,
        small_first,
        small_second,
        norms,
    )


def solution(mesh):
    whole = P()
    rows = P(None, "node", "hid")
    columns = P(None, "hid", "node")
    matrices = (rows, columns, rows, columns)
    in_specs = (
        P("node", None, None),
        P("node", None),
        P(("node", "hid"), None, None),
        P(("node", "hid")),
        P(("node", "hid"), None),
        P(),
        P("node"),
        P("node"),
        P("node", None),
        *matrices,
        *matrices,
        *matrices,
        whole,
        whole,
        whole,
        whole,
    )
    out_specs = (
        P(("node", "hid"), None, None),
        P(("node", "hid"), None, None),
        P(("node", "hid"), None),
        *matrices,
        *matrices,
        *matrices,
        *matrices,
        whole,
        whole,
        whole,
        whole,
    )
    return jax.shard_map(
        per_device, mesh=mesh, in_specs=in_specs, out_specs=out_specs, check_vma=False
    )
```

```python
import jax
import jax.numpy as jnp
from jax import lax
from jax.experimental import pallas as pl
from jax.experimental.pallas import tpu as pltpu
from jax.sharding import PartitionSpec as P

LAYERS = 2


NORM_EPS = 1e-05
BETA_FIRST = 0.5
BETA_SECOND = 0.5
ADAM_EPS = 1e-06
WEIGHT_DECAY = 0.01
BF16 = jnp.bfloat16
F32 = jnp.float32
VMEM_BYTES = 56 * 1024 * 1024


def matmul(left, right):
    return lax.dot_general(left, right, (((1,), (0,)), ((), ())), preferred_element_type=F32)


def matmul_nt(left, right):
    return lax.dot_general(left, right, (((1,), (1,)), ((), ())), preferred_element_type=F32)


def matmul_tn(left, right):
    return lax.dot_general(left, right, (((0,), (0,)), ((), ())), preferred_element_type=F32)


def sigmoid(values):
    return 0.5 + 0.5 * jnp.tanh(0.5 * values)


def silu_slope(values):
    gate = sigmoid(values)
    return gate * (1.0 + values * (1.0 - gate))


def norm_forward(values):
    center = values - jnp.mean(values, axis=-1, keepdims=True)
    spread = jnp.mean(center * center, axis=-1, keepdims=True)
    inverse = lax.rsqrt(spread + NORM_EPS)
    return center * inverse, inverse


def norm_backward(upstream, normed, inverse, gain_row):
    scaled = upstream * gain_row
    return inverse * (
        scaled
        - jnp.mean(scaled, axis=-1, keepdims=True)
        - normed * jnp.mean(scaled * normed, axis=-1, keepdims=True)
    )


def column_sum(values):
    return jnp.sum(values, axis=0, keepdims=True)


def assemble(source, order, rows, offset, target):
    own, arrived = source
    half, _, width = own.shape
    nodes, hids = target.shape[0] // rows, target.shape[1] // width
    for i in range(nodes):
        for j in range(hids):
            place = order[i * hids + j]
            index = jnp.where(place < half, place, place - half)
            target[i * rows : (i + 1) * rows, j * width : (j + 1) * width] = jnp.where(
                place < half,
                own[index, offset : offset + rows, :],
                arrived[index, offset : offset + rows, :],
            )


def store(target, begin, values):
    rows, width = values.shape[0], target.shape[2]
    for j in range(target.shape[0]):
        target[j, begin : begin + rows] = values[:, j * width : (j + 1) * width]


def add(target, begin, values):
    rows, width = values.shape[0], target.shape[2]
    for j in range(target.shape[0]):
        target[j, begin : begin + rows] += values[:, j * width : (j + 1) * width]


def pack(values, owners, rows, offset, kept, sent):
    half = kept.shape[0]

    def one(index, carry):
        for target, place in ((kept, index), (sent, index + half)):
            begin = pl.multiple_of(owners[2 * place] * rows, rows)
            target[index, offset : offset + rows, :] = values[
                owners[2 * place + 1], pl.ds(begin, rows), :
            ].astype(BF16)
        return carry

    lax.fori_loop(0, half, one, 0)


def per_sample(array):
    block = (1,) + array.shape[1:]
    return pl.BlockSpec(block, lambda s: (s,) + (0,) * (len(block) - 1))


def constant(array):
    return pl.BlockSpec(array.shape, lambda s: (0,) * len(array.shape))


def weight_blocks(halves, rows, place):
    blocks, _, width = halves[0].shape
    return [pl.BlockSpec((blocks, rows, width), lambda s: (0, place, 0)) for _ in halves]


def in_scalars():
    return pl.BlockSpec(memory_space=pltpu.SMEM)


def shape_of(shape, dtype):
    return jax.ShapeDtypeStruct(shape, dtype)


def run_kernel(kernel, name, samples, inputs, in_specs, outputs, scratch, flops):
    moved = sum(a.size * a.dtype.itemsize for a in inputs) + sum(
        shape.size * shape.dtype.itemsize for shape, _ in outputs
    )
    return pl.pallas_call(
        kernel,
        name=name,
        grid=(samples,),
        in_specs=in_specs,
        out_specs=[spec for _, spec in outputs],
        out_shape=[shape for shape, _ in outputs],
        scratch_shapes=scratch,
        compiler_params=pltpu.CompilerParams(
            dimension_semantics=("arbitrary",), vmem_limit_bytes=VMEM_BYTES
        ),
        cost_estimate=pl.CostEstimate(flops=4 * flops, bytes_accessed=moved, transcendentals=0),
    )(*inputs)


def sampled(shape, dtype):
    result = shape_of(shape, dtype)
    return (result, per_sample(result))


def shared(shape, dtype):
    result = shape_of(shape, dtype)
    return (result, constant(result))


def edge_forward(order, first, second, table, edge_low, edge_state, at_both, at_nodes, params, node_total, last):
    samples, table_total, latent = table.shape
    edges = edge_low.shape[1]
    alike = edge_low.shape[0] == 1

    def kernel(order, w1, w1x, w2, w2x, table, low, state, both, nodes, params, pre, act, normed, inverse, *rest):
        if last:
            pooled, w1s, w2s, projected = rest
        else:
            new_state, new_low, pooled, w1s, w2s, projected = rest

        @pl.when(pl.program_id(0) == 0)
        def _():
            assemble((w1, w1x), order, w1.shape[1], 0, w1s)
            assemble((w2, w2x), order, w2.shape[1], 0, w2s)

        rows = table[0]
        projected[:table_total] = matmul(rows, w1s[latent : 2 * latent]).astype(BF16)
        projected[table_total:] = matmul(rows[:node_total], w1s[2 * latent :]).astype(BF16)
        hidden = matmul(low[0], w1s[:latent]) + matmul(both[...], projected[...]) + params[0:1]
        pre[0] = hidden.astype(BF16)
        active = (hidden * sigmoid(hidden)).astype(BF16)
        act[0] = active
        output = matmul_nt(active, w2s[...]) + params[1:2]
        scaled, scale = norm_forward(output)
        normed[0] = scaled.astype(BF16)
        inverse[0] = scale
        state_new = state[0].astype(F32) + scaled * params[2:3] + params[3:4]
        low_new = state_new.astype(BF16)
        if not last:
            new_state[0] = state_new
            new_low[0] = low_new
        pooled[0] = matmul(nodes[...], low_new).astype(BF16)

    wide = (samples, edges, latent)
    outputs = [sampled(wide, BF16), sampled(wide, BF16), sampled(wide, BF16), sampled((samples, edges, 1), F32)]
    if not last:
        outputs += [sampled(wide, F32), sampled(wide, BF16)]
    outputs += [sampled((samples, node_total, latent), BF16)]
    of_edges = constant if alike else per_sample
    return run_kernel(
        kernel,
        "edge_forward",
        samples,
        [order, *first[0], *second[0], table, edge_low, edge_state, at_both, at_nodes, params],
        [
            in_scalars(),
            *weight_blocks(*first),
            *weight_blocks(*second),
            per_sample(table),
            of_edges(edge_low),
            of_edges(edge_state),
            constant(at_both),
            constant(at_nodes),
            constant(params),
        ],
        outputs,
        [
            pltpu.VMEM((3 * latent, latent), BF16),
            pltpu.VMEM((latent, latent), BF16),
            pltpu.VMEM((at_both.shape[1], latent), BF16),
        ],
        2 * samples * edges * latent * (3 * latent + at_both.shape[1]),
    )


def edge_backward(order, first, second, pooled_grad, edge_grad, normed, inverse, pre, at_receiver, at_both_t, gain, last, node_total):
    samples, edges, latent = normed.shape
    at_total = at_both_t.shape[0]
    table_total = at_total - node_total

    def kernel(order, w1, w1x, w2, w2x, upstream, *rest):
        if not last:
            later, rest = rest[0], rest[1:]
        normed, inverse, pre, receiver, both_t, gain, low, hidden_low, at_rows, partial, returned, grad_out, minor = rest[:13]
        if last:
            w1s, w2s = rest[13:]
        else:
            hidden_sum, w1s, w2s, hidden_acc = rest[13:]
        step = pl.program_id(0)

        @pl.when(step == 0)
        def _():
            assemble((w1, w1x), order, w1.shape[1], 0, w1s)
            assemble((w2, w2x), order, w2.shape[1], 0, w2s)
            minor[...] = jnp.zeros_like(minor)

        grad = matmul(receiver[...], upstream[0])
        if not last:
            grad = grad + later[0]
        scaled = normed[0].astype(F32)
        output_grad = norm_backward(grad, scaled, inverse[0], gain[0:1]).astype(BF16)
        low[0] = output_grad
        act_grad = matmul(output_grad, w2s[...])
        pre_grad = (act_grad * silu_slope(pre[0].astype(F32))).astype(BF16)
        hidden_low[0] = pre_grad
        minor[0:1] += column_sum(pre_grad.astype(F32))
        minor[1:2] += column_sum(output_grad.astype(F32))
        minor[2:3] += column_sum(grad * scaled)
        minor[3:4] += column_sum(grad)
        at_rows[0] = matmul(both_t[...], pre_grad).astype(BF16)
        send = w1s[latent : 2 * latent]
        partial[0] = matmul_nt(at_rows[0, :node_total], send) + matmul_nt(
            at_rows[0, table_total:], w1s[2 * latent :]
        )
        returned[0] = matmul_nt(at_rows[0, node_total:table_total], send).astype(BF16)
        if last:
            grad_out[0] = grad + matmul_nt(pre_grad, w1s[:latent])
        else:

            @pl.when(step == 0)
            def _():
                grad_out[...] = grad
                hidden_acc[...] = pre_grad.astype(F32)

            @pl.when(step > 0)
            def _():
                grad_out[...] += grad
                hidden_acc[...] += pre_grad.astype(F32)

            @pl.when(step == samples - 1)
            def _():
                total = hidden_acc[...].astype(BF16)
                hidden_sum[...] = total
                grad_out[...] += matmul_nt(total, w1s[:latent])

    wide = (samples, edges, latent)
    outputs = [
        sampled(wide, BF16),
        sampled(wide, BF16),
        sampled((samples, at_total, latent), BF16),
        sampled((samples, node_total, latent), F32),
        sampled((samples, table_total - node_total, latent), BF16),
        sampled(wide, F32) if last else shared((edges, latent), F32),
        shared((4, latent), F32),
    ]
    scratch = [pltpu.VMEM((3 * latent, latent), BF16), pltpu.VMEM((latent, latent), BF16)]
    inputs = [order, *first[0], *second[0], pooled_grad]
    specs = [in_scalars(), *weight_blocks(*first), *weight_blocks(*second), per_sample(pooled_grad)]
    if not last:
        outputs.append(shared((edges, latent), BF16))
        scratch.append(pltpu.VMEM((edges, latent), F32))
        inputs.append(edge_grad)
        specs.append(per_sample(edge_grad))
    inputs += [normed, inverse, pre, at_receiver, at_both_t, gain]
    specs += [
        per_sample(normed),
        per_sample(inverse),
        per_sample(pre),
        constant(at_receiver),
        constant(at_both_t),
        constant(gain),
    ]
    return run_kernel(
        kernel,
        "edge_backward",
        samples,
        inputs,
        specs,
        outputs,
        scratch,
        2 * samples * edges * latent * (2 * latent + 2 * at_total),
    )


def edge_weight_grads(owners, edge_low, table, hidden_low, at_rows, low, act, node_total, nodes, width, packed_before):
    samples, table_total, latent = table.shape
    alike = edge_low.ndim == 2
    first_rows, second_rows = 3 * latent // nodes, latent // nodes
    offset = 0 if packed_before is None else packed_before[0].shape[1]
    blocks, hids = owners.shape[0] // 2, latent // width

    def kernel(owners, edge_low, table, hidden_low, at_rows, low, act, *rest):
        before, rest = rest[:-4], rest[-4:]
        kept, sent, first, second = rest
        step = pl.program_id(0)

        @pl.when(step == 0)
        def _():
            first[...] = jnp.zeros_like(first)
            second[...] = jnp.zeros_like(second)
            for source, target in zip(before, (kept, sent)):
                target[:, :offset, :] = source[...]
            if alike:
                add(first, 0, matmul_tn(edge_low[...], hidden_low[...]))

        if not alike:
            add(first, 0, matmul_tn(edge_low[0], hidden_low[0]))
        add(first, latent, matmul_tn(table[0], at_rows[0, :table_total]))
        add(first, 2 * latent, matmul_tn(table[0, :node_total], at_rows[0, table_total:]))
        add(second, 0, matmul_tn(low[0], act[0]))

        @pl.when(step == samples - 1)
        def _():
            pack(first, owners, first_rows, offset, kept, sent)
            pack(second, owners, second_rows, offset + first_rows, kept, sent)

    of_edges = constant if alike else per_sample
    inputs = [owners, edge_low, table, hidden_low, at_rows, low, act]
    specs = [in_scalars(), of_edges(edge_low), per_sample(table), of_edges(hidden_low), per_sample(at_rows), per_sample(low), per_sample(act)]
    if packed_before is not None:
        inputs += packed_before
        specs += [constant(a) for a in packed_before]
    return run_kernel(
        kernel,
        "edge_weight_grads",
        samples,
        inputs,
        specs,
        [shared((blocks // 2, offset + first_rows + second_rows, width), BF16)] * 2,
        [pltpu.VMEM((hids, 3 * latent, width), F32), pltpu.VMEM((hids, latent, width), F32)],
        4 * low.size * latent,
    )


def node_pass(order, owners, weights, nodes, node_low, state, pooled_pair, params, at_halo, target, scaling, mask):
    samples, node_total, latent = node_low.shape
    halves, rows, place = weights
    width = halves[0].shape[2]
    second_rows, hids = latent // nodes, latent // width
    first_rows = rows - second_rows
    count = samples * node_total
    last = target is not None

    def kernel(order, *rest):
        if last:
            owners, rest = rest[0], rest[1:]
        w, wx, node_low, state, pooled_own, pooled_other, params, *rest = rest
        if last:
            target, scaling, mask, new_low, upstream, input_grad, kept, sent, minor, w1s, w2s, first, second = rest
        else:
            at_halo, pooled_out, pre, act, normed, inverse, new_state, new_low, halo, w1s, w2s = rest
        assemble((w, wx), order, first_rows, 0, w1s)
        assemble((w, wx), order, second_rows, first_rows, w2s)
        rows_low = node_low[...].reshape(count, latent)
        pooled = (pooled_own[...].astype(F32) + pooled_other[...].astype(F32)).astype(BF16)
        pooled = pooled.reshape(count, latent)
        hidden = matmul(rows_low, w1s[:latent]) + matmul(pooled, w1s[latent:]) + params[4:5]
        active = (hidden * sigmoid(hidden)).astype(BF16)
        output = matmul_nt(active, w2s[...]) + params[5:6]
        scaled, scale = norm_forward(output)
        state_new = state[...].astype(F32).reshape(count, latent) + scaled * params[6:7] + params[7:8]
        low_new = state_new.astype(BF16).reshape(new_low.shape)
        new_low[...] = low_new
        if not last:
            pooled_out[...] = pooled
            pre[...] = hidden.astype(BF16)
            act[...] = active
            normed[...] = scaled.astype(BF16)
            inverse[...] = scale
            new_state[...] = state_new.reshape(new_state.shape)
            for s in range(samples):
                halo[s] = matmul(at_halo[...], new_low[s]).astype(BF16)
        else:
            grad = (target[...].astype(F32) * scaling[...]).reshape(count, latent)
            node_gradients(
                grad, scaled, scale, hidden, active, rows_low, pooled, params, mask,
                w1s, w2s, first, second, upstream, input_grad, kept, sent, minor, owners, first_rows, second_rows,
            )

    shape = node_low.shape
    inputs = [*halves, node_low, state, *pooled_pair, params]
    scratch = [pltpu.VMEM((2 * latent, latent), BF16), pltpu.VMEM((latent, latent), BF16)]
    if last:
        inputs += [target, scaling, mask]
        outputs = [shared(shape, BF16), *gradient_outputs(shape, order.shape[0], rows, width)]
        scratch += [pltpu.VMEM((hids, 2 * latent, latent // hids), F32), pltpu.VMEM((hids, latent, latent // hids), F32)]
    else:
        inputs += [at_halo]
        outputs = [
            shared((count, latent), BF16),
            shared((count, latent), BF16),
            shared((count, latent), BF16),
            shared((count, latent), BF16),
            shared((count, 1), F32),
            shared(shape, F32),
            shared(shape, BF16),
            shared((samples, at_halo.shape[0], latent), BF16),
        ]
    tables = [order, owners] if last else [order]
    specs = [in_scalars() for _ in tables] + weight_blocks(*weights) + [constant(a) for a in inputs[2:]]
    inputs = tables + inputs
    return run_kernel(kernel, "node_pass", 1, inputs, specs, outputs, scratch, 6 * count * latent * latent * (3 if last else 1))


def gradient_outputs(shape, blocks, rows, width):
    return [
        shared(shape, BF16),
        shared(shape, F32),
        shared((blocks // 2, rows, width), BF16),
        shared((blocks // 2, rows, width), BF16),
        shared((4, shape[-1]), F32),
    ]


def node_gradients(
    grad, scaled, scale, hidden, active, rows_low, pooled, params, mask,
    w1s, w2s, first, second, upstream, input_grad, kept, sent, minor, owners, first_rows, second_rows,
):
    latent = w2s.shape[0]
    output_grad = norm_backward(grad, scaled, scale, params[6:7]).astype(BF16)
    pre_grad = (matmul(output_grad, w2s[...]) * silu_slope(hidden)).astype(BF16)
    upstream[...] = matmul_nt(pre_grad, w1s[latent:]).astype(BF16).reshape(upstream.shape)
    input_grad[...] = (grad + matmul_nt(pre_grad, w1s[:latent])).reshape(input_grad.shape)
    chosen = mask[...] > 0.5
    output_mine = jnp.where(chosen, output_grad.astype(F32), 0.0)
    pre_mine = jnp.where(chosen, pre_grad.astype(F32), 0.0)
    grad_mine = jnp.where(chosen, grad, 0.0)
    minor[0:1] = column_sum(pre_mine)
    minor[1:2] = column_sum(output_mine)
    minor[2:3] = column_sum(grad_mine * scaled)
    minor[3:4] = column_sum(grad_mine)
    pre_mine = pre_mine.astype(BF16)
    store(first, 0, matmul_tn(rows_low, pre_mine))
    store(first, latent, matmul_tn(pooled, pre_mine))
    store(second, 0, matmul_tn(output_mine.astype(BF16), active))
    pack(first, owners, first_rows, 0, kept, sent)
    pack(second, owners, second_rows, first_rows, kept, sent)


def node_backward(order, owners, weights, nodes, grads, node_low, pooled, pre, act, normed, inverse, params, mask):
    samples, node_total, latent = node_low.shape
    halves, rows, place = weights
    width = halves[0].shape[2]
    second_rows, hids = latent // nodes, latent // width
    first_rows = rows - second_rows
    count = samples * node_total

    def kernel(order, owners, w, wx, base, own, other, node_low, pooled, pre, act, normed, inverse, params, mask, upstream, input_grad, kept, sent, minor, w1s, w2s, first, second):
        assemble((w, wx), order, first_rows, 0, w1s)
        assemble((w, wx), order, second_rows, first_rows, w2s)
        grad = (base[...] + (own[...] + other[...].astype(F32))).reshape(count, latent)
        node_gradients(
            grad, normed[...].astype(F32), inverse[...], pre[...].astype(F32), act[...],
            node_low[...].reshape(count, latent), pooled[...], params, mask,
            w1s, w2s, first, second, upstream, input_grad, kept, sent, minor, owners, first_rows, second_rows,
        )

    inputs = [order, owners, *halves, *grads, node_low, pooled, pre, act, normed, inverse, params, mask]
    specs = [in_scalars(), in_scalars(), *weight_blocks(*weights)] + [constant(a) for a in inputs[4:]]
    return run_kernel(
        kernel,
        "node_backward",
        1,
        inputs,
        specs,
        gradient_outputs(node_low.shape, order.shape[0], rows, width),
        [
            pltpu.VMEM((2 * latent, latent), BF16),
            pltpu.VMEM((latent, latent), BF16),
            pltpu.VMEM((hids, 2 * latent, latent // hids), F32),
            pltpu.VMEM((hids, latent, latent // hids), F32),
        ],
        12 * count * latent * latent,
    )


def dot(spec, left, right):
    return jnp.einsum(spec, left, right, preferred_element_type=F32)


def swap(values, axis, offset):
    return lax.ppermute(values, axis, [(i, i ^ offset) for i in range(lax.axis_size(axis))])


def bits_of(axis):
    return lax.axis_size(axis).bit_length() - 1


def own_bit(axis, bit):
    return (lax.axis_index(axis) >> bit) & 1


def all_bits():
    return [(axis, bit) for axis in ("node", "hid") for bit in reversed(range(bits_of(axis)))]


def ordered(own, mine, other):
    low = jnp.where(own == 0, mine, other)
    high = jnp.where(own == 0, other, mine)
    return low, high


def double_up(part, axis, bit, place):
    low, high = ordered(own_bit(axis, bit), part, swap(part, axis, 1 << bit))
    return jnp.stack([low, high], axis=place)


def halve_sum(parts, axis, bit, place):
    own = own_bit(axis, bit)
    sent = lax.dynamic_index_in_dim(parts, 1 - own, place, keepdims=False)
    kept = lax.dynamic_index_in_dim(parts, own, place, keepdims=False)
    return kept.astype(F32) + swap(sent.astype(BF16), axis, 1 << bit).astype(F32)


def places():
    node_ids = jnp.arange(lax.axis_size("node"), dtype=jnp.int32) ^ lax.axis_index("node")
    hid_ids = jnp.arange(lax.axis_size("hid"), dtype=jnp.int32) ^ lax.axis_index("hid")
    place = 0
    for step, (axis, bit) in enumerate(all_bits()):
        ids = node_ids[:, None] if axis == "node" else hid_ids[None, :]
        place = place + (((ids >> bit) & 1) << step)
    return place.reshape(-1)


def owners_of_places():
    place = jnp.arange(1 << len(all_bits()), dtype=jnp.int32)
    owner = {"node": lax.axis_index("node"), "hid": lax.axis_index("hid")}
    for step, (axis, bit) in enumerate(all_bits()):
        owner[axis] = owner[axis] ^ (((place >> step) & 1) << bit)
    return jnp.stack([owner["node"], owner["hid"]], axis=1).reshape(-1)


def after(value, *earlier):
    return lax.optimization_barrier((value, *earlier))[0]


def exchange(values, first_step, flips):
    hid_bits = bits_of("hid")
    mask = 0
    for k in range(flips.bit_length()):
        if (flips >> k) & 1:
            axis, bit = all_bits()[first_step + k]
            mask |= 1 << (bit if axis == "hid" else bit + hid_bits)
    total = 1 << len(all_bits())
    return lax.ppermute(values, ("node", "hid"), [(i, i ^ mask) for i in range(total)])


def rounds(begin, end):
    return [(step, min(step + 2, end)) for step in range(begin, end, 2)]


def gather_round(held, begin, end, *under):
    arrived = [exchange(held, begin, flips) for flips in range(1, 1 << (end - begin))]
    if under:
        arrived = lax.optimization_barrier((*arrived, *under))[: len(arrived)]
    return jnp.concatenate([held, *arrived], axis=0)


def split(total, count):
    size = total.shape[0] // count
    pieces = [total[i * size : (i + 1) * size] for i in range(count)]
    return [pieces[0]] + [piece.astype(BF16) for piece in pieces[1:]]


def scatter_round(pieces, begin, *under):
    arrived = [exchange(pieces[flips], begin, flips) for flips in range(1, len(pieces))]
    if under:
        arrived = lax.optimization_barrier((*arrived, *under))[: len(arrived)]
    total = pieces[0].astype(F32)
    for piece in arrived:
        total = total + piece.astype(F32)
    return total


def scatter_rest(total, end, *under):
    for begin, stop in reversed(rounds(0, end)):
        total = scatter_round(split(total, 1 << (stop - begin)), begin, *under)
    return total[0]


def sum_round(values, begin, end):
    terms = [values] + [exchange(values, begin, flips) for flips in range(1, 1 << (end - begin))]
    while len(terms) > 1:
        terms = [terms[i] + terms[i + 1] for i in range(0, len(terms), 2)]
    return terms[0]


def sum_everywhere(values):
    steps = len(all_bits())
    values = sum_round(values, steps - 1, steps)
    for begin, end in reversed(rounds(0, steps - 1)):
        values = sum_round(values, begin, end)
    return values


def to_neighbours(rows, halo_width):
    count = lax.axis_size("node")
    onward = [(i, (i + 1) % count) for i in range(count)]
    back = [(target, source) for source, target in onward]
    from_previous = lax.ppermute(rows[:, halo_width:], "node", onward)
    from_next = lax.ppermute(rows[:, :halo_width], "node", back)
    return jnp.concatenate([from_previous, from_next], axis=1)


def neighbour_swaps(rows, halo_width):
    count = lax.axis_size("node")
    even = lax.axis_index("node") % 2 == 0
    to_previous, to_next = rows[:, :halo_width], rows[:, halo_width:]
    one = [(i, i ^ 1) for i in range(count)]
    two = [(i, (((i + 1) ^ 1) - 1) % count) for i in range(count)]
    first = lax.ppermute(jnp.where(even, to_next, to_previous), "node", one)
    second = lax.ppermute(jnp.where(even, to_previous, to_next), "node", two)
    return first, second


def from_neighbours(first, second):
    even = lax.axis_index("node") % 2 == 0
    return jnp.concatenate(
        [jnp.where(even, second, first), jnp.where(even, first, second)], axis=1
    )


def adam_terms(weight, grad, first, second, decay):
    first_new = BETA_FIRST * first + (1.0 - BETA_FIRST) * grad
    second_new = BETA_SECOND * second + (1.0 - BETA_SECOND) * grad * grad
    update = first_new / (jnp.sqrt(second_new) + ADAM_EPS) + decay * weight
    return (first_new, second_new, update)


def pack_shards(first, second):
    return jnp.concatenate([first, second.T], axis=0).astype(BF16)


def adam_terms(weight, grad, first, second, decay):
    first_new = BETA_FIRST * first + (1.0 - BETA_FIRST) * grad
    second_new = BETA_SECOND * second + (1.0 - BETA_SECOND) * grad * grad
    update = first_new / (jnp.sqrt(second_new) + ADAM_EPS) + decay * weight
    return (first_new, second_new, update)


def per_device(
    node_in,
    edge_in,
    cotangent,
    ocean_mask,
    present_mask,
    valid_counts,
    send_slot,
    recv_local,
    halo_lists,
    edge_first,
    edge_second,
    node_first,
    node_second,
    edge_first_m,
    edge_second_m,
    node_first_m,
    node_second_m,
    edge_first_v,
    edge_second_v,
    node_first_v,
    node_second_v,
    small_params,
    small_m,
    small_v,
    learn_rate,
):
    hid_count = lax.axis_size("hid")
    hid_index = lax.axis_index("hid")
    node_total, sample_count, latent = node_in.shape
    edge_part = edge_in.shape[0] // hid_count
    node_part = node_total // hid_count
    halo_width = halo_lists.shape[1]
    table_total = node_total + 2 * halo_width
    sample_half, edge_half = hid_index >> 1, hid_index & 1
    samples = sample_count // 2
    nodes, hids = lax.axis_size("node"), hid_count
    first_rows = edge_first.shape[1]
    second_rows = edge_second.shape[2]
    node_rows = node_first.shape[1] + second_rows
    width = edge_first.shape[2]

    order, owners = places(), owners_of_places()
    steps = len(all_bits())

    def layer_shards(depth, *earlier):
        shards = (node_first[depth], node_second[depth], edge_first[depth], edge_second[depth])
        if earlier:
            shards = after(shards, *earlier)
        return jnp.concatenate([pack_shards(*shards[:2]), pack_shards(*shards[2:])], axis=0)[None]

    def parted(held):
        return held[:, :node_rows], held[:, node_rows:]

    layer_zero = layer_shards(0)
    for begin, end in rounds(0, steps - 3):
        layer_zero = gather_round(layer_zero, begin, end)
    setup = layer_zero
    layer_zero = gather_round(layer_zero, steps - 3, steps - 2)
    node_zero, edge_zero = parted(layer_zero)
    layer_one = layer_shards(1, setup)
    layer_one = after(layer_one, edge_zero)
    z_rounds = rounds(0, steps - 3)
    for begin, end in z_rounds[:-1]:
        layer_one = gather_round(layer_one, begin, end)
    halo_gate = edge_zero
    masters = (edge_first, edge_second, node_first, node_second)
    weight_local = jnp.stack(
        [jnp.sum(matrix * matrix, axis=(1, 2)) for matrix in after(masters, setup)], axis=1
    )
    def edge_blocks(whole):
        return ((whole, first_rows, 0), (whole, second_rows, first_rows // second_rows))

    def own_edges(values):
        return lax.dynamic_index_in_dim(
            values.reshape(2, 2, edge_part, *values.shape[1:]), edge_half, 1, keepdims=False
        ).reshape(2 * edge_part, *values.shape[1:])

    def own_nodes(values):
        return lax.dynamic_index_in_dim(
            values.reshape(samples, 2, 2, node_part, latent), edge_half, 2, keepdims=False
        ).reshape(samples, 2 * node_part, latent)

    def own_samples(values):
        return lax.dynamic_slice_in_dim(values, sample_half * samples, samples, 1)

    def own_rows_exchanged(values):
        quarters = jnp.moveaxis(values.reshape(samples, 2, 2, node_part, latent), 0, 3)
        quarters = lax.dynamic_index_in_dim(quarters, edge_half, 1, keepdims=False)
        sent = lax.dynamic_index_in_dim(quarters, 1 - sample_half, 0, keepdims=False)
        kept = lax.dynamic_index_in_dim(quarters, sample_half, 0, keepdims=False)
        return kept, swap(sent, "hid", 2)

    def all_samples(kept, arrived):
        return jnp.concatenate(ordered(sample_half, kept, arrived), axis=1)

    send_slot, recv_local, halo_lists, node_in, edge_in = lax.optimization_barrier(
        (send_slot, recv_local, halo_lists, node_in, edge_in, setup)
    )[:5]
    sender = own_edges(send_slot)
    receiver = own_edges(recv_local)
    node_ids, table_ids = jnp.arange(node_total), jnp.arange(table_total)
    at_receiver = (receiver[:, None] == node_ids[None, :]).astype(BF16)
    at_both = jnp.concatenate(
        [(sender[:, None] == table_ids[None, :]).astype(BF16), at_receiver], axis=1
    )
    at_nodes = (node_ids[:, None] == receiver[None, :]).astype(BF16)
    at_both_t = jnp.concatenate(
        [(table_ids[:, None] == sender[None, :]).astype(BF16), at_nodes], axis=0
    )
    at_halo = (halo_lists.reshape(-1)[:, None] == node_ids[None, :]).astype(BF16)
    mask = ((node_ids // node_part) % 2 == edge_half).astype(F32)
    mask = jnp.tile(mask, samples)[:, None]

    node_low = jnp.transpose(own_samples(node_in), (1, 0, 2))
    edge_in_own = own_edges(edge_in)
    halo_rows = dot("hn,snl->shl", at_halo, node_low).astype(BF16)
    node_low_zero = node_low
    halo_rows = neighbour_swaps(after(halo_rows, halo_gate), halo_width)
    begin, end = z_rounds[-1]
    arrived = [exchange(layer_one, begin, flips) for flips in range(1, 1 << (end - begin))]
    constants = (at_receiver, at_both, at_nodes, at_both_t, at_halo, mask, order, owners)
    edge_arrived, first, second, weight_local, constants, *arrived = lax.optimization_barrier(
        (exchange(edge_zero, steps - 2, 1), *halo_rows, weight_local, constants, *arrived)
    )
    at_receiver, at_both, at_nodes, at_both_t, at_halo, mask, order, owners = constants
    halo_rows = from_neighbours(first, second)
    edge_zero = jnp.concatenate([edge_zero, edge_arrived], axis=0)
    layer_one = jnp.concatenate([layer_one, *arrived], axis=0)
    node_zero = after(node_zero, edge_zero)
    edge_zero = (edge_zero, exchange(edge_zero, steps - 1, 1))
    table_zero = jnp.concatenate([node_low, halo_rows], axis=1)
    pre_zero, act_zero, normed_zero, inverse_zero, edge_state, edge_low, pooled = edge_forward(
        order,
        *edge_blocks(edge_zero),
        table_zero,
        edge_in_own[None],
        edge_in_own[None],
        at_both,
        at_nodes,
        small_params[0],
        node_total,
        False,
    )
    pooled, *arrived = lax.optimization_barrier(
        (pooled, exchange(node_zero, steps - 2, 1), exchange(layer_one, steps - 3, 1))
    )
    node_zero = jnp.concatenate([node_zero, arrived[0]], axis=0)
    node_zero = (node_zero, exchange(node_zero, steps - 1, 1))
    layer_one = jnp.concatenate([layer_one, arrived[1]], axis=0)
    node_one, edge_one = parted(layer_one)
    other = after(swap(pooled, "hid", 1), edge_one)
    (
        pooled_zero,
        node_pre,
        node_act,
        node_normed,
        node_inverse,
        node_state,
        node_low,
        halo_rows,
    ) = node_pass(
        order,
        None,
        (node_zero, node_rows, 0),
        nodes,
        node_low_zero,
        node_low_zero,
        (pooled, other),
        small_params[0],
        at_halo,
        None,
        None,
        None,
    )
    halo_rows = to_neighbours(halo_rows, halo_width)
    arrived, halo_rows = lax.optimization_barrier((exchange(edge_one, steps - 2, 1), halo_rows))
    edge_one = jnp.concatenate([edge_one, arrived], axis=0)
    node_one = after(node_one, edge_one)
    edge_one = (edge_one, exchange(edge_one, steps - 1, 1))

    valid_mask = (ocean_mask[:, None] * present_mask).astype(BF16)
    masked = after(cotangent, pooled) * valid_mask[:, :, None]
    sent = lax.dynamic_slice_in_dim(masked, (1 - sample_half) * samples, samples, 1)
    scaling = node_total * lax.axis_size("node") / valid_counts.astype(F32)
    scaling = lax.dynamic_slice_in_dim(scaling, sample_half * samples, samples, 0)
    scaling = scaling[:, None, None]

    node_low_one = node_low
    table_one = jnp.concatenate([node_low, halo_rows], axis=1)
    pre_one, act_one, normed_one, inverse_one, pooled = edge_forward(
        order,
        *edge_blocks(edge_one),
        table_one,
        edge_low,
        edge_state,
        at_both,
        at_nodes,
        small_params[1],
        node_total,
        True,
    )
    pooled, arrived, cotangent_other = lax.optimization_barrier(
        (pooled, exchange(node_one, steps - 2, 1), swap(sent, "hid", 2))
    )
    node_one = jnp.concatenate([node_one, arrived], axis=0)
    masked = jnp.stack(ordered(sample_half, own_samples(masked), cotangent_other), axis=0)
    masked = double_up(masked, "hid", 0, 1).reshape(node_total, samples, latent)
    target = jnp.transpose(masked, (1, 0, 2))
    node_one = (node_one, exchange(node_one, steps - 1, 1))
    node_low, pooled_grad, node_grad, kept, sent, node_minor_one = node_pass(
        order,
        owners,
        (node_one, node_rows, 0),
        nodes,
        node_low_one,
        node_state,
        (pooled, swap(pooled, "hid", 1)),
        small_params[1],
        None,
        target,
        scaling,
        mask,
    )

    def from_edges(partial, returned):
        return partial + dot("hn,shl->snl", at_halo, returned)

    low, hidden_low, at_rows, partial, returned, edge_grad, edge_minor_one = edge_backward(
        order,
        *edge_blocks(edge_one),
        pooled_grad,
        None,
        normed_one,
        inverse_one,
        pre_one,
        at_receiver,
        at_both_t,
        small_params[1, 2:3],
        True,
        node_total,
    )
    low, *node_out = lax.optimization_barrier((low, *own_rows_exchanged(node_low)))
    node_out = all_samples(*node_out)
    chain_one = edge_weight_grads(
        owners,
        edge_low,
        table_one,
        hidden_low,
        at_rows,
        low,
        act_one,
        node_total,
        nodes,
        width,
        [kept, sent],
    )
    *returned, kept, sent = lax.optimization_barrier(
        (*neighbour_swaps(returned, halo_width), *chain_one)
    )
    returned, chain_one = from_neighbours(*returned), (kept, sent)
    partial = from_edges(partial, returned)
    chain_one = split(scatter_round(chain_one, steps - 1).astype(BF16), 2)
    other, *chain_one = lax.optimization_barrier((swap(partial.astype(BF16), "hid", 1), *chain_one))
    pooled_grad, node_grad, kept, sent, node_minor_zero = node_backward(
        order,
        owners,
        (node_zero, node_rows, 0),
        nodes,
        (node_grad, partial, other),
        node_low_zero,
        pooled_zero,
        node_pre,
        node_act,
        node_normed,
        node_inverse,
        small_params[0],
        mask,
    )
    low, hidden_low, at_rows, partial, returned, edge_input_grad, edge_minor_zero, hidden_sum = (
        edge_backward(
            order,
            *edge_blocks(edge_zero),
            pooled_grad,
            edge_grad,
            normed_zero,
            inverse_zero,
            pre_zero,
            at_receiver,
            at_both_t,
            small_params[0, 2:3],
            False,
            node_total,
        )
    )
    chain_one = split(scatter_round(chain_one, steps - 2, low), 2)
    chain_zero = split(scatter_round((kept, sent), steps - 1, low), 2)
    low = after(low, *chain_one, *chain_zero)
    chain_edge = edge_weight_grads(
        owners,
        edge_in_own,
        table_zero,
        hidden_sum,
        at_rows,
        low,
        act_zero,
        node_total,
        nodes,
        width,
        None,
    )
    kept, sent, one_arrived, zero_arrived, *returned = lax.optimization_barrier(
        (
            *chain_edge,
            exchange(chain_one[1], steps - 3, 1),
            exchange(chain_zero[1], steps - 2, 1),
            *neighbour_swaps(returned, halo_width),
        )
    )
    chain_one = chain_one[0].astype(F32) + one_arrived.astype(F32)
    chain_zero = split(chain_zero[0].astype(F32) + zero_arrived.astype(F32), 2)
    edge_arrived = exchange(sent, steps - 1, 1)
    kept, sent = split((kept.astype(F32) + edge_arrived.astype(F32)).astype(BF16), 2)
    zero_arrived = exchange(after(chain_zero[1], sent), steps - 3, 1)
    returned = after(returned, sent)
    chain_zero = chain_zero[0].astype(F32) + zero_arrived.astype(F32)
    for begin, end in reversed(z_rounds[1:]):
        chain_one = scatter_round(split(chain_one, 1 << (end - begin)), begin)
        chain_zero = scatter_round(split(chain_zero, 1 << (end - begin)), begin)
    begin, end = z_rounds[0]
    chain_one = split(chain_one, 1 << (end - begin))
    chain_zero = split(chain_zero, 1 << (end - begin))
    partial = from_edges(partial, from_neighbours(*returned))
    arrived, edge_input_grad, other, chain_zero, *others = lax.optimization_barrier(
        (
            exchange(sent, steps - 2, 1),
            edge_input_grad,
            swap(partial.astype(BF16), "hid", 1),
            chain_zero,
            *[exchange(chain_one[flips], begin, flips) for flips in range(1, len(chain_one))],
        )
    )
    layer_one_grads = chain_one[0]
    for piece in others:
        layer_one_grads = layer_one_grads + piece.astype(F32)
    layer_one_grads = layer_one_grads[0]
    chain_edge = split(kept + arrived.astype(F32), 2)
    chain_zero = after(chain_zero, chain_edge[1])
    arrived, *others = lax.optimization_barrier(
        (
            exchange(chain_edge[1], steps - 3, 1),
            *[exchange(chain_zero[flips], begin, flips) for flips in range(1, len(chain_zero))],
        )
    )
    node_zero_grads = chain_zero[0]
    for piece in others:
        node_zero_grads = node_zero_grads + piece.astype(F32)
    node_zero_grads = node_zero_grads[0]
    chain_edge = chain_edge[0] + arrived.astype(F32)
    halves = edge_input_grad.reshape(2, edge_part, latent)
    sent = lax.dynamic_index_in_dim(halves, 1 - sample_half, 0, keepdims=False).astype(BF16)
    kept = lax.dynamic_index_in_dim(halves, sample_half, 0, keepdims=False)
    node_grad = node_grad + (partial + other.astype(F32))
    grad_node = own_rows_exchanged(node_grad.astype(BF16))
    edge_zero_grads = scatter_rest(chain_edge, steps - 3)
    edge_zero_grads, arrived, *grad_node = lax.optimization_barrier(
        (edge_zero_grads, swap(sent, "hid", 2), *grad_node)
    )
    edge_input_grad = kept + arrived.astype(F32)
    grad_node = all_samples(*grad_node)

    node_one_grads, edge_one_grads = layer_one_grads[:node_rows], layer_one_grads[node_rows:]
    node_first_rows = node_rows - second_rows
    grads = [
        jnp.stack([edge_zero_grads[:first_rows], edge_one_grads[:first_rows]]),
        jnp.stack([edge_zero_grads[first_rows:].T, edge_one_grads[first_rows:].T]),
        jnp.stack([node_zero_grads[:node_first_rows], node_one_grads[:node_first_rows]]),
        jnp.stack([node_zero_grads[node_first_rows:].T, node_one_grads[node_first_rows:].T]),
    ]
    firsts = (edge_first_m, edge_second_m, node_first_m, node_second_m)
    seconds = (edge_first_v, edge_second_v, node_first_v, node_second_v)
    moment_list = [
        adam_terms(masters[place], grads[place], firsts[place], seconds[place], WEIGHT_DECAY)
        for place in range(4)
    ]
    update_local = jnp.stack(
        [jnp.sum(entry[2] * entry[2], axis=(1, 2)) for entry in moment_list], axis=1
    )
    squares = jnp.concatenate([weight_local.reshape(1, -1), update_local.reshape(1, -1)], axis=1)
    minor_packed = jnp.concatenate(
        [edge_minor_zero, node_minor_zero, edge_minor_one, node_minor_one]
        + [jnp.pad(squares, ((0, 0), (0, latent - squares.size)))],
        axis=0,
    )
    minor_packed = sum_everywhere(minor_packed)
    minor_total = minor_packed[: 8 * LAYERS].reshape(small_params.shape)
    squares = minor_packed[8 * LAYERS, : squares.size].reshape(2, *weight_local.shape)
    weight_squares, update_squares = squares[0], squares[1]
    weight_norm = jnp.sqrt(weight_squares)
    update_norm = jnp.sqrt(update_squares)
    new_weights = []
    for position in range(4):
        ratio = weight_norm[:, position] / update_norm[:, position]
        new_weights.append(
            masters[position] - learn_rate[0] * ratio[:, None, None] * moment_list[position][2]
        )
    small_first, small_second, small_update = adam_terms(
        small_params, minor_total, small_m, small_v, 0.0
    )
    small_wnorm = jnp.sqrt(jnp.sum(small_params * small_params, axis=2))
    small_unorm = jnp.sqrt(jnp.sum(small_update * small_update, axis=2))
    small_new = (
        small_params - learn_rate[0] * (small_wnorm / small_unorm)[:, :, None] * small_update
    )
    norms = jnp.stack(
        [
            jnp.concatenate([weight_norm, small_wnorm], axis=1),
            jnp.concatenate([update_norm, small_unorm], axis=1),
        ],
        axis=2,
    )
    return (
        node_out,
        grad_node,
        edge_input_grad.astype(BF16),
        *new_weights,
        *[entry[0] for entry in moment_list],
        *[entry[1] for entry in moment_list],
        *[weight.astype(BF16) for weight in new_weights],
        small_new,
        small_first,
        small_second,
        norms,
    )


def solution(mesh):
    whole = P()
    rows = P(None, "node", "hid")
    columns = P(None, "hid", "node")
    matrices = (rows, columns, rows, columns)
    in_specs = (
        P("node", None, None),
        P("node", None),
        P(("node", "hid"), None, None),
        P(("node", "hid")),
        P(("node", "hid"), None),
        P(),
        P("node"),
        P("node"),
        P("node", None),
        *matrices,
        *matrices,
        *matrices,
        whole,
        whole,
        whole,
        whole,
    )
    out_specs = (
        P(("node", "hid"), None, None),
        P(("node", "hid"), None, None),
        P(("node", "hid"), None),
        *matrices,
        *matrices,
        *matrices,
        *matrices,
        whole,
        whole,
        whole,
        whole,
    )
    return jax.shard_map(
        per_device, mesh=mesh, in_specs=in_specs, out_specs=out_specs, check_vma=False
    )
```
